32 devices in a mesh: expert: 4 (over z), head: 8 (over y, x, core).
Axes of the slice: x: 2, y: 2, z: 4, core: 2. Of those that a mesh axis runs over, the one named last changes fastest.
Arguments:
- tokens: bfloat16 [4096, 768], P(('expert', 'head')), may hold values from -6 to 6
- cotangent: float32 [4096, 768], P(('expert', 'head')), may hold values from -6 to 6
- lengths: int32 [32], P(('expert', 'head')), may hold values from 32 to 128, as said below
- routes: int32 [4096, 2], P('expert'), may hold values from 0 to 3, all different within a row; in each aligned block of 128 rows (0 to 127, 128 to 255, ...) at most 128 rows name the same one
- norm_gains: float32 [2, 768], P(None, ('expert', 'head')), may hold values from 0.5 to 1.5
- gains_first: float32 [2, 768], P(None, ('expert', 'head')), may hold values from -224 to 224
- gains_second: float32 [2, 768], P(None, ('expert', 'head')), may hold values from 1254.4 to 5017.6
- qkv_weight: float32 [768, 2304], P(('expert', 'head')), may hold values from -0.21875 to 0.21875
- qkv_first: float32 [768, 2304], P(('expert', 'head')), may hold values from -96 to 96
- qkv_second: float32 [768, 2304], P(('expert', 'head')), may hold values from 230.4 to 921.6
- out_weight: float32 [768, 768], P(None, ('expert', 'head')), may hold values from -1.25 to 1.25
- out_first: float32 [768, 768], P(None, ('expert', 'head')), may hold values from -32 to 32
- out_second: float32 [768, 768], P(None, ('expert', 'head')), may hold values from 25.6 to 102.4
- router_weight: float32 [768, 4], P(('expert', 'head')), may hold values from -0.15625 to 0.15625
- router_first: float32 [768, 4], P(('expert', 'head')), may hold values from -896 to 896
- router_second: float32 [768, 4], P(('expert', 'head')), may hold values from 20480 to 81920
- shared_in: float32 [768, 2, 2048], P('expert', None, 'head'), may hold values from -0.21875 to 0.21875
- shared_in_first: float32 [768, 2, 2048], P('expert', None, 'head'), may hold values from -96 to 96
- shared_in_second: float32 [768, 2, 2048], P('expert', None, 'head'), may hold values from 230.4 to 921.6
- shared_down: float32 [2048, 768], P('head', 'expert'), may hold values from -0.125 to 0.125
- shared_down_first: float32 [2048, 768], P('head', 'expert'), may hold values from -192 to 192
- shared_down_second: float32 [2048, 768], P('head', 'expert'), may hold values from 921.6 to 3686.4
- expert_in: float32 [4, 768, 2, 2048], P('expert', None, None, 'head'), may hold values from -0.21875 to 0.21875
- expert_in_first: float32 [4, 768, 2, 2048], P('expert', None, None, 'head'), may hold values from -32 to 32
- expert_in_second: float32 [4, 768, 2, 2048], P('expert', None, None, 'head'), may hold values from 28.8 to 115.2
- expert_down: float32 [4, 2048, 768], P('expert', 'head'), may hold values from -0.125 to 0.125
- expert_down_first: float32 [4, 2048, 768], P('expert', 'head'), may hold values from -64 to 64
- expert_down_second: float32 [4, 2048, 768], P('expert', 'head'), may hold values from 115.2 to 460.8
Outputs:
- layer_out: float32 [4096, 768], P(('expert', 'head'))
- input_grad: float32 [4096, 768], P(('expert', 'head'))
- gains_new: float32 [2, 768], P(None, ('expert', 'head'))
- gains_first_new: float32 [2, 768], P(None, ('expert', 'head'))
- gains_second_new: float32 [2, 768], P(None, ('expert', 'head'))
- qkv_new: float32 [768, 2304], P(('expert', 'head'))
- qkv_first_new: float32 [768, 2304], P(('expert', 'head'))
- qkv_second_new: float32 [768, 2304], P(('expert', 'head'))
- out_new: float32 [768, 768], P(None, ('expert', 'head'))
- out_first_new: float32 [768, 768], P(None, ('expert', 'head'))
- out_second_new: float32 [768, 768], P(None, ('expert', 'head'))
- router_new: float32 [768, 4], P(('expert', 'head'))
- router_first_new: float32 [768, 4], P(('expert', 'head'))
- router_second_new: float32 [768, 4], P(('expert', 'head'))
- shared_in_new: float32 [768, 2, 2048], P('expert', None, 'head')
- shared_in_first_new: float32 [768, 2, 2048], P('expert', None, 'head')
- shared_in_second_new: float32 [768, 2, 2048], P('expert', None, 'head')
- shared_down_new: float32 [2048, 768], P('head', 'expert')
- shared_down_first_new: float32 [2048, 768], P('head', 'expert')
- shared_down_second_new: float32 [2048, 768], P('head', 'expert')
- expert_in_new: float32 [4, 768, 2, 2048], P('expert', None, None, 'head')
- expert_in_first_new: float32 [4, 768, 2, 2048], P('expert', None, None, 'head')
- expert_in_second_new: float32 [4, 768, 2, 2048], P('expert', None, None, 'head')
- expert_down_new: float32 [4, 2048, 768], P('expert', 'head')
- expert_down_first_new: float32 [4, 2048, 768], P('expert', 'head')
- expert_down_second_new: float32 [4, 2048, 768], P('expert', 'head')
The draws below stay inside these ranges and needn't reach their ends.
Inputs may be any that keep to these rules, and one draw needn't show every extreme that they name: `lengths`: some slot is full in every draw. `routes`: the two experts of a token differ. Among the 128 tokens of one slot no expert is named more than 128 times, a bound that some block reaches.
All inputs are finite; a program needn't handle non-finite values.
Results may differ from the reference program's by a relative error of at most 0.018.
The reference program's roundings to bfloat16 on the way count: a program that leaves them out, or rounds other values in their place, can miss the bound.
Values may be sent and summed in bfloat16 or wider, within the bound.
A program may use at most 192 MiB of HBM per device.

```python
import math
import jax
import jax.numpy as jnp
import numpy as np
from jax import lax

D = 768
HEADS = 12
HDIM = 64
FF = 2048
FF_SH = 2048
SEQ = 128
STEP = 4
SLOTS = 32
TOKENS = 4096
EXPERTS = 4
CAP_DEV = 128


def draw_lengths(key, part):
    first_key, second_key = jax.random.split(jax.random.fold_in(key, 17))
    drawn = jax.random.randint(first_key, (SLOTS,), SEQ // 4, SEQ + 1)
    full_slot = jax.random.randint(second_key, (), 0, SLOTS)
    return jnp.where(jnp.arange(SLOTS) == full_slot, SEQ, drawn).astype(jnp.int32)


def strengthened(array, own_key, source, target, parts, factor):
    def block_of(dim):
        return (jnp.arange(array.shape[dim]) // (array.shape[dim] // parts)).reshape((-1,) + (1,) * (array.ndim - 1 - dim))

    near = jax.random.permutation(own_key, parts)[block_of(target)]
    other_side = (block_of(target) + parts // 2) % parts
    return jnp.where((block_of(source) == near) | (block_of(source) == other_side), factor * array, array)


def steps_of(own_key, dims, cuts, smallest, largest):
    def one(dim, blocks):
        steps = jax.random.uniform(jax.random.fold_in(jax.random.fold_in(own_key, 6), dim), (blocks,), jnp.float32, smallest / len(cuts), largest / len(cuts))
        return jnp.repeat(jnp.exp(steps), dims[dim] // blocks).reshape((-1,) + (1,) * (len(dims) - dim - 1))

    factor_of = one(*cuts[0])
    for cut in cuts[1:]:
        factor_of = factor_of * one(*cut)
    return factor_of


def routed_block(key, own, number, rows, amount, top, limit, slope):
    ranking = jax.random.permutation(key, amount)
    crowded, ordinary = load_shares(amount, rows * top, limit, slope, True), load_shares(amount, rows * top, limit, slope, False)
    places = jnp.arange(amount)

    def named(sizes, rotation):
        used = int((sizes > 0).sum())
        fixed = max(1, used // 4)
        shifted = fixed + (places - fixed + rotation * (used - fixed)) % max(1, amount - fixed)
        return jnp.zeros((amount,), jnp.int32).at[ranking[jnp.where(places < fixed, places, shifted)]].set(jnp.asarray(sizes, jnp.int32))

    sizes = jnp.where(number % 4 == 0, named(crowded, number // 4), named(ordinary, number - number // 4 - 1))
    mixed = jax.random.permutation(jax.random.fold_in(own, 3), amount)
    source_of, receiver = mixed[0:amount // 2 * 2:2], mixed[1:amount // 2 * 2:2]
    slack = jnp.minimum(sizes[source_of] - 1, limit - sizes[receiver]) // 2
    slack = jnp.where((source_of == ranking[0]) | (receiver == ranking[0]) | (sizes[receiver] == 0), 0, jnp.maximum(slack, 0))
    shifted = jax.random.randint(jax.random.fold_in(own, 4), (amount // 2,), 0, 1 << 20) % (slack + 1)
    sizes = sizes.at[source_of].add(-shifted).at[receiver].add(shifted)
    items = jnp.searchsorted(jnp.cumsum(sizes), jnp.arange(rows * top), side="right").astype(jnp.int32)
    table = items.reshape(top, rows).T
    table = table[jax.random.permutation(jax.random.fold_in(own, 1), rows)]
    rotation = jax.random.randint(jax.random.fold_in(own, 2), (rows, 1), 0, top)
    return jnp.take_along_axis(table, (jnp.arange(top)[None, :] + rotation) % top, axis=1)


def load_shares(number_of, total, limit, lean, full):
    weights = [(1 << 20) // math.isqrt(rank ** lean) + 1 for rank in range(1, number_of + 1)]
    largest = limit if full else min(limit, max(-(-total // number_of), total * weights[0] // sum(weights)))
    least = 1 if total - largest >= number_of - 1 else 0
    given, spare = [largest] + [least] * (number_of - 1), total - largest - least * (number_of - 1)
    while spare > 0:
        free = [i for i in range(1, number_of) if given[i] < largest] or [i for i in range(1, number_of) if given[i] < limit]
        mass, left = sum([weights[i] for i in free]), spare
        for i in free:
            addition = min(limit - given[i], max(1, left * weights[i] // mass), spare)
            given[i] = given[i] + addition
            spare = spare - addition
    return np.array(given)


def centred(key, dims, width, limit, pieces=(), kind=jnp.bfloat16):
    level = steps_of(key, dims, pieces, -0.22, 0.18) if pieces else 1.0
    values = jax.random.normal(key, dims, jnp.float32) * width * level
    return jnp.minimum(jnp.maximum(values, -limit), limit).astype(kind)


def gaussian_with(key, shape, scale, bound, cuts, heavy, kind=jnp.bfloat16):
    entries = scale * jax.random.normal(key, shape, jnp.float32)
    if cuts:
        entries = entries * steps_of(key, shape, cuts, -0.22, 0.18)
    return jnp.clip(strengthened(entries, jax.random.fold_in(key, 3), *heavy), -bound, bound).astype(kind)


def setup_inputs(seed: int = 0) -> dict:
    key_list = jax.random.split(jax.random.key(seed), 29)
    tokens = gaussian_with(key_list[0], (TOKENS, D), 1.0, 6.0, ((0, 32),), (0, 1, 32, 2.75))
    cotangent = gaussian_with(key_list[1], (TOKENS, D), 1.0, 6.0, ((0, 32),), (0, 1, 32, 2.75), jnp.float32)
    lengths = draw_lengths(jax.random.fold_in(key_list[28], 71), 0)
    routes_keys = jax.random.split(jax.random.fold_in(key_list[3], 1), TOKENS // SEQ)
    routes_turns = jax.random.permutation(jax.random.fold_in(key_list[3], 3), TOKENS // SEQ)
    routes = jax.vmap(lambda own, number: routed_block(jax.random.fold_in(key_list[3], 2), own, number, SEQ, EXPERTS, 2, CAP_DEV, 1))(routes_keys, routes_turns).reshape((TOKENS, 2))
    norm_gains = jnp.clip(1.0 + 0.1 * jax.random.normal(key_list[4], (2, D), jnp.float32), 0.5, 1.5)
    gains_first = centred(key_list[5], (2, D), (0.7 * (TOKENS * 5 // 8) ** 0.5), 224.0, ((1, 32),), jnp.float32)
    gains_second = jnp.clip(jnp.exp(math.log(5017.6) - 1.3862944 * jax.random.uniform(key_list[6], (2, D), jnp.float32) ** steps_of(key_list[6], (2, D), ((1, 32),), -0.2, 0.2)), 1254.4, 5017.6)
    qkv_weight = centred(key_list[7], (D, 3 * D), D ** -0.5, 0.21875, ((0, 32),), jnp.float32)
    qkv_first = centred(key_list[8], (D, 3 * D), (0.3 * (TOKENS * 5 // 8) ** 0.5), 96.0, ((0, 32),), jnp.float32)
    qkv_second = jnp.clip(jnp.exp(math.log(921.6) - 1.3862944 * jax.random.uniform(key_list[9], (D, 3 * D), jnp.float32) ** steps_of(key_list[9], (D, 3 * D), ((0, 32),), -0.2, 0.2)), 230.4, 921.6)
    out_weight = centred(key_list[10], (D, D), (4 * D // SEQ) ** -0.5, 1.25, ((1, 32),), jnp.float32)
    out_first = centred(key_list[11], (D, D), (0.1 * (TOKENS * 5 // 8) ** 0.5), 32.0, ((1, 32),), jnp.float32)
    out_second = jnp.clip(jnp.exp(math.log(102.4) - 1.3862944 * jax.random.uniform(key_list[12], (D, D), jnp.float32) ** steps_of(key_list[12], (D, D), ((1, 32),), -0.2, 0.2)), 25.6, 102.4)
    router_weight = centred(key_list[13], (D, EXPERTS), (2 * D) ** -0.5, 0.15625, ((0, 32),), jnp.float32)
    router_first = centred(key_list[14], (D, EXPERTS), (4.0 * (TOKENS * 5 // 4 // EXPERTS) ** 0.5), 896.0, ((0, 32),), jnp.float32)
    router_second = jnp.clip(jnp.exp(math.log(81920.0) - 1.3862944 * jax.random.uniform(key_list[15], (D, EXPERTS), jnp.float32) ** steps_of(key_list[15], (D, EXPERTS), ((0, 32),), -0.2, 0.2)), 20480.0, 81920.0)
    shared_in = centred(key_list[16], (D, 2, FF_SH), D ** -0.5, 0.21875, ((0, 4), (2, 8)), jnp.float32)
    shared_in_first = centred(key_list[17], (D, 2, FF_SH), (0.3 * (TOKENS * 5 // 8) ** 0.5), 96.0, ((0, 4), (2, 8)), jnp.float32)
    shared_in_second = jnp.clip(jnp.exp(math.log(921.6) - 1.3862944 * jax.random.uniform(key_list[18], (D, 2, FF_SH), jnp.float32) ** steps_of(key_list[18], (D, 2, FF_SH), ((0, 4), (2, 8)), -0.2, 0.2)), 230.4, 921.6)
    shared_down = centred(key_list[19], (FF_SH, D), FF_SH ** -0.5, 0.125, ((0, 8), (1, 4)), jnp.float32)
    shared_down_first = centred(key_list[20], (FF_SH, D), (0.6 * (TOKENS * 5 // 8) ** 0.5), 192.0, ((0, 8), (1, 4)), jnp.float32)
    shared_down_second = jnp.clip(jnp.exp(math.log(3686.4) - 1.3862944 * jax.random.uniform(key_list[21], (FF_SH, D), jnp.float32) ** steps_of(key_list[21], (FF_SH, D), ((0, 8), (1, 4)), -0.2, 0.2)), 921.6, 3686.4)
    expert_in = centred(key_list[22], (EXPERTS, D, 2, FF), D ** -0.5, 0.21875, ((0, 4), (3, 8)), jnp.float32)
    expert_in_first = centred(key_list[23], (EXPERTS, D, 2, FF), (0.15 * (TOKENS * 5 // 4 // EXPERTS) ** 0.5), 32.0, ((0, 4), (3, 8)), jnp.float32)
    expert_in_second = jnp.clip(jnp.exp(math.log(115.2) - 1.3862944 * jax.random.uniform(key_list[24], (EXPERTS, D, 2, FF), jnp.float32) ** steps_of(key_list[24], (EXPERTS, D, 2, FF), ((0, 4), (3, 8)), -0.2, 0.2)), 28.8, 115.2)
    expert_down = centred(key_list[25], (EXPERTS, FF, D), FF ** -0.5, 0.125, ((0, 4), (1, 8)), jnp.float32)
    expert_down_first = centred(key_list[26], (EXPERTS, FF, D), (0.3 * (TOKENS * 5 // 4 // EXPERTS) ** 0.5), 64.0, ((0, 4), (1, 8)), jnp.float32)
    expert_down_second = jnp.clip(jnp.exp(math.log(460.8) - 1.3862944 * jax.random.uniform(key_list[27], (EXPERTS, FF, D), jnp.float32) ** steps_of(key_list[27], (EXPERTS, FF, D), ((0, 4), (1, 8)), -0.2, 0.2)), 115.2, 460.8)
    return dict(tokens=tokens, cotangent=cotangent, lengths=lengths, routes=routes, norm_gains=norm_gains, gains_first=gains_first, gains_second=gains_second, qkv_weight=qkv_weight, qkv_first=qkv_first, qkv_second=qkv_second, out_weight=out_weight, out_first=out_first, out_second=out_second, router_weight=router_weight, router_first=router_first, router_second=router_second, shared_in=shared_in, shared_in_first=shared_in_first, shared_in_second=shared_in_second, shared_down=shared_down, shared_down_first=shared_down_first, shared_down_second=shared_down_second, expert_in=expert_in, expert_in_first=expert_in_first, expert_in_second=expert_in_second, expert_down=expert_down, expert_down_first=expert_down_first, expert_down_second=expert_down_second)


HIGH = lax.Precision.HIGHEST
NORM_EPS = 1e-06
BETA_FIRST = 0.5
BETA_SECOND = 0.5
ADAM_EPS = 1e-08
DECAY = 0.1
MASKED = -1e+30
ROPE_BASE = 10000.0

@jax.custom_vjp
def low(v):
    return lax.optimization_barrier(v.astype(jnp.bfloat16)).astype(jnp.float32)

@jax.custom_vjp
def low_back(v):
    return v

def low_keep(v):
    return (low(v), None)

def low_pass(kept, grad):
    return (grad,)

def back_keep(v):
    return (v, None)

def back_low(kept, grad):
    return (low(grad),)
low.defvjp(low_keep, low_pass)
low_back.defvjp(back_keep, back_low)

def rms_scaled(values, gain_vec):
    return values * lax.rsqrt(lax.optimization_barrier(jnp.mean(values * values, axis=-1, keepdims=True)) + NORM_EPS) * gain_vec

def rope_tables(row_count):
    half_dim = HDIM // 2
    positions = jnp.arange(row_count, dtype=jnp.float32)
    frequency = ROPE_BASE ** (-jnp.arange(half_dim, dtype=jnp.float32) / half_dim)
    angles = positions[:, None] * frequency[None, :]
    return (jnp.cos(angles)[:, None, :], jnp.sin(angles)[:, None, :])

def rotate(values, cosine_table, sine_table):
    half_dim = values.shape[-1] // 2
    first_half = values[..., :half_dim]
    second_half = values[..., half_dim:]
    return jnp.concatenate([first_half * cosine_table - second_half * sine_table, second_half * cosine_table + first_half * sine_table], axis=-1)

def attend_slot(slot_rows, length, gain_one, qkv_low, out_low):
    row_count = slot_rows.shape[0]
    normed = low(rms_scaled(slot_rows, gain_one))
    projected = low_back(jnp.dot(normed, qkv_low, precision=HIGH)).reshape(row_count, 3, HEADS, HDIM)
    cosine_table, sine_table = rope_tables(row_count)
    query_rows = low(rotate(projected[:, 0], cosine_table, sine_table))
    key_rows = low(rotate(projected[:, 1], cosine_table, sine_table))
    value_rows = low(projected[:, 2])
    scores = low_back(jnp.einsum('qhd,khd->hqk', query_rows, key_rows, precision=HIGH) * 0.125)
    positions = jnp.arange(row_count, dtype=jnp.int32)
    allowed = (positions[None, :] <= positions[:, None]) & (positions[None, :] < length)
    scores = jnp.where(allowed[None], scores, MASKED)
    row_top = lax.optimization_barrier(jnp.max(scores, axis=-1, keepdims=True))
    exponent = jnp.exp(scores - row_top)
    attn_probs = exponent / lax.optimization_barrier(jnp.sum(exponent, axis=-1, keepdims=True))
    context = low_back(jnp.einsum('hqk,khd->qhd', low(attn_probs), value_rows, precision=HIGH)).reshape(row_count, D)
    attended = low_back(jnp.dot(low(context), out_low, precision=HIGH))
    return slot_rows + attended

def expert_branch(row_block, weight_in, weight_down):
    mixed_pre = low_back(jnp.dot(row_block, weight_in.reshape(weight_in.shape[0], -1), precision=HIGH))
    hidden_width = weight_down.shape[0]
    gate_pre = mixed_pre[:, :hidden_width]
    up_pre = mixed_pre[:, hidden_width:]
    hidden = low(gate_pre * jax.nn.sigmoid(gate_pre) * up_pre)
    return jnp.dot(hidden, weight_down, precision=HIGH)

def layer_forward(weight_set, inputs, lengths, onehot, row_of, filled, live_rows):
    norm_gains, qkv_weight, out_weight, router_weight, shared_in, shared_down, expert_in, expert_down = weight_set
    gain_one = low(norm_gains[0])
    gain_two = low(norm_gains[1])
    qkv_low = low(qkv_weight)
    out_low = low(out_weight)
    per_step = math.gcd(SLOTS, max(1, 4096 // SEQ))
    grouped = inputs.reshape(SLOTS // per_step, per_step, SEQ, D)
    grouped_len = lengths.reshape(SLOTS // per_step, per_step)

    def attend_group(pair_in):
        return jax.checkpoint(jax.vmap(attend_slot, in_axes=(0, 0, None, None, None)))(pair_in[0], pair_in[1], gain_one, qkv_low, out_low)
    middle = lax.map(attend_group, (grouped, grouped_len)).reshape(TOKENS, D)
    normed_two = low(rms_scaled(middle, gain_two))
    logits = low_back(jnp.dot(normed_two, low(router_weight), precision=HIGH))
    chosen = lax.optimization_barrier(jnp.sum(logits[:, None, :] * onehot, axis=-1))
    chosen_top = lax.optimization_barrier(jnp.max(chosen, axis=-1, keepdims=True))
    chosen_exp = jnp.exp(chosen - chosen_top)
    gate_values = chosen_exp / lax.optimization_barrier(jnp.sum(chosen_exp, axis=-1, keepdims=True))
    gates_low = low(gate_values)
    shared_low_in = low(shared_in)
    shared_low_down = low(shared_down)
    block_rows = math.gcd(TOKENS, 4096)

    def shared_part(token_block):
        return jax.checkpoint(expert_branch)(token_block, shared_low_in, shared_low_down)
    shared_out = lax.map(shared_part, normed_two.reshape(TOKENS // block_rows, block_rows, D)).reshape(TOKENS, D)
    routed_in = (normed_two[row_of // 2] * filled[:, None]).reshape(EXPERTS, -1, D)

    def expert_part(triple):
        return jax.checkpoint(expert_branch)(triple[0], triple[1], triple[2])
    routed_out = lax.map(expert_part, (routed_in, low(expert_in), low(expert_down)))
    per_route = jnp.zeros((2 * TOKENS, D), jnp.float32).at[row_of].add(routed_out.reshape(-1, D) * filled[:, None])
    per_route = low_back(per_route.reshape(TOKENS, 2, D))
    mixed_out = low_back(shared_out + lax.optimization_barrier(jnp.sum(gates_low[:, :, None] * per_route, axis=1)))
    return live_rows[:, None] * (middle + mixed_out)

def adamw(weight, gradient, first_old, second_old, step_rate):
    first_new = BETA_FIRST * first_old + (1.0 - BETA_FIRST) * gradient
    second_new = BETA_SECOND * second_old + (1.0 - BETA_SECOND) * gradient * gradient
    first_hat = first_new / (1.0 - BETA_FIRST ** STEP)
    second_hat = second_new / (1.0 - BETA_SECOND ** STEP)
    new_weight = weight - step_rate * (first_hat / (jnp.sqrt(second_hat) + ADAM_EPS) + DECAY * weight)
    return (new_weight, first_new, second_new)

def step_rates():
    return (0.5, 1.5 / math.sqrt(D), 1.5 / math.sqrt(4 * D // SEQ), 1.0 / math.sqrt(D), 1.5 / math.sqrt(D), 1.5 / math.sqrt(FF_SH), 1.5 / math.sqrt(D), 1.5 / math.sqrt(FF))

def reference(tokens, cotangent, lengths, routes, norm_gains, gains_first, gains_second, qkv_weight, qkv_first, qkv_second, out_weight, out_first, out_second, router_weight, router_first, router_second, shared_in, shared_in_first, shared_in_second, shared_down, shared_down_first, shared_down_second, expert_in, expert_in_first, expert_in_second, expert_down, expert_down_first, expert_down_second):
    flat_routes = routes.reshape(-1).astype(jnp.int32)
    expert_ids = jnp.arange(EXPERTS, dtype=jnp.int32)
    hit_table = (flat_routes[:, None] == expert_ids[None, :]).astype(jnp.int32)
    rank_in = lax.optimization_barrier(jnp.sum((jnp.cumsum(hit_table, axis=0) - 1) * hit_table, axis=1))
    cap_all = SLOTS * CAP_DEV
    slot_of = (flat_routes * cap_all + rank_in).astype(jnp.int32)
    table_rows = jnp.zeros((EXPERTS * cap_all,), jnp.int32).at[slot_of].set(jnp.arange(2 * TOKENS, dtype=jnp.int32) + 1)
    filled = (table_rows > 0).astype(jnp.float32)
    row_of = jnp.maximum(table_rows - 1, 0).astype(jnp.int32)
    onehot = (routes[:, :, None] == expert_ids[None, None, :]).astype(jnp.float32)
    positions = jnp.arange(TOKENS, dtype=jnp.int32) % SEQ
    live_rows = (positions < jnp.repeat(lengths, SEQ)).astype(jnp.float32)
    weight_set = (norm_gains, qkv_weight, out_weight, router_weight, shared_in, shared_down, expert_in, expert_down)

    def forward_only(weight_args, inputs):
        return layer_forward(weight_args, inputs, lengths, onehot, row_of, filled, live_rows)
    layer_out, pullback = jax.vjp(forward_only, weight_set, tokens.astype(jnp.float32))
    weight_grads, input_grad = pullback(cotangent)
    firsts = (gains_first, qkv_first, out_first, router_first, shared_in_first, shared_down_first, expert_in_first, expert_down_first)
    seconds = (gains_second, qkv_second, out_second, router_second, shared_in_second, shared_down_second, expert_in_second, expert_down_second)
    updated = [adamw(weight, gradient, first_old, second_old, step_rate) for weight, gradient, first_old, second_old, step_rate in zip(weight_set, weight_grads, firsts, seconds, step_rates())]
    return (layer_out, input_grad, updated[0][0], updated[0][1], updated[0][2], updated[1][0], updated[1][1], updated[1][2], updated[2][0], updated[2][1], updated[2][2], updated[3][0], updated[3][1], updated[3][2], updated[4][0], updated[4][1], updated[4][2], updated[5][0], updated[5][1], updated[5][2], updated[6][0], updated[6][1], updated[6][2], updated[7][0], updated[7][1], updated[7][2])
```

```python
import math

import jax
import jax.numpy as jnp
from jax import lax
from jax.experimental import pallas as pl
from jax.experimental.pallas import tpu as pltpu
from jax.sharding import PartitionSpec as P

D = 768
HEADS = 12
HDIM = 64
FF = 2048
FF_SH = 2048
SEQ = 128
STEP = 4


NORM_EPS = 1e-06
BETA_FIRST = 0.5
BETA_SECOND = 0.5
ADAM_EPS = 1e-08
DECAY = 0.1
MASKED = -1e30
ROPE_BASE = 10000.0


def rope_tables(row_count):
    half_dim = HDIM // 2
    positions = jnp.arange(row_count, dtype=jnp.float32)
    frequency = ROPE_BASE ** (-jnp.arange(half_dim, dtype=jnp.float32) / half_dim)
    angles = positions[:, None] * frequency[None, :]
    return (jnp.cos(angles)[:, None, :], jnp.sin(angles)[:, None, :])


def rotate(values, cosine_table, sine_table):
    half_dim = values.shape[-1] // 2
    first_half = values[..., :half_dim]
    second_half = values[..., half_dim:]
    return jnp.concatenate(
        [
            first_half * cosine_table - second_half * sine_table,
            second_half * cosine_table + first_half * sine_table,
        ],
        axis=-1,
    )


def unrotate(gradient, cosine_table, sine_table):
    half_dim = gradient.shape[-1] // 2
    first_half = gradient[..., :half_dim]
    second_half = gradient[..., half_dim:]
    return jnp.concatenate(
        [
            first_half * cosine_table + second_half * sine_table,
            second_half * cosine_table - first_half * sine_table,
        ],
        axis=-1,
    )


def norm_forward(values, gain_vec):
    inverse = lax.rsqrt(jnp.mean(values * values, axis=-1, keepdims=True) + NORM_EPS)
    scaled = values * inverse
    return (scaled, inverse, scaled * gain_vec)


def norm_backward(grad_out, scaled, inverse, gain_vec):
    grad_scaled = grad_out * gain_vec
    grad_gain = jnp.sum(grad_out * scaled, axis=0)
    grad_in = inverse * (
        grad_scaled - scaled * jnp.mean(grad_scaled * scaled, axis=-1, keepdims=True)
    )
    return (grad_in, grad_gain)


def attention_scores(query_rows, key_rows, length):
    row_count = query_rows.shape[0]
    scores = (
        jnp.einsum("qhd,khd->hqk", query_rows, key_rows, preferred_element_type=jnp.float32) * 0.125
    )
    positions = jnp.arange(row_count, dtype=jnp.int32)
    allowed = (positions[None, :] <= positions[:, None]) & (positions[None, :] < length)
    return (jnp.where(allowed[None], scores, MASKED), allowed)


def expert_forward(row_block, weight_in, weight_down):
    mixed_pre = jnp.dot(row_block, weight_in, preferred_element_type=jnp.float32)
    hidden_width = weight_down.shape[0]
    gate_pre = mixed_pre[:, :hidden_width]
    up_pre = mixed_pre[:, hidden_width:]
    hidden = (gate_pre * jax.nn.sigmoid(gate_pre) * up_pre).astype(jnp.bfloat16)
    return (mixed_pre, hidden, jnp.dot(hidden, weight_down, preferred_element_type=jnp.float32))


def expert_backward(row_block, mixed_pre, hidden, grad_out, weight_in, weight_down):
    hidden_width = weight_down.shape[0]
    gate_pre = mixed_pre[:, :hidden_width]
    up_pre = mixed_pre[:, hidden_width:]
    grad_hidden = jnp.dot(grad_out, weight_down.T, preferred_element_type=jnp.float32)
    sigmoid_g = jax.nn.sigmoid(gate_pre)
    silu_g = gate_pre * sigmoid_g
    grad_gate = (grad_hidden * up_pre * sigmoid_g * (1.0 + gate_pre * (1.0 - sigmoid_g))).astype(
        jnp.bfloat16
    )
    grad_up = (grad_hidden * silu_g).astype(jnp.bfloat16)
    grad_mixed = jnp.concatenate([grad_gate, grad_up], axis=1)
    grad_down = jnp.dot(hidden.T, grad_out, preferred_element_type=jnp.float32)
    grad_weight_in = jnp.dot(row_block.T, grad_mixed, preferred_element_type=jnp.float32)
    grad_row_block = jnp.dot(grad_mixed, weight_in.T, preferred_element_type=jnp.float32)
    return (grad_row_block, grad_weight_in, grad_down)


def route_tables(route_rows, blocks, block_cap, expert_total):
    per_block = route_rows.reshape(blocks, -1)
    hit_table = (
        per_block[:, :, None] == jnp.arange(expert_total, dtype=jnp.int32)[None, None, :]
    ).astype(jnp.int32)
    entries = per_block.shape[1]
    earlier = jnp.tril(jnp.ones((entries, entries), jnp.bfloat16))
    running = jnp.einsum(
        "ij,bje->bie", earlier, hit_table.astype(jnp.bfloat16), preferred_element_type=jnp.float32
    ).astype(jnp.int32)
    rank_in = jnp.sum((running - 1) * hit_table, axis=2)
    offsets = jnp.arange(blocks, dtype=jnp.int32)[:, None] * block_cap
    dest_slot = (per_block * (blocks * block_cap) + offsets + rank_in).reshape(-1)
    source_row = (
        jnp.zeros((expert_total * blocks * block_cap,), jnp.int32)
        .at[dest_slot]
        .set(jnp.arange(dest_slot.shape[0], dtype=jnp.int32) + 1)
    )
    return (dest_slot, source_row)


def pack_tokens(token_rows, source_row):
    padded = jnp.concatenate(
        [jnp.zeros((1, token_rows.shape[1]), token_rows.dtype), token_rows], axis=0
    )
    pick_rows = jnp.where(source_row > 0, (source_row - 1) // 2 + 1, 0)
    return padded[pick_rows]


def pack_routes(route_values, source_row):
    padded = jnp.concatenate(
        [jnp.zeros((1, route_values.shape[1]), route_values.dtype), route_values], axis=0
    )
    return padded[source_row]


def adamw(weight, gradient, first_old, second_old, step_rate):
    first_new = BETA_FIRST * first_old + (1.0 - BETA_FIRST) * gradient
    second_new = BETA_SECOND * second_old + (1.0 - BETA_SECOND) * gradient * gradient
    first_hat = first_new / (1.0 - BETA_FIRST**STEP)
    second_hat = second_new / (1.0 - BETA_SECOND**STEP)
    new_weight = weight - step_rate * (
        first_hat / (jnp.sqrt(second_hat) + ADAM_EPS) + DECAY * weight
    )
    return (new_weight, first_new, second_new)


def routed_shards(
    tokens,
    cotangent,
    lengths,
    routes,
    norm_gains,
    gains_first,
    gains_second,
    qkv_weight,
    qkv_first,
    qkv_second,
    out_weight,
    out_first,
    out_second,
    router_weight,
    router_first,
    router_second,
    shared_in,
    shared_in_first,
    shared_in_second,
    shared_down,
    shared_down_first,
    shared_down_second,
    expert_in,
    expert_in_first,
    expert_in_second,
    expert_down,
    expert_down_first,
    expert_down_second,
):
    low_type = jnp.bfloat16
    seq_rows = tokens.shape[0]
    head_total = lax.axis_size("head")
    expert_total = lax.axis_size("expert")
    head_at = lax.axis_index("head")
    cap_dev = 4 * seq_rows // expert_total
    gains_all, qkv_all, out_all, router_all = (
        lax.all_gather(norm_gains.astype(low_type), ("expert", "head"), axis=1, tiled=True),
        lax.all_gather(qkv_weight.astype(low_type), ("expert", "head"), axis=0, tiled=True),
        lax.all_gather(out_weight.astype(low_type), ("expert", "head"), axis=1, tiled=True),
        lax.all_gather(router_weight.astype(low_type), ("expert", "head"), axis=0, tiled=True),
    )
    shared_in_all, shared_down_all = (
        lax.all_gather(shared_in.astype(low_type), "expert", axis=0, tiled=True),
        lax.all_gather(shared_down.astype(low_type), "expert", axis=1, tiled=True),
    )
    shared_in_flat = shared_in_all.reshape(D, -1)
    gain_one = gains_all[0].astype(jnp.float32)
    gain_two = gains_all[1].astype(jnp.float32)
    length = lengths[0]
    inputs = tokens.astype(jnp.float32)
    scaled_one, inverse_one, normed_one = norm_forward(inputs, gain_one)
    normed_low = normed_one.astype(low_type)
    projected = jnp.dot(normed_low, qkv_all, preferred_element_type=jnp.float32).reshape(
        seq_rows, 3, HEADS, HDIM
    )
    cosine_table, sine_table = rope_tables(seq_rows)
    query_rows = rotate(projected[:, 0], cosine_table, sine_table).astype(low_type)
    key_rows = rotate(projected[:, 1], cosine_table, sine_table).astype(low_type)
    value_rows = projected[:, 2].astype(low_type)
    scores, allowed = attention_scores(query_rows, key_rows, length)
    row_top = jnp.max(scores, axis=-1, keepdims=True)
    exponent = jnp.exp(scores - row_top)
    row_total = jnp.sum(exponent, axis=-1, keepdims=True)
    log_total = row_top + jnp.log(row_total)
    attn_probs = exponent / row_total
    context = (
        jnp.einsum(
            "hqk,khd->qhd",
            attn_probs.astype(low_type),
            value_rows,
            preferred_element_type=jnp.float32,
        )
        .reshape(seq_rows, D)
        .astype(low_type)
    )
    middle = inputs + jnp.dot(context, out_all, preferred_element_type=jnp.float32)
    scaled_two, inverse_two, normed_two = norm_forward(middle, gain_two)
    mixer_low = normed_two.astype(low_type)
    logits = jnp.dot(mixer_low, router_all, preferred_element_type=jnp.float32)
    own_routes = lax.dynamic_slice_in_dim(routes, head_at * seq_rows, seq_rows, 0)
    onehot = (
        own_routes[:, :, None] == jnp.arange(router_all.shape[1], dtype=jnp.int32)[None, None, :]
    ).astype(jnp.float32)
    chosen = jnp.sum(logits[:, None, :] * onehot, axis=-1)
    chosen_top = jnp.max(chosen, axis=-1, keepdims=True)
    chosen_exp = jnp.exp(chosen - chosen_top)
    gate_values = chosen_exp / jnp.sum(chosen_exp, axis=-1, keepdims=True)
    gates_low = gate_values.astype(low_type)
    group_rows, group_gates = (
        lax.all_gather(mixer_low, "head", axis=0, tiled=True),
        lax.all_gather(gates_low, "head", axis=0, tiled=True),
    )
    shared_mixed, shared_hidden, shared_out = expert_forward(
        group_rows, shared_in_flat, shared_down_all
    )
    dest_slot, source_row = route_tables(routes, head_total, cap_dev, expert_total)
    send_rows = pack_tokens(group_rows, source_row)
    expert_in_low = expert_in.astype(low_type)
    expert_down_low = expert_down.astype(low_type)
    weight_in = expert_in_low[0].reshape(D, -1)
    weight_down = expert_down_low[0]
    received = lax.all_to_all(
        send_rows.reshape(expert_total, -1, D), "expert", split_axis=0, concat_axis=0, tiled=True
    ).reshape(-1, D)
    expert_mixed, expert_hidden, expert_out = expert_forward(received, weight_in, weight_down)
    returned = (
        lax.all_to_all(
            expert_out.reshape(expert_total, -1, D).astype(jnp.bfloat16),
            "expert",
            split_axis=0,
            concat_axis=0,
            tiled=True,
        )
        .astype(jnp.float32)
        .reshape(-1, D)
    )
    routed = returned[dest_slot].reshape(-1, 2, D)
    partial_value = shared_out + jnp.sum(
        group_gates.astype(jnp.float32)[:, :, None] * routed, axis=1
    )
    mixed_out = lax.psum_scatter(
        partial_value.astype(jnp.bfloat16), "head", scatter_dimension=0, tiled=True
    ).astype(jnp.float32)
    live_rows = (jnp.arange(seq_rows, dtype=jnp.int32) < length).astype(jnp.float32)[:, None]
    layer_out = live_rows * (middle + mixed_out)
    grad_live = live_rows * cotangent
    grad_mix_low = grad_live.astype(low_type)
    group_grad = lax.all_gather(grad_mix_low, "head", axis=0, tiled=True)
    shared_row_grad, shared_grad_in, shared_grad_down = expert_backward(
        group_rows, shared_mixed, shared_hidden, group_grad, shared_in_flat, shared_down_all
    )
    group_grad_f = group_grad.astype(jnp.float32)
    grad_routed = (group_gates.astype(jnp.float32)[:, :, None] * group_grad_f[:, None, :]).astype(
        low_type
    )
    gate_grad_part = jnp.sum(group_grad_f[:, None, :] * routed, axis=-1)
    grad_send = pack_routes(grad_routed.reshape(-1, D), source_row)
    grad_received = lax.all_to_all(
        grad_send.reshape(expert_total, -1, D), "expert", split_axis=0, concat_axis=0, tiled=True
    ).reshape(-1, D)
    rows_grad, grad_in_local, grad_down_local = expert_backward(
        received, expert_mixed, expert_hidden, grad_received, weight_in, weight_down
    )
    rows_back = lax.all_to_all(
        rows_grad.reshape(expert_total, -1, D), "expert", split_axis=0, concat_axis=0, tiled=True
    ).reshape(-1, D)
    per_token = jnp.sum(rows_back[dest_slot].reshape(-1, 2, D), axis=1)
    rows_part = shared_row_grad + per_token
    grad_in_slice = grad_in_local.reshape(1, D, 2, -1)
    grad_down_slice = grad_down_local[None]
    grad_rows_own, grad_gates = (
        lax.psum_scatter(rows_part, "head", scatter_dimension=0, tiled=True),
        lax.psum_scatter(gate_grad_part, "head", scatter_dimension=0, tiled=True),
    )
    gate_dot = jnp.sum(gate_values * grad_gates, axis=-1, keepdims=True)
    grad_chosen = gate_values * (grad_gates - gate_dot)
    grad_logits = jnp.sum(grad_chosen[:, :, None] * onehot, axis=1).astype(low_type)
    grad_router = jnp.dot(mixer_low.T, grad_logits, preferred_element_type=jnp.float32)
    grad_normed_two = grad_rows_own + jnp.dot(
        grad_logits, router_all.T, preferred_element_type=jnp.float32
    )
    grad_from_norm, grad_gain_two = norm_backward(
        grad_normed_two, scaled_two, inverse_two, gain_two
    )
    grad_middle = grad_live + grad_from_norm
    grad_att_low = grad_middle.astype(low_type)
    grad_out_w = jnp.dot(context.T, grad_att_low, preferred_element_type=jnp.float32)
    grad_context = (
        jnp.dot(grad_att_low, out_all.T, preferred_element_type=jnp.float32)
        .astype(low_type)
        .reshape(seq_rows, HEADS, HDIM)
    )
    scores_again, allowed_again = attention_scores(query_rows, key_rows, length)
    probs_again = jnp.where(allowed_again[None], jnp.exp(scores_again - log_total), 0.0)
    grad_probs = jnp.einsum(
        "qhd,khd->hqk", grad_context, value_rows, preferred_element_type=jnp.float32
    )
    grad_value = jnp.einsum(
        "hqk,qhd->khd",
        probs_again.astype(low_type),
        grad_context,
        preferred_element_type=jnp.float32,
    )
    row_dot = jnp.sum(grad_probs * probs_again, axis=-1, keepdims=True)
    grad_scores = (probs_again * (grad_probs - row_dot)).astype(low_type)
    grad_query = (
        jnp.einsum("hqk,khd->qhd", grad_scores, key_rows, preferred_element_type=jnp.float32)
        * 0.125
    )
    grad_key = (
        jnp.einsum("hqk,qhd->khd", grad_scores, query_rows, preferred_element_type=jnp.float32)
        * 0.125
    )
    grad_projected = (
        jnp.stack(
            [
                unrotate(grad_query, cosine_table, sine_table),
                unrotate(grad_key, cosine_table, sine_table),
                grad_value,
            ],
            axis=1,
        )
        .reshape(seq_rows, 3 * D)
        .astype(low_type)
    )
    grad_qkv = jnp.dot(normed_low.T, grad_projected, preferred_element_type=jnp.float32)
    grad_normed_one = jnp.dot(grad_projected, qkv_all.T, preferred_element_type=jnp.float32)
    grad_input_norm, grad_gain_one = norm_backward(
        grad_normed_one, scaled_one, inverse_one, gain_one
    )
    input_grad = grad_middle + grad_input_norm
    gains_grad = jnp.stack([grad_gain_one, grad_gain_two], axis=0)
    gains_part, qkv_part, out_part, router_part = (
        lax.psum_scatter(gains_grad, ("expert", "head"), scatter_dimension=1, tiled=True),
        lax.psum_scatter(grad_qkv, ("expert", "head"), scatter_dimension=0, tiled=True),
        lax.psum_scatter(grad_out_w, ("expert", "head"), scatter_dimension=1, tiled=True),
        lax.psum_scatter(grad_router, ("expert", "head"), scatter_dimension=0, tiled=True),
    )
    shared_in_part, shared_down_part = (
        lax.psum_scatter(
            shared_grad_in.reshape(D, 2, -1).astype(jnp.bfloat16),
            "expert",
            scatter_dimension=0,
            tiled=True,
        ).astype(jnp.float32),
        lax.psum_scatter(
            shared_grad_down.astype(jnp.bfloat16), "expert", scatter_dimension=1, tiled=True
        ).astype(jnp.float32),
    )
    gains_new, gains_first_new, gains_second_new = adamw(
        norm_gains, gains_part, gains_first, gains_second, 0.5
    )
    qkv_new, qkv_first_new, qkv_second_new = adamw(
        qkv_weight, qkv_part, qkv_first, qkv_second, 1.5 / math.sqrt(D)
    )
    out_new, out_first_new, out_second_new = adamw(
        out_weight, out_part, out_first, out_second, 1.5 / math.sqrt(4 * D // SEQ)
    )
    router_new, router_first_new, router_second_new = adamw(
        router_weight, router_part, router_first, router_second, 1.0 / math.sqrt(D)
    )
    shin_new, shin_first_new, shin_second_new = adamw(
        shared_in, shared_in_part, shared_in_first, shared_in_second, 1.5 / math.sqrt(D)
    )
    shdown_new, shdown_first_new, shdown_second_new = adamw(
        shared_down, shared_down_part, shared_down_first, shared_down_second, 1.5 / math.sqrt(FF_SH)
    )
    exin_new, exin_first_new, exin_second_new = adamw(
        expert_in, grad_in_slice, expert_in_first, expert_in_second, 1.5 / math.sqrt(D)
    )
    exdown_new, exdown_first_new, exdown_second_new = adamw(
        expert_down, grad_down_slice, expert_down_first, expert_down_second, 1.5 / math.sqrt(FF)
    )
    return (
        layer_out,
        input_grad,
        gains_new,
        gains_first_new,
        gains_second_new,
        qkv_new,
        qkv_first_new,
        qkv_second_new,
        out_new,
        out_first_new,
        out_second_new,
        router_new,
        router_first_new,
        router_second_new,
        shin_new,
        shin_first_new,
        shin_second_new,
        shdown_new,
        shdown_first_new,
        shdown_second_new,
        exin_new,
        exin_first_new,
        exin_second_new,
        exdown_new,
        exdown_first_new,
        exdown_second_new,
    )


MESH = pl.DeviceIdType.MESH
GROUPS = 4
PLANE = 8
ALL = GROUPS * PLANE


def place():
    group, member = lax.axis_index("expert"), lax.axis_index("head")
    core, column, row = member % 2, (member // 2) % 2, member // 4
    twin = member + 1 - 2 * core
    beside, across = member + 2 - 4 * column, member + 4 - 8 * row
    near = beside * (1 - core) + across * core
    far = across * (1 - core) + beside * core
    corner = member + (2 - 4 * column) + (4 - 8 * row)
    return (group, member, core, twin, near, far, corner)


def meet(group, member, twin, near, far):
    barrier = pltpu.get_barrier_semaphore()
    others = [(group, twin), (group, near), (group, far)]
    others += [((group + step) % GROUPS, member) for step in (1, 2, 3)]
    for other in others:
        pl.semaphore_signal(barrier, inc=1, device_id=other, device_id_type=MESH)
    pl.semaphore_wait(barrier, len(others))


def gather_kernel(own_ref, all_ref, send_sem, recv_sem, local_sem):
    group, member, core, twin, near, far, corner = place()
    meet(group, member, twin, near, far)
    mine = group * PLANE + member
    started = []

    def send(source, slot, device):
        copy = pltpu.make_async_remote_copy(
            src_ref=source,
            dst_ref=all_ref.at[slot],
            send_sem=send_sem.at[len(started)],
            recv_sem=recv_sem.at[slot],
            device_id=device,
            device_id_type=MESH,
        )
        copy.start()
        started.append(copy)

    def arrive(slot):
        pltpu.make_async_remote_copy(
            src_ref=own_ref,
            dst_ref=all_ref.at[slot],
            send_sem=send_sem.at[0],
            recv_sem=recv_sem.at[slot],
            device_id=(group, twin),
            device_id_type=MESH,
        ).wait_recv()

    local = pltpu.make_async_copy(own_ref, all_ref.at[mine], local_sem)
    local.start()
    for step in (1, 3, 2):
        send(own_ref, mine, ((group + step) % GROUPS, member))
    for partner in (near, far, twin):
        send(own_ref, mine, (group, partner))
    for step in (0, 1, 3, 2):
        base = (group + step) % GROUPS * PLANE
        if step:
            arrive(base + member)
            for partner in (near, far, twin):
                send(all_ref.at[base + member], base + member, (group, partner))
        arrive(base + near)
        for partner in (far, twin):
            send(all_ref.at[base + near], base + near, (group, partner))
    for step in (0, 1, 3, 2):
        base = (group + step) % GROUPS * PLANE
        for origin in (far, corner):
            arrive(base + origin)
            send(all_ref.at[base + origin], base + origin, (group, twin))
    for other in range(GROUPS):
        for pair in range(PLANE // 2):
            arrive(other * PLANE + pair * 2 + 1 - core)
    for copy in started:
        copy.wait_send()
    local.wait()


def gather(shard, collective):
    return pl.pallas_call(
        gather_kernel,
        out_shape=jax.ShapeDtypeStruct((ALL,) + shard.shape, shard.dtype),
        in_specs=[pl.BlockSpec(memory_space=pltpu.VMEM)],
        out_specs=pl.BlockSpec(memory_space=pltpu.VMEM),
        scratch_shapes=[
            pltpu.SemaphoreType.DMA((ALL - 1,)),
            pltpu.SemaphoreType.DMA((ALL,)),
            pltpu.SemaphoreType.DMA(()),
        ],
        compiler_params=pltpu.CompilerParams(
            collective_id=collective, has_side_effects=True, vmem_limit_bytes=48 << 20
        ),
    )(shard)


def scatter_kernel(
    part_ref, sum_ref, twin_buf, far_buf, near_buf, group_buf, send_sem, twin_sem, far_sem, near_sem, group_sem
):
    group, member, core, twin, near, far, corner = place()
    meet(group, member, twin, near, far)
    started = []

    def send(source, target, semaphore, device):
        copy = pltpu.make_async_remote_copy(
            src_ref=source,
            dst_ref=target,
            send_sem=send_sem.at[len(started)],
            recv_sem=semaphore,
            device_id=device,
            device_id_type=MESH,
        )
        copy.start()
        started.append(copy)

    def arrive(target, semaphore):
        pltpu.make_async_remote_copy(
            src_ref=target,
            dst_ref=target,
            send_sem=send_sem.at[0],
            recv_sem=semaphore,
            device_id=(group, twin),
            device_id_type=MESH,
        ).wait_recv()

    def add(target, other):
        target[...] = (target[...].astype(jnp.float32) + other[...].astype(jnp.float32)).astype(
            target.dtype
        )

    order = (2, 1, 3, 0)
    twin_of = {}
    for step in order:
        base = (group + step) % GROUPS
        for spot, origin in enumerate((corner, far, near, member)):
            slot = base * 4 + origin // 2
            theirs = base * PLANE + origin // 2 * 2 + 1 - core
            send(part_ref.at[theirs], twin_buf.at[slot], twin_sem.at[slot], (group, twin))

    def from_twin(base, origin):
        slot = base * 4 + origin // 2
        arrive(twin_buf.at[slot], twin_sem.at[slot])
        add(twin_buf.at[slot], part_ref.at[base * PLANE + origin])
        return twin_buf.at[slot]

    for step in order:
        base = (group + step) % GROUPS
        for spot, origin in ((0, corner), (1, far)):
            ready = from_twin(base, origin)
            slot = base * 2 + spot
            send(ready, far_buf.at[slot], far_sem.at[slot], (group, far))
    for step in order:
        base = (group + step) % GROUPS
        ready = from_twin(base, near)
        slot = base * 2
        arrive(far_buf.at[slot], far_sem.at[slot])
        add(ready, far_buf.at[slot])
        send(ready, near_buf.at[base], near_sem.at[base], (group, near))
    total = None
    for step in order:
        base = (group + step) % GROUPS
        ready = from_twin(base, member)
        slot = base * 2 + 1
        arrive(far_buf.at[slot], far_sem.at[slot])
        add(ready, far_buf.at[slot])
        arrive(near_buf.at[base], near_sem.at[base])
        if step:
            add(ready, near_buf.at[base])
            send(ready, group_buf.at[step - 1], group_sem.at[step - 1], (base, member))
        else:
            sum_ref[...] = ready[...].astype(jnp.float32) + near_buf[base].astype(jnp.float32)
    for step in (1, 3, 2):
        arrive(group_buf.at[step - 1], group_sem.at[step - 1])
        sum_ref[...] += group_buf[step - 1].astype(jnp.float32)
    for copy in started:
        copy.wait_send()


def scatter(parts, collective):
    block = parts.shape[1:]
    kind = parts.dtype
    return pl.pallas_call(
        scatter_kernel,
        out_shape=jax.ShapeDtypeStruct(block, jnp.float32),
        in_specs=[pl.BlockSpec(memory_space=pltpu.VMEM)],
        out_specs=pl.BlockSpec(memory_space=pltpu.VMEM),
        scratch_shapes=[
            pltpu.VMEM((16,) + block, kind),
            pltpu.VMEM((8,) + block, kind),
            pltpu.VMEM((4,) + block, kind),
            pltpu.VMEM((3,) + block, kind),
            pltpu.SemaphoreType.DMA((16 + 8 + 4 + 3,)),
            pltpu.SemaphoreType.DMA((16,)),
            pltpu.SemaphoreType.DMA((8,)),
            pltpu.SemaphoreType.DMA((4,)),
            pltpu.SemaphoreType.DMA((3,)),
        ],
        compiler_params=pltpu.CompilerParams(
            collective_id=collective, has_side_effects=True, vmem_limit_bytes=48 << 20
        ),
    )(parts)


def dense_shards(
    tokens,
    cotangent,
    lengths,
    routes,
    norm_gains,
    gains_first,
    gains_second,
    qkv_weight,
    qkv_first,
    qkv_second,
    out_weight,
    out_first,
    out_second,
    router_weight,
    router_first,
    router_second,
    shared_in,
    shared_in_first,
    shared_in_second,
    shared_down,
    shared_down_first,
    shared_down_second,
    expert_in,
    expert_in_first,
    expert_in_second,
    expert_down,
    expert_down_first,
    expert_down_second,
):
    low_type = jnp.bfloat16
    seq_rows = tokens.shape[0]
    group_at, head_at = lax.axis_index("expert"), lax.axis_index("head")
    length = lengths[0]
    live_rows = (jnp.arange(seq_rows, dtype=jnp.int32) < length).astype(jnp.float32)[:, None]
    grad_live = live_rows * cotangent
    grad_all = gather(grad_live.astype(low_type), 0).reshape(-1, D)
    small = jnp.concatenate([router_weight, norm_gains.T], axis=1)
    small = jnp.pad(small, ((0, 0), (0, 128 - small.shape[1])))
    owned = jnp.concatenate([qkv_weight, out_weight.T, small], axis=1).astype(low_type)
    weights = gather(owned, 1).reshape(D, -1)
    qkv_all = weights[:, : 3 * D]
    out_turned = weights[:, 3 * D : 4 * D]
    router_all = weights[:, 4 * D : 4 * D + 4]
    gain_one = weights[:, 4 * D + 4].astype(jnp.float32)
    gain_two = weights[:, 4 * D + 5].astype(jnp.float32)
    width = FF_SH // ALL
    shared_pieces = jnp.concatenate(
        [
            shared_in.astype(low_type).reshape(-1, 2, GROUPS, width).transpose(2, 0, 1, 3).reshape(GROUPS, -1, 2 * width),
            shared_down.astype(low_type).T.reshape(-1, GROUPS, width).transpose(1, 0, 2),
        ],
        axis=2,
    )
    shared_low = lax.all_to_all(
        shared_pieces, "expert", split_axis=0, concat_axis=0, tiled=True
    ).reshape(D, 3 * width)
    hidden_width = expert_down.shape[1]
    weight_in = jnp.concatenate(
        [expert_in.astype(low_type).reshape(D, -1), shared_low[:, : 2 * width]], axis=1
    )
    weight_down = jnp.concatenate(
        [expert_down.astype(low_type)[0], shared_low[:, 2 * width :].T], axis=0
    )

    inputs = tokens.astype(jnp.float32)
    scaled_one, inverse_one, normed_one = norm_forward(inputs, gain_one)
    normed_low = normed_one.astype(low_type)
    projected = jnp.dot(normed_low, qkv_all, preferred_element_type=jnp.float32).reshape(
        seq_rows, 3, HEADS, HDIM
    )
    cosine_table, sine_table = rope_tables(seq_rows)
    query_rows = rotate(projected[:, 0], cosine_table, sine_table).astype(low_type)
    key_rows = rotate(projected[:, 1], cosine_table, sine_table).astype(low_type)
    value_rows = projected[:, 2].astype(low_type)
    scores, allowed = attention_scores(query_rows, key_rows, length)
    row_top = jnp.max(scores, axis=-1, keepdims=True)
    exponent = jnp.exp(scores - row_top)
    row_total = jnp.sum(exponent, axis=-1, keepdims=True)
    attn_probs = exponent / row_total
    probs_low = attn_probs.astype(low_type)
    context = (
        jnp.einsum("hqk,khd->qhd", probs_low, value_rows, preferred_element_type=jnp.float32)
        .reshape(seq_rows, D)
        .astype(low_type)
    )
    middle = inputs + lax.dot_general(
        context, out_turned, (((1,), (1,)), ((), ())), preferred_element_type=jnp.float32
    )
    scaled_two, inverse_two, normed_two = norm_forward(middle, gain_two)
    mixer_low = normed_two.astype(low_type)
    logits = jnp.dot(mixer_low, router_all, preferred_element_type=jnp.float32)
    own_routes = lax.dynamic_slice_in_dim(routes, head_at * seq_rows, seq_rows, 0)
    onehot = (
        own_routes[:, :, None] == jnp.arange(GROUPS, dtype=jnp.int32)[None, None, :]
    ).astype(jnp.float32)
    chosen = jnp.sum(logits[:, None, :] * onehot, axis=-1)
    chosen_top = jnp.max(chosen, axis=-1, keepdims=True)
    chosen_exp = jnp.exp(chosen - chosen_top)
    gate_values = chosen_exp / jnp.sum(chosen_exp, axis=-1, keepdims=True)
    gates_low = gate_values.astype(low_type)
    gate_table = jnp.sum(gates_low.astype(jnp.float32)[:, :, None] * onehot, axis=1)
    gate_rows = jnp.pad(gate_table.astype(low_type).T, ((0, 16 - GROUPS), (0, D - seq_rows)))
    mixer_all = gather(jnp.concatenate([mixer_low, gate_rows], axis=0), 2)
    rows_all = mixer_all[:, :seq_rows].reshape(-1, D)
    gate_own = lax.dynamic_slice_in_dim(mixer_all, seq_rows + group_at, 1, 1)[:, 0, :seq_rows]
    gate_own = gate_own.reshape(-1, 1).astype(jnp.float32)

    mixed = jnp.dot(rows_all, weight_in, preferred_element_type=jnp.float32)
    grad_hidden = lax.dot_general(
        grad_all, weight_down, (((1,), (1,)), ((), ())), preferred_element_type=jnp.float32
    )

    def units(gate_pre, up_pre, hidden_grad, scale):
        sigmoid_g = jax.nn.sigmoid(gate_pre)
        silu_g = gate_pre * sigmoid_g
        hidden = (silu_g * up_pre).astype(low_type)
        gate_part = jnp.sum(hidden.astype(jnp.float32) * hidden_grad, axis=-1)
        if scale is not None:
            hidden_grad = hidden_grad * scale
            hidden = (hidden.astype(jnp.float32) * scale).astype(low_type)
        grad_gate = hidden_grad * up_pre * sigmoid_g * (1.0 + gate_pre * (1.0 - sigmoid_g))
        return (hidden, grad_gate.astype(low_type), (hidden_grad * silu_g).astype(low_type), gate_part)

    hw = hidden_width
    hidden_e, grad_gate_e, grad_up_e, gate_part = units(
        mixed[:, :hw], mixed[:, hw : 2 * hw], grad_hidden[:, :hw], gate_own
    )
    hidden_s, grad_gate_s, grad_up_s, _ = units(
        mixed[:, 2 * hw : 2 * hw + width], mixed[:, 2 * hw + width :], grad_hidden[:, hw:], None
    )
    hidden = jnp.concatenate([hidden_e, hidden_s], axis=1)
    grad_mixed = jnp.concatenate([grad_gate_e, grad_up_e, grad_gate_s, grad_up_s], axis=1)
    out_part = jnp.dot(hidden, weight_down, preferred_element_type=low_type)
    grad_down = lax.dot_general(
        hidden, grad_all, (((0,), (0,)), ((), ())), preferred_element_type=jnp.float32
    )
    grad_in = lax.dot_general(
        rows_all, grad_mixed, (((0,), (0,)), ((), ())), preferred_element_type=jnp.float32
    )
    rows_part = lax.dot_general(
        grad_mixed, weight_in, (((1,), (1,)), ((), ())), preferred_element_type=low_type
    )
    gate_part = jnp.where(
        jnp.arange(16)[None, :, None] == group_at, gate_part.reshape(ALL, 1, seq_rows), 0.0
    ).astype(low_type)
    gate_part = jnp.pad(gate_part, ((0, 0), (0, 0), (0, D - seq_rows)))
    back = scatter(jnp.concatenate([rows_part.reshape(ALL, seq_rows, D), gate_part], axis=1), 3)
    mixed_out = scatter(out_part.reshape(ALL, seq_rows, D), 4)
    layer_out = live_rows * (middle + mixed_out)
    grad_rows_own = back[:seq_rows]
    grad_gates = jnp.sum(back[seq_rows : seq_rows + GROUPS, :seq_rows].T[:, None, :] * onehot, axis=-1)

    gate_dot = jnp.sum(gate_values * grad_gates, axis=-1, keepdims=True)
    grad_chosen = gate_values * (grad_gates - gate_dot)
    grad_logits = jnp.sum(grad_chosen[:, :, None] * onehot, axis=1).astype(low_type)
    grad_router = jnp.dot(mixer_low.T, grad_logits, preferred_element_type=jnp.float32)
    grad_normed_two = grad_rows_own + jnp.dot(
        grad_logits, router_all.T, preferred_element_type=jnp.float32
    )
    grad_from_norm, grad_gain_two = norm_backward(
        grad_normed_two, scaled_two, inverse_two, gain_two
    )
    grad_middle = grad_live + grad_from_norm
    grad_att_low = grad_middle.astype(low_type)
    grad_out_turned = jnp.dot(grad_att_low.T, context, preferred_element_type=jnp.float32)
    grad_context = (
        jnp.dot(grad_att_low, out_turned, preferred_element_type=jnp.float32)
        .astype(low_type)
        .reshape(seq_rows, HEADS, HDIM)
    )
    grad_probs = jnp.einsum(
        "qhd,khd->hqk", grad_context, value_rows, preferred_element_type=jnp.float32
    )
    grad_value = jnp.einsum(
        "hqk,qhd->khd", probs_low, grad_context, preferred_element_type=jnp.float32
    )
    row_dot = jnp.sum(grad_probs * attn_probs, axis=-1, keepdims=True)
    grad_scores = (attn_probs * (grad_probs - row_dot)).astype(low_type)
    grad_query = (
        jnp.einsum("hqk,khd->qhd", grad_scores, key_rows, preferred_element_type=jnp.float32)
        * 0.125
    )
    grad_key = (
        jnp.einsum("hqk,qhd->khd", grad_scores, query_rows, preferred_element_type=jnp.float32)
        * 0.125
    )
    grad_projected = (
        jnp.stack(
            [
                unrotate(grad_query, cosine_table, sine_table),
                unrotate(grad_key, cosine_table, sine_table),
                grad_value,
            ],
            axis=1,
        )
        .reshape(seq_rows, 3 * D)
        .astype(low_type)
    )
    grad_qkv = jnp.dot(normed_low.T, grad_projected, preferred_element_type=low_type)
    grad_normed_one = lax.dot_general(
        grad_projected, qkv_all, (((1,), (1,)), ((), ())), preferred_element_type=jnp.float32
    )
    grad_input_norm, grad_gain_one = norm_backward(
        grad_normed_one, scaled_one, inverse_one, gain_one
    )
    input_grad = grad_middle + grad_input_norm
    grad_small = jnp.concatenate(
        [grad_router, grad_gain_one[:, None], grad_gain_two[:, None]], axis=1
    )
    grad_small = jnp.pad(grad_small, ((0, 0), (0, 128 - grad_small.shape[1])))
    grad_owned = jnp.concatenate(
        [grad_qkv, grad_out_turned.astype(low_type), grad_small.astype(low_type)], axis=1
    )
    summed = scatter(grad_owned.reshape(ALL, D // ALL, -1), 5)
    qkv_part = summed[:, : 3 * D]
    out_part_grad = summed[:, 3 * D : 4 * D].T
    router_part = summed[:, 4 * D : 4 * D + 4]
    gains_part = summed[:, 4 * D + 4 : 4 * D + 6].T

    shared_grad = jnp.concatenate(
        [grad_in[:, 2 * hw :].astype(low_type), grad_down[hw:].T.astype(low_type)], axis=1
    ).reshape(GROUPS, -1, 3 * width)
    shared_grad = lax.all_to_all(
        shared_grad, "expert", split_axis=0, concat_axis=0, tiled=True
    ).astype(jnp.float32)
    shared_in_part = (
        shared_grad[:, :, : 2 * width].reshape(GROUPS, -1, 2, width).transpose(1, 2, 0, 3)
    ).reshape(shared_in.shape)
    shared_down_part = (
        shared_grad[:, :, 2 * width :].transpose(1, 0, 2).reshape(shared_down.shape[1], -1).T
    )
    grad_in_slice = grad_in[:, : 2 * hw].reshape(1, D, 2, hw)
    grad_down_slice = grad_down[:hw][None]
    results = [layer_out, input_grad]
    for weight, gradient, first, second, rate in (
        (norm_gains, gains_part, gains_first, gains_second, 0.5),
        (qkv_weight, qkv_part, qkv_first, qkv_second, 1.5 / math.sqrt(D)),
        (out_weight, out_part_grad, out_first, out_second, 1.5 / math.sqrt(4 * D // SEQ)),
        (router_weight, router_part, router_first, router_second, 1.0 / math.sqrt(D)),
        (shared_in, shared_in_part, shared_in_first, shared_in_second, 1.5 / math.sqrt(D)),
        (shared_down, shared_down_part, shared_down_first, shared_down_second, 1.5 / math.sqrt(FF_SH)),
        (expert_in, grad_in_slice, expert_in_first, expert_in_second, 1.5 / math.sqrt(D)),
        (expert_down, grad_down_slice, expert_down_first, expert_down_second, 1.5 / math.sqrt(FF)),
    ):
        results.extend(adamw(weight, gradient, first, second, rate))
    return tuple(results)


def solution(mesh):
    placed = (
        P(("expert", "head"), None),
        P(("expert", "head"), None),
        P(("expert", "head")),
        P("expert", None),
        P(None, ("expert", "head")),
        P(None, ("expert", "head")),
        P(None, ("expert", "head")),
        P(("expert", "head"), None),
        P(("expert", "head"), None),
        P(("expert", "head"), None),
        P(None, ("expert", "head")),
        P(None, ("expert", "head")),
        P(None, ("expert", "head")),
        P(("expert", "head"), None),
        P(("expert", "head"), None),
        P(("expert", "head"), None),
        P("expert", None, "head"),
        P("expert", None, "head"),
        P("expert", None, "head"),
        P("head", "expert"),
        P("head", "expert"),
        P("head", "expert"),
        P("expert", None, None, "head"),
        P("expert", None, None, "head"),
        P("expert", None, None, "head"),
        P("expert", "head", None),
        P("expert", "head", None),
        P("expert", "head", None),
    )
    return jax.shard_map(
        dense_shards if (mesh.shape["expert"], mesh.shape["head"]) == (4, 8) else routed_shards,
        mesh=mesh,
        in_specs=placed,
        out_specs=(
            P(("expert", "head"), None),
            P(("expert", "head"), None),
            P(None, ("expert", "head")),
            P(None, ("expert", "head")),
            P(None, ("expert", "head")),
            P(("expert", "head"), None),
            P(("expert", "head"), None),
            P(("expert", "head"), None),
            P(None, ("expert", "head")),
            P(None, ("expert", "head")),
            P(None, ("expert", "head")),
            P(("expert", "head"), None),
            P(("expert", "head"), None),
            P(("expert", "head"), None),
            P("expert", None, "head"),
            P("expert", None, "head"),
            P("expert", None, "head"),
            P("head", "expert"),
            P("head", "expert"),
            P("head", "expert"),
            P("expert", None, None, "head"),
            P("expert", None, None, "head"),
            P("expert", None, None, "head"),
            P("expert", "head", None),
            P("expert", "head", None),
            P("expert", "head", None),
        ),
        check_vma=False,
    )
```

```python
import math

import jax
import jax.numpy as jnp
import numpy as np
from jax import lax
from jax.experimental import pallas as pl
from jax.experimental.pallas import tpu as pltpu
from jax.sharding import PartitionSpec as P

D = 768
HEADS = 12
HDIM = 64
FF = 2048
FF_SH = 2048
SEQ = 128
STEP = 4


NORM_EPS = 1e-06
BETA_FIRST = 0.5
BETA_SECOND = 0.5
ADAM_EPS = 1e-08
DECAY = 0.1
MASKED = -1e30
ROPE_BASE = 10000.0


def rope_tables(row_count):
    half_dim = HDIM // 2
    positions = jnp.arange(row_count, dtype=jnp.float32)
    frequency = ROPE_BASE ** (-jnp.arange(half_dim, dtype=jnp.float32) / half_dim)
    angles = positions[:, None] * frequency[None, :]
    return (jnp.cos(angles)[:, None, :], jnp.sin(angles)[:, None, :])


def rotate(values, cosine_table, sine_table):
    half_dim = values.shape[-1] // 2
    first_half = values[..., :half_dim]
    second_half = values[..., half_dim:]
    return jnp.concatenate(
        [
            first_half * cosine_table - second_half * sine_table,
            second_half * cosine_table + first_half * sine_table,
        ],
        axis=-1,
    )


def unrotate(gradient, cosine_table, sine_table):
    half_dim = gradient.shape[-1] // 2
    first_half = gradient[..., :half_dim]
    second_half = gradient[..., half_dim:]
    return jnp.concatenate(
        [
            first_half * cosine_table + second_half * sine_table,
            second_half * cosine_table - first_half * sine_table,
        ],
        axis=-1,
    )


def norm_forward(values, gain_vec):
    inverse = lax.rsqrt(jnp.mean(values * values, axis=-1, keepdims=True) + NORM_EPS)
    scaled = values * inverse
    return (scaled, inverse, scaled * gain_vec)


def norm_backward(grad_out, scaled, inverse, gain_vec):
    grad_scaled = grad_out * gain_vec
    grad_gain = jnp.sum(grad_out * scaled, axis=0)
    grad_in = inverse * (
        grad_scaled - scaled * jnp.mean(grad_scaled * scaled, axis=-1, keepdims=True)
    )
    return (grad_in, grad_gain)


def attention_scores(query_rows, key_rows, length):
    row_count = query_rows.shape[0]
    scores = (
        jnp.einsum("qhd,khd->hqk", query_rows, key_rows, preferred_element_type=jnp.float32) * 0.125
    )
    positions = jnp.arange(row_count, dtype=jnp.int32)
    allowed = (positions[None, :] <= positions[:, None]) & (positions[None, :] < length)
    return (jnp.where(allowed[None], scores, MASKED), allowed)


def expert_forward(row_block, weight_in, weight_down):
    mixed_pre = jnp.dot(row_block, weight_in, preferred_element_type=jnp.float32)
    hidden_width = weight_down.shape[0]
    gate_pre = mixed_pre[:, :hidden_width]
    up_pre = mixed_pre[:, hidden_width:]
    hidden = (gate_pre * jax.nn.sigmoid(gate_pre) * up_pre).astype(jnp.bfloat16)
    return (mixed_pre, hidden, jnp.dot(hidden, weight_down, preferred_element_type=jnp.float32))


def expert_backward(row_block, mixed_pre, hidden, grad_out, weight_in, weight_down):
    hidden_width = weight_down.shape[0]
    gate_pre = mixed_pre[:, :hidden_width]
    up_pre = mixed_pre[:, hidden_width:]
    grad_hidden = jnp.dot(grad_out, weight_down.T, preferred_element_type=jnp.float32)
    sigmoid_g = jax.nn.sigmoid(gate_pre)
    silu_g = gate_pre * sigmoid_g
    grad_gate = (grad_hidden * up_pre * sigmoid_g * (1.0 + gate_pre * (1.0 - sigmoid_g))).astype(
        jnp.bfloat16
    )
    grad_up = (grad_hidden * silu_g).astype(jnp.bfloat16)
    grad_mixed = jnp.concatenate([grad_gate, grad_up], axis=1)
    grad_down = jnp.dot(hidden.T, grad_out, preferred_element_type=jnp.float32)
    grad_weight_in = jnp.dot(row_block.T, grad_mixed, preferred_element_type=jnp.float32)
    grad_row_block = jnp.dot(grad_mixed, weight_in.T, preferred_element_type=jnp.float32)
    return (grad_row_block, grad_weight_in, grad_down)


def route_tables(route_rows, blocks, block_cap, expert_total):
    per_block = route_rows.reshape(blocks, -1)
    hit_table = (
        per_block[:, :, None] == jnp.arange(expert_total, dtype=jnp.int32)[None, None, :]
    ).astype(jnp.int32)
    entries = per_block.shape[1]
    earlier = jnp.tril(jnp.ones((entries, entries), jnp.bfloat16))
    running = jnp.einsum(
        "ij,bje->bie", earlier, hit_table.astype(jnp.bfloat16), preferred_element_type=jnp.float32
    ).astype(jnp.int32)
    rank_in = jnp.sum((running - 1) * hit_table, axis=2)
    offsets = jnp.arange(blocks, dtype=jnp.int32)[:, None] * block_cap
    dest_slot = (per_block * (blocks * block_cap) + offsets + rank_in).reshape(-1)
    source_row = (
        jnp.zeros((expert_total * blocks * block_cap,), jnp.int32)
        .at[dest_slot]
        .set(jnp.arange(dest_slot.shape[0], dtype=jnp.int32) + 1)
    )
    return (dest_slot, source_row)


def pack_tokens(token_rows, source_row):
    padded = jnp.concatenate(
        [jnp.zeros((1, token_rows.shape[1]), token_rows.dtype), token_rows], axis=0
    )
    pick_rows = jnp.where(source_row > 0, (source_row - 1) // 2 + 1, 0)
    return padded[pick_rows]


def pack_routes(route_values, source_row):
    padded = jnp.concatenate(
        [jnp.zeros((1, route_values.shape[1]), route_values.dtype), route_values], axis=0
    )
    return padded[source_row]


def adamw(weight, gradient, first_old, second_old, step_rate):
    first_new = BETA_FIRST * first_old + (1.0 - BETA_FIRST) * gradient
    second_new = BETA_SECOND * second_old + (1.0 - BETA_SECOND) * gradient * gradient
    first_hat = first_new / (1.0 - BETA_FIRST**STEP)
    second_hat = second_new / (1.0 - BETA_SECOND**STEP)
    new_weight = weight - step_rate * (
        first_hat / (jnp.sqrt(second_hat) + ADAM_EPS) + DECAY * weight
    )
    return (new_weight, first_new, second_new)


def routed_shards(
    tokens,
    cotangent,
    lengths,
    routes,
    norm_gains,
    gains_first,
    gains_second,
    qkv_weight,
    qkv_first,
    qkv_second,
    out_weight,
    out_first,
    out_second,
    router_weight,
    router_first,
    router_second,
    shared_in,
    shared_in_first,
    shared_in_second,
    shared_down,
    shared_down_first,
    shared_down_second,
    expert_in,
    expert_in_first,
    expert_in_second,
    expert_down,
    expert_down_first,
    expert_down_second,
):
    low_type = jnp.bfloat16
    seq_rows = tokens.shape[0]
    head_total = lax.axis_size("head")
    expert_total = lax.axis_size("expert")
    head_at = lax.axis_index("head")
    cap_dev = 4 * seq_rows // expert_total
    gains_all, qkv_all, out_all, router_all = (
        lax.all_gather(norm_gains.astype(low_type), ("expert", "head"), axis=1, tiled=True),
        lax.all_gather(qkv_weight.astype(low_type), ("expert", "head"), axis=0, tiled=True),
        lax.all_gather(out_weight.astype(low_type), ("expert", "head"), axis=1, tiled=True),
        lax.all_gather(router_weight.astype(low_type), ("expert", "head"), axis=0, tiled=True),
    )
    shared_in_all, shared_down_all = (
        lax.all_gather(shared_in.astype(low_type), "expert", axis=0, tiled=True),
        lax.all_gather(shared_down.astype(low_type), "expert", axis=1, tiled=True),
    )
    shared_in_flat = shared_in_all.reshape(D, -1)
    gain_one = gains_all[0].astype(jnp.float32)
    gain_two = gains_all[1].astype(jnp.float32)
    length = lengths[0]
    inputs = tokens.astype(jnp.float32)
    scaled_one, inverse_one, normed_one = norm_forward(inputs, gain_one)
    normed_low = normed_one.astype(low_type)
    projected = jnp.dot(normed_low, qkv_all, preferred_element_type=jnp.float32).reshape(
        seq_rows, 3, HEADS, HDIM
    )
    cosine_table, sine_table = rope_tables(seq_rows)
    query_rows = rotate(projected[:, 0], cosine_table, sine_table).astype(low_type)
    key_rows = rotate(projected[:, 1], cosine_table, sine_table).astype(low_type)
    value_rows = projected[:, 2].astype(low_type)
    scores, allowed = attention_scores(query_rows, key_rows, length)
    row_top = jnp.max(scores, axis=-1, keepdims=True)
    exponent = jnp.exp(scores - row_top)
    row_total = jnp.sum(exponent, axis=-1, keepdims=True)
    log_total = row_top + jnp.log(row_total)
    attn_probs = exponent / row_total
    context = (
        jnp.einsum(
            "hqk,khd->qhd",
            attn_probs.astype(low_type),
            value_rows,
            preferred_element_type=jnp.float32,
        )
        .reshape(seq_rows, D)
        .astype(low_type)
    )
    middle = inputs + jnp.dot(context, out_all, preferred_element_type=jnp.float32)
    scaled_two, inverse_two, normed_two = norm_forward(middle, gain_two)
    mixer_low = normed_two.astype(low_type)
    logits = jnp.dot(mixer_low, router_all, preferred_element_type=jnp.float32)
    own_routes = lax.dynamic_slice_in_dim(routes, head_at * seq_rows, seq_rows, 0)
    onehot = (
        own_routes[:, :, None] == jnp.arange(router_all.shape[1], dtype=jnp.int32)[None, None, :]
    ).astype(jnp.float32)
    chosen = jnp.sum(logits[:, None, :] * onehot, axis=-1)
    chosen_top = jnp.max(chosen, axis=-1, keepdims=True)
    chosen_exp = jnp.exp(chosen - chosen_top)
    gate_values = chosen_exp / jnp.sum(chosen_exp, axis=-1, keepdims=True)
    gates_low = gate_values.astype(low_type)
    group_rows, group_gates = (
        lax.all_gather(mixer_low, "head", axis=0, tiled=True),
        lax.all_gather(gates_low, "head", axis=0, tiled=True),
    )
    shared_mixed, shared_hidden, shared_out = expert_forward(
        group_rows, shared_in_flat, shared_down_all
    )
    dest_slot, source_row = route_tables(routes, head_total, cap_dev, expert_total)
    send_rows = pack_tokens(group_rows, source_row)
    expert_in_low = expert_in.astype(low_type)
    expert_down_low = expert_down.astype(low_type)
    weight_in = expert_in_low[0].reshape(D, -1)
    weight_down = expert_down_low[0]
    received = lax.all_to_all(
        send_rows.reshape(expert_total, -1, D), "expert", split_axis=0, concat_axis=0, tiled=True
    ).reshape(-1, D)
    expert_mixed, expert_hidden, expert_out = expert_forward(received, weight_in, weight_down)
    returned = (
        lax.all_to_all(
            expert_out.reshape(expert_total, -1, D).astype(jnp.bfloat16),
            "expert",
            split_axis=0,
            concat_axis=0,
            tiled=True,
        )
        .astype(jnp.float32)
        .reshape(-1, D)
    )
    routed = returned[dest_slot].reshape(-1, 2, D)
    partial_value = shared_out + jnp.sum(
        group_gates.astype(jnp.float32)[:, :, None] * routed, axis=1
    )
    mixed_out = lax.psum_scatter(
        partial_value.astype(jnp.bfloat16), "head", scatter_dimension=0, tiled=True
    ).astype(jnp.float32)
    live_rows = (jnp.arange(seq_rows, dtype=jnp.int32) < length).astype(jnp.float32)[:, None]
    layer_out = live_rows * (middle + mixed_out)
    grad_live = live_rows * cotangent
    grad_mix_low = grad_live.astype(low_type)
    group_grad = lax.all_gather(grad_mix_low, "head", axis=0, tiled=True)
    shared_row_grad, shared_grad_in, shared_grad_down = expert_backward(
        group_rows, shared_mixed, shared_hidden, group_grad, shared_in_flat, shared_down_all
    )
    group_grad_f = group_grad.astype(jnp.float32)
    grad_routed = (group_gates.astype(jnp.float32)[:, :, None] * group_grad_f[:, None, :]).astype(
        low_type
    )
    gate_grad_part = jnp.sum(group_grad_f[:, None, :] * routed, axis=-1)
    grad_send = pack_routes(grad_routed.reshape(-1, D), source_row)
    grad_received = lax.all_to_all(
        grad_send.reshape(expert_total, -1, D), "expert", split_axis=0, concat_axis=0, tiled=True
    ).reshape(-1, D)
    rows_grad, grad_in_local, grad_down_local = expert_backward(
        received, expert_mixed, expert_hidden, grad_received, weight_in, weight_down
    )
    rows_back = lax.all_to_all(
        rows_grad.reshape(expert_total, -1, D), "expert", split_axis=0, concat_axis=0, tiled=True
    ).reshape(-1, D)
    per_token = jnp.sum(rows_back[dest_slot].reshape(-1, 2, D), axis=1)
    rows_part = shared_row_grad + per_token
    grad_in_slice = grad_in_local.reshape(1, D, 2, -1)
    grad_down_slice = grad_down_local[None]
    grad_rows_own, grad_gates = (
        lax.psum_scatter(rows_part, "head", scatter_dimension=0, tiled=True),
        lax.psum_scatter(gate_grad_part, "head", scatter_dimension=0, tiled=True),
    )
    gate_dot = jnp.sum(gate_values * grad_gates, axis=-1, keepdims=True)
    grad_chosen = gate_values * (grad_gates - gate_dot)
    grad_logits = jnp.sum(grad_chosen[:, :, None] * onehot, axis=1).astype(low_type)
    grad_router = jnp.dot(mixer_low.T, grad_logits, preferred_element_type=jnp.float32)
    grad_normed_two = grad_rows_own + jnp.dot(
        grad_logits, router_all.T, preferred_element_type=jnp.float32
    )
    grad_from_norm, grad_gain_two = norm_backward(
        grad_normed_two, scaled_two, inverse_two, gain_two
    )
    grad_middle = grad_live + grad_from_norm
    grad_att_low = grad_middle.astype(low_type)
    grad_out_w = jnp.dot(context.T, grad_att_low, preferred_element_type=jnp.float32)
    grad_context = (
        jnp.dot(grad_att_low, out_all.T, preferred_element_type=jnp.float32)
        .astype(low_type)
        .reshape(seq_rows, HEADS, HDIM)
    )
    scores_again, allowed_again = attention_scores(query_rows, key_rows, length)
    probs_again = jnp.where(allowed_again[None], jnp.exp(scores_again - log_total), 0.0)
    grad_probs = jnp.einsum(
        "qhd,khd->hqk", grad_context, value_rows, preferred_element_type=jnp.float32
    )
    grad_value = jnp.einsum(
        "hqk,qhd->khd",
        probs_again.astype(low_type),
        grad_context,
        preferred_element_type=jnp.float32,
    )
    row_dot = jnp.sum(grad_probs * probs_again, axis=-1, keepdims=True)
    grad_scores = (probs_again * (grad_probs - row_dot)).astype(low_type)
    grad_query = (
        jnp.einsum("hqk,khd->qhd", grad_scores, key_rows, preferred_element_type=jnp.float32)
        * 0.125
    )
    grad_key = (
        jnp.einsum("hqk,qhd->khd", grad_scores, query_rows, preferred_element_type=jnp.float32)
        * 0.125
    )
    grad_projected = (
        jnp.stack(
            [
                unrotate(grad_query, cosine_table, sine_table),
                unrotate(grad_key, cosine_table, sine_table),
                grad_value,
            ],
            axis=1,
        )
        .reshape(seq_rows, 3 * D)
        .astype(low_type)
    )
    grad_qkv = jnp.dot(normed_low.T, grad_projected, preferred_element_type=jnp.float32)
    grad_normed_one = jnp.dot(grad_projected, qkv_all.T, preferred_element_type=jnp.float32)
    grad_input_norm, grad_gain_one = norm_backward(
        grad_normed_one, scaled_one, inverse_one, gain_one
    )
    input_grad = grad_middle + grad_input_norm
    gains_grad = jnp.stack([grad_gain_one, grad_gain_two], axis=0)
    gains_part, qkv_part, out_part, router_part = (
        lax.psum_scatter(gains_grad, ("expert", "head"), scatter_dimension=1, tiled=True),
        lax.psum_scatter(grad_qkv, ("expert", "head"), scatter_dimension=0, tiled=True),
        lax.psum_scatter(grad_out_w, ("expert", "head"), scatter_dimension=1, tiled=True),
        lax.psum_scatter(grad_router, ("expert", "head"), scatter_dimension=0, tiled=True),
    )
    shared_in_part, shared_down_part = (
        lax.psum_scatter(
            shared_grad_in.reshape(D, 2, -1).astype(jnp.bfloat16),
            "expert",
            scatter_dimension=0,
            tiled=True,
        ).astype(jnp.float32),
        lax.psum_scatter(
            shared_grad_down.astype(jnp.bfloat16), "expert", scatter_dimension=1, tiled=True
        ).astype(jnp.float32),
    )
    gains_new, gains_first_new, gains_second_new = adamw(
        norm_gains, gains_part, gains_first, gains_second, 0.5
    )
    qkv_new, qkv_first_new, qkv_second_new = adamw(
        qkv_weight, qkv_part, qkv_first, qkv_second, 1.5 / math.sqrt(D)
    )
    out_new, out_first_new, out_second_new = adamw(
        out_weight, out_part, out_first, out_second, 1.5 / math.sqrt(4 * D // SEQ)
    )
    router_new, router_first_new, router_second_new = adamw(
        router_weight, router_part, router_first, router_second, 1.0 / math.sqrt(D)
    )
    shin_new, shin_first_new, shin_second_new = adamw(
        shared_in, shared_in_part, shared_in_first, shared_in_second, 1.5 / math.sqrt(D)
    )
    shdown_new, shdown_first_new, shdown_second_new = adamw(
        shared_down, shared_down_part, shared_down_first, shared_down_second, 1.5 / math.sqrt(FF_SH)
    )
    exin_new, exin_first_new, exin_second_new = adamw(
        expert_in, grad_in_slice, expert_in_first, expert_in_second, 1.5 / math.sqrt(D)
    )
    exdown_new, exdown_first_new, exdown_second_new = adamw(
        expert_down, grad_down_slice, expert_down_first, expert_down_second, 1.5 / math.sqrt(FF)
    )
    return (
        layer_out,
        input_grad,
        gains_new,
        gains_first_new,
        gains_second_new,
        qkv_new,
        qkv_first_new,
        qkv_second_new,
        out_new,
        out_first_new,
        out_second_new,
        router_new,
        router_first_new,
        router_second_new,
        shin_new,
        shin_first_new,
        shin_second_new,
        shdown_new,
        shdown_first_new,
        shdown_second_new,
        exin_new,
        exin_first_new,
        exin_second_new,
        exdown_new,
        exdown_first_new,
        exdown_second_new,
    )


MESH = pl.DeviceIdType.MESH
VMEM_BYTES = 61 << 20
GROUPS = 4
PLANE = 8
ALL = GROUPS * PLANE
EXTRA = 16
TURN = (1, 3, 2)


def nn(left, right):
    return jnp.dot(left, right, preferred_element_type=jnp.float32)


def nt(left, right):
    return lax.dot_general(
        left, right, (((1,), (1,)), ((), ())), preferred_element_type=jnp.float32
    )


def tn(left, right):
    return lax.dot_general(
        left, right, (((0,), (0,)), ((), ())), preferred_element_type=jnp.float32
    )


def slot_of(group, member):
    return member * GROUPS + group


class Place:
    def __init__(self):
        self.group = group = lax.axis_index("expert")
        self.member = member = lax.axis_index("head")
        self.core = core = member % 2
        column, row = (member // 2) % 2, member // 4
        self.chip = group * (PLANE // 2) + member // 2
        side = 1 - 2 * core
        self.twin = member + side
        beside, across = member + 2 - 4 * column, member + 4 - 8 * row
        self.near = beside * (1 - core) + across * core
        self.far = across * (1 - core) + beside * core
        self.corner = member + (2 - 4 * column) + (4 - 8 * row)
        self.near_twin = self.near + side
        self.far_twin = self.far + side
        self.corner_twin = self.corner + side
        self.mine = slot_of(group, member)

    def around(self, step):
        return (self.group + step) % GROUPS

    def others(self):
        near = [(self.group, self.twin), (self.group, self.near), (self.group, self.far)]
        return near + [(self.around(step), self.member) for step in TURN]

    def tell(self, semaphore):
        for other in self.others():
            pl.semaphore_signal(semaphore, inc=1, device_id=other, device_id_type=MESH)

    def hear(self, semaphore):
        pl.semaphore_wait(semaphore, 6)


class Mover:
    def __init__(self, place, send_sem):
        self.place, self.send_sem, self.sizes = place, send_sem, []

    def copy(self, source, target, index, recv, device):
        return pltpu.make_async_remote_copy(
            src_ref=source,
            dst_ref=target,
            send_sem=self.send_sem.at[index],
            recv_sem=recv,
            device_id=device,
            device_id_type=MESH,
        )

    def send(self, source, target, recv, device):
        self.copy(source, target, len(self.sizes), recv, device).start()
        self.sizes.append(source)

    def arrive(self, target, recv):
        self.copy(target, target, 0, recv, (self.place.group, self.place.twin)).wait_recv()

    def drain(self, unit):
        for index in range(len(self.sizes)):
            self.copy(unit, unit, index, self.send_sem.at[index], (self.place.group, self.place.twin)).wait_send()


class Gather(Mover):
    def __init__(self, place, at, send_sem, recv_sem, pair=True):
        super().__init__(place, send_sem)
        self.at, self.recv_sem, self.pair = at, recv_sem, pair

    def forward(self, group, member, partners):
        for partner in partners:
            if partner is self.place.twin and not self.pair:
                continue
            ref = self.at(group, member)
            self.send(ref, ref, self.recv_sem.at[slot_of(group, member)], (self.place.group, partner))

    def wait(self, group, member):
        self.arrive(self.at(group, member), self.recv_sem.at[slot_of(group, member)])

    def start(self):
        place = self.place
        own = self.at(place.group, place.member)
        for step in TURN:
            self.send(own, own, self.recv_sem.at[place.mine], (place.around(step), place.member))
        self.forward(place.group, place.member, (place.near, place.far, place.twin))

    def own_column(self, step):
        place = self.place
        self.wait(place.around(step), place.member)
        self.forward(place.around(step), place.member, (place.near, place.far, place.twin))

    def near_column(self, step):
        place = self.place
        self.wait(place.around(step), place.near)
        self.forward(place.around(step), place.near, (place.far, place.twin))

    def last_column(self, step, member):
        self.wait(self.place.around(step), member)
        self.forward(self.place.around(step), member, (self.place.twin,))

    def twin_column(self, member):
        for step in (0,) + TURN:
            self.wait(self.place.around(step), member)


class Scatter(Mover):
    def __init__(self, place, part, rows, bufs, send_sem, sems):
        super().__init__(place, send_sem)
        self.part, self.rows = part, rows
        self.twin_buf, self.far_buf, self.near_buf, self.group_buf = bufs
        self.twin_sem, self.far_sem, self.near_sem, self.group_sem = sems

    def view(self, buf, index):
        return buf.at[index, pl.ds(0, self.rows)]

    def add(self, target, others):
        def some(block, carry):
            at = pl.ds(pl.multiple_of(block * 16, 16), 16)
            total = target[at].astype(jnp.float32)
            for other in others:
                total = total + other[at].astype(jnp.float32)
            target[at] = total.astype(target.dtype)
            return carry

        lax.fori_loop(0, self.rows // 16, some, 0)

    def twin_index(self, group, member):
        return (member // 2) * GROUPS + group

    def to_twin(self, group, member):
        index = self.twin_index(group, member)
        self.send(
            self.part(group, member),
            self.view(self.twin_buf, index),
            self.twin_sem.at[index],
            (self.place.group, self.place.twin),
        )

    def from_twin(self, group, member):
        index = self.twin_index(group, member)
        ready = self.view(self.twin_buf, index)
        self.arrive(ready, self.twin_sem.at[index])
        return ready

    def from_far(self, group, spot):
        other = self.view(self.far_buf, spot * GROUPS + group)
        self.arrive(other, self.far_sem.at[spot * GROUPS + group])
        return other

    def outward(self, step, spot):
        group = self.place.around(step)
        member = (self.place.corner, self.place.far)[spot]
        ready = self.from_twin(group, member)
        self.add(ready, [self.part(group, member)])
        index = spot * GROUPS + group
        self.send(
            ready,
            self.view(self.far_buf, index),
            self.far_sem.at[index],
            (self.place.group, self.place.far),
        )

    def sideways(self, step):
        group, near = self.place.around(step), self.place.near
        ready = self.from_twin(group, near)
        self.add(ready, [self.part(group, near), self.from_far(group, 0)])
        self.send(
            ready,
            self.view(self.near_buf, group),
            self.near_sem.at[group],
            (self.place.group, near),
        )

    def homeward(self, step):
        group, member = self.place.around(step), self.place.member
        ready = self.from_twin(group, member)
        other = self.view(self.near_buf, group)
        far = self.from_far(group, 1)
        self.arrive(other, self.near_sem.at[group])
        self.add(ready, [self.part(group, member), far, other])
        if step:
            self.send(
                ready,
                self.view(self.group_buf, step - 1),
                self.group_sem.at[step - 1],
                (group, member),
            )

    def finish(self, store):
        for step in TURN:
            self.arrive(self.view(self.group_buf, step - 1), self.group_sem.at[step - 1])
        ready = self.view(self.twin_buf, self.twin_index(self.place.group, self.place.member))

        def some(block, carry):
            at = pl.ds(pl.multiple_of(block * 16, 16), 16)
            total = ready[at].astype(jnp.float32)
            for step in TURN:
                total = total + self.view(self.group_buf, step - 1)[at].astype(jnp.float32)
            store(at, total)
            return carry

        lax.fori_loop(0, self.rows // 16, some, 0)


BACKWARD = (2, 1, 3, 0)


def iota(shape, dim):
    return lax.broadcasted_iota(jnp.int32, shape, dim)


def swap_halves(block):
    lane = iota(block.shape, 1)
    return jnp.where(
        lane % HDIM < HDIM // 2, pltpu.roll(block, 128 - HDIM // 2, 1), pltpu.roll(block, HDIM // 2, 1)
    )


def step_kernel(
    length_ref,
    tokens_ref,
    cotangent_ref,
    routes_ref,
    owned_ref,
    small_ref,
    pieces_ref,
    cosine_ref,
    sine_ref,
    expert_in_ref,
    expert_down_ref,
    layer_out_ref,
    input_grad_ref,
    owned_grad_ref,
    small_grad_ref,
    grad_in_ref,
    grad_down_ref,
    shared_grad_ref,
    stage,
    small_stage,
    mats,
    small_all,
    first_all,
    second_all,
    pieces,
    shared_send,
    weight_in,
    weight_down,
    hidden_all,
    mixed_all,
    pre,
    back_hidden,
    queries,
    keys,
    values,
    probs,
    normed_low,
    context,
    middle_ref,
    mixer,
    rows_sum,
    grad_mid,
    grad_context,
    grad_proj,
    gate_keep,
    twin_a,
    far_a,
    near_a,
    group_a,
    twin_b,
    far_b,
    near_b,
    group_b,
    pair_send,
    pair_recv,
    local_sem,
    mats_send,
    mats_recv,
    small_send,
    small_recv,
    cot_send,
    cot_recv,
    mix_send,
    mix_recv,
    piece_send,
    piece_recv,
    rows_send,
    out_send,
    own_send,
    twin_sems,
    far_sems,
    near_sems,
    group_sems,
    free_sem,
):
    low = jnp.bfloat16
    rows = tokens_ref.shape[0]
    place = Place()
    group, member, core = place.group, place.member, place.core
    barrier = pltpu.get_barrier_semaphore()
    place.tell(barrier)
    place.hear(barrier)

    twin_device = (group, place.twin)
    own_rows = pl.ds(pl.multiple_of(24 * core, 8), 24)
    owned = pltpu.make_async_remote_copy(
        src_ref=owned_ref.at[pl.ds(2 * (1 - core), 2)],
        dst_ref=stage.at[:, own_rows],
        send_sem=pair_send.at[0],
        recv_sem=pair_recv.at[0],
        device_id=twin_device,
        device_id_type=MESH,
    )
    owned.start()
    small_pair = pltpu.make_async_remote_copy(
        src_ref=small_ref,
        dst_ref=small_stage.at[own_rows],
        send_sem=pair_send.at[1],
        recv_sem=pair_recv.at[1],
        device_id=twin_device,
        device_id_type=MESH,
    )
    small_pair.start()
    loads = [
        pltpu.make_async_copy(expert_in_ref.at[0, :, 0, :], grad_in_ref.at[:, pl.ds(0, 256)], local_sem.at[0]),
        pltpu.make_async_copy(expert_in_ref.at[0, :, 1, :], grad_in_ref.at[:, pl.ds(256, 256)], local_sem.at[1]),
        pltpu.make_async_copy(expert_down_ref.at[0], grad_down_ref.at[pl.ds(0, 256)], local_sem.at[2]),
    ]
    for load in loads:
        load.start()
    stage[:, own_rows] = owned_ref[pl.ds(2 * core, 2)]
    small_stage[own_rows] = small_ref[...]
    owned.wait()
    small_pair.wait()

    def mats_at(group, member):
        chip = group * (PLANE // 2) + member // 2
        return mats.at[pl.ds(2 * (member % 2), 2), pl.ds(pl.multiple_of(48 * chip, 16), 48)]

    def small_at(group, member):
        chip = group * (PLANE // 2) + member // 2
        return small_all.at[pl.ds(pl.multiple_of(48 * chip, 16), 48)]

    mats_at(group, member)[...] = stage[...].astype(low)
    small_at(group, member)[...] = small_stage[...].astype(low)
    send_small = Gather(place, small_at, small_send, small_recv, pair=False)
    send_mats = Gather(place, mats_at, mats_send, mats_recv)
    send_small.start()
    send_mats.start()

    def move_piece(source, target, sems, base):
        for step in TURN:
            pltpu.make_async_remote_copy(
                src_ref=source.at[place.around(step)],
                dst_ref=target.at[group],
                send_sem=piece_send.at[base + step - 1],
                recv_sem=piece_recv.at[base + (GROUPS - step) - 1],
                device_id=(place.around(step), member),
                device_id_type=MESH,
            ).start()
        target[group] = source[group]

    def wait_pieces(source, target, base):
        for step in TURN:
            copy = pltpu.make_async_remote_copy(
                src_ref=source.at[place.around(step)],
                dst_ref=target.at[place.around(step)],
                send_sem=piece_send.at[base + step - 1],
                recv_sem=piece_recv.at[base + step - 1],
                device_id=(place.around(step), member),
                device_id_type=MESH,
            )
            copy.wait()

    move_piece(pieces_ref, pieces, piece_send, 0)

    length = length_ref[0]
    row_at = iota((rows, 1), 0)
    live = (row_at < length).astype(jnp.float32)
    first_all[place.mine, pl.ds(0, rows)] = (cotangent_ref[...] * live).astype(low)

    for step in (0,) + TURN:
        if step:
            send_small.own_column(step)
            send_mats.own_column(step)
        send_small.near_column(step)
        send_mats.near_column(step)

    send_cot = Gather(
        place,
        lambda group, member: first_all.at[slot_of(group, member), pl.ds(0, rows)],
        cot_send,
        cot_recv,
    )
    send_cot.start()

    for load in loads:
        load.wait()
    weight_in[:, pl.ds(0, 512)] = grad_in_ref[:, pl.ds(0, 512)].astype(low)
    weight_down[pl.ds(0, 256)] = grad_down_ref[pl.ds(0, 256)].astype(low)
    wait_pieces(pieces_ref, pieces, 0)
    for piece in range(GROUPS):
        at = pl.ds(192 * piece, 192)
        weight_in[at, pl.ds(512, 256)] = pieces[piece, :, pl.ds(0, 256)]
    turned = pieces[:, :, pl.ds(256, 128)].reshape(D, 128).astype(jnp.float32)
    weight_down[pl.ds(256, 128)] = turned.T.astype(low)
    grad_down_ref[...] = jnp.zeros_like(grad_down_ref)
    grad_in_ref[...] = jnp.zeros_like(grad_in_ref)

    for step in (0,) + TURN:
        for origin in (place.far, place.corner):
            send_small.wait(place.around(step), origin)
            send_mats.last_column(step, origin)
    for step in TURN:
        send_cot.own_column(step)
    for origin in (place.twin, place.near_twin, place.far_twin, place.corner_twin):
        send_mats.twin_column(origin)

    inputs = tokens_ref[...].astype(jnp.float32)
    inverse_one = lax.rsqrt(jnp.mean(inputs * inputs, axis=-1, keepdims=True) + NORM_EPS)
    pick = (iota((8, 128), 1) == iota((8, 128), 0) + GROUPS).astype(low)
    gains = nt(pick, small_all[...])
    gain_one, gain_two = gains[0:1], gains[1:2]
    normed_low[...] = (inputs * inverse_one * gain_one).astype(low)
    for part, target in ((0, queries), (1, keys), (2, values)):
        pre[pl.ds(0, rows)] = nn(normed_low[...], mats[part])
        for block in range(D // 128):
            at = pl.ds(128 * block, 128)
            piece = pre[pl.ds(0, rows), at]
            if part < 2:
                piece = piece * cosine_ref[...] + swap_halves(piece) * sine_ref[...]
            target[:, at] = piece.astype(low)
    for step in (0, 1):
        send_cot.near_column(step)
    query_at, key_at = iota((rows, rows), 0), iota((rows, rows), 1)
    allowed = (key_at <= query_at) & (key_at < length)
    lower = iota((rows, 128), 1) < HDIM

    def attend(pair, carry):
        at = pl.ds(pl.multiple_of(pair * 128, 128), 128)
        query, key, value = queries[:, at], keys[:, at], values[:, at]
        found = []
        for half in (0, 1):
            own = lower if half == 0 else jnp.logical_not(lower)
            scores = nt(jnp.where(own, query, jnp.zeros_like(query)), key) * 0.125
            scores = jnp.where(allowed, scores, MASKED)
            exponent = jnp.exp(scores - jnp.max(scores, axis=-1, keepdims=True))
            prob = exponent / jnp.sum(exponent, axis=-1, keepdims=True)
            probs[pair * 2 + half] = prob
            found.append(nn(prob.astype(low), value))
        context[:, at] = jnp.where(lower, found[0], found[1]).astype(low)
        for serve in range(2):

            @pl.when(pair == serve)
            def _():
                send_cot.near_column((3, 2)[serve])

        return carry

    lax.fori_loop(0, HEADS // 2, attend, 0)
    middle = inputs + nt(context[...], mats[3])
    middle_ref[...] = middle
    inverse_two = lax.rsqrt(jnp.mean(middle * middle, axis=-1, keepdims=True) + NORM_EPS)
    mixer[...] = (middle * inverse_two * gain_two).astype(low)
    logits = nn(mixer[...], small_all[...])
    lane = iota((rows, 128), 1)
    chosen, hits = [], []
    for choice in (0, 1):
        hit = (lane == routes_ref[:, choice : choice + 1]).astype(jnp.float32)
        hits.append(hit)
        chosen.append(jnp.sum(logits * hit, axis=-1, keepdims=True))
    top = jnp.maximum(chosen[0], chosen[1])
    exponents = [jnp.exp(value - top) for value in chosen]
    total = exponents[0] + exponents[1]
    gates = [value / total for value in exponents]
    gate_keep[...] = jnp.where(lane == 0, gates[0], jnp.where(lane == 1, gates[1], 0.0))
    table = sum(gate.astype(low).astype(jnp.float32) * hit for gate, hit in zip(gates, hits))
    second_all[place.mine, pl.ds(0, rows)] = mixer[...]
    second_all[place.mine, pl.ds(rows, EXTRA)] = jnp.zeros((EXTRA, D), low)
    second_all[place.mine, pl.ds(rows, EXTRA), pl.ds(0, 128)] = table.T[:EXTRA].astype(low)
    send_mix = Gather(
        place, lambda group, member: second_all.at[slot_of(group, member)], mix_send, mix_recv
    )
    send_mix.start()
    for step in (0,) + TURN:
        for origin in (place.far, place.corner):
            send_cot.last_column(step, origin)
    for step in TURN:
        send_mix.own_column(step)
    for origin in (place.twin, place.near_twin, place.far_twin, place.corner_twin):
        send_cot.twin_column(origin)
    send_cot.drain(first_all.at[0, pl.ds(0, rows)])

    columns = (
        place.member,
        place.twin,
        place.near,
        place.far_twin,
        place.far,
        place.near_twin,
        place.corner,
        place.corner_twin,
    )

    def column(index):
        found = columns[0]
        for at in range(1, PLANE):
            found = jnp.where(index == at, columns[at], found)
        return found

    rows_move = Scatter(
        place,
        lambda group, member: first_all.at[slot_of(group, member)],
        rows + EXTRA,
        (twin_a, far_a, near_a, group_a),
        rows_send,
        (twin_sems.at[0], far_sems.at[0], near_sems.at[0], group_sems.at[0]),
    )
    diagonal = iota((rows, rows), 0) == iota((rows, rows), 1)
    extra_row = iota((EXTRA, 128), 0) == group

    def forward_column(index, carry):
        def serve_mix():
            for step in (0,) + TURN:
                send_mix.near_column(step)
            send_mix.twin_column(place.twin)

        def serve_far():
            for step in (0,) + TURN:
                send_mix.last_column(step, place.far)

        def serve_corner():
            for step in (0,) + TURN:
                send_mix.last_column(step, place.corner)

        for at, serve in (
            (1, serve_mix),
            (3, lambda: send_mix.twin_column(place.far_twin)),
            (4, serve_far),
            (5, lambda: send_mix.twin_column(place.near_twin)),
            (6, serve_corner),
            (7, lambda: send_mix.twin_column(place.corner_twin)),
        ):

            @pl.when(index == at)
            def _():
                serve()

        base = pl.multiple_of(column(index) * GROUPS, GROUPS)
        four = pl.ds(base, GROUPS)
        taken = second_all[four, pl.ds(0, rows)].reshape(GROUPS * rows, D)
        pre[...] = nn(taken, weight_in[...])
        cot = first_all[four, pl.ds(0, rows)].reshape(GROUPS * rows, D)
        back_hidden[...] = nt(cot, weight_down[...])

        def units(block, carry):
            slot = base + block
            gate_block = second_all[slot, pl.ds(rows, EXTRA), pl.ds(0, 128)].astype(jnp.float32)
            gate_row = jnp.sum(jnp.where(extra_row, gate_block, 0.0), axis=0, keepdims=True)
            scale = jnp.sum(jnp.where(diagonal, gate_row, 0.0), axis=1, keepdims=True)
            at = pl.ds(pl.multiple_of(block * rows, rows), rows)
            here = pl.ds(pl.multiple_of(slot * rows, rows), rows)
            weigh = jnp.zeros((rows, 1), jnp.float32)
            for gate_at, up_at, hidden_at, routed in (
                (0, 256, 0, True),
                (128, 384, 128, True),
                (512, 640, 256, False),
            ):
                gate_pre = pre[at, pl.ds(gate_at, 128)]
                up_pre = pre[at, pl.ds(up_at, 128)]
                hidden_grad = back_hidden[at, pl.ds(hidden_at, 128)]
                sigmoid_g = jax.nn.sigmoid(gate_pre)
                silu_g = gate_pre * sigmoid_g
                hidden = (silu_g * up_pre).astype(low)
                if routed:
                    wide = hidden.astype(jnp.float32)
                    weigh = weigh + jnp.sum(wide * hidden_grad, axis=-1, keepdims=True)
                    hidden_grad = hidden_grad * scale
                    hidden = (wide * scale).astype(low)
                grad_gate = hidden_grad * up_pre * sigmoid_g * (1.0 + gate_pre * (1.0 - sigmoid_g))
                hidden_all[here, pl.ds(hidden_at, 128)] = hidden
                mixed_all[here, pl.ds(gate_at, 128)] = grad_gate.astype(low)
                mixed_all[here, pl.ds(up_at, 128)] = (hidden_grad * silu_g).astype(low)
            weigh_row = jnp.sum(jnp.where(diagonal, weigh, 0.0), axis=0, keepdims=True)
            extra = jnp.where(extra_row, weigh_row, 0.0).astype(low)
            first_all[slot, pl.ds(rows, EXTRA)] = jnp.zeros((EXTRA, D), low)
            first_all[slot, pl.ds(rows, EXTRA), pl.ds(0, 128)] = extra
            return carry

        lax.fori_loop(0, GROUPS, units, 0)
        every = pl.ds(pl.multiple_of(base * rows, rows), GROUPS * rows)
        grad_down_ref[...] += tn(hidden_all[every], cot)
        pre[...] = nt(mixed_all[every], weight_in[...])
        first_all[four, pl.ds(0, rows)] = pre[...].astype(low).reshape(GROUPS, rows, D)
        for at in range(1, PLANE, 2):

            @pl.when(index == at)
            def _():
                for step in BACKWARD:
                    rows_move.to_twin(place.around(step), columns[at])

        return carry

    lax.fori_loop(0, PLANE, forward_column, 0)
    for step in BACKWARD:
        for spot in (0, 1):
            rows_move.outward(step, spot)
    send_mix.drain(second_all.at[0])

    out_move = Scatter(
        place,
        lambda group, member: second_all.at[slot_of(group, member), pl.ds(0, rows)],
        rows,
        (twin_b, far_b, near_b, group_b),
        out_send,
        (twin_sems.at[1], far_sems.at[1], near_sems.at[1], group_sems.at[1]),
    )

    def second_column(index, carry):
        base = pl.multiple_of(column(index) * GROUPS, GROUPS)
        four = pl.ds(base, GROUPS)
        every = pl.ds(pl.multiple_of(base * rows, rows), GROUPS * rows)
        taken = second_all[four, pl.ds(0, rows)].reshape(GROUPS * rows, D)
        grad_in_ref[...] += tn(taken, mixed_all[every])
        pre[...] = nn(hidden_all[every], weight_down[...])
        second_all[four, pl.ds(0, rows)] = pre[...].astype(low).reshape(GROUPS, rows, D)
        for at in range(PLANE):

            @pl.when(index == at)
            def _():
                if at % 2:
                    for step in BACKWARD:
                        out_move.to_twin(place.around(step), columns[at])
                if at < GROUPS:
                    rows_move.sideways(BACKWARD[at])
                else:
                    rows_move.homeward(BACKWARD[at - GROUPS])

        return carry

    lax.fori_loop(0, PLANE, second_column, 0)

    for piece in range(GROUPS):
        shared_send[piece, :, pl.ds(0, 256)] = grad_in_ref[pl.ds(192 * piece, 192), pl.ds(512, 256)].astype(low)
    turned = grad_down_ref[pl.ds(256, 128)].T
    shared_send[:, :, pl.ds(256, 128)] = turned.astype(low).reshape(GROUPS, 192, 128)
    move_piece(shared_send, shared_grad_ref, piece_send, 3)

    def keep_rows(at, total):
        rows_sum[at] = total

    rows_move.finish(keep_rows)
    rows_move.drain(first_all.at[0])
    place.tell(free_sem)

    gate_grads = rows_sum[pl.ds(rows, EXTRA), pl.ds(0, 128)]
    gate_grads = jnp.concatenate([gate_grads, jnp.zeros((rows - EXTRA, 128), jnp.float32)], axis=0).T
    grad_gates = [jnp.sum(gate_grads * hit, axis=-1, keepdims=True) for hit in hits]
    kept = [
        jnp.sum(jnp.where(lane == choice, gate_keep[...], 0.0), axis=-1, keepdims=True)
        for choice in (0, 1)
    ]
    gate_dot = kept[0] * grad_gates[0] + kept[1] * grad_gates[1]
    grad_logits = sum(
        hit * (gate * (grad - gate_dot)) for hit, gate, grad in zip(hits, kept, grad_gates)
    ).astype(low)
    grad_router = tn(grad_logits, mixer[...])[:8]
    middle = middle_ref[...]
    inverse_two = lax.rsqrt(jnp.mean(middle * middle, axis=-1, keepdims=True) + NORM_EPS)
    scaled_two = middle * inverse_two
    gains = nt(pick, small_all[...])
    gain_one, gain_two = gains[0:1], gains[1:2]
    grad_normed = rows_sum[pl.ds(0, rows)] + nt(grad_logits, small_all[...])
    grad_gain_two = jnp.sum(grad_normed * scaled_two, axis=0, keepdims=True)
    grad_scaled = grad_normed * gain_two
    grad_middle = cotangent_ref[...] * live + inverse_two * (
        grad_scaled - scaled_two * jnp.mean(grad_scaled * scaled_two, axis=-1, keepdims=True)
    )
    grad_mid[...] = grad_middle
    grad_att = grad_middle.astype(low)
    grad_context[...] = nn(grad_att, mats[3]).astype(low)

    own_move = Scatter(
        place,
        lambda group, member: first_all.at[slot_of(group, member), pl.ds(0, 96 + EXTRA)],
        96 + EXTRA,
        (twin_a, far_a, near_a, group_a),
        own_send,
        (twin_sems.at[2], far_sems.at[2], near_sems.at[2], group_sems.at[2]),
    )

    def put_part(which, left, right):
        for half in (0, 1):
            product = tn(left[:, 384 * half : 384 * half + 384], right).astype(low)
            for place_in in range(8):
                chip = half * 8 + place_in
                slot = slot_of(chip // 4, (chip % 4) * 2 + which // 2)
                first_all[slot, pl.ds(48 * (which % 2), 48)] = product[48 * place_in : 48 * place_in + 48]

    put_part(3, grad_att, context[...])

    def attend_back(pair, carry):
        at = pl.ds(pl.multiple_of(pair * 128, 128), 128)
        query, key, value = queries[:, at], keys[:, at], values[:, at]
        grad_ctx = grad_context[:, at]
        grad_query, grad_key, grad_value = [], [], []
        for half in (0, 1):
            own = lower if half == 0 else jnp.logical_not(lower)
            prob = probs[pair * 2 + half]
            grad_prob = nt(jnp.where(own, grad_ctx, jnp.zeros_like(grad_ctx)), value)
            grad_value.append(tn(prob.astype(low), grad_ctx))
            row_dot = jnp.sum(grad_prob * prob, axis=-1, keepdims=True)
            grad_score = (prob * (grad_prob - row_dot)).astype(low)
            grad_query.append(nn(grad_score, key))
            grad_key.append(tn(grad_score, query))
        grad_q = jnp.where(lower, grad_query[0], grad_query[1]) * 0.125
        grad_k = jnp.where(lower, grad_key[0], grad_key[1]) * 0.125
        grad_q = grad_q * cosine_ref[...] - swap_halves(grad_q) * sine_ref[...]
        grad_k = grad_k * cosine_ref[...] - swap_halves(grad_k) * sine_ref[...]
        grad_proj[0, :, at] = grad_q.astype(low)
        grad_proj[1, :, at] = grad_k.astype(low)
        grad_proj[2, :, at] = jnp.where(lower, grad_value[0], grad_value[1]).astype(low)
        for serve in range(4):

            @pl.when(pair == serve)
            def _():
                for spot in (0, 1):
                    out_move.outward(BACKWARD[serve], spot)

        return carry

    lax.fori_loop(0, HEADS // 2, attend_back, 0)
    grad_one = nt(grad_proj[0], mats[0]) + nt(grad_proj[1], mats[1]) + nt(grad_proj[2], mats[2])
    inputs = tokens_ref[...].astype(jnp.float32)
    inverse_one = lax.rsqrt(jnp.mean(inputs * inputs, axis=-1, keepdims=True) + NORM_EPS)
    scaled_one = inputs * inverse_one
    grad_gain_one = jnp.sum(grad_one * scaled_one, axis=0, keepdims=True)
    grad_scaled = grad_one * gain_one
    input_grad_ref[...] = grad_mid[...] + inverse_one * (
        grad_scaled - scaled_one * jnp.mean(grad_scaled * scaled_one, axis=-1, keepdims=True)
    )
    for which in range(3):
        put_part(which, normed_low[...], grad_proj[which])
    at_row = iota((8, D), 0)
    small_rows = jnp.where(
        at_row < GROUPS, grad_router, jnp.where(at_row == GROUPS, grad_gain_one, grad_gain_two)
    )
    small_rows = jnp.concatenate([small_rows, jnp.zeros((8, D), jnp.float32)], axis=0).astype(low)

    def put_small(slot, carry):
        first_all[slot, pl.ds(96, EXTRA)] = small_rows
        return carry

    lax.fori_loop(0, ALL, put_small, 0)
    place.hear(free_sem)
    for step in BACKWARD:
        for origin in (place.corner_twin, place.near_twin, place.far_twin, place.twin):
            own_move.to_twin(place.around(step), origin)
    for step in BACKWARD:
        for spot in (0, 1):
            own_move.outward(step, spot)
    for step in BACKWARD:
        out_move.sideways(step)
    for step in BACKWARD:
        own_move.sideways(step)
    for step in BACKWARD:
        out_move.homeward(step)
    for step in BACKWARD:
        own_move.homeward(step)

    def keep_out(at, total):
        here = pl.ds(at.start, 16)
        live_here = (iota((16, 1), 0) + at.start < length).astype(jnp.float32)
        layer_out_ref[here] = live_here * (middle_ref[here] + total)

    out_move.finish(keep_out)

    def keep_own(at, total):
        rows_sum[at] = total

    own_move.finish(keep_own)
    for matrix in (0, 1):
        stage[matrix] = rows_sum[pl.ds(48 * matrix, 48)]
    theirs = pl.ds(pl.multiple_of(24 * (1 - core), 8), 24)
    mine = pl.ds(2 * core, 2)
    last = pltpu.make_async_remote_copy(
        src_ref=stage.at[:, theirs],
        dst_ref=owned_grad_ref.at[mine],
        send_sem=pair_send.at[2],
        recv_sem=pair_recv.at[2],
        device_id=twin_device,
        device_id_type=MESH,
    )
    last.start()
    owned_grad_ref[mine] = stage[:, own_rows]
    small_grad_ref[...] = rows_sum[pl.ds(96, EXTRA)]
    wait_pieces(shared_send, shared_grad_ref, 3)
    last.wait()
    out_move.drain(second_all.at[0, pl.ds(0, rows)])
    own_move.drain(first_all.at[0, pl.ds(0, 96 + EXTRA)])
    send_mats.drain(mats_at(group, member))
    send_small.drain(small_at(group, member))


def dense_shards(
    tokens,
    cotangent,
    lengths,
    routes,
    norm_gains,
    gains_first,
    gains_second,
    qkv_weight,
    qkv_first,
    qkv_second,
    out_weight,
    out_first,
    out_second,
    router_weight,
    router_first,
    router_second,
    shared_in,
    shared_in_first,
    shared_in_second,
    shared_down,
    shared_down_first,
    shared_down_second,
    expert_in,
    expert_in_first,
    expert_in_second,
    expert_down,
    expert_down_first,
    expert_down_second,
):
    low_type = jnp.bfloat16
    seq_rows = tokens.shape[0]
    head_at = lax.axis_index("head")
    own_routes = lax.dynamic_slice_in_dim(routes, head_at * seq_rows, seq_rows, 0)
    per_device = D // ALL
    owned = jnp.concatenate(
        [qkv_weight.reshape(per_device, 3, D).transpose(1, 0, 2), out_weight.T[None]], axis=0
    )
    small = jnp.concatenate([router_weight, norm_gains.T], axis=1)
    small = jnp.pad(small, ((0, 0), (0, 128 - small.shape[1])))
    width = FF_SH // ALL
    half_pad = ((0, 0), (0, 0), (0, 128 - width))
    gate_up = shared_in.astype(low_type).reshape(-1, 2, GROUPS, width).transpose(2, 0, 1, 3)
    down = shared_down.astype(low_type).T.reshape(-1, GROUPS, width).transpose(1, 0, 2)
    pieces = jnp.concatenate(
        [
            jnp.pad(gate_up[:, :, 0], half_pad),
            jnp.pad(gate_up[:, :, 1], half_pad),
            jnp.pad(down, half_pad),
        ],
        axis=2,
    )
    half_dim = HDIM // 2
    positions = np.arange(seq_rows, dtype=np.float32)[:, None]
    angles = positions * np.tile(ROPE_BASE ** (-np.arange(half_dim) / half_dim), 4)[None]
    sign = np.tile(np.repeat([-1.0, 1.0], half_dim), 2)[None]
    cosine = jnp.asarray(np.cos(angles), jnp.float32)
    sine = jnp.asarray(np.sin(angles) * sign, jnp.float32)
    vmem = pl.BlockSpec(memory_space=pltpu.VMEM)
    wide, f32, i32 = low_type, jnp.float32, jnp.int32
    tall = seq_rows + EXTRA
    dma = pltpu.SemaphoreType.DMA
    (
        layer_out,
        input_grad,
        owned_grad,
        small_grad,
        grad_in,
        grad_down,
        shared_grad,
    ) = pl.pallas_call(
        step_kernel,
        out_shape=(
            jax.ShapeDtypeStruct((seq_rows, D), f32),
            jax.ShapeDtypeStruct((seq_rows, D), f32),
            jax.ShapeDtypeStruct((4, per_device, D), f32),
            jax.ShapeDtypeStruct((EXTRA, D), f32),
            jax.ShapeDtypeStruct((D, 768), f32),
            jax.ShapeDtypeStruct((384, D), f32),
            jax.ShapeDtypeStruct((GROUPS, 192, 384), low_type),
        ),
        in_specs=[pl.BlockSpec(memory_space=pltpu.SMEM)]
        + [vmem] * 8
        + [pl.BlockSpec(memory_space=pl.ANY)] * 2,
        out_specs=(vmem,) * 7,
        scratch_shapes=[
            pltpu.VMEM((2, 48, D), f32),
            pltpu.VMEM((48, 128), f32),
            pltpu.VMEM((4, D, D), wide),
            pltpu.VMEM((D, 128), wide),
            pltpu.VMEM((ALL, tall, D), wide),
            pltpu.VMEM((ALL, tall, D), wide),
            pltpu.VMEM((GROUPS, 192, 384), wide),
            pltpu.VMEM((GROUPS, 192, 384), wide),
            pltpu.VMEM((D, 768), wide),
            pltpu.VMEM((384, D), wide),
            pltpu.VMEM((ALL * seq_rows, 384), wide),
            pltpu.VMEM((ALL * seq_rows, 768), wide),
            pltpu.VMEM((GROUPS * seq_rows, 768), f32),
            pltpu.VMEM((GROUPS * seq_rows, 384), f32),
            pltpu.VMEM((seq_rows, D), wide),
            pltpu.VMEM((seq_rows, D), wide),
            pltpu.VMEM((seq_rows, D), wide),
            pltpu.VMEM((HEADS, seq_rows, seq_rows), f32),
            pltpu.VMEM((seq_rows, D), wide),
            pltpu.VMEM((seq_rows, D), wide),
            pltpu.VMEM((seq_rows, D), f32),
            pltpu.VMEM((seq_rows, D), wide),
            pltpu.VMEM((tall, D), f32),
            pltpu.VMEM((seq_rows, D), f32),
            pltpu.VMEM((seq_rows, D), wide),
            pltpu.VMEM((3, seq_rows, D), wide),
            pltpu.VMEM((seq_rows, 128), f32),
            pltpu.VMEM((16, tall, D), wide),
            pltpu.VMEM((8, tall, D), wide),
            pltpu.VMEM((4, tall, D), wide),
            pltpu.VMEM((3, tall, D), wide),
            pltpu.VMEM((16, seq_rows, D), wide),
            pltpu.VMEM((8, seq_rows, D), wide),
            pltpu.VMEM((4, seq_rows, D), wide),
            pltpu.VMEM((3, seq_rows, D), wide),
            dma((3,)),
            dma((3,)),
            dma((3,)),
            dma((31,)),
            dma((32,)),
            dma((31,)),
            dma((32,)),
            dma((31,)),
            dma((32,)),
            dma((31,)),
            dma((32,)),
            dma((6,)),
            dma((6,)),
            dma((31,)),
            dma((31,)),
            dma((31,)),
            dma((3, 16)),
            dma((3, 8)),
            dma((3, 4)),
            dma((3, 3)),
            pltpu.SemaphoreType.REGULAR,
        ],
        compiler_params=pltpu.CompilerParams(
            collective_id=0, has_side_effects=True, vmem_limit_bytes=VMEM_BYTES
        ),
    )(
        lengths,
        tokens,
        cotangent,
        own_routes,
        owned,
        small,
        pieces,
        cosine,
        sine,
        expert_in,
        expert_down,
    )
    qkv_part = owned_grad[:3].transpose(1, 0, 2).reshape(per_device, 3 * D)
    out_part = owned_grad[3].T
    first_lane = (lax.axis_index("expert") * PLANE + head_at) * per_device
    small_own = lax.dynamic_slice_in_dim(small_grad, first_lane, per_device, 1)
    router_part = small_own[:GROUPS].T
    gains_part = small_own[GROUPS : GROUPS + 2]
    shared_grad = shared_grad.astype(f32)
    shared_in_part = jnp.stack(
        [shared_grad[:, :, :width], shared_grad[:, :, 128 : 128 + width]], axis=2
    )
    shared_in_part = shared_in_part.transpose(1, 2, 0, 3).reshape(shared_in.shape)
    shared_down_part = (
        shared_grad[:, :, 256 : 256 + width].transpose(0, 2, 1).reshape(shared_down.shape)
    )
    hidden_width = expert_down.shape[1]
    grad_in_slice = grad_in[:, : 2 * hidden_width].reshape(1, D, 2, hidden_width)
    grad_down_slice = grad_down[:hidden_width][None]
    results = [layer_out, input_grad]
    for weight, gradient, first, second, rate in (
        (norm_gains, gains_part, gains_first, gains_second, 0.5),
        (qkv_weight, qkv_part, qkv_first, qkv_second, 1.5 / math.sqrt(D)),
        (out_weight, out_part, out_first, out_second, 1.5 / math.sqrt(4 * D // SEQ)),
        (router_weight, router_part, router_first, router_second, 1.0 / math.sqrt(D)),
        (shared_in, shared_in_part, shared_in_first, shared_in_second, 1.5 / math.sqrt(D)),
        (shared_down, shared_down_part, shared_down_first, shared_down_second, 1.5 / math.sqrt(FF_SH)),
        (expert_in, grad_in_slice, expert_in_first, expert_in_second, 1.5 / math.sqrt(D)),
        (expert_down, grad_down_slice, expert_down_first, expert_down_second, 1.5 / math.sqrt(FF)),
    ):
        results.extend(adamw(weight, gradient, first, second, rate))
    return tuple(results)


def solution(mesh):
    placed = (
        P(("expert", "head"), None),
        P(("expert", "head"), None),
        P(("expert", "head")),
        P("expert", None),
        P(None, ("expert", "head")),
        P(None, ("expert", "head")),
        P(None, ("expert", "head")),
        P(("expert", "head"), None),
        P(("expert", "head"), None),
        P(("expert", "head"), None),
        P(None, ("expert", "head")),
        P(None, ("expert", "head")),
        P(None, ("expert", "head")),
        P(("expert", "head"), None),
        P(("expert", "head"), None),
        P(("expert", "head"), None),
        P("expert", None, "head"),
        P("expert", None, "head"),
        P("expert", None, "head"),
        P("head", "expert"),
        P("head", "expert"),
        P("head", "expert"),
        P("expert", None, None, "head"),
        P("expert", None, None, "head"),
        P("expert", None, None, "head"),
        P("expert", "head", None),
        P("expert", "head", None),
        P("expert", "head", None),
    )
    return jax.shard_map(
        dense_shards if (mesh.shape["expert"], mesh.shape["head"]) == (4, 8) else routed_shards,
        mesh=mesh,
        in_specs=placed,
        out_specs=(
            P(("expert", "head"), None),
            P(("expert", "head"), None),
            P(None, ("expert", "head")),
            P(None, ("expert", "head")),
            P(None, ("expert", "head")),
            P(("expert", "head"), None),
            P(("expert", "head"), None),
            P(("expert", "head"), None),
            P(None, ("expert", "head")),
            P(None, ("expert", "head")),
            P(None, ("expert", "head")),
            P(("expert", "head"), None),
            P(("expert", "head"), None),
            P(("expert", "head"), None),
            P("expert", None, "head"),
            P("expert", None, "head"),
            P("expert", None, "head"),
            P("head", "expert"),
            P("head", "expert"),
            P("head", "expert"),
            P("expert", None, None, "head"),
            P("expert", None, None, "head"),
            P("expert", None, None, "head"),
            P("expert", "head", None),
            P("expert", "head", None),
            P("expert", "head", None),
        ),
        check_vma=False,
    )
```

```python
import math

import jax
import jax.numpy as jnp
import numpy as np
from jax import lax
from jax.experimental import pallas as pl
from jax.experimental.pallas import tpu as pltpu
from jax.sharding import PartitionSpec as P

D = 768
HEADS = 12
HDIM = 64
FF = 2048
FF_SH = 2048
SEQ = 128
STEP = 4


NORM_EPS = 1e-06
BETA_FIRST = 0.5
BETA_SECOND = 0.5
ADAM_EPS = 1e-08
DECAY = 0.1
MASKED = -1e30
ROPE_BASE = 10000.0


def rope_tables(row_count):
    half_dim = HDIM // 2
    positions = jnp.arange(row_count, dtype=jnp.float32)
    frequency = ROPE_BASE ** (-jnp.arange(half_dim, dtype=jnp.float32) / half_dim)
    angles = positions[:, None] * frequency[None, :]
    return (jnp.cos(angles)[:, None, :], jnp.sin(angles)[:, None, :])


def rotate(values, cosine_table, sine_table):
    half_dim = values.shape[-1] // 2
    first_half = values[..., :half_dim]
    second_half = values[..., half_dim:]
    return jnp.concatenate(
        [
            first_half * cosine_table - second_half * sine_table,
            second_half * cosine_table + first_half * sine_table,
        ],
        axis=-1,
    )


def unrotate(gradient, cosine_table, sine_table):
    half_dim = gradient.shape[-1] // 2
    first_half = gradient[..., :half_dim]
    second_half = gradient[..., half_dim:]
    return jnp.concatenate(
        [
            first_half * cosine_table + second_half * sine_table,
            second_half * cosine_table - first_half * sine_table,
        ],
        axis=-1,
    )


def norm_forward(values, gain_vec):
    inverse = lax.rsqrt(jnp.mean(values * values, axis=-1, keepdims=True) + NORM_EPS)
    scaled = values * inverse
    return (scaled, inverse, scaled * gain_vec)


def norm_backward(grad_out, scaled, inverse, gain_vec):
    grad_scaled = grad_out * gain_vec
    grad_gain = jnp.sum(grad_out * scaled, axis=0)
    grad_in = inverse * (
        grad_scaled - scaled * jnp.mean(grad_scaled * scaled, axis=-1, keepdims=True)
    )
    return (grad_in, grad_gain)


def attention_scores(query_rows, key_rows, length):
    row_count = query_rows.shape[0]
    scores = (
        jnp.einsum("qhd,khd->hqk", query_rows, key_rows, preferred_element_type=jnp.float32) * 0.125
    )
    positions = jnp.arange(row_count, dtype=jnp.int32)
    allowed = (positions[None, :] <= positions[:, None]) & (positions[None, :] < length)
    return (jnp.where(allowed[None], scores, MASKED), allowed)


def expert_forward(row_block, weight_in, weight_down):
    mixed_pre = jnp.dot(row_block, weight_in, preferred_element_type=jnp.float32)
    hidden_width = weight_down.shape[0]
    gate_pre = mixed_pre[:, :hidden_width]
    up_pre = mixed_pre[:, hidden_width:]
    hidden = (gate_pre * jax.nn.sigmoid(gate_pre) * up_pre).astype(jnp.bfloat16)
    return (mixed_pre, hidden, jnp.dot(hidden, weight_down, preferred_element_type=jnp.float32))


def expert_backward(row_block, mixed_pre, hidden, grad_out, weight_in, weight_down):
    hidden_width = weight_down.shape[0]
    gate_pre = mixed_pre[:, :hidden_width]
    up_pre = mixed_pre[:, hidden_width:]
    grad_hidden = jnp.dot(grad_out, weight_down.T, preferred_element_type=jnp.float32)
    sigmoid_g = jax.nn.sigmoid(gate_pre)
    silu_g = gate_pre * sigmoid_g
    grad_gate = (grad_hidden * up_pre * sigmoid_g * (1.0 + gate_pre * (1.0 - sigmoid_g))).astype(
        jnp.bfloat16
    )
    grad_up = (grad_hidden * silu_g).astype(jnp.bfloat16)
    grad_mixed = jnp.concatenate([grad_gate, grad_up], axis=1)
    grad_down = jnp.dot(hidden.T, grad_out, preferred_element_type=jnp.float32)
    grad_weight_in = jnp.dot(row_block.T, grad_mixed, preferred_element_type=jnp.float32)
    grad_row_block = jnp.dot(grad_mixed, weight_in.T, preferred_element_type=jnp.float32)
    return (grad_row_block, grad_weight_in, grad_down)


def route_tables(route_rows, blocks, block_cap, expert_total):
    per_block = route_rows.reshape(blocks, -1)
    hit_table = (
        per_block[:, :, None] == jnp.arange(expert_total, dtype=jnp.int32)[None, None, :]
    ).astype(jnp.int32)
    entries = per_block.shape[1]
    earlier = jnp.tril(jnp.ones((entries, entries), jnp.bfloat16))
    running = jnp.einsum(
        "ij,bje->bie", earlier, hit_table.astype(jnp.bfloat16), preferred_element_type=jnp.float32
    ).astype(jnp.int32)
    rank_in = jnp.sum((running - 1) * hit_table, axis=2)
    offsets = jnp.arange(blocks, dtype=jnp.int32)[:, None] * block_cap
    dest_slot = (per_block * (blocks * block_cap) + offsets + rank_in).reshape(-1)
    source_row = (
        jnp.zeros((expert_total * blocks * block_cap,), jnp.int32)
        .at[dest_slot]
        .set(jnp.arange(dest_slot.shape[0], dtype=jnp.int32) + 1)
    )
    return (dest_slot, source_row)


def pack_tokens(token_rows, source_row):
    padded = jnp.concatenate(
        [jnp.zeros((1, token_rows.shape[1]), token_rows.dtype), token_rows], axis=0
    )
    pick_rows = jnp.where(source_row > 0, (source_row - 1) // 2 + 1, 0)
    return padded[pick_rows]


def pack_routes(route_values, source_row):
    padded = jnp.concatenate(
        [jnp.zeros((1, route_values.shape[1]), route_values.dtype), route_values], axis=0
    )
    return padded[source_row]


def adamw(weight, gradient, first_old, second_old, step_rate):
    first_new = BETA_FIRST * first_old + (1.0 - BETA_FIRST) * gradient
    second_new = BETA_SECOND * second_old + (1.0 - BETA_SECOND) * gradient * gradient
    first_hat = first_new / (1.0 - BETA_FIRST**STEP)
    second_hat = second_new / (1.0 - BETA_SECOND**STEP)
    new_weight = weight - step_rate * (
        first_hat / (jnp.sqrt(second_hat) + ADAM_EPS) + DECAY * weight
    )
    return (new_weight, first_new, second_new)


def routed_shards(
    tokens,
    cotangent,
    lengths,
    routes,
    norm_gains,
    gains_first,
    gains_second,
    qkv_weight,
    qkv_first,
    qkv_second,
    out_weight,
    out_first,
    out_second,
    router_weight,
    router_first,
    router_second,
    shared_in,
    shared_in_first,
    shared_in_second,
    shared_down,
    shared_down_first,
    shared_down_second,
    expert_in,
    expert_in_first,
    expert_in_second,
    expert_down,
    expert_down_first,
    expert_down_second,
):
    low_type = jnp.bfloat16
    seq_rows = tokens.shape[0]
    head_total = lax.axis_size("head")
    expert_total = lax.axis_size("expert")
    head_at = lax.axis_index("head")
    cap_dev = 4 * seq_rows // expert_total
    gains_all, qkv_all, out_all, router_all = (
        lax.all_gather(norm_gains.astype(low_type), ("expert", "head"), axis=1, tiled=True),
        lax.all_gather(qkv_weight.astype(low_type), ("expert", "head"), axis=0, tiled=True),
        lax.all_gather(out_weight.astype(low_type), ("expert", "head"), axis=1, tiled=True),
        lax.all_gather(router_weight.astype(low_type), ("expert", "head"), axis=0, tiled=True),
    )
    shared_in_all, shared_down_all = (
        lax.all_gather(shared_in.astype(low_type), "expert", axis=0, tiled=True),
        lax.all_gather(shared_down.astype(low_type), "expert", axis=1, tiled=True),
    )
    shared_in_flat = shared_in_all.reshape(D, -1)
    gain_one = gains_all[0].astype(jnp.float32)
    gain_two = gains_all[1].astype(jnp.float32)
    length = lengths[0]
    inputs = tokens.astype(jnp.float32)
    scaled_one, inverse_one, normed_one = norm_forward(inputs, gain_one)
    normed_low = normed_one.astype(low_type)
    projected = jnp.dot(normed_low, qkv_all, preferred_element_type=jnp.float32).reshape(
        seq_rows, 3, HEADS, HDIM
    )
    cosine_table, sine_table = rope_tables(seq_rows)
    query_rows = rotate(projected[:, 0], cosine_table, sine_table).astype(low_type)
    key_rows = rotate(projected[:, 1], cosine_table, sine_table).astype(low_type)
    value_rows = projected[:, 2].astype(low_type)
    scores, allowed = attention_scores(query_rows, key_rows, length)
    row_top = jnp.max(scores, axis=-1, keepdims=True)
    exponent = jnp.exp(scores - row_top)
    row_total = jnp.sum(exponent, axis=-1, keepdims=True)
    log_total = row_top + jnp.log(row_total)
    attn_probs = exponent / row_total
    context = (
        jnp.einsum(
            "hqk,khd->qhd",
            attn_probs.astype(low_type),
            value_rows,
            preferred_element_type=jnp.float32,
        )
        .reshape(seq_rows, D)
        .astype(low_type)
    )
    middle = inputs + jnp.dot(context, out_all, preferred_element_type=jnp.float32)
    scaled_two, inverse_two, normed_two = norm_forward(middle, gain_two)
    mixer_low = normed_two.astype(low_type)
    logits = jnp.dot(mixer_low, router_all, preferred_element_type=jnp.float32)
    own_routes = lax.dynamic_slice_in_dim(routes, head_at * seq_rows, seq_rows, 0)
    onehot = (
        own_routes[:, :, None] == jnp.arange(router_all.shape[1], dtype=jnp.int32)[None, None, :]
    ).astype(jnp.float32)
    chosen = jnp.sum(logits[:, None, :] * onehot, axis=-1)
    chosen_top = jnp.max(chosen, axis=-1, keepdims=True)
    chosen_exp = jnp.exp(chosen - chosen_top)
    gate_values = chosen_exp / jnp.sum(chosen_exp, axis=-1, keepdims=True)
    gates_low = gate_values.astype(low_type)
    group_rows, group_gates = (
        lax.all_gather(mixer_low, "head", axis=0, tiled=True),
        lax.all_gather(gates_low, "head", axis=0, tiled=True),
    )
    shared_mixed, shared_hidden, shared_out = expert_forward(
        group_rows, shared_in_flat, shared_down_all
    )
    dest_slot, source_row = route_tables(routes, head_total, cap_dev, expert_total)
    send_rows = pack_tokens(group_rows, source_row)
    expert_in_low = expert_in.astype(low_type)
    expert_down_low = expert_down.astype(low_type)
    weight_in = expert_in_low[0].reshape(D, -1)
    weight_down = expert_down_low[0]
    received = lax.all_to_all(
        send_rows.reshape(expert_total, -1, D), "expert", split_axis=0, concat_axis=0, tiled=True
    ).reshape(-1, D)
    expert_mixed, expert_hidden, expert_out = expert_forward(received, weight_in, weight_down)
    returned = (
        lax.all_to_all(
            expert_out.reshape(expert_total, -1, D).astype(jnp.bfloat16),
            "expert",
            split_axis=0,
            concat_axis=0,
            tiled=True,
        )
        .astype(jnp.float32)
        .reshape(-1, D)
    )
    routed = returned[dest_slot].reshape(-1, 2, D)
    partial_value = shared_out + jnp.sum(
        group_gates.astype(jnp.float32)[:, :, None] * routed, axis=1
    )
    mixed_out = lax.psum_scatter(
        partial_value.astype(jnp.bfloat16), "head", scatter_dimension=0, tiled=True
    ).astype(jnp.float32)
    live_rows = (jnp.arange(seq_rows, dtype=jnp.int32) < length).astype(jnp.float32)[:, None]
    layer_out = live_rows * (middle + mixed_out)
    grad_live = live_rows * cotangent
    grad_mix_low = grad_live.astype(low_type)
    group_grad = lax.all_gather(grad_mix_low, "head", axis=0, tiled=True)
    shared_row_grad, shared_grad_in, shared_grad_down = expert_backward(
        group_rows, shared_mixed, shared_hidden, group_grad, shared_in_flat, shared_down_all
    )
    group_grad_f = group_grad.astype(jnp.float32)
    grad_routed = (group_gates.astype(jnp.float32)[:, :, None] * group_grad_f[:, None, :]).astype(
        low_type
    )
    gate_grad_part = jnp.sum(group_grad_f[:, None, :] * routed, axis=-1)
    grad_send = pack_routes(grad_routed.reshape(-1, D), source_row)
    grad_received = lax.all_to_all(
        grad_send.reshape(expert_total, -1, D), "expert", split_axis=0, concat_axis=0, tiled=True
    ).reshape(-1, D)
    rows_grad, grad_in_local, grad_down_local = expert_backward(
        received, expert_mixed, expert_hidden, grad_received, weight_in, weight_down
    )
    rows_back = lax.all_to_all(
        rows_grad.reshape(expert_total, -1, D), "expert", split_axis=0, concat_axis=0, tiled=True
    ).reshape(-1, D)
    per_token = jnp.sum(rows_back[dest_slot].reshape(-1, 2, D), axis=1)
    rows_part = shared_row_grad + per_token
    grad_in_slice = grad_in_local.reshape(1, D, 2, -1)
    grad_down_slice = grad_down_local[None]
    grad_rows_own, grad_gates = (
        lax.psum_scatter(rows_part, "head", scatter_dimension=0, tiled=True),
        lax.psum_scatter(gate_grad_part, "head", scatter_dimension=0, tiled=True),
    )
    gate_dot = jnp.sum(gate_values * grad_gates, axis=-1, keepdims=True)
    grad_chosen = gate_values * (grad_gates - gate_dot)
    grad_logits = jnp.sum(grad_chosen[:, :, None] * onehot, axis=1).astype(low_type)
    grad_router = jnp.dot(mixer_low.T, grad_logits, preferred_element_type=jnp.float32)
    grad_normed_two = grad_rows_own + jnp.dot(
        grad_logits, router_all.T, preferred_element_type=jnp.float32
    )
    grad_from_norm, grad_gain_two = norm_backward(
        grad_normed_two, scaled_two, inverse_two, gain_two
    )
    grad_middle = grad_live + grad_from_norm
    grad_att_low = grad_middle.astype(low_type)
    grad_out_w = jnp.dot(context.T, grad_att_low, preferred_element_type=jnp.float32)
    grad_context = (
        jnp.dot(grad_att_low, out_all.T, preferred_element_type=jnp.float32)
        .astype(low_type)
        .reshape(seq_rows, HEADS, HDIM)
    )
    scores_again, allowed_again = attention_scores(query_rows, key_rows, length)
    probs_again = jnp.where(allowed_again[None], jnp.exp(scores_again - log_total), 0.0)
    grad_probs = jnp.einsum(
        "qhd,khd->hqk", grad_context, value_rows, preferred_element_type=jnp.float32
    )
    grad_value = jnp.einsum(
        "hqk,qhd->khd",
        probs_again.astype(low_type),
        grad_context,
        preferred_element_type=jnp.float32,
    )
    row_dot = jnp.sum(grad_probs * probs_again, axis=-1, keepdims=True)
    grad_scores = (probs_again * (grad_probs - row_dot)).astype(low_type)
    grad_query = (
        jnp.einsum("hqk,khd->qhd", grad_scores, key_rows, preferred_element_type=jnp.float32)
        * 0.125
    )
    grad_key = (
        jnp.einsum("hqk,qhd->khd", grad_scores, query_rows, preferred_element_type=jnp.float32)
        * 0.125
    )
    grad_projected = (
        jnp.stack(
            [
                unrotate(grad_query, cosine_table, sine_table),
                unrotate(grad_key, cosine_table, sine_table),
                grad_value,
            ],
            axis=1,
        )
        .reshape(seq_rows, 3 * D)
        .astype(low_type)
    )
    grad_qkv = jnp.dot(normed_low.T, grad_projected, preferred_element_type=jnp.float32)
    grad_normed_one = jnp.dot(grad_projected, qkv_all.T, preferred_element_type=jnp.float32)
    grad_input_norm, grad_gain_one = norm_backward(
        grad_normed_one, scaled_one, inverse_one, gain_one
    )
    input_grad = grad_middle + grad_input_norm
    gains_grad = jnp.stack([grad_gain_one, grad_gain_two], axis=0)
    gains_part, qkv_part, out_part, router_part = (
        lax.psum_scatter(gains_grad, ("expert", "head"), scatter_dimension=1, tiled=True),
        lax.psum_scatter(grad_qkv, ("expert", "head"), scatter_dimension=0, tiled=True),
        lax.psum_scatter(grad_out_w, ("expert", "head"), scatter_dimension=1, tiled=True),
        lax.psum_scatter(grad_router, ("expert", "head"), scatter_dimension=0, tiled=True),
    )
    shared_in_part, shared_down_part = (
        lax.psum_scatter(
            shared_grad_in.reshape(D, 2, -1).astype(jnp.bfloat16),
            "expert",
            scatter_dimension=0,
            tiled=True,
        ).astype(jnp.float32),
        lax.psum_scatter(
            shared_grad_down.astype(jnp.bfloat16), "expert", scatter_dimension=1, tiled=True
        ).astype(jnp.float32),
    )
    gains_new, gains_first_new, gains_second_new = adamw(
        norm_gains, gains_part, gains_first, gains_second, 0.5
    )
    qkv_new, qkv_first_new, qkv_second_new = adamw(
        qkv_weight, qkv_part, qkv_first, qkv_second, 1.5 / math.sqrt(D)
    )
    out_new, out_first_new, out_second_new = adamw(
        out_weight, out_part, out_first, out_second, 1.5 / math.sqrt(4 * D // SEQ)
    )
    router_new, router_first_new, router_second_new = adamw(
        router_weight, router_part, router_first, router_second, 1.0 / math.sqrt(D)
    )
    shin_new, shin_first_new, shin_second_new = adamw(
        shared_in, shared_in_part, shared_in_first, shared_in_second, 1.5 / math.sqrt(D)
    )
    shdown_new, shdown_first_new, shdown_second_new = adamw(
        shared_down, shared_down_part, shared_down_first, shared_down_second, 1.5 / math.sqrt(FF_SH)
    )
    exin_new, exin_first_new, exin_second_new = adamw(
        expert_in, grad_in_slice, expert_in_first, expert_in_second, 1.5 / math.sqrt(D)
    )
    exdown_new, exdown_first_new, exdown_second_new = adamw(
        expert_down, grad_down_slice, expert_down_first, expert_down_second, 1.5 / math.sqrt(FF)
    )
    return (
        layer_out,
        input_grad,
        gains_new,
        gains_first_new,
        gains_second_new,
        qkv_new,
        qkv_first_new,
        qkv_second_new,
        out_new,
        out_first_new,
        out_second_new,
        router_new,
        router_first_new,
        router_second_new,
        shin_new,
        shin_first_new,
        shin_second_new,
        shdown_new,
        shdown_first_new,
        shdown_second_new,
        exin_new,
        exin_first_new,
        exin_second_new,
        exdown_new,
        exdown_first_new,
        exdown_second_new,
    )


MESH = pl.DeviceIdType.MESH
VMEM_BYTES = 61 << 20
GROUPS = 4
PLANE = 8
ALL = GROUPS * PLANE
EXTRA = 16
TURN = (1, 3, 2)


def nn(left, right):
    return jnp.dot(left, right, preferred_element_type=jnp.float32)


def nt(left, right):
    return lax.dot_general(
        left, right, (((1,), (1,)), ((), ())), preferred_element_type=jnp.float32
    )


def tn(left, right):
    return lax.dot_general(
        left, right, (((0,), (0,)), ((), ())), preferred_element_type=jnp.float32
    )


def slot_of(group, member):
    return group * PLANE + (member % 2) * (PLANE // 2) + member // 2


class Place:
    def __init__(self):
        self.group = group = lax.axis_index("expert")
        self.member = member = lax.axis_index("head")
        self.core = core = member % 2
        column, row = (member // 2) % 2, member // 4
        self.chip = group * (PLANE // 2) + member // 2
        side = 1 - 2 * core
        self.twin = member + side
        beside, across = member + 2 - 4 * column, member + 4 - 8 * row
        self.near = beside * (1 - core) + across * core
        self.far = across * (1 - core) + beside * core
        self.corner = member + (2 - 4 * column) + (4 - 8 * row)
        self.near_twin = self.near + side
        self.far_twin = self.far + side
        self.corner_twin = self.corner + side
        self.mine = slot_of(group, member)

    def around(self, step):
        return (self.group + step) % GROUPS

    def others(self):
        near = [(self.group, self.twin), (self.group, self.near), (self.group, self.far)]
        return near + [(self.around(step), self.member) for step in TURN]

    def tell(self, semaphore):
        for other in self.others():
            pl.semaphore_signal(semaphore, inc=1, device_id=other, device_id_type=MESH)

    def hear(self, semaphore):
        pl.semaphore_wait(semaphore, 6)


class Mover:
    def __init__(self, place, send_sem):
        self.place, self.send_sem, self.sizes = place, send_sem, []

    def copy(self, source, target, index, recv, device):
        return pltpu.make_async_remote_copy(
            src_ref=source,
            dst_ref=target,
            send_sem=self.send_sem.at[index],
            recv_sem=recv,
            device_id=device,
            device_id_type=MESH,
        )

    def send(self, source, target, recv, device):
        self.copy(source, target, len(self.sizes), recv, device).start()
        self.sizes.append(source)

    def arrive(self, target, recv):
        self.copy(target, target, 0, recv, (self.place.group, self.place.twin)).wait_recv()

    def drain(self, unit):
        for index in range(len(self.sizes)):
            self.copy(unit, unit, index, self.send_sem.at[index], (self.place.group, self.place.twin)).wait_send()


class Gather(Mover):
    def __init__(self, place, at, send_sem, recv_sem, pair=True):
        super().__init__(place, send_sem)
        self.at, self.recv_sem, self.pair = at, recv_sem, pair

    def forward(self, group, member, partners):
        for partner in partners:
            if partner is self.place.twin and not self.pair:
                continue
            ref = self.at(group, member)
            self.send(ref, ref, self.recv_sem.at[slot_of(group, member)], (self.place.group, partner))

    def wait(self, group, member):
        self.arrive(self.at(group, member), self.recv_sem.at[slot_of(group, member)])

    def start(self):
        place = self.place
        own = self.at(place.group, place.member)
        for step in TURN:
            self.send(own, own, self.recv_sem.at[place.mine], (place.around(step), place.member))
        self.forward(place.group, place.member, (place.near, place.far, place.twin))

    def own_column(self, step):
        place = self.place
        self.wait(place.around(step), place.member)
        self.forward(place.around(step), place.member, (place.near, place.far, place.twin))

    def near_column(self, step):
        place = self.place
        self.wait(place.around(step), place.near)
        self.forward(place.around(step), place.near, (place.far, place.twin))

    def last_column(self, step, member):
        self.wait(self.place.around(step), member)
        self.forward(self.place.around(step), member, (self.place.twin,))

    def twin_column(self, member):
        for step in (0,) + TURN:
            self.wait(self.place.around(step), member)

    def twin_plane(self, step):
        place = self.place
        for member in (place.twin, place.far_twin, place.near_twin, place.corner_twin):
            self.wait(place.around(step), member)

    def last_plane(self, step):
        for member in (self.place.far, self.place.corner):
            self.last_column(step, member)


class Scatter(Mover):
    def __init__(self, place, part, rows, bufs, send_sem, sems):
        super().__init__(place, send_sem)
        self.part, self.rows = part, rows
        self.twin_buf, self.far_buf, self.near_buf, self.group_buf = bufs
        self.twin_sem, self.far_sem, self.near_sem, self.group_sem = sems

    def view(self, buf, index):
        return buf.at[index, pl.ds(0, self.rows)]

    def add(self, target, others):
        def some(block, carry):
            at = pl.ds(pl.multiple_of(block * 16, 16), 16)
            total = target[at].astype(jnp.float32)
            for other in others:
                total = total + other[at].astype(jnp.float32)
            target[at] = total.astype(target.dtype)
            return carry

        lax.fori_loop(0, self.rows // 16, some, 0)

    def twin_index(self, group, member):
        return (member // 2) * GROUPS + group

    def to_twin(self, group, member):
        index = self.twin_index(group, member)
        self.send(
            self.part(group, member),
            self.view(self.twin_buf, index),
            self.twin_sem.at[index],
            (self.place.group, self.place.twin),
        )

    def from_twin(self, group, member):
        index = self.twin_index(group, member)
        ready = self.view(self.twin_buf, index)
        self.arrive(ready, self.twin_sem.at[index])
        return ready

    def from_far(self, group, spot):
        other = self.view(self.far_buf, spot * GROUPS + group)
        self.arrive(other, self.far_sem.at[spot * GROUPS + group])
        return other

    def outward(self, step, spot):
        group = self.place.around(step)
        member = (self.place.corner, self.place.far)[spot]
        ready = self.from_twin(group, member)
        self.add(ready, [self.part(group, member)])
        index = spot * GROUPS + group
        self.send(
            ready,
            self.view(self.far_buf, index),
            self.far_sem.at[index],
            (self.place.group, self.place.far),
        )

    def sideways(self, step):
        group, near = self.place.around(step), self.place.near
        ready = self.from_twin(group, near)
        self.add(ready, [self.part(group, near), self.from_far(group, 0)])
        self.send(
            ready,
            self.view(self.near_buf, group),
            self.near_sem.at[group],
            (self.place.group, near),
        )

    def homeward(self, step):
        group, member = self.place.around(step), self.place.member
        ready = self.from_twin(group, member)
        other = self.view(self.near_buf, group)
        far = self.from_far(group, 1)
        self.arrive(other, self.near_sem.at[group])
        self.add(ready, [self.part(group, member), far, other])
        if step:
            self.send(
                ready,
                self.view(self.group_buf, step - 1),
                self.group_sem.at[step - 1],
                (group, member),
            )

    def finish(self, store):
        for step in TURN:
            self.arrive(self.view(self.group_buf, step - 1), self.group_sem.at[step - 1])
        ready = self.view(self.twin_buf, self.twin_index(self.place.group, self.place.member))

        def some(block, carry):
            at = pl.ds(pl.multiple_of(block * 16, 16), 16)
            total = ready[at].astype(jnp.float32)
            for step in TURN:
                total = total + self.view(self.group_buf, step - 1)[at].astype(jnp.float32)
            store(at, total)
            return carry

        lax.fori_loop(0, self.rows // 16, some, 0)


BACKWARD = (1, 3, 2, 0)


def iota(shape, dim):
    return lax.broadcasted_iota(jnp.int32, shape, dim)


def swap_halves(block):
    lane = iota(block.shape, 1)
    return jnp.where(
        lane % HDIM < HDIM // 2, pltpu.roll(block, 128 - HDIM // 2, 1), pltpu.roll(block, HDIM // 2, 1)
    )


def step_kernel(
    length_ref,
    tokens_hbm,
    cotangent_hbm,
    routes_hbm,
    qkv_hbm,
    out_hbm,
    router_hbm,
    gains_hbm,
    shared_in_hbm,
    shared_down_hbm,
    cosine_hbm,
    sine_hbm,
    expert_in_hbm,
    expert_down_hbm,
    layer_out_hbm,
    input_grad_hbm,
    owned_grad_hbm,
    small_grad_hbm,
    grad_in_hbm,
    grad_down_hbm,
    shared_grad_hbm,
    tokens_ref,
    cotangent_ref,
    routes_ref,
    qkv_ref,
    router_ref,
    gains_ref,
    shared_in_ref,
    shared_down_ref,
    cosine_ref,
    sine_ref,
    owned_ref,
    small_ref,
    small_square,
    layer_out_ref,
    input_grad_ref,
    owned_grad_ref,
    small_grad_ref,
    grad_in_ref,
    grad_down_ref,
    shared_grad_ref,
    pieces_ref,
    stage,
    small_stage,
    mats,
    small_all,
    first_all,
    second_all,
    pieces,
    shared_send,
    weight_in,
    weight_down,
    out_all,
    hidden_low,
    mixed_low,
    pre,
    back_hidden,
    queries,
    keys,
    values,
    probs,
    normed_low,
    context,
    middle_ref,
    mixer,
    rows_sum,
    grad_mid,
    grad_context,
    grad_proj,
    gate_keep,
    twin_a,
    far_a,
    near_a,
    group_a,
    twin_b,
    far_b,
    near_b,
    group_b,
    pair_send,
    pair_recv,
    local_sem,
    store_sem,
    mats_send,
    mats_recv,
    small_send,
    small_recv,
    cot_send,
    cot_recv,
    mix_send,
    mix_recv,
    piece_send,
    piece_recv,
    rows_send,
    out_send,
    own_send,
    twin_sems,
    far_sems,
    near_sems,
    group_sems,
    free_sem,
):
    low = jnp.bfloat16
    rows = tokens_ref.shape[0]
    fetched = {}
    for name, source, target in (
        ("qkv", qkv_hbm, qkv_ref),
        ("out", out_hbm, owned_ref.at[3]),
        ("router", router_hbm, router_ref),
        ("gains", gains_hbm, gains_ref),
        ("cotangent", cotangent_hbm, cotangent_ref),
        ("tokens", tokens_hbm, tokens_ref),
        ("routes", routes_hbm, routes_ref),
        ("cosine", cosine_hbm, cosine_ref),
        ("sine", sine_hbm, sine_ref),
        ("shared_gate", shared_in_hbm.at[:, 0, :], shared_in_ref.at[0]),
        ("shared_up", shared_in_hbm.at[:, 1, :], shared_in_ref.at[1]),
        ("shared_down", shared_down_hbm, shared_down_ref),
        ("gate", expert_in_hbm.at[0, :, 0, :], grad_in_ref.at[:, pl.ds(0, 256)]),
        ("up", expert_in_hbm.at[0, :, 1, :], grad_in_ref.at[:, pl.ds(256, 256)]),
        ("down", expert_down_hbm.at[0], grad_down_ref.at[pl.ds(0, 256)]),
    ):
        fetched[name] = pltpu.make_async_copy(source, target, local_sem.at[len(fetched)])
        fetched[name].start()
    stored = []

    def store_out(source, target):
        copy = pltpu.make_async_copy(source, target, store_sem.at[len(stored)])
        copy.start()
        stored.append(copy)
    place = Place()
    group, member, core = place.group, place.member, place.core
    barrier = pltpu.get_barrier_semaphore()
    place.tell(barrier)
    place.hear(barrier)

    twin_device = (group, place.twin)
    for name in ("qkv", "out", "router", "gains"):
        fetched[name].wait()
    for part in range(3):
        owned_ref[part] = qkv_ref[:, D * part : D * part + D]
    small_square[...] = jnp.zeros_like(small_square)
    small_square[pl.ds(0, GROUPS), pl.ds(0, 24)] = router_ref[...]
    small_square[pl.ds(GROUPS, 2), pl.ds(0, 24)] = gains_ref[...]
    small_ref[...] = small_square[...].T[:24]
    own_rows = pl.ds(pl.multiple_of(24 * core, 8), 24)
    owned = pltpu.make_async_remote_copy(
        src_ref=owned_ref.at[pl.ds(2 * (1 - core), 2)],
        dst_ref=stage.at[:, own_rows],
        send_sem=pair_send.at[0],
        recv_sem=pair_recv.at[0],
        device_id=twin_device,
        device_id_type=MESH,
    )
    owned.start()
    small_pair = pltpu.make_async_remote_copy(
        src_ref=small_ref,
        dst_ref=small_stage.at[own_rows],
        send_sem=pair_send.at[1],
        recv_sem=pair_recv.at[1],
        device_id=twin_device,
        device_id_type=MESH,
    )
    small_pair.start()
    stage[:, own_rows] = owned_ref[pl.ds(2 * core, 2)]
    small_stage[own_rows] = small_ref[...]
    owned.wait()
    small_pair.wait()

    def mats_at(group, member):
        chip = group * (PLANE // 2) + member // 2
        return mats.at[pl.ds(2 * (member % 2), 2), pl.ds(pl.multiple_of(48 * chip, 16), 48)]

    def small_at(group, member):
        chip = group * (PLANE // 2) + member // 2
        return small_all.at[pl.ds(pl.multiple_of(48 * chip, 16), 48)]

    mats_at(group, member)[...] = stage[...].astype(low)
    small_at(group, member)[...] = small_stage[...].astype(low)
    send_small = Gather(place, small_at, small_send, small_recv, pair=False)
    send_mats = Gather(place, mats_at, mats_send, mats_recv)
    send_small.start()
    send_mats.start()

    def move_piece(source, target, sems, base):
        for step in TURN:
            pltpu.make_async_remote_copy(
                src_ref=source.at[place.around(step)],
                dst_ref=target.at[group],
                send_sem=piece_send.at[base + step - 1],
                recv_sem=piece_recv.at[base + (GROUPS - step) - 1],
                device_id=(place.around(step), member),
                device_id_type=MESH,
            ).start()
        target[group] = source[group]

    def wait_pieces(source, target, base):
        for step in TURN:
            copy = pltpu.make_async_remote_copy(
                src_ref=source.at[place.around(step)],
                dst_ref=target.at[place.around(step)],
                send_sem=piece_send.at[base + step - 1],
                recv_sem=piece_recv.at[base + step - 1],
                device_id=(place.around(step), member),
                device_id_type=MESH,
            )
            copy.wait()

    length = length_ref[0]
    row_at = iota((rows, 1), 0)
    live = (row_at < length).astype(jnp.float32)
    fetched["cotangent"].wait()
    first_all[place.mine, pl.ds(0, rows)] = (cotangent_ref[...] * live).astype(low)

    for step in (0,) + TURN:
        if step:
            send_small.own_column(step)
            send_mats.own_column(step)
        send_small.near_column(step)
        send_mats.near_column(step)

    send_cot = Gather(
        place,
        lambda group, member: first_all.at[slot_of(group, member), pl.ds(0, rows)],
        cot_send,
        cot_recv,
    )
    send_cot.start()
    for name in ("shared_gate", "shared_up", "shared_down"):
        fetched[name].wait()
    for piece in range(GROUPS):
        at = pl.ds(64 * piece, 64)
        both_halves = [shared_in_ref[0, :, at], shared_in_ref[1, :, at]]
        pieces_ref[piece, :, pl.ds(0, 128)] = jnp.concatenate(both_halves, axis=1).astype(low)
        last = shared_down_ref[:, at]
        last = jnp.concatenate([last, jnp.zeros_like(last)], axis=1)
        pieces_ref[piece, :, pl.ds(128, 128)] = last.astype(low)
    move_piece(pieces_ref, pieces, piece_send, 0)

    for name in ("gate", "up", "down"):
        fetched[name].wait()
    weight_in[:, pl.ds(0, 512)] = grad_in_ref[:, pl.ds(0, 512)].astype(low)
    weight_down[pl.ds(0, 256)] = grad_down_ref[pl.ds(0, 256)].astype(low)
    grad_down_ref[...] = jnp.zeros_like(grad_down_ref)
    grad_in_ref[...] = jnp.zeros_like(grad_in_ref)

    for step in (0,) + TURN:
        for origin in (place.far, place.corner):
            send_small.wait(place.around(step), origin)
            send_mats.last_column(step, origin)
    for step in TURN:
        send_cot.own_column(step)
    for origin in (place.twin, place.near_twin, place.far_twin, place.corner_twin):
        send_mats.twin_column(origin)

    for name in ("tokens", "routes", "cosine", "sine"):
        fetched[name].wait()
    inputs = tokens_ref[...].astype(jnp.float32)
    inverse_one = lax.rsqrt(jnp.mean(inputs * inputs, axis=-1, keepdims=True) + NORM_EPS)
    pick = (iota((8, 128), 1) == iota((8, 128), 0) + GROUPS).astype(low)
    gains = nt(pick, small_all[...])
    gain_one, gain_two = gains[0:1], gains[1:2]
    normed_low[...] = (inputs * inverse_one * gain_one).astype(low)
    for part, target in ((0, queries), (1, keys), (2, values)):
        pre[pl.ds(0, rows)] = nn(normed_low[...], mats[part])
        for block in range(D // 128):
            at = pl.ds(128 * block, 128)
            piece = pre[pl.ds(0, rows), at]
            if part < 2:
                piece = piece * cosine_ref[...] + swap_halves(piece) * sine_ref[...]
            target[:, at] = piece.astype(low)
    for step in (0, 1):
        send_cot.near_column(step)
    diagonal = iota((rows, rows), 0) == iota((rows, rows), 1)
    query_at, key_at = iota((rows, rows), 0), iota((rows, rows), 1)
    allowed = (key_at <= query_at) & (key_at < length)
    lower = iota((rows, 128), 1) < HDIM

    def attend(pair, carry):
        at = pl.ds(pl.multiple_of(pair * 128, 128), 128)
        query, key, value = queries[:, at], keys[:, at], values[:, at]
        found = []
        for half in (0, 1):
            own = lower if half == 0 else jnp.logical_not(lower)
            scores = nt(jnp.where(own, query, jnp.zeros_like(query)), key) * 0.125
            scores = jnp.where(allowed, scores, MASKED)
            exponent = jnp.exp(scores - jnp.max(scores, axis=-1, keepdims=True))
            prob = exponent / jnp.sum(exponent, axis=-1, keepdims=True)
            probs[pair * 2 + half] = prob
            found.append(nn(prob.astype(low), value))
        context[:, at] = jnp.where(lower, found[0], found[1]).astype(low)
        for serve in range(2):

            @pl.when(pair == serve)
            def _():
                send_cot.near_column((3, 2)[serve])

        return carry

    lax.fori_loop(0, HEADS // 2, attend, 0)
    middle = inputs + nt(context[...], mats[3])
    middle_ref[...] = middle
    inverse_two = lax.rsqrt(jnp.mean(middle * middle, axis=-1, keepdims=True) + NORM_EPS)
    mixer[...] = (middle * inverse_two * gain_two).astype(low)
    logits = nn(mixer[...], small_all[...])
    lane = iota((rows, 128), 1)
    chosen, hits = [], []
    for choice in (0, 1):
        row = routes_ref[choice : choice + 1, pl.ds(pl.multiple_of(member * rows, rows), rows)]
        picked = jnp.sum(jnp.where(diagonal, row.astype(jnp.float32), 0.0), axis=1, keepdims=True)
        hit = (lane.astype(jnp.float32) == picked).astype(jnp.float32)
        hits.append(hit)
        chosen.append(jnp.sum(logits * hit, axis=-1, keepdims=True))
    top = jnp.maximum(chosen[0], chosen[1])
    exponents = [jnp.exp(value - top) for value in chosen]
    total = exponents[0] + exponents[1]
    gates = [value / total for value in exponents]
    gate_keep[...] = jnp.where(lane == 0, gates[0], jnp.where(lane == 1, gates[1], 0.0))
    table = sum(gate.astype(low).astype(jnp.float32) * hit for gate, hit in zip(gates, hits))
    second_all[place.mine, pl.ds(0, rows)] = mixer[...]
    second_all[place.mine, pl.ds(rows, EXTRA)] = jnp.zeros((EXTRA, D), low)
    second_all[place.mine, pl.ds(rows, EXTRA), pl.ds(0, 128)] = table.T[:EXTRA].astype(low)
    send_mix = Gather(
        place, lambda group, member: second_all.at[slot_of(group, member)], mix_send, mix_recv
    )
    send_mix.start()
    for step in (0,) + TURN:
        for origin in (place.far, place.corner):
            send_cot.last_column(step, origin)
    for origin in (place.twin, place.near_twin, place.far_twin, place.corner_twin):
        send_cot.twin_column(origin)
    send_cot.drain(first_all.at[0, pl.ds(0, rows)])

    wait_pieces(pieces_ref, pieces, 0)
    first_half = iota((192, 128), 1) < 64
    for piece in range(GROUPS):
        at = pl.ds(192 * piece, 192)
        both_halves = pieces[piece, :, pl.ds(0, 128)].astype(jnp.float32)
        weight_in[at, pl.ds(512, 128)] = jnp.where(first_half, both_halves, 0.0).astype(low)
        other = pltpu.roll(both_halves, 64, 1)
        weight_in[at, pl.ds(640, 128)] = jnp.where(first_half, other, 0.0).astype(low)
    turned = pieces[:, :, pl.ds(128, 128)].reshape(D, 128).astype(jnp.float32)
    weight_down[pl.ds(256, 128)] = turned.T.astype(low)
    rows_move = Scatter(
        place,
        lambda group, member: first_all.at[slot_of(group, member)],
        rows + EXTRA,
        (twin_a, far_a, near_a, group_a),
        rows_send,
        (twin_sems.at[0], far_sems.at[0], near_sems.at[0], group_sems.at[0]),
    )
    out_move = Scatter(
        place,
        lambda group, member: out_all.at[slot_of(group, member)],
        rows,
        (twin_b, far_b, near_b, group_b),
        out_send,
        (twin_sems.at[1], far_sems.at[1], near_sems.at[1], group_sems.at[1]),
    )
    extra_row = iota((EXTRA, 128), 0) == group
    twins = (place.corner_twin, place.near_twin, place.far_twin, place.twin)

    def both(step):
        for spot in (0, 1):
            rows_move.outward(step, spot)

    serve_before = (
        lambda: (
            send_mix.own_column(1),
            send_mix.near_column(1),
            send_mix.own_column(3),
            send_mix.last_plane(1),
        ),
        lambda: (send_mix.near_column(3), send_mix.own_column(2), send_mix.twin_plane(1)),
        lambda: (send_mix.near_column(2), send_mix.near_column(0), send_mix.last_plane(3)),
        lambda: (both(1), send_mix.twin_plane(3)),
        lambda: send_mix.last_plane(2),
        lambda: (both(3), rows_move.sideways(1), send_mix.twin_plane(2)),
        lambda: send_mix.last_plane(0),
        lambda: (
            both(2),
            rows_move.sideways(3),
            rows_move.homeward(1),
            send_mix.twin_plane(0),
        ),
    )

    def tokens_part(index, carry):
        for at in range(PLANE):

            @pl.when(index == at)
            def _():
                serve_before[at]()

        half = index // 2
        step = jnp.where(half == 0, 1, jnp.where(half == 1, 3, jnp.where(half == 2, 2, 0)))
        side = (core + index) % 2
        base = pl.multiple_of(place.around(step) * PLANE + side * GROUPS, GROUPS)
        four = pl.ds(base, GROUPS)
        taken = second_all[four, pl.ds(0, rows)].reshape(GROUPS * rows, D)
        pre[...] = nn(taken, weight_in[...])
        cot = first_all[four, pl.ds(0, rows)].reshape(GROUPS * rows, D)
        back_hidden[...] = nt(cot, weight_down[...])

        def units(block, carry):
            slot = base + block
            gate_block = second_all[slot, pl.ds(rows, EXTRA), pl.ds(0, 128)].astype(jnp.float32)
            gate_row = jnp.sum(jnp.where(extra_row, gate_block, 0.0), axis=0, keepdims=True)
            scale = jnp.sum(jnp.where(diagonal, gate_row, 0.0), axis=1, keepdims=True)
            at = pl.ds(pl.multiple_of(block * rows, rows), rows)
            weigh = jnp.zeros((rows, 1), jnp.float32)
            for gate_at, up_at, hidden_at, routed in (
                (0, 256, 0, True),
                (128, 384, 128, True),
                (512, 640, 256, False),
            ):
                gate_pre = pre[at, pl.ds(gate_at, 128)]
                up_pre = pre[at, pl.ds(up_at, 128)]
                hidden_grad = back_hidden[at, pl.ds(hidden_at, 128)]
                sigmoid_g = jax.nn.sigmoid(gate_pre)
                silu_g = gate_pre * sigmoid_g
                hidden = (silu_g * up_pre).astype(low)
                if routed:
                    wide = hidden.astype(jnp.float32)
                    weigh = weigh + jnp.sum(wide * hidden_grad, axis=-1, keepdims=True)
                    hidden_grad = hidden_grad * scale
                    hidden = (wide * scale).astype(low)
                grad_gate = hidden_grad * up_pre * sigmoid_g * (1.0 + gate_pre * (1.0 - sigmoid_g))
                hidden_low[at, pl.ds(hidden_at, 128)] = hidden
                mixed_low[at, pl.ds(gate_at, 128)] = grad_gate.astype(low)
                mixed_low[at, pl.ds(up_at, 128)] = (hidden_grad * silu_g).astype(low)
            weigh_row = jnp.sum(jnp.where(diagonal, weigh, 0.0), axis=0, keepdims=True)
            extra = jnp.where(extra_row, weigh_row, 0.0).astype(low)
            first_all[slot, pl.ds(rows, EXTRA)] = jnp.zeros((EXTRA, D), low)
            first_all[slot, pl.ds(rows, EXTRA), pl.ds(0, 128)] = extra
            return carry

        lax.fori_loop(0, GROUPS, units, 0)
        grad_down_ref[...] += tn(hidden_low[...], cot)
        pre[...] = nt(mixed_low[...], weight_in[...])
        first_all[four, pl.ds(0, rows)] = pre[...].astype(low).reshape(GROUPS, rows, D)
        for at in range(1, PLANE, 2):

            @pl.when(index == at)
            def _():
                for origin in twins:
                    rows_move.to_twin(place.around(BACKWARD[at // 2]), origin)

        taken = second_all[four, pl.ds(0, rows)].reshape(GROUPS * rows, D)
        grad_in_ref[...] += tn(taken, mixed_low[...])
        pre[...] = nn(hidden_low[...], weight_down[...])
        out_all[four] = pre[...].astype(low).reshape(GROUPS, rows, D)
        for at in range(1, PLANE, 2):

            @pl.when(index == at)
            def _():
                for origin in twins:
                    out_move.to_twin(place.around(BACKWARD[at // 2]), origin)

        return carry

    lax.fori_loop(0, PLANE, tokens_part, 0)
    both(0)
    rows_move.sideways(2)
    rows_move.homeward(3)
    rows_move.sideways(0)
    rows_move.homeward(2)
    rows_move.homeward(0)
    send_mix.drain(second_all.at[0])

    for piece in range(GROUPS):
        at = pl.ds(192 * piece, 192)
        both_halves = [grad_in_ref[at, pl.ds(512, 64)], grad_in_ref[at, pl.ds(640, 64)]]
        shared_send[piece, :, pl.ds(0, 128)] = jnp.concatenate(both_halves, axis=1).astype(low)
    turned = grad_down_ref[pl.ds(256, 128)].T
    shared_send[:, :, pl.ds(128, 128)] = turned.astype(low).reshape(GROUPS, 192, 128)
    store_out(grad_in_ref.at[:, pl.ds(0, 512)], grad_in_hbm)
    store_out(grad_down_ref.at[pl.ds(0, 256)], grad_down_hbm)
    move_piece(shared_send, shared_grad_ref, piece_send, 3)

    def keep_rows(at, total):
        rows_sum[at] = total

    rows_move.finish(keep_rows)
    rows_move.drain(first_all.at[0])
    place.tell(free_sem)

    gate_grads = rows_sum[pl.ds(rows, EXTRA), pl.ds(0, 128)]
    gate_grads = jnp.concatenate([gate_grads, jnp.zeros((rows - EXTRA, 128), jnp.float32)], axis=0).T
    grad_gates = [jnp.sum(gate_grads * hit, axis=-1, keepdims=True) for hit in hits]
    kept = [
        jnp.sum(jnp.where(lane == choice, gate_keep[...], 0.0), axis=-1, keepdims=True)
        for choice in (0, 1)
    ]
    gate_dot = kept[0] * grad_gates[0] + kept[1] * grad_gates[1]
    grad_logits = sum(
        hit * (gate * (grad - gate_dot)) for hit, gate, grad in zip(hits, kept, grad_gates)
    ).astype(low)
    grad_router = tn(grad_logits, mixer[...])[:8]
    middle = middle_ref[...]
    inverse_two = lax.rsqrt(jnp.mean(middle * middle, axis=-1, keepdims=True) + NORM_EPS)
    scaled_two = middle * inverse_two
    gains = nt(pick, small_all[...])
    gain_one, gain_two = gains[0:1], gains[1:2]
    grad_normed = rows_sum[pl.ds(0, rows)] + nt(grad_logits, small_all[...])
    grad_gain_two = jnp.sum(grad_normed * scaled_two, axis=0, keepdims=True)
    grad_scaled = grad_normed * gain_two
    grad_middle = cotangent_ref[...] * live + inverse_two * (
        grad_scaled - scaled_two * jnp.mean(grad_scaled * scaled_two, axis=-1, keepdims=True)
    )
    grad_mid[...] = grad_middle
    grad_att = grad_middle.astype(low)
    grad_context[...] = nn(grad_att, mats[3]).astype(low)

    own_move = Scatter(
        place,
        lambda group, member: first_all.at[slot_of(group, member), pl.ds(0, 96 + EXTRA)],
        96 + EXTRA,
        (twin_a, far_a, near_a, group_a),
        own_send,
        (twin_sems.at[2], far_sems.at[2], near_sems.at[2], group_sems.at[2]),
    )

    def put_part(which, left, right):
        for half in (0, 1):
            product = tn(left[:, 384 * half : 384 * half + 384], right).astype(low)
            for place_in in range(8):
                chip = half * 8 + place_in
                slot = slot_of(chip // 4, (chip % 4) * 2 + which // 2)
                first_all[slot, pl.ds(48 * (which % 2), 48)] = product[48 * place_in : 48 * place_in + 48]

    put_part(3, grad_att, context[...])

    def attend_back(pair, carry):
        at = pl.ds(pl.multiple_of(pair * 128, 128), 128)
        query, key, value = queries[:, at], keys[:, at], values[:, at]
        grad_ctx = grad_context[:, at]
        grad_query, grad_key, grad_value = [], [], []
        for half in (0, 1):
            own = lower if half == 0 else jnp.logical_not(lower)
            prob = probs[pair * 2 + half]
            grad_prob = nt(jnp.where(own, grad_ctx, jnp.zeros_like(grad_ctx)), value)
            grad_value.append(tn(prob.astype(low), grad_ctx))
            row_dot = jnp.sum(grad_prob * prob, axis=-1, keepdims=True)
            grad_score = (prob * (grad_prob - row_dot)).astype(low)
            grad_query.append(nn(grad_score, key))
            grad_key.append(tn(grad_score, query))
        grad_q = jnp.where(lower, grad_query[0], grad_query[1]) * 0.125
        grad_k = jnp.where(lower, grad_key[0], grad_key[1]) * 0.125
        grad_q = grad_q * cosine_ref[...] - swap_halves(grad_q) * sine_ref[...]
        grad_k = grad_k * cosine_ref[...] - swap_halves(grad_k) * sine_ref[...]
        grad_proj[0, :, at] = grad_q.astype(low)
        grad_proj[1, :, at] = grad_k.astype(low)
        grad_proj[2, :, at] = jnp.where(lower, grad_value[0], grad_value[1]).astype(low)
        for serve in range(4):

            @pl.when(pair == serve)
            def _():
                for spot in (0, 1):
                    out_move.outward(BACKWARD[serve], spot)

        return carry

    lax.fori_loop(0, HEADS // 2, attend_back, 0)
    grad_one = nt(grad_proj[0], mats[0]) + nt(grad_proj[1], mats[1]) + nt(grad_proj[2], mats[2])
    inputs = tokens_ref[...].astype(jnp.float32)
    inverse_one = lax.rsqrt(jnp.mean(inputs * inputs, axis=-1, keepdims=True) + NORM_EPS)
    scaled_one = inputs * inverse_one
    grad_gain_one = jnp.sum(grad_one * scaled_one, axis=0, keepdims=True)
    grad_scaled = grad_one * gain_one
    input_grad_ref[...] = grad_mid[...] + inverse_one * (
        grad_scaled - scaled_one * jnp.mean(grad_scaled * scaled_one, axis=-1, keepdims=True)
    )
    store_out(input_grad_ref, input_grad_hbm)
    for which in range(3):
        put_part(which, normed_low[...], grad_proj[which])
    at_row = iota((8, D), 0)
    small_rows = jnp.where(
        at_row < GROUPS, grad_router, jnp.where(at_row == GROUPS, grad_gain_one, grad_gain_two)
    )
    small_rows = jnp.concatenate([small_rows, jnp.zeros((8, D), jnp.float32)], axis=0).astype(low)

    def put_small(slot, carry):
        first_all[slot, pl.ds(96, EXTRA)] = small_rows
        return carry

    lax.fori_loop(0, ALL, put_small, 0)
    place.hear(free_sem)
    for step in BACKWARD:
        for origin in (place.corner_twin, place.near_twin, place.far_twin, place.twin):
            own_move.to_twin(place.around(step), origin)
    for step in BACKWARD:
        for spot in (0, 1):
            own_move.outward(step, spot)
    for step in BACKWARD:
        out_move.sideways(step)
    for step in BACKWARD:
        own_move.sideways(step)
    for step in BACKWARD:
        out_move.homeward(step)
    for step in BACKWARD:
        own_move.homeward(step)

    def keep_out(at, total):
        here = pl.ds(at.start, 16)
        live_here = (iota((16, 1), 0) + at.start < length).astype(jnp.float32)
        layer_out_ref[here] = live_here * (middle_ref[here] + total)

    out_move.finish(keep_out)
    store_out(layer_out_ref, layer_out_hbm)
    wait_pieces(shared_send, shared_grad_ref, 3)
    store_out(shared_grad_ref, shared_grad_hbm)

    def keep_own(at, total):
        rows_sum[at] = total

    own_move.finish(keep_own)
    for matrix in (0, 1):
        stage[matrix] = rows_sum[pl.ds(48 * matrix, 48)]
    theirs = pl.ds(pl.multiple_of(24 * (1 - core), 8), 24)
    mine = pl.ds(2 * core, 2)
    last = pltpu.make_async_remote_copy(
        src_ref=stage.at[:, theirs],
        dst_ref=owned_grad_ref.at[mine],
        send_sem=pair_send.at[2],
        recv_sem=pair_recv.at[2],
        device_id=twin_device,
        device_id_type=MESH,
    )
    last.start()
    owned_grad_ref[mine] = stage[:, own_rows]
    first_lane = (group * PLANE + member) * 24
    turned = pltpu.roll(rows_sum[pl.ds(96, 8)], D - first_lane, 1)
    small_grad_ref[...] = turned[:, :128]
    store_out(small_grad_ref, small_grad_hbm)
    last.wait()
    store_out(owned_grad_ref, owned_grad_hbm)
    out_move.drain(out_all.at[0])
    own_move.drain(first_all.at[0, pl.ds(0, 96 + EXTRA)])
    send_mats.drain(mats_at(group, member))
    send_small.drain(small_at(group, member))
    for copy in stored:
        copy.wait()


def update_kernel(*refs):
    (
        owned_grad,
        small_grad,
        grad_in,
        grad_down,
        shared_grad,
        layer_in,
        input_in,
    ) = refs[:7]
    olds = [refs[7 + 3 * at : 10 + 3 * at] for at in range(8)]
    layer_out, input_out = refs[31:33]
    news = [refs[33 + 3 * at : 36 + 3 * at] for at in range(8)]
    owned_buf, small_buf, in_buf, down_buf, shared_buf, layer_buf, input_buf = refs[57:64]
    bufs, load_sem, store_sem = refs[64:-2], refs[-2], refs[-1]
    counts = [0, 0]

    def copy(source, target, which):
        made = pltpu.make_async_copy(source, target, (load_sem, store_sem)[which].at[counts[which]])
        counts[which] += 1
        made.start()
        return made

    half = D // 2
    jobs = []
    for at in range(2):
        for block in range(2):
            jobs.append((6, lambda ref, at=at, block=block: ref.at[0, pl.ds(half * block, half), at, :], (half, 256)))
    jobs.append((7, lambda ref: ref.at[0], (256, D)))
    for at in range(2):
        jobs.append((4, lambda ref, at=at: ref.at[:, at, :], (192, 256)))
    for which in (5, 1, 2, 3, 0):
        jobs.append((which, lambda ref: ref, None))
    passes, loaded = [], []
    through = [copy(layer_in, layer_buf, 0), copy(input_in, input_buf, 0)]
    first_grads = [copy(grad_in, in_buf, 0), copy(grad_down, down_buf, 0)]
    other_grads = [copy(shared_grad, shared_buf, 0), copy(owned_grad, owned_buf, 0), copy(small_grad, small_buf, 0)]
    for at, (which, view, _) in enumerate(jobs):
        loaded.append([copy(view(olds[which][k]), bufs[3 * at + k], 0) for k in range(3)])
    for made in first_grads + through:
        made.wait()
    passes += [copy(layer_buf, layer_out, 1), copy(input_buf, input_out, 1)]
    rates = (
        0.5,
        1.5 / math.sqrt(D),
        1.5 / math.sqrt(4 * D // SEQ),
        1.0 / math.sqrt(D),
        1.5 / math.sqrt(D),
        1.5 / math.sqrt(FF_SH),
        1.5 / math.sqrt(D),
        1.5 / math.sqrt(FF),
    )

    def pair_up(part, swap_first, swap_second):
        left = iota((192, 128), 1) < 64
        tiles = []
        for tile in range(2):
            pair = [
                shared_buf[2 * tile + k, :, pl.ds(128 * part, 128)].astype(jnp.float32) for k in (0, 1)
            ]
            if swap_first:
                pair[0] = pltpu.roll(pair[0], 64, 1)
            if swap_second:
                pair[1] = pltpu.roll(pair[1], 64, 1)
            tiles.append(jnp.where(left, pair[0], pair[1]))
        return jnp.concatenate(tiles, axis=1)

    for at, (which, view, shape) in enumerate(jobs):
        if at == 5:
            for made in other_grads:
                made.wait()
        for made in loaded[at]:
            made.wait()
        mine = bufs[3 * at : 3 * at + 3]
        rate = rates[which]

        def update(index, gradient):
            weight, first_old, second_old = (ref[index] for ref in mine)
            results = adamw(weight, gradient, first_old, second_old, rate)
            for ref, value in zip(mine, results):
                ref[index] = value

        if which == 6:
            part, block = at // 2, at % 2

            def chunk(number, carry):
                here = pl.ds(pl.multiple_of(number * 32, 32), 32)
                there = pl.ds(pl.multiple_of(half * block + number * 32, 32), 32)
                update(here, in_buf[there, pl.ds(256 * part, 256)])
                return carry

            lax.fori_loop(0, half // 32, chunk, 0)
        elif which == 7:

            def chunk(number, carry):
                here = pl.ds(pl.multiple_of(number * 8, 8), 8)
                update(here, down_buf[here])
                return carry

            lax.fori_loop(0, 32, chunk, 0)
        elif which == 4:
            update(..., pair_up(0, at == 6, at == 5))
        elif which == 5:
            update(..., pair_up(1, False, True))
        elif which == 1:
            for part in range(3):
                update((slice(None), pl.ds(D * part, D)), owned_buf[part])
        elif which == 2:
            update(..., owned_buf[3])
        elif which == 3:
            update(..., small_buf[:4, :24])
        else:
            update(..., small_buf[4:6, :24])
        for k in range(3):
            passes.append(copy(mine[k], view(news[which][k]), 1))
    for made in passes:
        made.wait()


def dense_shards(
    tokens,
    cotangent,
    lengths,
    routes,
    norm_gains,
    gains_first,
    gains_second,
    qkv_weight,
    qkv_first,
    qkv_second,
    out_weight,
    out_first,
    out_second,
    router_weight,
    router_first,
    router_second,
    shared_in,
    shared_in_first,
    shared_in_second,
    shared_down,
    shared_down_first,
    shared_down_second,
    expert_in,
    expert_in_first,
    expert_in_second,
    expert_down,
    expert_down_first,
    expert_down_second,
):
    low_type = jnp.bfloat16
    seq_rows = tokens.shape[0]
    per_device = D // ALL
    half_dim = HDIM // 2
    positions = np.arange(seq_rows, dtype=np.float32)[:, None]
    angles = positions * np.tile(ROPE_BASE ** (-np.arange(half_dim) / half_dim), 4)[None]
    sign = np.tile(np.repeat([-1.0, 1.0], half_dim), 2)[None]
    cosine = jnp.asarray(np.cos(angles), jnp.float32)
    sine = jnp.asarray(np.sin(angles) * sign, jnp.float32)
    wide, f32, i32 = low_type, jnp.float32, jnp.int32
    tall = seq_rows + EXTRA
    dma = pltpu.SemaphoreType.DMA
    anywhere = pl.BlockSpec(memory_space=pltpu.HBM)
    passed = pl.pallas_call(
        step_kernel,
        out_shape=(
            jax.ShapeDtypeStruct((seq_rows, D), f32),
            jax.ShapeDtypeStruct((seq_rows, D), f32),
            jax.ShapeDtypeStruct((4, per_device, D), f32),
            jax.ShapeDtypeStruct((8, 128), f32),
            jax.ShapeDtypeStruct((D, 512), f32),
            jax.ShapeDtypeStruct((256, D), f32),
            jax.ShapeDtypeStruct((GROUPS, 192, 256), wide),
        ),
        in_specs=[pl.BlockSpec(memory_space=pltpu.SMEM)] + [anywhere] * 13,
        out_specs=(anywhere,) * 7,
        scratch_shapes=[
            pltpu.VMEM((seq_rows, D), wide),
            pltpu.VMEM((seq_rows, D), f32),
            pltpu.VMEM((2, PLANE * seq_rows), i32),
            pltpu.VMEM((per_device, 3 * D), f32),
            pltpu.VMEM((GROUPS, per_device), f32),
            pltpu.VMEM((2, per_device), f32),
            pltpu.VMEM((2, 192, 256), f32),
            pltpu.VMEM((192, 256), f32),
            pltpu.VMEM((seq_rows, 128), f32),
            pltpu.VMEM((seq_rows, 128), f32),
            pltpu.VMEM((4, per_device, D), f32),
            pltpu.VMEM((per_device, 128), f32),
            pltpu.VMEM((128, 128), f32),
            pltpu.VMEM((seq_rows, D), f32),
            pltpu.VMEM((seq_rows, D), f32),
            pltpu.VMEM((4, per_device, D), f32),
            pltpu.VMEM((8, 128), f32),
            pltpu.VMEM((D, 768), f32),
            pltpu.VMEM((384, D), f32),
            pltpu.VMEM((GROUPS, 192, 256), wide),
            pltpu.VMEM((GROUPS, 192, 256), wide),
            pltpu.VMEM((2, 48, D), f32),
            pltpu.VMEM((48, 128), f32),
            pltpu.VMEM((4, D, D), wide),
            pltpu.VMEM((D, 128), wide),
            pltpu.VMEM((ALL, tall, D), wide),
            pltpu.VMEM((ALL, tall, D), wide),
            pltpu.VMEM((GROUPS, 192, 256), wide),
            pltpu.VMEM((GROUPS, 192, 256), wide),
            pltpu.VMEM((D, 768), wide),
            pltpu.VMEM((384, D), wide),
            pltpu.VMEM((ALL, seq_rows, D), wide),
            pltpu.VMEM((GROUPS * seq_rows, 384), wide),
            pltpu.VMEM((GROUPS * seq_rows, 768), wide),
            pltpu.VMEM((GROUPS * seq_rows, 768), f32),
            pltpu.VMEM((GROUPS * seq_rows, 384), f32),
            pltpu.VMEM((seq_rows, D), wide),
            pltpu.VMEM((seq_rows, D), wide),
            pltpu.VMEM((seq_rows, D), wide),
            pltpu.VMEM((HEADS, seq_rows, seq_rows), f32),
            pltpu.VMEM((seq_rows, D), wide),
            pltpu.VMEM((seq_rows, D), wide),
            pltpu.VMEM((seq_rows, D), f32),
            pltpu.VMEM((seq_rows, D), wide),
            pltpu.VMEM((tall, D), f32),
            pltpu.VMEM((seq_rows, D), f32),
            pltpu.VMEM((seq_rows, D), wide),
            pltpu.VMEM((3, seq_rows, D), wide),
            pltpu.VMEM((seq_rows, 128), f32),
            pltpu.VMEM((16, tall, D), wide),
            pltpu.VMEM((8, tall, D), wide),
            pltpu.VMEM((4, tall, D), wide),
            pltpu.VMEM((3, tall, D), wide),
            pltpu.VMEM((16, seq_rows, D), wide),
            pltpu.VMEM((8, seq_rows, D), wide),
            pltpu.VMEM((4, seq_rows, D), wide),
            pltpu.VMEM((3, seq_rows, D), wide),
            dma((3,)),
            dma((3,)),
            dma((15,)),
            dma((7,)),
            dma((31,)),
            dma((32,)),
            dma((31,)),
            dma((32,)),
            dma((31,)),
            dma((32,)),
            dma((31,)),
            dma((32,)),
            dma((6,)),
            dma((6,)),
            dma((31,)),
            dma((31,)),
            dma((31,)),
            dma((3, 16)),
            dma((3, 8)),
            dma((3, 4)),
            dma((3, 3)),
            pltpu.SemaphoreType.REGULAR,
        ],
        compiler_params=pltpu.CompilerParams(
            collective_id=0, has_side_effects=True, vmem_limit_bytes=VMEM_BYTES
        ),
    )(
        lengths,
        tokens,
        cotangent,
        routes.T,
        qkv_weight,
        out_weight.T,
        router_weight.T,
        norm_gains,
        shared_in,
        shared_down.T,
        cosine,
        sine,
        expert_in,
        expert_down,
    )
    layer_out, input_grad, owned_grad, small_grad, grad_in, grad_down, shared_grad = passed
    olds = [
        (norm_gains, gains_first, gains_second),
        (qkv_weight, qkv_first, qkv_second),
        (out_weight.T, out_first.T, out_second.T),
        (router_weight.T, router_first.T, router_second.T),
        (shared_in, shared_in_first, shared_in_second),
        (shared_down.T, shared_down_first.T, shared_down_second.T),
        (expert_in, expert_in_first, expert_in_second),
        (expert_down, expert_down_first, expert_down_second),
    ]
    flat = [old for three in olds for old in three]
    gradients = (owned_grad, small_grad, grad_in, grad_down, shared_grad)
    shapes = [(D // 2, 256)] * 4 + [(256, D)] + [(192, 256)] * 2 + [(192, 256)]
    shapes += [(per_device, 3 * D), (per_device, D), (GROUPS, per_device), (2, per_device)]
    results = pl.pallas_call(
        update_kernel,
        out_shape=tuple(
            jax.ShapeDtypeStruct(value.shape, value.dtype) for value in [layer_out, input_grad] + flat
        ),
        in_specs=[anywhere] * 31,
        out_specs=(anywhere,) * 26,
        scratch_shapes=[pltpu.VMEM(value.shape, value.dtype) for value in gradients + (layer_out, input_grad)]
        + [pltpu.VMEM(shape, f32) for shape in shapes for _ in range(3)]
        + [dma((43,)), dma((38,))],
        compiler_params=pltpu.CompilerParams(vmem_limit_bytes=VMEM_BYTES),
    )(*gradients, layer_out, input_grad, *flat)
    results = list(results)
    for at in (2 + 6, 2 + 9, 2 + 15):
        for k in range(3):
            results[at + k] = results[at + k].T
    return tuple(results)


def solution(mesh):
    placed = (
        P(("expert", "head"), None),
        P(("expert", "head"), None),
        P(("expert", "head")),
        P("expert", None),
        P(None, ("expert", "head")),
        P(None, ("expert", "head")),
        P(None, ("expert", "head")),
        P(("expert", "head"), None),
        P(("expert", "head"), None),
        P(("expert", "head"), None),
        P(None, ("expert", "head")),
        P(None, ("expert", "head")),
        P(None, ("expert", "head")),
        P(("expert", "head"), None),
        P(("expert", "head"), None),
        P(("expert", "head"), None),
        P("expert", None, "head"),
        P("expert", None, "head"),
        P("expert", None, "head"),
        P("head", "expert"),
        P("head", "expert"),
        P("head", "expert"),
        P("expert", None, None, "head"),
        P("expert", None, None, "head"),
        P("expert", None, None, "head"),
        P("expert", "head", None),
        P("expert", "head", None),
        P("expert", "head", None),
    )
    return jax.shard_map(
        dense_shards if (mesh.shape["expert"], mesh.shape["head"]) == (4, 8) else routed_shards,
        mesh=mesh,
        in_specs=placed,
        out_specs=(
            P(("expert", "head"), None),
            P(("expert", "head"), None),
            P(None, ("expert", "head")),
            P(None, ("expert", "head")),
            P(None, ("expert", "head")),
            P(("expert", "head"), None),
            P(("expert", "head"), None),
            P(("expert", "head"), None),
            P(None, ("expert", "head")),
            P(None, ("expert", "head")),
            P(None, ("expert", "head")),
            P(("expert", "head"), None),
            P(("expert", "head"), None),
            P(("expert", "head"), None),
            P("expert", None, "head"),
            P("expert", None, "head"),
            P("expert", None, "head"),
            P("head", "expert"),
            P("head", "expert"),
            P("head", "expert"),
            P("expert", None, None, "head"),
            P("expert", None, None, "head"),
            P("expert", None, None, "head"),
            P("expert", "head", None),
            P("expert", "head", None),
            P("expert", "head", None),
        ),
        check_vma=False,
    )
```

```python
import math

import jax
import jax.numpy as jnp
import numpy as np
from jax import lax
from jax.experimental import pallas as pl
from jax.experimental.pallas import tpu as pltpu
from jax.sharding import PartitionSpec as P

D = 768
HEADS = 12
HDIM = 64
FF = 2048
FF_SH = 2048
SEQ = 128
STEP = 4


NORM_EPS = 1e-06
BETA_FIRST = 0.5
BETA_SECOND = 0.5
ADAM_EPS = 1e-08
DECAY = 0.1
MASKED = -1e30
ROPE_BASE = 10000.0


def rope_tables(row_count):
    half_dim = HDIM // 2
    positions = jnp.arange(row_count, dtype=jnp.float32)
    frequency = ROPE_BASE ** (-jnp.arange(half_dim, dtype=jnp.float32) / half_dim)
    angles = positions[:, None] * frequency[None, :]
    return (jnp.cos(angles)[:, None, :], jnp.sin(angles)[:, None, :])


def rotate(values, cosine_table, sine_table):
    half_dim = values.shape[-1] // 2
    first_half = values[..., :half_dim]
    second_half = values[..., half_dim:]
    return jnp.concatenate(
        [
            first_half * cosine_table - second_half * sine_table,
            second_half * cosine_table + first_half * sine_table,
        ],
        axis=-1,
    )


def unrotate(gradient, cosine_table, sine_table):
    half_dim = gradient.shape[-1] // 2
    first_half = gradient[..., :half_dim]
    second_half = gradient[..., half_dim:]
    return jnp.concatenate(
        [
            first_half * cosine_table + second_half * sine_table,
            second_half * cosine_table - first_half * sine_table,
        ],
        axis=-1,
    )


def norm_forward(values, gain_vec):
    inverse = lax.rsqrt(jnp.mean(values * values, axis=-1, keepdims=True) + NORM_EPS)
    scaled = values * inverse
    return (scaled, inverse, scaled * gain_vec)


def norm_backward(grad_out, scaled, inverse, gain_vec):
    grad_scaled = grad_out * gain_vec
    grad_gain = jnp.sum(grad_out * scaled, axis=0)
    grad_in = inverse * (
        grad_scaled - scaled * jnp.mean(grad_scaled * scaled, axis=-1, keepdims=True)
    )
    return (grad_in, grad_gain)


def attention_scores(query_rows, key_rows, length):
    row_count = query_rows.shape[0]
    scores = (
        jnp.einsum("qhd,khd->hqk", query_rows, key_rows, preferred_element_type=jnp.float32) * 0.125
    )
    positions = jnp.arange(row_count, dtype=jnp.int32)
    allowed = (positions[None, :] <= positions[:, None]) & (positions[None, :] < length)
    return (jnp.where(allowed[None], scores, MASKED), allowed)


def expert_forward(row_block, weight_in, weight_down):
    mixed_pre = jnp.dot(row_block, weight_in, preferred_element_type=jnp.float32)
    hidden_width = weight_down.shape[0]
    gate_pre = mixed_pre[:, :hidden_width]
    up_pre = mixed_pre[:, hidden_width:]
    hidden = (gate_pre * jax.nn.sigmoid(gate_pre) * up_pre).astype(jnp.bfloat16)
    return (mixed_pre, hidden, jnp.dot(hidden, weight_down, preferred_element_type=jnp.float32))


def expert_backward(row_block, mixed_pre, hidden, grad_out, weight_in, weight_down):
    hidden_width = weight_down.shape[0]
    gate_pre = mixed_pre[:, :hidden_width]
    up_pre = mixed_pre[:, hidden_width:]
    grad_hidden = jnp.dot(grad_out, weight_down.T, preferred_element_type=jnp.float32)
    sigmoid_g = jax.nn.sigmoid(gate_pre)
    silu_g = gate_pre * sigmoid_g
    grad_gate = (grad_hidden * up_pre * sigmoid_g * (1.0 + gate_pre * (1.0 - sigmoid_g))).astype(
        jnp.bfloat16
    )
    grad_up = (grad_hidden * silu_g).astype(jnp.bfloat16)
    grad_mixed = jnp.concatenate([grad_gate, grad_up], axis=1)
    grad_down = jnp.dot(hidden.T, grad_out, preferred_element_type=jnp.float32)
    grad_weight_in = jnp.dot(row_block.T, grad_mixed, preferred_element_type=jnp.float32)
    grad_row_block = jnp.dot(grad_mixed, weight_in.T, preferred_element_type=jnp.float32)
    return (grad_row_block, grad_weight_in, grad_down)


def route_tables(route_rows, blocks, block_cap, expert_total):
    per_block = route_rows.reshape(blocks, -1)
    hit_table = (
        per_block[:, :, None] == jnp.arange(expert_total, dtype=jnp.int32)[None, None, :]
    ).astype(jnp.int32)
    entries = per_block.shape[1]
    earlier = jnp.tril(jnp.ones((entries, entries), jnp.bfloat16))
    running = jnp.einsum(
        "ij,bje->bie", earlier, hit_table.astype(jnp.bfloat16), preferred_element_type=jnp.float32
    ).astype(jnp.int32)
    rank_in = jnp.sum((running - 1) * hit_table, axis=2)
    offsets = jnp.arange(blocks, dtype=jnp.int32)[:, None] * block_cap
    dest_slot = (per_block * (blocks * block_cap) + offsets + rank_in).reshape(-1)
    source_row = (
        jnp.zeros((expert_total * blocks * block_cap,), jnp.int32)
        .at[dest_slot]
        .set(jnp.arange(dest_slot.shape[0], dtype=jnp.int32) + 1)
    )
    return (dest_slot, source_row)


def pack_tokens(token_rows, source_row):
    padded = jnp.concatenate(
        [jnp.zeros((1, token_rows.shape[1]), token_rows.dtype), token_rows], axis=0
    )
    pick_rows = jnp.where(source_row > 0, (source_row - 1) // 2 + 1, 0)
    return padded[pick_rows]


def pack_routes(route_values, source_row):
    padded = jnp.concatenate(
        [jnp.zeros((1, route_values.shape[1]), route_values.dtype), route_values], axis=0
    )
    return padded[source_row]


def adamw(weight, gradient, first_old, second_old, step_rate):
    first_new = BETA_FIRST * first_old + (1.0 - BETA_FIRST) * gradient
    second_new = BETA_SECOND * second_old + (1.0 - BETA_SECOND) * gradient * gradient
    first_hat = first_new / (1.0 - BETA_FIRST**STEP)
    second_hat = second_new / (1.0 - BETA_SECOND**STEP)
    new_weight = weight - step_rate * (
        first_hat / (jnp.sqrt(second_hat) + ADAM_EPS) + DECAY * weight
    )
    return (new_weight, first_new, second_new)


def routed_shards(
    tokens,
    cotangent,
    lengths,
    routes,
    norm_gains,
    gains_first,
    gains_second,
    qkv_weight,
    qkv_first,
    qkv_second,
    out_weight,
    out_first,
    out_second,
    router_weight,
    router_first,
    router_second,
    shared_in,
    shared_in_first,
    shared_in_second,
    shared_down,
    shared_down_first,
    shared_down_second,
    expert_in,
    expert_in_first,
    expert_in_second,
    expert_down,
    expert_down_first,
    expert_down_second,
):
    low_type = jnp.bfloat16
    seq_rows = tokens.shape[0]
    head_total = lax.axis_size("head")
    expert_total = lax.axis_size("expert")
    head_at = lax.axis_index("head")
    cap_dev = 4 * seq_rows // expert_total
    gains_all, qkv_all, out_all, router_all = (
        lax.all_gather(norm_gains.astype(low_type), ("expert", "head"), axis=1, tiled=True),
        lax.all_gather(qkv_weight.astype(low_type), ("expert", "head"), axis=0, tiled=True),
        lax.all_gather(out_weight.astype(low_type), ("expert", "head"), axis=1, tiled=True),
        lax.all_gather(router_weight.astype(low_type), ("expert", "head"), axis=0, tiled=True),
    )
    shared_in_all, shared_down_all = (
        lax.all_gather(shared_in.astype(low_type), "expert", axis=0, tiled=True),
        lax.all_gather(shared_down.astype(low_type), "expert", axis=1, tiled=True),
    )
    shared_in_flat = shared_in_all.reshape(D, -1)
    gain_one = gains_all[0].astype(jnp.float32)
    gain_two = gains_all[1].astype(jnp.float32)
    length = lengths[0]
    inputs = tokens.astype(jnp.float32)
    scaled_one, inverse_one, normed_one = norm_forward(inputs, gain_one)
    normed_low = normed_one.astype(low_type)
    projected = jnp.dot(normed_low, qkv_all, preferred_element_type=jnp.float32).reshape(
        seq_rows, 3, HEADS, HDIM
    )
    cosine_table, sine_table = rope_tables(seq_rows)
    query_rows = rotate(projected[:, 0], cosine_table, sine_table).astype(low_type)
    key_rows = rotate(projected[:, 1], cosine_table, sine_table).astype(low_type)
    value_rows = projected[:, 2].astype(low_type)
    scores, allowed = attention_scores(query_rows, key_rows, length)
    row_top = jnp.max(scores, axis=-1, keepdims=True)
    exponent = jnp.exp(scores - row_top)
    row_total = jnp.sum(exponent, axis=-1, keepdims=True)
    log_total = row_top + jnp.log(row_total)
    attn_probs = exponent / row_total
    context = (
        jnp.einsum(
            "hqk,khd->qhd",
            attn_probs.astype(low_type),
            value_rows,
            preferred_element_type=jnp.float32,
        )
        .reshape(seq_rows, D)
        .astype(low_type)
    )
    middle = inputs + jnp.dot(context, out_all, preferred_element_type=jnp.float32)
    scaled_two, inverse_two, normed_two = norm_forward(middle, gain_two)
    mixer_low = normed_two.astype(low_type)
    logits = jnp.dot(mixer_low, router_all, preferred_element_type=jnp.float32)
    own_routes = lax.dynamic_slice_in_dim(routes, head_at * seq_rows, seq_rows, 0)
    onehot = (
        own_routes[:, :, None] == jnp.arange(router_all.shape[1], dtype=jnp.int32)[None, None, :]
    ).astype(jnp.float32)
    chosen = jnp.sum(logits[:, None, :] * onehot, axis=-1)
    chosen_top = jnp.max(chosen, axis=-1, keepdims=True)
    chosen_exp = jnp.exp(chosen - chosen_top)
    gate_values = chosen_exp / jnp.sum(chosen_exp, axis=-1, keepdims=True)
    gates_low = gate_values.astype(low_type)
    group_rows, group_gates = (
        lax.all_gather(mixer_low, "head", axis=0, tiled=True),
        lax.all_gather(gates_low, "head", axis=0, tiled=True),
    )
    shared_mixed, shared_hidden, shared_out = expert_forward(
        group_rows, shared_in_flat, shared_down_all
    )
    dest_slot, source_row = route_tables(routes, head_total, cap_dev, expert_total)
    send_rows = pack_tokens(group_rows, source_row)
    expert_in_low = expert_in.astype(low_type)
    expert_down_low = expert_down.astype(low_type)
    weight_in = expert_in_low[0].reshape(D, -1)
    weight_down = expert_down_low[0]
    received = lax.all_to_all(
        send_rows.reshape(expert_total, -1, D), "expert", split_axis=0, concat_axis=0, tiled=True
    ).reshape(-1, D)
    expert_mixed, expert_hidden, expert_out = expert_forward(received, weight_in, weight_down)
    returned = (
        lax.all_to_all(
            expert_out.reshape(expert_total, -1, D).astype(jnp.bfloat16),
            "expert",
            split_axis=0,
            concat_axis=0,
            tiled=True,
        )
        .astype(jnp.float32)
        .reshape(-1, D)
    )
    routed = returned[dest_slot].reshape(-1, 2, D)
    partial_value = shared_out + jnp.sum(
        group_gates.astype(jnp.float32)[:, :, None] * routed, axis=1
    )
    mixed_out = lax.psum_scatter(
        partial_value.astype(jnp.bfloat16), "head", scatter_dimension=0, tiled=True
    ).astype(jnp.float32)
    live_rows = (jnp.arange(seq_rows, dtype=jnp.int32) < length).astype(jnp.float32)[:, None]
    layer_out = live_rows * (middle + mixed_out)
    grad_live = live_rows * cotangent
    grad_mix_low = grad_live.astype(low_type)
    group_grad = lax.all_gather(grad_mix_low, "head", axis=0, tiled=True)
    shared_row_grad, shared_grad_in, shared_grad_down = expert_backward(
        group_rows, shared_mixed, shared_hidden, group_grad, shared_in_flat, shared_down_all
    )
    group_grad_f = group_grad.astype(jnp.float32)
    grad_routed = (group_gates.astype(jnp.float32)[:, :, None] * group_grad_f[:, None, :]).astype(
        low_type
    )
    gate_grad_part = jnp.sum(group_grad_f[:, None, :] * routed, axis=-1)
    grad_send = pack_routes(grad_routed.reshape(-1, D), source_row)
    grad_received = lax.all_to_all(
        grad_send.reshape(expert_total, -1, D), "expert", split_axis=0, concat_axis=0, tiled=True
    ).reshape(-1, D)
    rows_grad, grad_in_local, grad_down_local = expert_backward(
        received, expert_mixed, expert_hidden, grad_received, weight_in, weight_down
    )
    rows_back = lax.all_to_all(
        rows_grad.reshape(expert_total, -1, D), "expert", split_axis=0, concat_axis=0, tiled=True
    ).reshape(-1, D)
    per_token = jnp.sum(rows_back[dest_slot].reshape(-1, 2, D), axis=1)
    rows_part = shared_row_grad + per_token
    grad_in_slice = grad_in_local.reshape(1, D, 2, -1)
    grad_down_slice = grad_down_local[None]
    grad_rows_own, grad_gates = (
        lax.psum_scatter(rows_part, "head", scatter_dimension=0, tiled=True),
        lax.psum_scatter(gate_grad_part, "head", scatter_dimension=0, tiled=True),
    )
    gate_dot = jnp.sum(gate_values * grad_gates, axis=-1, keepdims=True)
    grad_chosen = gate_values * (grad_gates - gate_dot)
    grad_logits = jnp.sum(grad_chosen[:, :, None] * onehot, axis=1).astype(low_type)
    grad_router = jnp.dot(mixer_low.T, grad_logits, preferred_element_type=jnp.float32)
    grad_normed_two = grad_rows_own + jnp.dot(
        grad_logits, router_all.T, preferred_element_type=jnp.float32
    )
    grad_from_norm, grad_gain_two = norm_backward(
        grad_normed_two, scaled_two, inverse_two, gain_two
    )
    grad_middle = grad_live + grad_from_norm
    grad_att_low = grad_middle.astype(low_type)
    grad_out_w = jnp.dot(context.T, grad_att_low, preferred_element_type=jnp.float32)
    grad_context = (
        jnp.dot(grad_att_low, out_all.T, preferred_element_type=jnp.float32)
        .astype(low_type)
        .reshape(seq_rows, HEADS, HDIM)
    )
    scores_again, allowed_again = attention_scores(query_rows, key_rows, length)
    probs_again = jnp.where(allowed_again[None], jnp.exp(scores_again - log_total), 0.0)
    grad_probs = jnp.einsum(
        "qhd,khd->hqk", grad_context, value_rows, preferred_element_type=jnp.float32
    )
    grad_value = jnp.einsum(
        "hqk,qhd->khd",
        probs_again.astype(low_type),
        grad_context,
        preferred_element_type=jnp.float32,
    )
    row_dot = jnp.sum(grad_probs * probs_again, axis=-1, keepdims=True)
    grad_scores = (probs_again * (grad_probs - row_dot)).astype(low_type)
    grad_query = (
        jnp.einsum("hqk,khd->qhd", grad_scores, key_rows, preferred_element_type=jnp.float32)
        * 0.125
    )
    grad_key = (
        jnp.einsum("hqk,qhd->khd", grad_scores, query_rows, preferred_element_type=jnp.float32)
        * 0.125
    )
    grad_projected = (
        jnp.stack(
            [
                unrotate(grad_query, cosine_table, sine_table),
                unrotate(grad_key, cosine_table, sine_table),
                grad_value,
            ],
            axis=1,
        )
        .reshape(seq_rows, 3 * D)
        .astype(low_type)
    )
    grad_qkv = jnp.dot(normed_low.T, grad_projected, preferred_element_type=jnp.float32)
    grad_normed_one = jnp.dot(grad_projected, qkv_all.T, preferred_element_type=jnp.float32)
    grad_input_norm, grad_gain_one = norm_backward(
        grad_normed_one, scaled_one, inverse_one, gain_one
    )
    input_grad = grad_middle + grad_input_norm
    gains_grad = jnp.stack([grad_gain_one, grad_gain_two], axis=0)
    gains_part, qkv_part, out_part, router_part = (
        lax.psum_scatter(gains_grad, ("expert", "head"), scatter_dimension=1, tiled=True),
        lax.psum_scatter(grad_qkv, ("expert", "head"), scatter_dimension=0, tiled=True),
        lax.psum_scatter(grad_out_w, ("expert", "head"), scatter_dimension=1, tiled=True),
        lax.psum_scatter(grad_router, ("expert", "head"), scatter_dimension=0, tiled=True),
    )
    shared_in_part, shared_down_part = (
        lax.psum_scatter(
            shared_grad_in.reshape(D, 2, -1).astype(jnp.bfloat16),
            "expert",
            scatter_dimension=0,
            tiled=True,
        ).astype(jnp.float32),
        lax.psum_scatter(
            shared_grad_down.astype(jnp.bfloat16), "expert", scatter_dimension=1, tiled=True
        ).astype(jnp.float32),
    )
    gains_new, gains_first_new, gains_second_new = adamw(
        norm_gains, gains_part, gains_first, gains_second, 0.5
    )
    qkv_new, qkv_first_new, qkv_second_new = adamw(
        qkv_weight, qkv_part, qkv_first, qkv_second, 1.5 / math.sqrt(D)
    )
    out_new, out_first_new, out_second_new = adamw(
        out_weight, out_part, out_first, out_second, 1.5 / math.sqrt(4 * D // SEQ)
    )
    router_new, router_first_new, router_second_new = adamw(
        router_weight, router_part, router_first, router_second, 1.0 / math.sqrt(D)
    )
    shin_new, shin_first_new, shin_second_new = adamw(
        shared_in, shared_in_part, shared_in_first, shared_in_second, 1.5 / math.sqrt(D)
    )
    shdown_new, shdown_first_new, shdown_second_new = adamw(
        shared_down, shared_down_part, shared_down_first, shared_down_second, 1.5 / math.sqrt(FF_SH)
    )
    exin_new, exin_first_new, exin_second_new = adamw(
        expert_in, grad_in_slice, expert_in_first, expert_in_second, 1.5 / math.sqrt(D)
    )
    exdown_new, exdown_first_new, exdown_second_new = adamw(
        expert_down, grad_down_slice, expert_down_first, expert_down_second, 1.5 / math.sqrt(FF)
    )
    return (
        layer_out,
        input_grad,
        gains_new,
        gains_first_new,
        gains_second_new,
        qkv_new,
        qkv_first_new,
        qkv_second_new,
        out_new,
        out_first_new,
        out_second_new,
        router_new,
        router_first_new,
        router_second_new,
        shin_new,
        shin_first_new,
        shin_second_new,
        shdown_new,
        shdown_first_new,
        shdown_second_new,
        exin_new,
        exin_first_new,
        exin_second_new,
        exdown_new,
        exdown_first_new,
        exdown_second_new,
    )


MESH = pl.DeviceIdType.MESH
VMEM_BYTES = 61 << 20
GROUPS = 4
PLANE = 8
ALL = GROUPS * PLANE
EXTRA = 16
TURN = (1, 3, 2)


def nn(left, right):
    return jnp.dot(left, right, preferred_element_type=jnp.float32)


def nt(left, right):
    return lax.dot_general(
        left, right, (((1,), (1,)), ((), ())), preferred_element_type=jnp.float32
    )


def tn(left, right):
    return lax.dot_general(
        left, right, (((0,), (0,)), ((), ())), preferred_element_type=jnp.float32
    )


def slot_of(group, member):
    return group * PLANE + (member % 2) * (PLANE // 2) + member // 2


class Place:
    def __init__(self):
        self.group = group = lax.axis_index("expert")
        self.member = member = lax.axis_index("head")
        self.core = core = member % 2
        column, row = (member // 2) % 2, member // 4
        self.chip = group * (PLANE // 2) + member // 2
        side = 1 - 2 * core
        self.twin = member + side
        beside, across = member + 2 - 4 * column, member + 4 - 8 * row
        self.near = beside * (1 - core) + across * core
        self.far = across * (1 - core) + beside * core
        self.corner = member + (2 - 4 * column) + (4 - 8 * row)
        self.near_twin = self.near + side
        self.far_twin = self.far + side
        self.corner_twin = self.corner + side
        self.mine = slot_of(group, member)

    def around(self, step):
        return (self.group + step) % GROUPS

    def others(self):
        near = [(self.group, self.twin), (self.group, self.near), (self.group, self.far)]
        return near + [(self.around(step), self.member) for step in TURN]

    def tell(self, semaphore):
        for other in self.others():
            pl.semaphore_signal(semaphore, inc=1, device_id=other, device_id_type=MESH)

    def hear(self, semaphore):
        pl.semaphore_wait(semaphore, 6)


class Mover:
    def __init__(self, place, send_sem):
        self.place, self.send_sem, self.sizes = place, send_sem, []

    def copy(self, source, target, index, recv, device):
        return pltpu.make_async_remote_copy(
            src_ref=source,
            dst_ref=target,
            send_sem=self.send_sem.at[index],
            recv_sem=recv,
            device_id=device,
            device_id_type=MESH,
        )

    def send(self, source, target, recv, device):
        self.copy(source, target, len(self.sizes), recv, device).start()
        self.sizes.append(source)

    def arrive(self, target, recv):
        self.copy(target, target, 0, recv, (self.place.group, self.place.twin)).wait_recv()

    def drain(self, unit):
        for index in range(len(self.sizes)):
            self.copy(unit, unit, index, self.send_sem.at[index], (self.place.group, self.place.twin)).wait_send()


class Gather(Mover):
    def __init__(self, place, at, send_sem, recv_sem, pair=True):
        super().__init__(place, send_sem)
        self.at, self.recv_sem, self.pair = at, recv_sem, pair

    def forward(self, group, member, partners):
        for partner in partners:
            if partner is self.place.twin and not self.pair:
                continue
            ref = self.at(group, member)
            self.send(ref, ref, self.recv_sem.at[slot_of(group, member)], (self.place.group, partner))

    def wait(self, group, member):
        self.arrive(self.at(group, member), self.recv_sem.at[slot_of(group, member)])

    def start(self):
        place = self.place
        own = self.at(place.group, place.member)
        for step in TURN:
            self.send(own, own, self.recv_sem.at[place.mine], (place.around(step), place.member))
        self.forward(place.group, place.member, (place.near, place.far, place.twin))

    def own_column(self, step):
        place = self.place
        self.wait(place.around(step), place.member)
        self.forward(place.around(step), place.member, (place.near, place.far, place.twin))

    def near_column(self, step):
        place = self.place
        self.wait(place.around(step), place.near)
        self.forward(place.around(step), place.near, (place.far, place.twin))

    def last_column(self, step, member):
        self.wait(self.place.around(step), member)
        self.forward(self.place.around(step), member, (self.place.twin,))

    def twin_column(self, member):
        for step in (0,) + TURN:
            self.wait(self.place.around(step), member)

    def twin_plane(self, step):
        place = self.place
        for member in (place.twin, place.far_twin, place.near_twin, place.corner_twin):
            self.wait(place.around(step), member)

    def last_plane(self, step):
        for member in (self.place.far, self.place.corner):
            self.last_column(step, member)


class Together:
    def __init__(self, *moves):
        self.moves = moves

    def __getattr__(self, name):
        def each(*given):
            for move in self.moves:
                getattr(move, name)(*given)

        return each


class Scatter(Mover):
    def __init__(self, place, part, rows, bufs, send_sem, sems):
        super().__init__(place, send_sem)
        self.part, self.rows = part, rows
        self.twin_buf, self.far_buf, self.near_buf, self.group_buf = bufs
        self.twin_sem, self.far_sem, self.near_sem, self.group_sem = sems

    def view(self, buf, index):
        return buf.at[index, pl.ds(0, self.rows)]

    def add(self, target, others):
        def some(block, carry):
            at = pl.ds(pl.multiple_of(block * 16, 16), 16)
            total = target[at].astype(jnp.float32)
            for other in others:
                total = total + other[at].astype(jnp.float32)
            target[at] = total.astype(target.dtype)
            return carry

        lax.fori_loop(0, self.rows // 16, some, 0)

    def twin_index(self, group, member):
        return (member // 2) * GROUPS + group

    def to_twin(self, group, member):
        index = self.twin_index(group, member)
        self.send(
            self.part(group, member),
            self.view(self.twin_buf, index),
            self.twin_sem.at[index],
            (self.place.group, self.place.twin),
        )

    def from_twin(self, group, member):
        index = self.twin_index(group, member)
        ready = self.view(self.twin_buf, index)
        self.arrive(ready, self.twin_sem.at[index])
        return ready

    def from_far(self, group, spot):
        other = self.view(self.far_buf, spot * GROUPS + group)
        self.arrive(other, self.far_sem.at[spot * GROUPS + group])
        return other

    def outward(self, step, spot):
        group = self.place.around(step)
        member = (self.place.corner, self.place.far)[spot]
        ready = self.from_twin(group, member)
        self.add(ready, [self.part(group, member)])
        index = spot * GROUPS + group
        self.send(
            ready,
            self.view(self.far_buf, index),
            self.far_sem.at[index],
            (self.place.group, self.place.far),
        )

    def sideways(self, step):
        group, near = self.place.around(step), self.place.near
        ready = self.from_twin(group, near)
        self.add(ready, [self.part(group, near), self.from_far(group, 0)])
        self.send(
            ready,
            self.view(self.near_buf, group),
            self.near_sem.at[group],
            (self.place.group, near),
        )

    def homeward(self, step):
        group, member = self.place.around(step), self.place.member
        ready = self.from_twin(group, member)
        other = self.view(self.near_buf, group)
        far = self.from_far(group, 1)
        self.arrive(other, self.near_sem.at[group])
        self.add(ready, [self.part(group, member), far, other])
        if step:
            self.send(
                ready,
                self.view(self.group_buf, step - 1),
                self.group_sem.at[step - 1],
                (group, member),
            )

    def finish(self, store):
        for step in TURN:
            self.arrive(self.view(self.group_buf, step - 1), self.group_sem.at[step - 1])
        ready = self.view(self.twin_buf, self.twin_index(self.place.group, self.place.member))

        def some(block, carry):
            at = pl.ds(pl.multiple_of(block * 16, 16), 16)
            total = ready[at].astype(jnp.float32)
            for step in TURN:
                total = total + self.view(self.group_buf, step - 1)[at].astype(jnp.float32)
            store(at, total)
            return carry

        lax.fori_loop(0, self.rows // 16, some, 0)


BACKWARD = (1, 3, 2, 0)


def iota(shape, dim):
    return lax.broadcasted_iota(jnp.int32, shape, dim)


def swap_halves(block):
    lane = iota(block.shape, 1)
    return jnp.where(
        lane % HDIM < HDIM // 2, pltpu.roll(block, 128 - HDIM // 2, 1), pltpu.roll(block, HDIM // 2, 1)
    )


def step_kernel(
    length_ref,
    tokens_hbm,
    cotangent_hbm,
    routes_hbm,
    qkv_hbm,
    out_hbm,
    router_hbm,
    gains_hbm,
    shared_in_hbm,
    shared_down_hbm,
    cosine_hbm,
    sine_hbm,
    expert_in_hbm,
    expert_down_hbm,
    layer_out_hbm,
    input_grad_hbm,
    owned_grad_hbm,
    small_grad_hbm,
    grad_in_hbm,
    grad_down_hbm,
    shared_grad_hbm,
    tokens_ref,
    cotangent_ref,
    routes_ref,
    qkv_ref,
    router_ref,
    gains_ref,
    shared_in_ref,
    shared_down_ref,
    cosine_ref,
    sine_ref,
    owned_ref,
    small_ref,
    small_square,
    layer_out_ref,
    input_grad_ref,
    owned_grad_ref,
    small_grad_ref,
    grad_in_ref,
    grad_down_ref,
    shared_grad_ref,
    pieces_ref,
    stage,
    small_stage,
    mats,
    small_all,
    first_all,
    second_all,
    pieces,
    shared_send,
    weight_in,
    weight_down,
    out_all,
    hidden_low,
    mixed_low,
    pre,
    back_hidden,
    queries,
    keys,
    values,
    probs,
    normed_low,
    context,
    middle_ref,
    mixer,
    rows_sum,
    grad_mid,
    grad_context,
    grad_proj,
    gate_keep,
    twin_a,
    far_a,
    near_a,
    group_a,
    twin_b,
    far_b,
    near_b,
    group_b,
    gate_all,
    gate_part,
    small_part,
    gate_sum,
    twin_g,
    far_g,
    near_g,
    group_g,
    twin_s,
    far_s,
    near_s,
    group_s,
    gate_send,
    gate_recv,
    gate_back_send,
    small_back_send,
    pair_send,
    pair_recv,
    local_sem,
    store_sem,
    mats_send,
    mats_recv,
    small_send,
    small_recv,
    cot_send,
    cot_recv,
    mix_send,
    mix_recv,
    piece_send,
    piece_recv,
    rows_send,
    out_send,
    own_send,
    twin_sems,
    far_sems,
    near_sems,
    group_sems,
    free_sem,
):
    low = jnp.bfloat16
    rows = tokens_ref.shape[0]
    fetched = {}
    for name, source, target in (
        ("qkv", qkv_hbm, qkv_ref),
        ("out", out_hbm, owned_ref.at[3]),
        ("router", router_hbm, router_ref),
        ("gains", gains_hbm, gains_ref),
        ("cotangent", cotangent_hbm, cotangent_ref),
        ("tokens", tokens_hbm, tokens_ref),
        ("routes", routes_hbm, routes_ref),
        ("cosine", cosine_hbm, cosine_ref),
        ("sine", sine_hbm, sine_ref),
        ("shared_gate", shared_in_hbm.at[:, 0, :], shared_in_ref.at[0]),
        ("shared_up", shared_in_hbm.at[:, 1, :], shared_in_ref.at[1]),
        ("shared_down", shared_down_hbm, shared_down_ref),
        ("gate", expert_in_hbm.at[0, :, 0, :], grad_in_ref.at[:, pl.ds(0, 256)]),
        ("up", expert_in_hbm.at[0, :, 1, :], grad_in_ref.at[:, pl.ds(256, 256)]),
        ("down", expert_down_hbm.at[0], grad_down_ref.at[pl.ds(0, 256)]),
    ):
        fetched[name] = pltpu.make_async_copy(source, target, local_sem.at[len(fetched)])
        fetched[name].start()
    stored = []

    def store_out(source, target):
        copy = pltpu.make_async_copy(source, target, store_sem.at[len(stored)])
        copy.start()
        stored.append(copy)
    place = Place()
    group, member, core = place.group, place.member, place.core
    barrier = pltpu.get_barrier_semaphore()
    place.tell(barrier)
    place.hear(barrier)

    twin_device = (group, place.twin)
    for name in ("qkv", "out", "router", "gains"):
        fetched[name].wait()
    for part in range(3):
        owned_ref[part] = qkv_ref[:, D * part : D * part + D]
    small_square[...] = jnp.zeros_like(small_square)
    small_square[pl.ds(0, GROUPS), pl.ds(0, 24)] = router_ref[...]
    small_square[pl.ds(GROUPS, 2), pl.ds(0, 24)] = gains_ref[...]
    small_ref[...] = small_square[...].T[:24]
    own_rows = pl.ds(pl.multiple_of(24 * core, 8), 24)
    owned = pltpu.make_async_remote_copy(
        src_ref=owned_ref.at[pl.ds(2 * (1 - core), 2)],
        dst_ref=stage.at[:, own_rows],
        send_sem=pair_send.at[0],
        recv_sem=pair_recv.at[0],
        device_id=twin_device,
        device_id_type=MESH,
    )
    owned.start()
    small_pair = pltpu.make_async_remote_copy(
        src_ref=small_ref,
        dst_ref=small_stage.at[own_rows],
        send_sem=pair_send.at[1],
        recv_sem=pair_recv.at[1],
        device_id=twin_device,
        device_id_type=MESH,
    )
    small_pair.start()
    stage[:, own_rows] = owned_ref[pl.ds(2 * core, 2)]
    small_stage[own_rows] = small_ref[...]
    owned.wait()
    small_pair.wait()

    def mats_at(group, member):
        chip = group * (PLANE // 2) + member // 2
        return mats.at[pl.ds(2 * (member % 2), 2), pl.ds(pl.multiple_of(48 * chip, 16), 48)]

    def small_at(group, member):
        chip = group * (PLANE // 2) + member // 2
        return small_all.at[pl.ds(pl.multiple_of(48 * chip, 16), 48)]

    mats_at(group, member)[...] = stage[...].astype(low)
    small_at(group, member)[...] = small_stage[...].astype(low)
    send_small = Gather(place, small_at, small_send, small_recv, pair=False)
    send_mats = Gather(place, mats_at, mats_send, mats_recv)
    send_small.start()
    send_mats.start()
    length = length_ref[0]
    row_at = iota((rows, 1), 0)
    live = (row_at < length).astype(jnp.float32)
    fetched["cotangent"].wait()
    first_all[place.mine] = (cotangent_ref[...] * live).astype(low)

    send_cot = Gather(
        place,
        lambda group, member: first_all.at[slot_of(group, member)],
        cot_send,
        cot_recv,
    )

    def move_piece(source, target, sems, base):
        for step in TURN:
            pltpu.make_async_remote_copy(
                src_ref=source.at[place.around(step)],
                dst_ref=target.at[group],
                send_sem=piece_send.at[base + step - 1],
                recv_sem=piece_recv.at[base + (GROUPS - step) - 1],
                device_id=(place.around(step), member),
                device_id_type=MESH,
            ).start()
        target[group] = source[group]

    def wait_pieces(source, target, base):
        for step in TURN:
            copy = pltpu.make_async_remote_copy(
                src_ref=source.at[place.around(step)],
                dst_ref=target.at[place.around(step)],
                send_sem=piece_send.at[base + step - 1],
                recv_sem=piece_recv.at[base + step - 1],
                device_id=(place.around(step), member),
                device_id_type=MESH,
            )
            copy.wait()

    for step in (0,) + TURN:
        if step:
            send_small.own_column(step)
            send_mats.own_column(step)
        send_small.near_column(step)
        send_mats.near_column(step)
        if step == 0:
            send_cot.start()

    for name in ("shared_gate", "shared_up", "shared_down"):
        fetched[name].wait()
    for piece in range(GROUPS):
        at = pl.ds(64 * piece, 64)
        both_halves = [shared_in_ref[0, :, at], shared_in_ref[1, :, at]]
        pieces_ref[piece, :, pl.ds(0, 128)] = jnp.concatenate(both_halves, axis=1).astype(low)
        last = shared_down_ref[:, at]
        last = jnp.concatenate([last, jnp.zeros_like(last)], axis=1)
        pieces_ref[piece, :, pl.ds(128, 128)] = last.astype(low)
    move_piece(pieces_ref, pieces, piece_send, 0)

    for name in ("gate", "up", "down"):
        fetched[name].wait()
    weight_in[:, pl.ds(0, 512)] = grad_in_ref[:, pl.ds(0, 512)].astype(low)
    weight_down[pl.ds(0, 256)] = grad_down_ref[pl.ds(0, 256)].astype(low)
    grad_down_ref[...] = jnp.zeros_like(grad_down_ref)
    grad_in_ref[...] = jnp.zeros_like(grad_in_ref)

    for step in (0,) + TURN:
        for origin in (place.far, place.corner):
            send_small.wait(place.around(step), origin)
            send_mats.last_column(step, origin)
    for step in TURN:
        send_cot.own_column(step)
    for origin in (place.twin, place.near_twin, place.far_twin, place.corner_twin):
        send_mats.twin_column(origin)

    for name in ("tokens", "routes", "cosine", "sine"):
        fetched[name].wait()
    inputs = tokens_ref[...].astype(jnp.float32)
    inverse_one = lax.rsqrt(jnp.mean(inputs * inputs, axis=-1, keepdims=True) + NORM_EPS)
    pick = (iota((8, 128), 1) == iota((8, 128), 0) + GROUPS).astype(low)
    gains = nt(pick, small_all[...])
    gain_one, gain_two = gains[0:1], gains[1:2]
    normed_low[...] = (inputs * inverse_one * gain_one).astype(low)
    for part, target in ((0, queries), (1, keys), (2, values)):
        pre[pl.ds(0, rows)] = nn(normed_low[...], mats[part])
        for block in range(D // 128):
            at = pl.ds(128 * block, 128)
            piece = pre[pl.ds(0, rows), at]
            if part < 2:
                piece = piece * cosine_ref[...] + swap_halves(piece) * sine_ref[...]
            target[:, at] = piece.astype(low)
    for step in (0, 1):
        send_cot.near_column(step)
    diagonal = iota((rows, rows), 0) == iota((rows, rows), 1)
    query_at, key_at = iota((rows, rows), 0), iota((rows, rows), 1)
    allowed = (key_at <= query_at) & (key_at < length)
    lower = iota((rows, 128), 1) < HDIM

    def attend(pair, carry):
        at = pl.ds(pl.multiple_of(pair * 128, 128), 128)
        query, key, value = queries[:, at], keys[:, at], values[:, at]
        found = []
        for half in (0, 1):
            own = lower if half == 0 else jnp.logical_not(lower)
            scores = nt(jnp.where(own, query, jnp.zeros_like(query)), key) * 0.125
            scores = jnp.where(allowed, scores, MASKED)
            exponent = jnp.exp(scores - jnp.max(scores, axis=-1, keepdims=True))
            prob = exponent / jnp.sum(exponent, axis=-1, keepdims=True)
            probs[pair * 2 + half] = prob
            found.append(nn(prob.astype(low), value))
        context[:, at] = jnp.where(lower, found[0], found[1]).astype(low)
        for serve in range(2):

            @pl.when(pair == serve)
            def _():
                send_cot.near_column((3, 2)[serve])

        return carry

    lax.fori_loop(0, HEADS // 2, attend, 0)
    middle = inputs + nt(context[...], mats[3])
    middle_ref[...] = middle
    inverse_two = lax.rsqrt(jnp.mean(middle * middle, axis=-1, keepdims=True) + NORM_EPS)
    mixer[...] = (middle * inverse_two * gain_two).astype(low)
    logits = nn(mixer[...], small_all[...])
    lane = iota((rows, 128), 1)
    chosen, hits = [], []
    for choice in (0, 1):
        row = routes_ref[choice : choice + 1, pl.ds(pl.multiple_of(member * rows, rows), rows)]
        picked = jnp.sum(jnp.where(diagonal, row.astype(jnp.float32), 0.0), axis=1, keepdims=True)
        hit = (lane.astype(jnp.float32) == picked).astype(jnp.float32)
        hits.append(hit)
        chosen.append(jnp.sum(logits * hit, axis=-1, keepdims=True))
    top = jnp.maximum(chosen[0], chosen[1])
    exponents = [jnp.exp(value - top) for value in chosen]
    total = exponents[0] + exponents[1]
    gates = [value / total for value in exponents]
    gate_keep[...] = jnp.where(lane == 0, gates[0], jnp.where(lane == 1, gates[1], 0.0))
    table = sum(gate.astype(low).astype(jnp.float32) * hit for gate, hit in zip(gates, hits))
    second_all[place.mine] = mixer[...]
    gate_all[place.mine] = table.T[:EXTRA].astype(low)
    send_rows = Gather(
        place, lambda group, member: second_all.at[slot_of(group, member)], mix_send, mix_recv
    )
    send_gates = Gather(
        place, lambda group, member: gate_all.at[slot_of(group, member)], gate_send, gate_recv
    )
    send_mix = Together(send_gates, send_rows)
    send_mix.start()
    for step in (0,) + TURN:
        for origin in (place.far, place.corner):
            send_cot.last_column(step, origin)
    for origin in (place.twin, place.near_twin, place.far_twin, place.corner_twin):
        send_cot.twin_column(origin)
    send_cot.drain(first_all.at[0])

    wait_pieces(pieces_ref, pieces, 0)
    first_half = iota((192, 128), 1) < 64
    for piece in range(GROUPS):
        at = pl.ds(192 * piece, 192)
        both_halves = pieces[piece, :, pl.ds(0, 128)].astype(jnp.float32)
        weight_in[at, pl.ds(512, 128)] = jnp.where(first_half, both_halves, 0.0).astype(low)
        other = pltpu.roll(both_halves, 64, 1)
        weight_in[at, pl.ds(640, 128)] = jnp.where(first_half, other, 0.0).astype(low)
    turned = pieces[:, :, pl.ds(128, 128)].reshape(D, 128).astype(jnp.float32)
    weight_down[pl.ds(256, 128)] = turned.T.astype(low)
    big_move = Scatter(
        place,
        lambda group, member: first_all.at[slot_of(group, member)],
        rows,
        (twin_a, far_a, near_a, group_a),
        rows_send,
        (twin_sems.at[0], far_sems.at[0], near_sems.at[0], group_sems.at[0]),
    )
    gate_move = Scatter(
        place,
        lambda group, member: gate_part.at[slot_of(group, member)],
        EXTRA,
        (twin_g, far_g, near_g, group_g),
        gate_back_send,
        (twin_sems.at[3], far_sems.at[3], near_sems.at[3], group_sems.at[3]),
    )
    rows_move = Together(big_move, gate_move)
    out_move = Scatter(
        place,
        lambda group, member: out_all.at[slot_of(group, member)],
        rows,
        (twin_b, far_b, near_b, group_b),
        out_send,
        (twin_sems.at[1], far_sems.at[1], near_sems.at[1], group_sems.at[1]),
    )
    extra_row = iota((EXTRA, 128), 0) == group
    twins = (place.corner_twin, place.near_twin, place.far_twin, place.twin)

    def both(step):
        for spot in (0, 1):
            rows_move.outward(step, spot)

    serve_before = (
        lambda: (
            send_mix.own_column(1),
            send_mix.near_column(1),
            send_mix.own_column(3),
            send_mix.last_plane(1),
        ),
        lambda: (send_mix.near_column(3), send_mix.own_column(2), send_mix.twin_plane(1)),
        lambda: (send_mix.near_column(2), send_mix.near_column(0), send_mix.last_plane(3)),
        lambda: (both(1), send_mix.twin_plane(3)),
        lambda: send_mix.last_plane(2),
        lambda: (both(3), rows_move.sideways(1), send_mix.twin_plane(2)),
        lambda: send_mix.last_plane(0),
        lambda: (
            both(2),
            rows_move.sideways(3),
            rows_move.homeward(1),
            send_mix.twin_plane(0),
        ),
    )

    def tokens_part(index, carry):
        for at in range(PLANE):

            @pl.when(index == at)
            def _():
                serve_before[at]()

        half = index // 2
        step = jnp.where(half == 0, 1, jnp.where(half == 1, 3, jnp.where(half == 2, 2, 0)))
        side = (core + index) % 2
        base = pl.multiple_of(place.around(step) * PLANE + side * GROUPS, GROUPS)
        four = pl.ds(base, GROUPS)
        taken = second_all[four].reshape(GROUPS * rows, D)
        pre[...] = nn(taken, weight_in[...])
        cot = first_all[four].reshape(GROUPS * rows, D)
        back_hidden[...] = nt(cot, weight_down[...])

        def units(block, carry):
            slot = base + block
            gate_block = gate_all[slot].astype(jnp.float32)
            gate_row = jnp.sum(jnp.where(extra_row, gate_block, 0.0), axis=0, keepdims=True)
            scale = jnp.sum(jnp.where(diagonal, gate_row, 0.0), axis=1, keepdims=True)
            at = pl.ds(pl.multiple_of(block * rows, rows), rows)
            weigh = jnp.zeros((rows, 1), jnp.float32)
            for gate_at, up_at, hidden_at, routed in (
                (0, 256, 0, True),
                (128, 384, 128, True),
                (512, 640, 256, False),
            ):
                gate_pre = pre[at, pl.ds(gate_at, 128)]
                up_pre = pre[at, pl.ds(up_at, 128)]
                hidden_grad = back_hidden[at, pl.ds(hidden_at, 128)]
                sigmoid_g = jax.nn.sigmoid(gate_pre)
                silu_g = gate_pre * sigmoid_g
                hidden = (silu_g * up_pre).astype(low)
                if routed:
                    wide = hidden.astype(jnp.float32)
                    weigh = weigh + jnp.sum(wide * hidden_grad, axis=-1, keepdims=True)
                    hidden_grad = hidden_grad * scale
                    hidden = (wide * scale).astype(low)
                grad_gate = hidden_grad * up_pre * sigmoid_g * (1.0 + gate_pre * (1.0 - sigmoid_g))
                hidden_low[at, pl.ds(hidden_at, 128)] = hidden
                mixed_low[at, pl.ds(gate_at, 128)] = grad_gate.astype(low)
                mixed_low[at, pl.ds(up_at, 128)] = (hidden_grad * silu_g).astype(low)
            weigh_row = jnp.sum(jnp.where(diagonal, weigh, 0.0), axis=0, keepdims=True)
            gate_part[slot] = jnp.where(extra_row, weigh_row, 0.0)
            return carry

        lax.fori_loop(0, GROUPS, units, 0)
        grad_down_ref[...] += tn(hidden_low[...], cot)
        pre[...] = nt(mixed_low[...], weight_in[...])
        first_all[four] = pre[...].astype(low).reshape(GROUPS, rows, D)
        for at in range(1, PLANE, 2):

            @pl.when(index == at)
            def _():
                for origin in twins:
                    rows_move.to_twin(place.around(BACKWARD[at // 2]), origin)

        taken = second_all[four].reshape(GROUPS * rows, D)
        grad_in_ref[...] += tn(taken, mixed_low[...])
        pre[...] = nn(hidden_low[...], weight_down[...])
        out_all[four] = pre[...].astype(low).reshape(GROUPS, rows, D)
        for at in range(1, PLANE, 2):

            @pl.when(index == at)
            def _():
                for origin in twins:
                    out_move.to_twin(place.around(BACKWARD[at // 2]), origin)

        return carry

    lax.fori_loop(0, PLANE, tokens_part, 0)
    both(0)
    rows_move.sideways(2)
    rows_move.homeward(3)
    rows_move.sideways(0)
    rows_move.homeward(2)
    rows_move.homeward(0)
    send_rows.drain(second_all.at[0])
    send_gates.drain(gate_all.at[0])

    for piece in range(GROUPS):
        at = pl.ds(192 * piece, 192)
        both_halves = [grad_in_ref[at, pl.ds(512, 64)], grad_in_ref[at, pl.ds(640, 64)]]
        shared_send[piece, :, pl.ds(0, 128)] = jnp.concatenate(both_halves, axis=1).astype(low)
    turned = grad_down_ref[pl.ds(256, 128)].T
    shared_send[:, :, pl.ds(128, 128)] = turned.astype(low).reshape(GROUPS, 192, 128)
    store_out(grad_in_ref.at[:, pl.ds(0, 512)], grad_in_hbm)
    store_out(grad_down_ref.at[pl.ds(0, 256)], grad_down_hbm)

    def keep_rows(at, total):
        rows_sum[at] = total

    def keep_gates(at, total):
        gate_sum[at] = total

    big_move.finish(keep_rows)
    gate_move.finish(keep_gates)
    big_move.drain(first_all.at[0])
    gate_move.drain(gate_part.at[0])
    place.tell(free_sem)
    move_piece(shared_send, shared_grad_ref, piece_send, 3)

    gate_grads = gate_sum[...]
    gate_grads = jnp.concatenate([gate_grads, jnp.zeros((rows - EXTRA, 128), jnp.float32)], axis=0).T
    grad_gates = [jnp.sum(gate_grads * hit, axis=-1, keepdims=True) for hit in hits]
    kept = [
        jnp.sum(jnp.where(lane == choice, gate_keep[...], 0.0), axis=-1, keepdims=True)
        for choice in (0, 1)
    ]
    gate_dot = kept[0] * grad_gates[0] + kept[1] * grad_gates[1]
    grad_logits = sum(
        hit * (gate * (grad - gate_dot)) for hit, gate, grad in zip(hits, kept, grad_gates)
    ).astype(low)
    grad_router = tn(grad_logits, mixer[...])[:8]
    middle = middle_ref[...]
    inverse_two = lax.rsqrt(jnp.mean(middle * middle, axis=-1, keepdims=True) + NORM_EPS)
    scaled_two = middle * inverse_two
    gains = nt(pick, small_all[...])
    gain_one, gain_two = gains[0:1], gains[1:2]
    grad_normed = rows_sum[pl.ds(0, rows)] + nt(grad_logits, small_all[...])
    grad_gain_two = jnp.sum(grad_normed * scaled_two, axis=0, keepdims=True)
    grad_scaled = grad_normed * gain_two
    grad_middle = cotangent_ref[...] * live + inverse_two * (
        grad_scaled - scaled_two * jnp.mean(grad_scaled * scaled_two, axis=-1, keepdims=True)
    )
    grad_mid[...] = grad_middle
    grad_att = grad_middle.astype(low)
    grad_context[...] = nn(grad_att, mats[3]).astype(low)

    mats_move = Scatter(
        place,
        lambda group, member: first_all.at[slot_of(group, member), pl.ds(0, 96)],
        96,
        (twin_a, far_a, near_a, group_a),
        own_send,
        (twin_sems.at[2], far_sems.at[2], near_sems.at[2], group_sems.at[2]),
    )
    small_move = Scatter(
        place,
        lambda group, member: small_part.at[group * (PLANE // 2) + member // 2],
        EXTRA,
        (twin_s, far_s, near_s, group_s),
        small_back_send,
        (twin_sems.at[4], far_sems.at[4], near_sems.at[4], group_sems.at[4]),
    )
    own_move = Together(mats_move, small_move)

    def put_part(which, left, right):
        for half in (0, 1):
            product = tn(left[:, 384 * half : 384 * half + 384], right).astype(low)
            for place_in in range(8):
                chip = half * 8 + place_in
                slot = slot_of(chip // 4, (chip % 4) * 2 + which // 2)
                first_all[slot, pl.ds(48 * (which % 2), 48)] = product[48 * place_in : 48 * place_in + 48]

    put_part(3, grad_att, context[...])

    def attend_back(pair, carry):
        at = pl.ds(pl.multiple_of(pair * 128, 128), 128)
        query, key, value = queries[:, at], keys[:, at], values[:, at]
        grad_ctx = grad_context[:, at]
        grad_query, grad_key, grad_value = [], [], []
        for half in (0, 1):
            own = lower if half == 0 else jnp.logical_not(lower)
            prob = probs[pair * 2 + half]
            grad_prob = nt(jnp.where(own, grad_ctx, jnp.zeros_like(grad_ctx)), value)
            grad_value.append(tn(prob.astype(low), grad_ctx))
            row_dot = jnp.sum(grad_prob * prob, axis=-1, keepdims=True)
            grad_score = (prob * (grad_prob - row_dot)).astype(low)
            grad_query.append(nn(grad_score, key))
            grad_key.append(tn(grad_score, query))
        grad_q = jnp.where(lower, grad_query[0], grad_query[1]) * 0.125
        grad_k = jnp.where(lower, grad_key[0], grad_key[1]) * 0.125
        grad_q = grad_q * cosine_ref[...] - swap_halves(grad_q) * sine_ref[...]
        grad_k = grad_k * cosine_ref[...] - swap_halves(grad_k) * sine_ref[...]
        grad_proj[0, :, at] = grad_q.astype(low)
        grad_proj[1, :, at] = grad_k.astype(low)
        grad_proj[2, :, at] = jnp.where(lower, grad_value[0], grad_value[1]).astype(low)
        for serve in range(4):

            @pl.when(pair == serve)
            def _():
                for spot in (0, 1):
                    out_move.outward(BACKWARD[serve], spot)

        return carry

    lax.fori_loop(0, HEADS // 2, attend_back, 0)
    grad_one = nt(grad_proj[0], mats[0]) + nt(grad_proj[1], mats[1]) + nt(grad_proj[2], mats[2])
    inputs = tokens_ref[...].astype(jnp.float32)
    inverse_one = lax.rsqrt(jnp.mean(inputs * inputs, axis=-1, keepdims=True) + NORM_EPS)
    scaled_one = inputs * inverse_one
    grad_gain_one = jnp.sum(grad_one * scaled_one, axis=0, keepdims=True)
    grad_scaled = grad_one * gain_one
    input_grad_ref[...] = grad_mid[...] + inverse_one * (
        grad_scaled - scaled_one * jnp.mean(grad_scaled * scaled_one, axis=-1, keepdims=True)
    )
    store_out(input_grad_ref, input_grad_hbm)
    for which in range(3):
        put_part(which, normed_low[...], grad_proj[which])
    at_row = iota((8, D), 0)
    small_rows = jnp.where(
        at_row < GROUPS, grad_router, jnp.where(at_row == GROUPS, grad_gain_one, grad_gain_two)
    )
    small_part[...] = jnp.zeros_like(small_part)
    for chip in range(ALL // 2):
        turned = pltpu.roll(small_rows, (D - 48 * chip) % D, 1) if chip else small_rows
        small_part[chip, pl.ds(0, 8)] = turned[:, :128]
    place.hear(free_sem)
    for step in BACKWARD:
        for origin in (place.corner_twin, place.near_twin, place.far_twin, place.twin):
            own_move.to_twin(place.around(step), origin)
    for move, name, step in (
        (out_move, "sideways", 1),
        (out_move, "sideways", 3),
        (own_move, "outward", 1),
        (out_move, "homeward", 1),
        (out_move, "sideways", 2),
        (own_move, "outward", 3),
        (out_move, "homeward", 3),
        (out_move, "sideways", 0),
        (own_move, "sideways", 1),
        (own_move, "outward", 2),
        (out_move, "homeward", 2),
        (own_move, "sideways", 3),
        (own_move, "homeward", 1),
        (own_move, "outward", 0),
        (out_move, "homeward", 0),
        (own_move, "sideways", 2),
        (own_move, "homeward", 3),
        (own_move, "sideways", 0),
        (own_move, "homeward", 2),
        (own_move, "homeward", 0),
    ):
        if name == "outward":
            move.outward(step, 0)
            move.outward(step, 1)
        elif name == "sideways":
            move.sideways(step)
        else:
            move.homeward(step)

    def keep_out(at, total):
        here = pl.ds(at.start, 16)
        live_here = (iota((16, 1), 0) + at.start < length).astype(jnp.float32)
        layer_out_ref[here] = live_here * (middle_ref[here] + total)

    out_move.finish(keep_out)
    store_out(layer_out_ref, layer_out_hbm)
    wait_pieces(shared_send, shared_grad_ref, 3)
    store_out(shared_grad_ref, shared_grad_hbm)

    def keep_own(at, total):
        rows_sum[at] = total

    def keep_small(at, total):
        gate_sum[at] = total

    mats_move.finish(keep_own)
    small_move.finish(keep_small)
    for matrix in (0, 1):
        stage[matrix] = rows_sum[pl.ds(48 * matrix, 48)]
    theirs = pl.ds(pl.multiple_of(24 * (1 - core), 8), 24)
    mine = pl.ds(2 * core, 2)
    last = pltpu.make_async_remote_copy(
        src_ref=stage.at[:, theirs],
        dst_ref=owned_grad_ref.at[mine],
        send_sem=pair_send.at[2],
        recv_sem=pair_recv.at[2],
        device_id=twin_device,
        device_id_type=MESH,
    )
    last.start()
    owned_grad_ref[mine] = stage[:, own_rows]
    block = gate_sum[pl.ds(0, 8)]
    small_grad_ref[...] = jnp.where(core == 0, block, pltpu.roll(block, 128 - 24, 1))
    store_out(small_grad_ref, small_grad_hbm)
    last.wait()
    store_out(owned_grad_ref, owned_grad_hbm)
    out_move.drain(out_all.at[0])
    mats_move.drain(first_all.at[0, pl.ds(0, 96)])
    small_move.drain(small_part.at[0])
    send_mats.drain(mats_at(group, member))
    send_small.drain(small_at(group, member))
    for copy in stored:
        copy.wait()


def update_kernel(*refs):
    (
        owned_grad,
        small_grad,
        grad_in,
        grad_down,
        shared_grad,
        layer_in,
        input_in,
    ) = refs[:7]
    olds = [refs[7 + 3 * at : 10 + 3 * at] for at in range(8)]
    layer_out, input_out = refs[31:33]
    news = [refs[33 + 3 * at : 36 + 3 * at] for at in range(8)]
    owned_buf, small_buf, in_buf, down_buf, shared_buf, layer_buf, input_buf = refs[57:64]
    bufs, load_sem, store_sem = refs[64:-2], refs[-2], refs[-1]
    counts = [0, 0]

    def copy(source, target, which):
        made = pltpu.make_async_copy(source, target, (load_sem, store_sem)[which].at[counts[which]])
        counts[which] += 1
        made.start()
        return made

    half = D // 2
    jobs = []
    for at in range(2):
        for block in range(2):
            jobs.append((6, lambda ref, at=at, block=block: ref.at[0, pl.ds(half * block, half), at, :], (half, 256)))
    jobs.append((7, lambda ref: ref.at[0], (256, D)))
    for at in range(2):
        jobs.append((4, lambda ref, at=at: ref.at[:, at, :], (192, 256)))
    for which in (5, 1, 2, 3, 0):
        jobs.append((which, lambda ref: ref, None))
    passes, loaded = [], []
    through = [copy(layer_in, layer_buf, 0), copy(input_in, input_buf, 0)]
    first_grads = [copy(grad_in, in_buf, 0), copy(grad_down, down_buf, 0)]
    other_grads = [copy(shared_grad, shared_buf, 0), copy(owned_grad, owned_buf, 0), copy(small_grad, small_buf, 0)]
    for at, (which, view, _) in enumerate(jobs):
        loaded.append([copy(view(olds[which][k]), bufs[3 * at + k], 0) for k in range(3)])
    for made in first_grads + through:
        made.wait()
    passes += [copy(layer_buf, layer_out, 1), copy(input_buf, input_out, 1)]
    rates = (
        0.5,
        1.5 / math.sqrt(D),
        1.5 / math.sqrt(4 * D // SEQ),
        1.0 / math.sqrt(D),
        1.5 / math.sqrt(D),
        1.5 / math.sqrt(FF_SH),
        1.5 / math.sqrt(D),
        1.5 / math.sqrt(FF),
    )

    def pair_up(part, swap_first, swap_second):
        left = iota((192, 128), 1) < 64
        tiles = []
        for tile in range(2):
            pair = [
                shared_buf[2 * tile + k, :, pl.ds(128 * part, 128)].astype(jnp.float32) for k in (0, 1)
            ]
            if swap_first:
                pair[0] = pltpu.roll(pair[0], 64, 1)
            if swap_second:
                pair[1] = pltpu.roll(pair[1], 64, 1)
            tiles.append(jnp.where(left, pair[0], pair[1]))
        return jnp.concatenate(tiles, axis=1)

    for at, (which, view, shape) in enumerate(jobs):
        if at == 5:
            for made in other_grads:
                made.wait()
        for made in loaded[at]:
            made.wait()
        mine = bufs[3 * at : 3 * at + 3]
        rate = rates[which]

        def update(index, gradient):
            weight, first_old, second_old = (ref[index] for ref in mine)
            results = adamw(weight, gradient, first_old, second_old, rate)
            for ref, value in zip(mine, results):
                ref[index] = value

        if which == 6:
            part, block = at // 2, at % 2

            def chunk(number, carry):
                here = pl.ds(pl.multiple_of(number * 32, 32), 32)
                there = pl.ds(pl.multiple_of(half * block + number * 32, 32), 32)
                update(here, in_buf[there, pl.ds(256 * part, 256)])
                return carry

            lax.fori_loop(0, half // 32, chunk, 0)
        elif which == 7:

            def chunk(number, carry):
                here = pl.ds(pl.multiple_of(number * 8, 8), 8)
                update(here, down_buf[here])
                return carry

            lax.fori_loop(0, 32, chunk, 0)
        elif which == 4:
            update(..., pair_up(0, at == 6, at == 5))
        elif which == 5:
            update(..., pair_up(1, False, True))
        elif which == 1:
            for part in range(3):
                update((slice(None), pl.ds(D * part, D)), owned_buf[part])
        elif which == 2:
            update(..., owned_buf[3])
        elif which == 3:
            update(..., small_buf[:4, :24])
        else:
            update(..., small_buf[4:6, :24])
        for k in range(3):
            passes.append(copy(mine[k], view(news[which][k]), 1))
    for made in passes:
        made.wait()


def dense_shards(
    tokens,
    cotangent,
    lengths,
    routes,
    norm_gains,
    gains_first,
    gains_second,
    qkv_weight,
    qkv_first,
    qkv_second,
    out_weight,
    out_first,
    out_second,
    router_weight,
    router_first,
    router_second,
    shared_in,
    shared_in_first,
    shared_in_second,
    shared_down,
    shared_down_first,
    shared_down_second,
    expert_in,
    expert_in_first,
    expert_in_second,
    expert_down,
    expert_down_first,
    expert_down_second,
):
    low_type = jnp.bfloat16
    seq_rows = tokens.shape[0]
    per_device = D // ALL
    half_dim = HDIM // 2
    positions = np.arange(seq_rows, dtype=np.float32)[:, None]
    angles = positions * np.tile(ROPE_BASE ** (-np.arange(half_dim) / half_dim), 4)[None]
    sign = np.tile(np.repeat([-1.0, 1.0], half_dim), 2)[None]
    cosine = jnp.asarray(np.cos(angles), jnp.float32)
    sine = jnp.asarray(np.sin(angles) * sign, jnp.float32)
    wide, f32, i32 = low_type, jnp.float32, jnp.int32
    dma = pltpu.SemaphoreType.DMA
    anywhere = pl.BlockSpec(memory_space=pltpu.HBM)
    passed = pl.pallas_call(
        step_kernel,
        out_shape=(
            jax.ShapeDtypeStruct((seq_rows, D), f32),
            jax.ShapeDtypeStruct((seq_rows, D), f32),
            jax.ShapeDtypeStruct((4, per_device, D), f32),
            jax.ShapeDtypeStruct((8, 128), f32),
            jax.ShapeDtypeStruct((D, 512), f32),
            jax.ShapeDtypeStruct((256, D), f32),
            jax.ShapeDtypeStruct((GROUPS, 192, 256), wide),
        ),
        in_specs=[pl.BlockSpec(memory_space=pltpu.SMEM)] + [anywhere] * 13,
        out_specs=(anywhere,) * 7,
        scratch_shapes=[
            pltpu.VMEM((seq_rows, D), wide),
            pltpu.VMEM((seq_rows, D), f32),
            pltpu.VMEM((2, PLANE * seq_rows), i32),
            pltpu.VMEM((per_device, 3 * D), f32),
            pltpu.VMEM((GROUPS, per_device), f32),
            pltpu.VMEM((2, per_device), f32),
            pltpu.VMEM((2, 192, 256), f32),
            pltpu.VMEM((192, 256), f32),
            pltpu.VMEM((seq_rows, 128), f32),
            pltpu.VMEM((seq_rows, 128), f32),
            pltpu.VMEM((4, per_device, D), f32),
            pltpu.VMEM((per_device, 128), f32),
            pltpu.VMEM((128, 128), f32),
            pltpu.VMEM((seq_rows, D), f32),
            pltpu.VMEM((seq_rows, D), f32),
            pltpu.VMEM((4, per_device, D), f32),
            pltpu.VMEM((8, 128), f32),
            pltpu.VMEM((D, 768), f32),
            pltpu.VMEM((384, D), f32),
            pltpu.VMEM((GROUPS, 192, 256), wide),
            pltpu.VMEM((GROUPS, 192, 256), wide),
            pltpu.VMEM((2, 48, D), f32),
            pltpu.VMEM((48, 128), f32),
            pltpu.VMEM((4, D, D), wide),
            pltpu.VMEM((D, 128), wide),
            pltpu.VMEM((ALL, seq_rows, D), wide),
            pltpu.VMEM((ALL, seq_rows, D), wide),
            pltpu.VMEM((GROUPS, 192, 256), wide),
            pltpu.VMEM((GROUPS, 192, 256), wide),
            pltpu.VMEM((D, 768), wide),
            pltpu.VMEM((384, D), wide),
            pltpu.VMEM((ALL, seq_rows, D), wide),
            pltpu.VMEM((GROUPS * seq_rows, 384), wide),
            pltpu.VMEM((GROUPS * seq_rows, 768), wide),
            pltpu.VMEM((GROUPS * seq_rows, 768), f32),
            pltpu.VMEM((GROUPS * seq_rows, 384), f32),
            pltpu.VMEM((seq_rows, D), wide),
            pltpu.VMEM((seq_rows, D), wide),
            pltpu.VMEM((seq_rows, D), wide),
            pltpu.VMEM((HEADS, seq_rows, seq_rows), f32),
            pltpu.VMEM((seq_rows, D), wide),
            pltpu.VMEM((seq_rows, D), wide),
            pltpu.VMEM((seq_rows, D), f32),
            pltpu.VMEM((seq_rows, D), wide),
            pltpu.VMEM((seq_rows, D), f32),
            pltpu.VMEM((seq_rows, D), f32),
            pltpu.VMEM((seq_rows, D), wide),
            pltpu.VMEM((3, seq_rows, D), wide),
            pltpu.VMEM((seq_rows, 128), f32),
            pltpu.VMEM((16, seq_rows, D), wide),
            pltpu.VMEM((8, seq_rows, D), wide),
            pltpu.VMEM((4, seq_rows, D), wide),
            pltpu.VMEM((3, seq_rows, D), wide),
            pltpu.VMEM((16, seq_rows, D), wide),
            pltpu.VMEM((8, seq_rows, D), wide),
            pltpu.VMEM((4, seq_rows, D), wide),
            pltpu.VMEM((3, seq_rows, D), wide),
            pltpu.VMEM((ALL, EXTRA, 128), wide),
            pltpu.VMEM((ALL, EXTRA, 128), f32),
            pltpu.VMEM((ALL // 2, EXTRA, 128), f32),
            pltpu.VMEM((EXTRA, 128), f32),
        ]
        + [pltpu.VMEM((count, EXTRA, 128), f32) for count in (16, 8, 4, 3) * 2]
        + [
            dma((31,)),
            dma((32,)),
            dma((31,)),
            dma((31,)),
            dma((3,)),
            dma((3,)),
            dma((15,)),
            dma((7,)),
            dma((31,)),
            dma((32,)),
            dma((31,)),
            dma((32,)),
            dma((31,)),
            dma((32,)),
            dma((31,)),
            dma((32,)),
            dma((6,)),
            dma((6,)),
            dma((31,)),
            dma((31,)),
            dma((31,)),
            dma((5, 16)),
            dma((5, 8)),
            dma((5, 4)),
            dma((5, 3)),
            pltpu.SemaphoreType.REGULAR,
        ],
        compiler_params=pltpu.CompilerParams(
            collective_id=0, has_side_effects=True, vmem_limit_bytes=VMEM_BYTES
        ),
    )(
        lengths,
        tokens,
        cotangent,
        routes.T,
        qkv_weight,
        out_weight.T,
        router_weight.T,
        norm_gains,
        shared_in,
        shared_down.T,
        cosine,
        sine,
        expert_in,
        expert_down,
    )
    layer_out, input_grad, owned_grad, small_grad, grad_in, grad_down, shared_grad = passed
    olds = [
        (norm_gains, gains_first, gains_second),
        (qkv_weight, qkv_first, qkv_second),
        (out_weight.T, out_first.T, out_second.T),
        (router_weight.T, router_first.T, router_second.T),
        (shared_in, shared_in_first, shared_in_second),
        (shared_down.T, shared_down_first.T, shared_down_second.T),
        (expert_in, expert_in_first, expert_in_second),
        (expert_down, expert_down_first, expert_down_second),
    ]
    flat = [old for three in olds for old in three]
    gradients = (owned_grad, small_grad, grad_in, grad_down, shared_grad)
    shapes = [(D // 2, 256)] * 4 + [(256, D)] + [(192, 256)] * 2 + [(192, 256)]
    shapes += [(per_device, 3 * D), (per_device, D), (GROUPS, per_device), (2, per_device)]
    results = pl.pallas_call(
        update_kernel,
        out_shape=tuple(
            jax.ShapeDtypeStruct(value.shape, value.dtype) for value in [layer_out, input_grad] + flat
        ),
        in_specs=[anywhere] * 31,
        out_specs=(anywhere,) * 26,
        scratch_shapes=[pltpu.VMEM(value.shape, value.dtype) for value in gradients + (layer_out, input_grad)]
        + [pltpu.VMEM(shape, f32) for shape in shapes for _ in range(3)]
        + [dma((43,)), dma((38,))],
        compiler_params=pltpu.CompilerParams(vmem_limit_bytes=VMEM_BYTES),
    )(*gradients, layer_out, input_grad, *flat)
    results = list(results)
    for at in (2 + 6, 2 + 9, 2 + 15):
        for k in range(3):
            results[at + k] = results[at + k].T
    return tuple(results)


def solution(mesh):
    placed = (
        P(("expert", "head"), None),
        P(("expert", "head"), None),
        P(("expert", "head")),
        P("expert", None),
        P(None, ("expert", "head")),
        P(None, ("expert", "head")),
        P(None, ("expert", "head")),
        P(("expert", "head"), None),
        P(("expert", "head"), None),
        P(("expert", "head"), None),
        P(None, ("expert", "head")),
        P(None, ("expert", "head")),
        P(None, ("expert", "head")),
        P(("expert", "head"), None),
        P(("expert", "head"), None),
        P(("expert", "head"), None),
        P("expert", None, "head"),
        P("expert", None, "head"),
        P("expert", None, "head"),
        P("head", "expert"),
        P("head", "expert"),
        P("head", "expert"),
        P("expert", None, None, "head"),
        P("expert", None, None, "head"),
        P("expert", None, None, "head"),
        P("expert", "head", None),
        P("expert", "head", None),
        P("expert", "head", None),
    )
    return jax.shard_map(
        dense_shards if (mesh.shape["expert"], mesh.shape["head"]) == (4, 8) else routed_shards,
        mesh=mesh,
        in_specs=placed,
        out_specs=(
            P(("expert", "head"), None),
            P(("expert", "head"), None),
            P(None, ("expert", "head")),
            P(None, ("expert", "head")),
            P(None, ("expert", "head")),
            P(("expert", "head"), None),
            P(("expert", "head"), None),
            P(("expert", "head"), None),
            P(None, ("expert", "head")),
            P(None, ("expert", "head")),
            P(None, ("expert", "head")),
            P(("expert", "head"), None),
            P(("expert", "head"), None),
            P(("expert", "head"), None),
            P("expert", None, "head"),
            P("expert", None, "head"),
            P("expert", None, "head"),
            P("head", "expert"),
            P("head", "expert"),
            P("head", "expert"),
            P("expert", None, None, "head"),
            P("expert", None, None, "head"),
            P("expert", None, None, "head"),
            P("expert", "head", None),
            P("expert", "head", None),
            P("expert", "head", None),
        ),
        check_vma=False,
    )
```

```python
import math

import jax
import jax.numpy as jnp
import numpy as np
from jax import lax
from jax.experimental import pallas as pl
from jax.experimental.pallas import tpu as pltpu
from jax.sharding import PartitionSpec as P

D = 768
HEADS = 12
HDIM = 64
FF = 2048
FF_SH = 2048
SEQ = 128
STEP = 4


OUTER, INNER = "expert", "head"
NORM_EPS = 1e-06
BETA_FIRST = 0.5
BETA_SECOND = 0.5
ADAM_EPS = 1e-08
DECAY = 0.1
MASKED = -1e30
ROPE_BASE = 10000.0


def rope_tables(row_count):
    half_dim = HDIM // 2
    positions = jnp.arange(row_count, dtype=jnp.float32)
    frequency = ROPE_BASE ** (-jnp.arange(half_dim, dtype=jnp.float32) / half_dim)
    angles = positions[:, None] * frequency[None, :]
    return (jnp.cos(angles)[:, None, :], jnp.sin(angles)[:, None, :])


def rotate(values, cosine_table, sine_table):
    half_dim = values.shape[-1] // 2
    first_half = values[..., :half_dim]
    second_half = values[..., half_dim:]
    return jnp.concatenate(
        [
            first_half * cosine_table - second_half * sine_table,
            second_half * cosine_table + first_half * sine_table,
        ],
        axis=-1,
    )


def unrotate(gradient, cosine_table, sine_table):
    half_dim = gradient.shape[-1] // 2
    first_half = gradient[..., :half_dim]
    second_half = gradient[..., half_dim:]
    return jnp.concatenate(
        [
            first_half * cosine_table + second_half * sine_table,
            second_half * cosine_table - first_half * sine_table,
        ],
        axis=-1,
    )


def norm_forward(values, gain_vec):
    inverse = lax.rsqrt(jnp.mean(values * values, axis=-1, keepdims=True) + NORM_EPS)
    scaled = values * inverse
    return (scaled, inverse, scaled * gain_vec)


def norm_backward(grad_out, scaled, inverse, gain_vec):
    grad_scaled = grad_out * gain_vec
    grad_gain = jnp.sum(grad_out * scaled, axis=0)
    grad_in = inverse * (
        grad_scaled - scaled * jnp.mean(grad_scaled * scaled, axis=-1, keepdims=True)
    )
    return (grad_in, grad_gain)


def attention_scores(query_rows, key_rows, length):
    row_count = query_rows.shape[0]
    scores = (
        jnp.einsum("qhd,khd->hqk", query_rows, key_rows, preferred_element_type=jnp.float32) * 0.125
    )
    positions = jnp.arange(row_count, dtype=jnp.int32)
    allowed = (positions[None, :] <= positions[:, None]) & (positions[None, :] < length)
    return (jnp.where(allowed[None], scores, MASKED), allowed)


def expert_forward(row_block, weight_in, weight_down):
    mixed_pre = jnp.dot(row_block, weight_in, preferred_element_type=jnp.float32)
    hidden_width = weight_down.shape[0]
    gate_pre = mixed_pre[:, :hidden_width]
    up_pre = mixed_pre[:, hidden_width:]
    hidden = (gate_pre * jax.nn.sigmoid(gate_pre) * up_pre).astype(jnp.bfloat16)
    return (mixed_pre, hidden, jnp.dot(hidden, weight_down, preferred_element_type=jnp.float32))


def expert_backward(row_block, mixed_pre, hidden, grad_out, weight_in, weight_down):
    hidden_width = weight_down.shape[0]
    gate_pre = mixed_pre[:, :hidden_width]
    up_pre = mixed_pre[:, hidden_width:]
    grad_hidden = jnp.dot(grad_out, weight_down.T, preferred_element_type=jnp.float32)
    sigmoid_g = jax.nn.sigmoid(gate_pre)
    silu_g = gate_pre * sigmoid_g
    grad_gate = (grad_hidden * up_pre * sigmoid_g * (1.0 + gate_pre * (1.0 - sigmoid_g))).astype(
        jnp.bfloat16
    )
    grad_up = (grad_hidden * silu_g).astype(jnp.bfloat16)
    grad_mixed = jnp.concatenate([grad_gate, grad_up], axis=1)
    grad_down = jnp.dot(hidden.T, grad_out, preferred_element_type=jnp.float32)
    grad_weight_in = jnp.dot(row_block.T, grad_mixed, preferred_element_type=jnp.float32)
    grad_row_block = jnp.dot(grad_mixed, weight_in.T, preferred_element_type=jnp.float32)
    return (grad_row_block, grad_weight_in, grad_down)


def route_tables(route_rows, blocks, block_cap, expert_total):
    per_block = route_rows.reshape(blocks, -1)
    hit_table = (
        per_block[:, :, None] == jnp.arange(expert_total, dtype=jnp.int32)[None, None, :]
    ).astype(jnp.int32)
    entries = per_block.shape[1]
    earlier = jnp.tril(jnp.ones((entries, entries), jnp.bfloat16))
    running = jnp.einsum(
        "ij,bje->bie", earlier, hit_table.astype(jnp.bfloat16), preferred_element_type=jnp.float32
    ).astype(jnp.int32)
    rank_in = jnp.sum((running - 1) * hit_table, axis=2)
    offsets = jnp.arange(blocks, dtype=jnp.int32)[:, None] * block_cap
    dest_slot = (per_block * (blocks * block_cap) + offsets + rank_in).reshape(-1)
    source_row = (
        jnp.zeros((expert_total * blocks * block_cap,), jnp.int32)
        .at[dest_slot]
        .set(jnp.arange(dest_slot.shape[0], dtype=jnp.int32) + 1)
    )
    return (dest_slot, source_row)


def pack_tokens(token_rows, source_row):
    padded = jnp.concatenate(
        [jnp.zeros((1, token_rows.shape[1]), token_rows.dtype), token_rows], axis=0
    )
    pick_rows = jnp.where(source_row > 0, (source_row - 1) // 2 + 1, 0)
    return padded[pick_rows]


def pack_routes(route_values, source_row):
    padded = jnp.concatenate(
        [jnp.zeros((1, route_values.shape[1]), route_values.dtype), route_values], axis=0
    )
    return padded[source_row]


def adamw(weight, gradient, first_old, second_old, step_rate):
    first_new = BETA_FIRST * first_old + (1.0 - BETA_FIRST) * gradient
    second_new = BETA_SECOND * second_old + (1.0 - BETA_SECOND) * gradient * gradient
    first_hat = first_new / (1.0 - BETA_FIRST**STEP)
    second_hat = second_new / (1.0 - BETA_SECOND**STEP)
    new_weight = weight - step_rate * (
        first_hat / (jnp.sqrt(second_hat) + ADAM_EPS) + DECAY * weight
    )
    return (new_weight, first_new, second_new)


def routed_shards(
    tokens,
    cotangent,
    lengths,
    routes,
    norm_gains,
    gains_first,
    gains_second,
    qkv_weight,
    qkv_first,
    qkv_second,
    out_weight,
    out_first,
    out_second,
    router_weight,
    router_first,
    router_second,
    shared_in,
    shared_in_first,
    shared_in_second,
    shared_down,
    shared_down_first,
    shared_down_second,
    expert_in,
    expert_in_first,
    expert_in_second,
    expert_down,
    expert_down_first,
    expert_down_second,
):
    low_type = jnp.bfloat16
    seq_rows = tokens.shape[0]
    head_total = lax.axis_size(INNER)
    expert_total = lax.axis_size(OUTER)
    head_at = lax.axis_index(INNER)
    cap_dev = 4 * seq_rows // expert_total
    gains_all, qkv_all, out_all, router_all = (
        lax.all_gather(norm_gains.astype(low_type), (OUTER, INNER), axis=1, tiled=True),
        lax.all_gather(qkv_weight.astype(low_type), (OUTER, INNER), axis=0, tiled=True),
        lax.all_gather(out_weight.astype(low_type), (OUTER, INNER), axis=1, tiled=True),
        lax.all_gather(router_weight.astype(low_type), (OUTER, INNER), axis=0, tiled=True),
    )
    shared_in_all, shared_down_all = (
        lax.all_gather(shared_in.astype(low_type), OUTER, axis=0, tiled=True),
        lax.all_gather(shared_down.astype(low_type), OUTER, axis=1, tiled=True),
    )
    shared_in_flat = shared_in_all.reshape(D, -1)
    gain_one = gains_all[0].astype(jnp.float32)
    gain_two = gains_all[1].astype(jnp.float32)
    length = lengths[0]
    inputs = tokens.astype(jnp.float32)
    scaled_one, inverse_one, normed_one = norm_forward(inputs, gain_one)
    normed_low = normed_one.astype(low_type)
    projected = jnp.dot(normed_low, qkv_all, preferred_element_type=jnp.float32).reshape(
        seq_rows, 3, HEADS, HDIM
    )
    cosine_table, sine_table = rope_tables(seq_rows)
    query_rows = rotate(projected[:, 0], cosine_table, sine_table).astype(low_type)
    key_rows = rotate(projected[:, 1], cosine_table, sine_table).astype(low_type)
    value_rows = projected[:, 2].astype(low_type)
    scores, allowed = attention_scores(query_rows, key_rows, length)
    row_top = jnp.max(scores, axis=-1, keepdims=True)
    exponent = jnp.exp(scores - row_top)
    row_total = jnp.sum(exponent, axis=-1, keepdims=True)
    log_total = row_top + jnp.log(row_total)
    attn_probs = exponent / row_total
    context = (
        jnp.einsum(
            "hqk,khd->qhd",
            attn_probs.astype(low_type),
            value_rows,
            preferred_element_type=jnp.float32,
        )
        .reshape(seq_rows, D)
        .astype(low_type)
    )
    middle = inputs + jnp.dot(context, out_all, preferred_element_type=jnp.float32)
    scaled_two, inverse_two, normed_two = norm_forward(middle, gain_two)
    mixer_low = normed_two.astype(low_type)
    logits = jnp.dot(mixer_low, router_all, preferred_element_type=jnp.float32)
    own_routes = lax.dynamic_slice_in_dim(routes, head_at * seq_rows, seq_rows, 0)
    onehot = (
        own_routes[:, :, None] == jnp.arange(router_all.shape[1], dtype=jnp.int32)[None, None, :]
    ).astype(jnp.float32)
    chosen = jnp.sum(logits[:, None, :] * onehot, axis=-1)
    chosen_top = jnp.max(chosen, axis=-1, keepdims=True)
    chosen_exp = jnp.exp(chosen - chosen_top)
    gate_values = chosen_exp / jnp.sum(chosen_exp, axis=-1, keepdims=True)
    gates_low = gate_values.astype(low_type)
    group_rows, group_gates = (
        lax.all_gather(mixer_low, INNER, axis=0, tiled=True),
        lax.all_gather(gates_low, INNER, axis=0, tiled=True),
    )
    shared_mixed, shared_hidden, shared_out = expert_forward(
        group_rows, shared_in_flat, shared_down_all
    )
    dest_slot, source_row = route_tables(routes, head_total, cap_dev, expert_total)
    send_rows = pack_tokens(group_rows, source_row)
    expert_in_low = expert_in.astype(low_type)
    expert_down_low = expert_down.astype(low_type)
    weight_in = expert_in_low[0].reshape(D, -1)
    weight_down = expert_down_low[0]
    received = lax.all_to_all(
        send_rows.reshape(expert_total, -1, D), OUTER, split_axis=0, concat_axis=0, tiled=True
    ).reshape(-1, D)
    expert_mixed, expert_hidden, expert_out = expert_forward(received, weight_in, weight_down)
    returned = (
        lax.all_to_all(
            expert_out.reshape(expert_total, -1, D).astype(jnp.bfloat16),
            OUTER,
            split_axis=0,
            concat_axis=0,
            tiled=True,
        )
        .astype(jnp.float32)
        .reshape(-1, D)
    )
    routed = returned[dest_slot].reshape(-1, 2, D)
    partial_value = shared_out + jnp.sum(
        group_gates.astype(jnp.float32)[:, :, None] * routed, axis=1
    )
    mixed_out = lax.psum_scatter(
        partial_value.astype(jnp.bfloat16), INNER, scatter_dimension=0, tiled=True
    ).astype(jnp.float32)
    live_rows = (jnp.arange(seq_rows, dtype=jnp.int32) < length).astype(jnp.float32)[:, None]
    layer_out = live_rows * (middle + mixed_out)
    grad_live = live_rows * cotangent
    grad_mix_low = grad_live.astype(low_type)
    group_grad = lax.all_gather(grad_mix_low, INNER, axis=0, tiled=True)
    shared_row_grad, shared_grad_in, shared_grad_down = expert_backward(
        group_rows, shared_mixed, shared_hidden, group_grad, shared_in_flat, shared_down_all
    )
    group_grad_f = group_grad.astype(jnp.float32)
    grad_routed = (group_gates.astype(jnp.float32)[:, :, None] * group_grad_f[:, None, :]).astype(
        low_type
    )
    gate_grad_part = jnp.sum(group_grad_f[:, None, :] * routed, axis=-1)
    grad_send = pack_routes(grad_routed.reshape(-1, D), source_row)
    grad_received = lax.all_to_all(
        grad_send.reshape(expert_total, -1, D), OUTER, split_axis=0, concat_axis=0, tiled=True
    ).reshape(-1, D)
    rows_grad, grad_in_local, grad_down_local = expert_backward(
        received, expert_mixed, expert_hidden, grad_received, weight_in, weight_down
    )
    rows_back = lax.all_to_all(
        rows_grad.reshape(expert_total, -1, D), OUTER, split_axis=0, concat_axis=0, tiled=True
    ).reshape(-1, D)
    per_token = jnp.sum(rows_back[dest_slot].reshape(-1, 2, D), axis=1)
    rows_part = shared_row_grad + per_token
    grad_in_slice = grad_in_local.reshape(1, D, 2, -1)
    grad_down_slice = grad_down_local[None]
    grad_rows_own, grad_gates = (
        lax.psum_scatter(rows_part, INNER, scatter_dimension=0, tiled=True),
        lax.psum_scatter(gate_grad_part, INNER, scatter_dimension=0, tiled=True),
    )
    gate_dot = jnp.sum(gate_values * grad_gates, axis=-1, keepdims=True)
    grad_chosen = gate_values * (grad_gates - gate_dot)
    grad_logits = jnp.sum(grad_chosen[:, :, None] * onehot, axis=1).astype(low_type)
    grad_router = jnp.dot(mixer_low.T, grad_logits, preferred_element_type=jnp.float32)
    grad_normed_two = grad_rows_own + jnp.dot(
        grad_logits, router_all.T, preferred_element_type=jnp.float32
    )
    grad_from_norm, grad_gain_two = norm_backward(
        grad_normed_two, scaled_two, inverse_two, gain_two
    )
    grad_middle = grad_live + grad_from_norm
    grad_att_low = grad_middle.astype(low_type)
    grad_out_w = jnp.dot(context.T, grad_att_low, preferred_element_type=jnp.float32)
    grad_context = (
        jnp.dot(grad_att_low, out_all.T, preferred_element_type=jnp.float32)
        .astype(low_type)
        .reshape(seq_rows, HEADS, HDIM)
    )
    scores_again, allowed_again = attention_scores(query_rows, key_rows, length)
    probs_again = jnp.where(allowed_again[None], jnp.exp(scores_again - log_total), 0.0)
    grad_probs = jnp.einsum(
        "qhd,khd->hqk", grad_context, value_rows, preferred_element_type=jnp.float32
    )
    grad_value = jnp.einsum(
        "hqk,qhd->khd",
        probs_again.astype(low_type),
        grad_context,
        preferred_element_type=jnp.float32,
    )
    row_dot = jnp.sum(grad_probs * probs_again, axis=-1, keepdims=True)
    grad_scores = (probs_again * (grad_probs - row_dot)).astype(low_type)
    grad_query = (
        jnp.einsum("hqk,khd->qhd", grad_scores, key_rows, preferred_element_type=jnp.float32)
        * 0.125
    )
    grad_key = (
        jnp.einsum("hqk,qhd->khd", grad_scores, query_rows, preferred_element_type=jnp.float32)
        * 0.125
    )
    grad_projected = (
        jnp.stack(
            [
                unrotate(grad_query, cosine_table, sine_table),
                unrotate(grad_key, cosine_table, sine_table),
                grad_value,
            ],
            axis=1,
        )
        .reshape(seq_rows, 3 * D)
        .astype(low_type)
    )
    grad_qkv = jnp.dot(normed_low.T, grad_projected, preferred_element_type=jnp.float32)
    grad_normed_one = jnp.dot(grad_projected, qkv_all.T, preferred_element_type=jnp.float32)
    grad_input_norm, grad_gain_one = norm_backward(
        grad_normed_one, scaled_one, inverse_one, gain_one
    )
    input_grad = grad_middle + grad_input_norm
    gains_grad = jnp.stack([grad_gain_one, grad_gain_two], axis=0)
    gains_part, qkv_part, out_part, router_part = (
        lax.psum_scatter(gains_grad, (OUTER, INNER), scatter_dimension=1, tiled=True),
        lax.psum_scatter(grad_qkv, (OUTER, INNER), scatter_dimension=0, tiled=True),
        lax.psum_scatter(grad_out_w, (OUTER, INNER), scatter_dimension=1, tiled=True),
        lax.psum_scatter(grad_router, (OUTER, INNER), scatter_dimension=0, tiled=True),
    )
    shared_in_part, shared_down_part = (
        lax.psum_scatter(
            shared_grad_in.reshape(D, 2, -1).astype(jnp.bfloat16),
            OUTER,
            scatter_dimension=0,
            tiled=True,
        ).astype(jnp.float32),
        lax.psum_scatter(
            shared_grad_down.astype(jnp.bfloat16), OUTER, scatter_dimension=1, tiled=True
        ).astype(jnp.float32),
    )
    gains_new, gains_first_new, gains_second_new = adamw(
        norm_gains, gains_part, gains_first, gains_second, 0.5
    )
    qkv_new, qkv_first_new, qkv_second_new = adamw(
        qkv_weight, qkv_part, qkv_first, qkv_second, 1.5 / math.sqrt(D)
    )
    out_new, out_first_new, out_second_new = adamw(
        out_weight, out_part, out_first, out_second, 1.5 / math.sqrt(4 * D // SEQ)
    )
    router_new, router_first_new, router_second_new = adamw(
        router_weight, router_part, router_first, router_second, 1.0 / math.sqrt(D)
    )
    shin_new, shin_first_new, shin_second_new = adamw(
        shared_in, shared_in_part, shared_in_first, shared_in_second, 1.5 / math.sqrt(D)
    )
    shdown_new, shdown_first_new, shdown_second_new = adamw(
        shared_down, shared_down_part, shared_down_first, shared_down_second, 1.5 / math.sqrt(FF_SH)
    )
    exin_new, exin_first_new, exin_second_new = adamw(
        expert_in, grad_in_slice, expert_in_first, expert_in_second, 1.5 / math.sqrt(D)
    )
    exdown_new, exdown_first_new, exdown_second_new = adamw(
        expert_down, grad_down_slice, expert_down_first, expert_down_second, 1.5 / math.sqrt(FF)
    )
    return (
        layer_out,
        input_grad,
        gains_new,
        gains_first_new,
        gains_second_new,
        qkv_new,
        qkv_first_new,
        qkv_second_new,
        out_new,
        out_first_new,
        out_second_new,
        router_new,
        router_first_new,
        router_second_new,
        shin_new,
        shin_first_new,
        shin_second_new,
        shdown_new,
        shdown_first_new,
        shdown_second_new,
        exin_new,
        exin_first_new,
        exin_second_new,
        exdown_new,
        exdown_first_new,
        exdown_second_new,
    )


MESH = pl.DeviceIdType.MESH
VMEM_BYTES = 61 << 20
GROUPS = 4
PLANE = 8
ALL = GROUPS * PLANE
EXTRA = 16
TURN = (1, 3, 2)


def nn(left, right):
    return jnp.dot(left, right, preferred_element_type=jnp.float32)


def nt(left, right):
    return lax.dot_general(
        left, right, (((1,), (1,)), ((), ())), preferred_element_type=jnp.float32
    )


def tn(left, right):
    return lax.dot_general(
        left, right, (((0,), (0,)), ((), ())), preferred_element_type=jnp.float32
    )


def slot_of(group, member):
    return group * PLANE + (member % 2) * (PLANE // 2) + member // 2


class Place:
    def __init__(self):
        self.group = group = lax.axis_index(OUTER)
        self.member = member = lax.axis_index(INNER)
        self.core = core = member % 2
        column, row = (member // 2) % 2, member // 4
        self.chip = group * (PLANE // 2) + member // 2
        side = 1 - 2 * core
        self.twin = member + side
        beside, across = member + 2 - 4 * column, member + 4 - 8 * row
        self.near = beside * (1 - core) + across * core
        self.far = across * (1 - core) + beside * core
        self.corner = member + (2 - 4 * column) + (4 - 8 * row)
        self.near_twin = self.near + side
        self.far_twin = self.far + side
        self.corner_twin = self.corner + side
        self.mine = slot_of(group, member)

    def around(self, step):
        return (self.group + step) % GROUPS

    def others(self):
        near = [(self.group, self.twin), (self.group, self.near), (self.group, self.far)]
        return near + [(self.around(step), self.member) for step in TURN]

    def tell(self, semaphore):
        for other in self.others():
            pl.semaphore_signal(semaphore, inc=1, device_id=other, device_id_type=MESH)

    def hear(self, semaphore):
        pl.semaphore_wait(semaphore, 6)


class Mover:
    def __init__(self, place, send_sem):
        self.place, self.send_sem, self.sizes = place, send_sem, []

    def copy(self, source, target, index, recv, device):
        return pltpu.make_async_remote_copy(
            src_ref=source,
            dst_ref=target,
            send_sem=self.send_sem.at[index],
            recv_sem=recv,
            device_id=device,
            device_id_type=MESH,
        )

    def send(self, source, target, recv, device):
        self.copy(source, target, len(self.sizes), recv, device).start()
        self.sizes.append(source)

    def arrive(self, target, recv):
        self.copy(target, target, 0, recv, (self.place.group, self.place.twin)).wait_recv()

    def drain(self, unit):
        for index in range(len(self.sizes)):
            self.copy(unit, unit, index, self.send_sem.at[index], (self.place.group, self.place.twin)).wait_send()


class Gather(Mover):
    def __init__(self, place, at, send_sem, recv_sem, pair=True):
        super().__init__(place, send_sem)
        self.at, self.recv_sem, self.pair = at, recv_sem, pair

    def forward(self, group, member, partners):
        for partner in partners:
            if partner is self.place.twin and not self.pair:
                continue
            ref = self.at(group, member)
            self.send(ref, ref, self.recv_sem.at[slot_of(group, member)], (self.place.group, partner))

    def wait(self, group, member):
        self.arrive(self.at(group, member), self.recv_sem.at[slot_of(group, member)])

    def start(self):
        place = self.place
        own = self.at(place.group, place.member)
        for step in TURN:
            self.send(own, own, self.recv_sem.at[place.mine], (place.around(step), place.member))
        self.forward(place.group, place.member, (place.near, place.far, place.twin))

    def own_column(self, step):
        place = self.place
        self.wait(place.around(step), place.member)
        self.forward(place.around(step), place.member, (place.near, place.far, place.twin))

    def near_column(self, step):
        place = self.place
        self.wait(place.around(step), place.near)
        self.forward(place.around(step), place.near, (place.far, place.twin))

    def last_column(self, step, member):
        self.wait(self.place.around(step), member)
        self.forward(self.place.around(step), member, (self.place.twin,))

    def twin_column(self, member):
        for step in (0,) + TURN:
            self.wait(self.place.around(step), member)

    def twin_plane(self, step):
        place = self.place
        for member in (place.twin, place.far_twin, place.near_twin, place.corner_twin):
            self.wait(place.around(step), member)

    def last_plane(self, step):
        for member in (self.place.far, self.place.corner):
            self.last_column(step, member)


class Together:
    def __init__(self, *moves):
        self.moves = moves

    def __getattr__(self, name):
        def each(*given):
            for move in self.moves:
                getattr(move, name)(*given)

        return each


class Scatter(Mover):
    def __init__(self, place, part, rows, bufs, send_sem, sems):
        super().__init__(place, send_sem)
        self.part, self.rows = part, rows
        self.twin_buf, self.far_buf, self.near_buf, self.group_buf = bufs
        self.twin_sem, self.far_sem, self.near_sem, self.group_sem = sems

    def view(self, buf, index):
        return buf.at[index, pl.ds(0, self.rows)]

    def add(self, target, others):
        def some(block, carry):
            at = pl.ds(pl.multiple_of(block * 16, 16), 16)
            total = target[at].astype(jnp.float32)
            for other in others:
                total = total + other[at].astype(jnp.float32)
            target[at] = total.astype(target.dtype)
            return carry

        lax.fori_loop(0, self.rows // 16, some, 0)

    def twin_index(self, group, member):
        return (member // 2) * GROUPS + group

    def to_twin(self, group, member):
        index = self.twin_index(group, member)
        self.send(
            self.part(group, member),
            self.view(self.twin_buf, index),
            self.twin_sem.at[index],
            (self.place.group, self.place.twin),
        )

    def from_twin(self, group, member):
        index = self.twin_index(group, member)
        ready = self.view(self.twin_buf, index)
        self.arrive(ready, self.twin_sem.at[index])
        return ready

    def from_far(self, group, spot):
        other = self.view(self.far_buf, spot * GROUPS + group)
        self.arrive(other, self.far_sem.at[spot * GROUPS + group])
        return other

    def outward(self, step):
        for spot, member in ((0, self.place.corner), (1, self.place.far)):
            group = self.place.around(step)
            ready = self.from_twin(group, member)
            self.add(ready, [self.part(group, member)])
            index = spot * GROUPS + group
            self.send(
                ready,
                self.view(self.far_buf, index),
                self.far_sem.at[index],
                (self.place.group, self.place.far),
            )

    def sideways(self, step):
        group, near = self.place.around(step), self.place.near
        ready = self.from_twin(group, near)
        self.add(ready, [self.part(group, near), self.from_far(group, 0)])
        self.send(
            ready,
            self.view(self.near_buf, group),
            self.near_sem.at[group],
            (self.place.group, near),
        )

    def homeward(self, step):
        group, member = self.place.around(step), self.place.member
        ready = self.from_twin(group, member)
        other = self.view(self.near_buf, group)
        far = self.from_far(group, 1)
        self.arrive(other, self.near_sem.at[group])
        self.add(ready, [self.part(group, member), far, other])
        if step:
            self.send(
                ready,
                self.view(self.group_buf, step - 1),
                self.group_sem.at[step - 1],
                (group, member),
            )

    def finish(self, store):
        for step in TURN:
            self.arrive(self.view(self.group_buf, step - 1), self.group_sem.at[step - 1])
        ready = self.view(self.twin_buf, self.twin_index(self.place.group, self.place.member))

        def some(block, carry):
            at = pl.ds(pl.multiple_of(block * 16, 16), 16)
            total = ready[at].astype(jnp.float32)
            for step in TURN:
                total = total + self.view(self.group_buf, step - 1)[at].astype(jnp.float32)
            store(at, total)
            return carry

        lax.fori_loop(0, self.rows // 16, some, 0)


BACKWARD = (1, 3, 2, 0)


def iota(shape, dim):
    return lax.broadcasted_iota(jnp.int32, shape, dim)


def swap_halves(block):
    lane = iota(block.shape, 1)
    return jnp.where(
        lane % HDIM < HDIM // 2, pltpu.roll(block, 128 - HDIM // 2, 1), pltpu.roll(block, HDIM // 2, 1)
    )


def step_kernel(
    length_ref,
    tokens_hbm,
    cotangent_hbm,
    routes_hbm,
    qkv_hbm,
    out_hbm,
    router_hbm,
    gains_hbm,
    shared_in_hbm,
    shared_down_hbm,
    cosine_hbm,
    sine_hbm,
    expert_in_hbm,
    expert_down_hbm,
    layer_out_hbm,
    input_grad_hbm,
    owned_grad_hbm,
    small_grad_hbm,
    grad_in_hbm,
    grad_down_hbm,
    shared_grad_hbm,
    tokens_ref,
    cotangent_ref,
    routes_ref,
    qkv_ref,
    router_ref,
    gains_ref,
    shared_in_ref,
    shared_down_ref,
    cosine_ref,
    sine_ref,
    owned_ref,
    small_ref,
    small_square,
    layer_out_ref,
    input_grad_ref,
    owned_grad_ref,
    small_grad_ref,
    grad_in_ref,
    grad_down_ref,
    shared_grad_ref,
    pieces_ref,
    stage,
    small_stage,
    mats,
    small_all,
    first_all,
    second_all,
    pieces,
    shared_send,
    weight_in,
    weight_down,
    out_all,
    hidden_low,
    mixed_low,
    pre,
    back_hidden,
    queries,
    keys,
    values,
    probs,
    normed_low,
    context,
    middle_ref,
    mixer,
    rows_sum,
    grad_mid,
    grad_context,
    grad_proj,
    gate_keep,
    twin_a,
    far_a,
    near_a,
    group_a,
    twin_b,
    far_b,
    near_b,
    group_b,
    gate_all,
    gate_part,
    small_part,
    gate_sum,
    twin_g,
    far_g,
    near_g,
    group_g,
    twin_s,
    far_s,
    near_s,
    group_s,
    gate_send,
    gate_recv,
    gate_back_send,
    small_back_send,
    pair_send,
    pair_recv,
    local_sem,
    store_sem,
    mats_send,
    mats_recv,
    small_send,
    small_recv,
    cot_send,
    cot_recv,
    mix_send,
    mix_recv,
    piece_send,
    piece_recv,
    rows_send,
    out_send,
    own_send,
    twin_sems,
    far_sems,
    near_sems,
    group_sems,
    free_sem,
):
    low = jnp.bfloat16
    rows = tokens_ref.shape[0]
    fetched = []
    for source, target in (
        (qkv_hbm, qkv_ref),
        (out_hbm, owned_ref.at[3]),
        (router_hbm, router_ref),
        (gains_hbm, gains_ref),
        (cotangent_hbm, cotangent_ref),
        (tokens_hbm, tokens_ref),
        (routes_hbm, routes_ref),
        (cosine_hbm, cosine_ref),
        (sine_hbm, sine_ref),
        (shared_in_hbm.at[:, 0, :], shared_in_ref.at[0]),
        (shared_in_hbm.at[:, 1, :], shared_in_ref.at[1]),
        (shared_down_hbm, shared_down_ref),
        (expert_in_hbm.at[0, :, 0, :], grad_in_ref.at[:, pl.ds(0, 256)]),
        (expert_in_hbm.at[0, :, 1, :], grad_in_ref.at[:, pl.ds(256, 256)]),
        (expert_down_hbm.at[0], grad_down_ref.at[pl.ds(0, 256)]),
    ):
        fetched.append(pltpu.make_async_copy(source, target, local_sem.at[len(fetched)]))
        fetched[-1].start()
    stored = []

    def store_out(source, target):
        copy = pltpu.make_async_copy(source, target, store_sem.at[len(stored)])
        copy.start()
        stored.append(copy)
    place = Place()
    group, member, core = place.group, place.member, place.core
    barrier = pltpu.get_barrier_semaphore()
    place.tell(barrier)
    place.hear(barrier)

    twin_device = (group, place.twin)
    for name in (0, 1, 2, 3):
        fetched[name].wait()
    for part in range(3):
        owned_ref[part] = qkv_ref[:, D * part : D * part + D]
    small_square[...] = jnp.zeros_like(small_square)
    small_square[pl.ds(0, GROUPS), pl.ds(0, 24)] = router_ref[...]
    small_square[pl.ds(GROUPS, 2), pl.ds(0, 24)] = gains_ref[...]
    small_ref[...] = small_square[...].T[:24]
    own_rows = pl.ds(pl.multiple_of(24 * core, 8), 24)
    owned = pltpu.make_async_remote_copy(
        src_ref=owned_ref.at[pl.ds(2 * (1 - core), 2)],
        dst_ref=stage.at[:, own_rows],
        send_sem=pair_send.at[0],
        recv_sem=pair_recv.at[0],
        device_id=twin_device,
        device_id_type=MESH,
    )
    owned.start()
    small_pair = pltpu.make_async_remote_copy(
        src_ref=small_ref,
        dst_ref=small_stage.at[own_rows],
        send_sem=pair_send.at[1],
        recv_sem=pair_recv.at[1],
        device_id=twin_device,
        device_id_type=MESH,
    )
    small_pair.start()
    stage[:, own_rows] = owned_ref[pl.ds(2 * core, 2)]
    small_stage[own_rows] = small_ref[...]
    owned.wait()
    small_pair.wait()

    def mats_at(group, member):
        chip = group * (PLANE // 2) + member // 2
        return mats.at[pl.ds(2 * (member % 2), 2), pl.ds(pl.multiple_of(48 * chip, 16), 48)]

    def small_at(group, member):
        chip = group * (PLANE // 2) + member // 2
        return small_all.at[pl.ds(pl.multiple_of(48 * chip, 16), 48)]

    mats_at(group, member)[...] = stage[...].astype(low)
    small_at(group, member)[...] = small_stage[...].astype(low)
    send_small = Gather(place, small_at, small_send, small_recv, pair=False)
    send_mats = Gather(place, mats_at, mats_send, mats_recv)
    send_small.start()
    send_mats.start()
    length = length_ref[0]
    row_at = iota((rows, 1), 0)
    live = (row_at < length).astype(jnp.float32)
    fetched[4].wait()
    first_all[place.mine] = (cotangent_ref[...] * live).astype(low)

    send_cot = Gather(
        place,
        lambda group, member: first_all.at[slot_of(group, member)],
        cot_send,
        cot_recv,
    )

    def move_piece(source, target, sems, base):
        for step in TURN:
            pltpu.make_async_remote_copy(
                src_ref=source.at[place.around(step)],
                dst_ref=target.at[group],
                send_sem=piece_send.at[base + step - 1],
                recv_sem=piece_recv.at[base + (GROUPS - step) - 1],
                device_id=(place.around(step), member),
                device_id_type=MESH,
            ).start()
        target[group] = source[group]

    def wait_pieces(source, target, base):
        for step in TURN:
            copy = pltpu.make_async_remote_copy(
                src_ref=source.at[place.around(step)],
                dst_ref=target.at[place.around(step)],
                send_sem=piece_send.at[base + step - 1],
                recv_sem=piece_recv.at[base + step - 1],
                device_id=(place.around(step), member),
                device_id_type=MESH,
            )
            copy.wait()

    for step in (0,) + TURN:
        if step:
            send_small.own_column(step)
            send_mats.own_column(step)
        send_small.near_column(step)
        send_mats.near_column(step)
        if step == 0:
            send_cot.start()

    for name in (9, 10, 11):
        fetched[name].wait()
    for piece in range(GROUPS):
        at = pl.ds(64 * piece, 64)
        both_halves = [shared_in_ref[0, :, at], shared_in_ref[1, :, at]]
        pieces_ref[piece, :, pl.ds(0, 128)] = jnp.concatenate(both_halves, axis=1).astype(low)
        last = shared_down_ref[:, at]
        last = jnp.concatenate([last, jnp.zeros_like(last)], axis=1)
        pieces_ref[piece, :, pl.ds(128, 128)] = last.astype(low)
    move_piece(pieces_ref, pieces, piece_send, 0)

    for name in (12, 13, 14):
        fetched[name].wait()
    weight_in[:, pl.ds(0, 512)] = grad_in_ref[:, pl.ds(0, 512)].astype(low)
    weight_down[pl.ds(0, 256)] = grad_down_ref[pl.ds(0, 256)].astype(low)
    grad_down_ref[...] = jnp.zeros_like(grad_down_ref)
    grad_in_ref[...] = jnp.zeros_like(grad_in_ref)

    for step in (0,) + TURN:
        for origin in (place.far, place.corner):
            send_small.wait(place.around(step), origin)
            send_mats.last_column(step, origin)
    for step in TURN:
        send_cot.own_column(step)
    for origin in (place.twin, place.near_twin, place.far_twin, place.corner_twin):
        send_mats.twin_column(origin)

    for name in (5, 6, 7, 8):
        fetched[name].wait()
    inputs = tokens_ref[...].astype(jnp.float32)
    inverse_one = lax.rsqrt(jnp.mean(inputs * inputs, axis=-1, keepdims=True) + NORM_EPS)
    pick = (iota((8, 128), 1) == iota((8, 128), 0) + GROUPS).astype(low)
    gains = nt(pick, small_all[...])
    gain_one, gain_two = gains[0:1], gains[1:2]
    normed_low[...] = (inputs * inverse_one * gain_one).astype(low)
    for part, target in ((0, queries), (1, keys), (2, values)):
        pre[pl.ds(0, rows)] = nn(normed_low[...], mats[part])
        for block in range(D // 128):
            at = pl.ds(128 * block, 128)
            piece = pre[pl.ds(0, rows), at]
            if part < 2:
                piece = piece * cosine_ref[...] + swap_halves(piece) * sine_ref[...]
            target[:, at] = piece.astype(low)
    for step in (0, 1):
        send_cot.near_column(step)
    diagonal = iota((rows, rows), 0) == iota((rows, rows), 1)
    query_at, key_at = iota((rows, rows), 0), iota((rows, rows), 1)
    allowed = (key_at <= query_at) & (key_at < length)
    lower = iota((rows, 128), 1) < HDIM

    def attend(pair, carry):
        at = pl.ds(pl.multiple_of(pair * 128, 128), 128)
        query, key, value = queries[:, at], keys[:, at], values[:, at]
        found = []
        for half in (0, 1):
            own = lower if half == 0 else jnp.logical_not(lower)
            scores = nt(jnp.where(own, query, jnp.zeros_like(query)), key) * 0.125
            scores = jnp.where(allowed, scores, MASKED)
            exponent = jnp.exp(scores - jnp.max(scores, axis=-1, keepdims=True))
            prob = exponent / jnp.sum(exponent, axis=-1, keepdims=True)
            probs[pair * 2 + half] = prob
            found.append(nn(prob.astype(low), value))
        context[:, at] = jnp.where(lower, found[0], found[1]).astype(low)
        for serve in range(2):

            @pl.when(pair == serve)
            def _():
                send_cot.near_column((3, 2)[serve])

        return carry

    lax.fori_loop(0, HEADS // 2, attend, 0)
    middle = inputs + nt(context[...], mats[3])
    middle_ref[...] = middle
    inverse_two = lax.rsqrt(jnp.mean(middle * middle, axis=-1, keepdims=True) + NORM_EPS)
    mixer[...] = (middle * inverse_two * gain_two).astype(low)
    logits = nn(mixer[...], small_all[...])
    lane = iota((rows, 128), 1)
    chosen, hits = [], []
    for choice in (0, 1):
        row = routes_ref[choice : choice + 1, pl.ds(pl.multiple_of(member * rows, rows), rows)]
        picked = jnp.sum(jnp.where(diagonal, row.astype(jnp.float32), 0.0), axis=1, keepdims=True)
        hit = (lane.astype(jnp.float32) == picked).astype(jnp.float32)
        hits.append(hit)
        chosen.append(jnp.sum(logits * hit, axis=-1, keepdims=True))
    top = jnp.maximum(chosen[0], chosen[1])
    exponents = [jnp.exp(value - top) for value in chosen]
    total = exponents[0] + exponents[1]
    gates = [value / total for value in exponents]
    gate_keep[...] = jnp.where(lane == 0, gates[0], jnp.where(lane == 1, gates[1], 0.0))
    table = sum(gate.astype(low).astype(jnp.float32) * hit for gate, hit in zip(gates, hits))
    second_all[place.mine] = mixer[...]
    gate_all[place.mine] = table.T[:EXTRA].astype(low)
    send_rows = Gather(
        place, lambda group, member: second_all.at[slot_of(group, member)], mix_send, mix_recv
    )
    send_gates = Gather(
        place, lambda group, member: gate_all.at[slot_of(group, member)], gate_send, gate_recv
    )
    send_mix = Together(send_gates, send_rows)
    send_mix.start()
    for step in (0,) + TURN:
        for origin in (place.far, place.corner):
            send_cot.last_column(step, origin)
    for origin in (place.twin, place.near_twin, place.far_twin, place.corner_twin):
        send_cot.twin_column(origin)
    send_cot.drain(first_all.at[0])

    wait_pieces(pieces_ref, pieces, 0)
    first_half = iota((192, 128), 1) < 64
    for piece in range(GROUPS):
        at = pl.ds(192 * piece, 192)
        both_halves = pieces[piece, :, pl.ds(0, 128)].astype(jnp.float32)
        weight_in[at, pl.ds(512, 128)] = jnp.where(first_half, both_halves, 0.0).astype(low)
        other = pltpu.roll(both_halves, 64, 1)
        weight_in[at, pl.ds(640, 128)] = jnp.where(first_half, other, 0.0).astype(low)
    turned = pieces[:, :, pl.ds(128, 128)].reshape(D, 128).astype(jnp.float32)
    weight_down[pl.ds(256, 128)] = turned.T.astype(low)
    big_move = Scatter(
        place,
        lambda group, member: first_all.at[slot_of(group, member)],
        rows,
        (twin_a, far_a, near_a, group_a),
        rows_send,
        (twin_sems.at[0], far_sems.at[0], near_sems.at[0], group_sems.at[0]),
    )
    gate_move = Scatter(
        place,
        lambda group, member: gate_part.at[slot_of(group, member)],
        EXTRA,
        (twin_g, far_g, near_g, group_g),
        gate_back_send,
        (twin_sems.at[3], far_sems.at[3], near_sems.at[3], group_sems.at[3]),
    )
    rows_move = Together(gate_move, big_move)
    out_move = Scatter(
        place,
        lambda group, member: out_all.at[slot_of(group, member)],
        rows,
        (twin_b, far_b, near_b, group_b),
        out_send,
        (twin_sems.at[1], far_sems.at[1], near_sems.at[1], group_sems.at[1]),
    )
    own_expert = (iota((EXTRA, 128), 0) == group).astype(low)
    twins = (place.corner_twin, place.near_twin, place.far_twin, place.twin)

    serve_before = (
        lambda: (
            send_mix.own_column(1),
            send_mix.near_column(1),
            send_mix.own_column(3),
            send_mix.last_plane(1),
        ),
        lambda: (send_mix.near_column(3), send_mix.own_column(2), send_mix.twin_plane(1)),
        lambda: (send_mix.near_column(2), send_mix.near_column(0), send_mix.last_plane(3)),
        lambda: (rows_move.outward(1), send_mix.twin_plane(3)),
        lambda: send_mix.last_plane(2),
        lambda: (rows_move.outward(3), rows_move.sideways(1), send_mix.twin_plane(2)),
        lambda: send_mix.last_plane(0),
        lambda: (
            rows_move.outward(2),
            rows_move.sideways(3),
            rows_move.homeward(1),
            send_mix.twin_plane(0),
        ),
    )

    def tokens_part(index, carry):
        for at in range(PLANE):

            @pl.when(index == at)
            def _():
                serve_before[at]()

        half = index // 2
        step = jnp.where(half == 0, 1, jnp.where(half == 1, 3, jnp.where(half == 2, 2, 0)))
        side = (core + index) % 2
        base = pl.multiple_of(place.around(step) * PLANE + side * GROUPS, GROUPS)
        four = pl.ds(base, GROUPS)
        taken = second_all[four].reshape(GROUPS * rows, D)
        pre[...] = nn(taken, weight_in[...])
        cot = first_all[four].reshape(GROUPS * rows, D)
        back_hidden[...] = nt(cot, weight_down[...])

        def units(block, carry):
            slot = base + block
            scale = tn(gate_all[slot], own_expert)
            at = pl.ds(pl.multiple_of(block * rows, rows), rows)
            weigh = jnp.zeros((rows, 128), jnp.float32)
            for gate_at, up_at, hidden_at, routed in (
                (0, 256, 0, True),
                (128, 384, 128, True),
                (512, 640, 256, False),
            ):
                gate_pre = pre[at, pl.ds(gate_at, 128)]
                up_pre = pre[at, pl.ds(up_at, 128)]
                hidden_grad = back_hidden[at, pl.ds(hidden_at, 128)]
                sigmoid_g = 0.5 * jnp.tanh(0.5 * gate_pre) + 0.5
                silu_g = gate_pre * sigmoid_g
                hidden = (silu_g * up_pre).astype(low)
                if routed:
                    wide = hidden.astype(jnp.float32)
                    weigh = weigh + wide * hidden_grad
                    hidden_grad = hidden_grad * scale
                    hidden = (wide * scale).astype(low)
                grad_gate = hidden_grad * up_pre * (sigmoid_g + silu_g * (1.0 - sigmoid_g))
                hidden_low[at, pl.ds(hidden_at, 128)] = hidden
                mixed_low[at, pl.ds(gate_at, 128)] = grad_gate.astype(low)
                mixed_low[at, pl.ds(up_at, 128)] = (hidden_grad * silu_g).astype(low)
            high = weigh.astype(low)
            rest = (weigh - high.astype(jnp.float32)).astype(low)
            gate_part[slot] = nt(own_expert, high) + nt(own_expert, rest)
            return carry

        lax.fori_loop(0, GROUPS, units, 0)
        grad_down_ref[...] += tn(hidden_low[...], cot)
        pre[...] = nt(mixed_low[...], weight_in[...])
        first_all[four] = pre[...].astype(low).reshape(GROUPS, rows, D)
        for at in range(1, PLANE, 2):

            @pl.when(index == at)
            def _():
                for origin in twins:
                    rows_move.to_twin(place.around(BACKWARD[at // 2]), origin)

        taken = second_all[four].reshape(GROUPS * rows, D)
        grad_in_ref[...] += tn(taken, mixed_low[...])
        pre[...] = nn(hidden_low[...], weight_down[...])
        out_all[four] = pre[...].astype(low).reshape(GROUPS, rows, D)
        for at in range(1, PLANE, 2):

            @pl.when(index == at)
            def _():
                for origin in twins:
                    out_move.to_twin(place.around(BACKWARD[at // 2]), origin)

        return carry

    lax.fori_loop(0, PLANE, tokens_part, 0)
    rows_move.outward(0)
    rows_move.sideways(2)
    rows_move.homeward(3)
    rows_move.sideways(0)
    rows_move.homeward(2)
    rows_move.homeward(0)
    send_rows.drain(second_all.at[0])
    send_gates.drain(gate_all.at[0])

    for piece in range(GROUPS):
        at = pl.ds(192 * piece, 192)
        both_halves = [grad_in_ref[at, pl.ds(512, 64)], grad_in_ref[at, pl.ds(640, 64)]]
        shared_send[piece, :, pl.ds(0, 128)] = jnp.concatenate(both_halves, axis=1).astype(low)
    turned = grad_down_ref[pl.ds(256, 128)].T
    shared_send[:, :, pl.ds(128, 128)] = turned.astype(low).reshape(GROUPS, 192, 128)
    store_out(grad_in_ref.at[:, pl.ds(0, 512)], grad_in_hbm)
    store_out(grad_down_ref.at[pl.ds(0, 256)], grad_down_hbm)

    def keep_rows(at, total):
        rows_sum[at] = total

    def keep_gates(at, total):
        gate_sum[at] = total

    big_move.finish(keep_rows)
    gate_move.finish(keep_gates)
    big_move.drain(first_all.at[0])
    gate_move.drain(gate_part.at[0])
    place.tell(free_sem)
    move_piece(shared_send, shared_grad_ref, piece_send, 3)

    gate_grads = gate_sum[...]
    gate_grads = jnp.concatenate([gate_grads, jnp.zeros((rows - EXTRA, 128), jnp.float32)], axis=0).T
    grad_gates = [jnp.sum(gate_grads * hit, axis=-1, keepdims=True) for hit in hits]
    kept = [
        jnp.sum(jnp.where(lane == choice, gate_keep[...], 0.0), axis=-1, keepdims=True)
        for choice in (0, 1)
    ]
    gate_dot = kept[0] * grad_gates[0] + kept[1] * grad_gates[1]
    grad_logits = sum(
        hit * (gate * (grad - gate_dot)) for hit, gate, grad in zip(hits, kept, grad_gates)
    ).astype(low)
    grad_router = tn(grad_logits, mixer[...])[:8]
    middle = middle_ref[...]
    inverse_two = lax.rsqrt(jnp.mean(middle * middle, axis=-1, keepdims=True) + NORM_EPS)
    scaled_two = middle * inverse_two
    gains = nt(pick, small_all[...])
    gain_one, gain_two = gains[0:1], gains[1:2]
    grad_normed = rows_sum[pl.ds(0, rows)] + nt(grad_logits, small_all[...])
    grad_gain_two = jnp.sum(grad_normed * scaled_two, axis=0, keepdims=True)
    grad_scaled = grad_normed * gain_two
    grad_middle = cotangent_ref[...] * live + inverse_two * (
        grad_scaled - scaled_two * jnp.mean(grad_scaled * scaled_two, axis=-1, keepdims=True)
    )
    grad_mid[...] = grad_middle
    grad_att = grad_middle.astype(low)
    grad_context[...] = nn(grad_att, mats[3]).astype(low)

    mats_move = Scatter(
        place,
        lambda group, member: first_all.at[slot_of(group, member), pl.ds(0, 96)],
        96,
        (twin_a, far_a, near_a, group_a),
        own_send,
        (twin_sems.at[2], far_sems.at[2], near_sems.at[2], group_sems.at[2]),
    )
    small_move = Scatter(
        place,
        lambda group, member: small_part.at[group * (PLANE // 2) + member // 2],
        EXTRA,
        (twin_s, far_s, near_s, group_s),
        small_back_send,
        (twin_sems.at[4], far_sems.at[4], near_sems.at[4], group_sems.at[4]),
    )
    own_move = Together(small_move, mats_move)

    def put_part(which, left, right):
        for half in (0, 1):
            product = tn(left[:, 384 * half : 384 * half + 384], right).astype(low)
            for place_in in range(8):
                chip = half * 8 + place_in
                slot = slot_of(chip // 4, (chip % 4) * 2 + which // 2)
                first_all[slot, pl.ds(48 * (which % 2), 48)] = product[48 * place_in : 48 * place_in + 48]

    put_part(3, grad_att, context[...])

    def attend_back(pair, carry):
        at = pl.ds(pl.multiple_of(pair * 128, 128), 128)
        query, key, value = queries[:, at], keys[:, at], values[:, at]
        grad_ctx = grad_context[:, at]
        grad_query, grad_key, grad_value = [], [], []
        for half in (0, 1):
            own = lower if half == 0 else jnp.logical_not(lower)
            prob = probs[pair * 2 + half]
            grad_prob = nt(jnp.where(own, grad_ctx, jnp.zeros_like(grad_ctx)), value)
            grad_value.append(tn(prob.astype(low), grad_ctx))
            row_dot = jnp.sum(grad_prob * prob, axis=-1, keepdims=True)
            grad_score = (prob * (grad_prob - row_dot)).astype(low)
            grad_query.append(nn(grad_score, key))
            grad_key.append(tn(grad_score, query))
        grad_q = jnp.where(lower, grad_query[0], grad_query[1]) * 0.125
        grad_k = jnp.where(lower, grad_key[0], grad_key[1]) * 0.125
        grad_q = grad_q * cosine_ref[...] - swap_halves(grad_q) * sine_ref[...]
        grad_k = grad_k * cosine_ref[...] - swap_halves(grad_k) * sine_ref[...]
        grad_proj[0, :, at] = grad_q.astype(low)
        grad_proj[1, :, at] = grad_k.astype(low)
        grad_proj[2, :, at] = jnp.where(lower, grad_value[0], grad_value[1]).astype(low)
        for serve in range(4):

            @pl.when(pair == serve)
            def _():
                out_move.outward(BACKWARD[serve])

        return carry

    lax.fori_loop(0, HEADS // 2, attend_back, 0)
    grad_one = nt(grad_proj[0], mats[0]) + nt(grad_proj[1], mats[1]) + nt(grad_proj[2], mats[2])
    inputs = tokens_ref[...].astype(jnp.float32)
    inverse_one = lax.rsqrt(jnp.mean(inputs * inputs, axis=-1, keepdims=True) + NORM_EPS)
    scaled_one = inputs * inverse_one
    grad_gain_one = jnp.sum(grad_one * scaled_one, axis=0, keepdims=True)
    grad_scaled = grad_one * gain_one
    input_grad_ref[...] = grad_mid[...] + inverse_one * (
        grad_scaled - scaled_one * jnp.mean(grad_scaled * scaled_one, axis=-1, keepdims=True)
    )
    store_out(input_grad_ref, input_grad_hbm)
    for which in range(3):
        put_part(which, normed_low[...], grad_proj[which])
    at_row = iota((8, D), 0)
    small_rows = jnp.where(
        at_row < GROUPS, grad_router, jnp.where(at_row == GROUPS, grad_gain_one, grad_gain_two)
    )
    small_part[...] = jnp.zeros_like(small_part)
    for chip in range(ALL // 2):
        turned = pltpu.roll(small_rows, (D - 48 * chip) % D, 1) if chip else small_rows
        small_part[chip, pl.ds(0, 8)] = turned[:, :128]
    place.hear(free_sem)
    for step in BACKWARD:
        for origin in (place.corner_twin, place.near_twin, place.far_twin, place.twin):
            own_move.to_twin(place.around(step), origin)
    for act, step in (
        (out_move.sideways, 1),
        (out_move.sideways, 3),
        (own_move.outward, 1),
        (out_move.homeward, 1),
        (out_move.sideways, 2),
        (own_move.outward, 3),
        (out_move.homeward, 3),
        (out_move.sideways, 0),
        (own_move.sideways, 1),
        (own_move.outward, 2),
        (out_move.homeward, 2),
        (own_move.sideways, 3),
        (own_move.homeward, 1),
        (own_move.outward, 0),
        (out_move.homeward, 0),
        (own_move.sideways, 2),
        (own_move.homeward, 3),
        (own_move.sideways, 0),
        (own_move.homeward, 2),
        (own_move.homeward, 0),
    ):
        act(step)

    def keep_out(at, total):
        here = pl.ds(at.start, 16)
        live_here = (iota((16, 1), 0) + at.start < length).astype(jnp.float32)
        layer_out_ref[here] = live_here * (middle_ref[here] + total)

    out_move.finish(keep_out)
    store_out(layer_out_ref, layer_out_hbm)
    wait_pieces(shared_send, shared_grad_ref, 3)
    store_out(shared_grad_ref, shared_grad_hbm)

    def keep_own(at, total):
        rows_sum[at] = total

    def keep_small(at, total):
        gate_sum[at] = total

    mats_move.finish(keep_own)
    small_move.finish(keep_small)
    for matrix in (0, 1):
        stage[matrix] = rows_sum[pl.ds(48 * matrix, 48)]
    theirs = pl.ds(pl.multiple_of(24 * (1 - core), 8), 24)
    mine = pl.ds(2 * core, 2)
    last = pltpu.make_async_remote_copy(
        src_ref=stage.at[:, theirs],
        dst_ref=owned_grad_ref.at[mine],
        send_sem=pair_send.at[2],
        recv_sem=pair_recv.at[2],
        device_id=twin_device,
        device_id_type=MESH,
    )
    last.start()
    owned_grad_ref[mine] = stage[:, own_rows]
    block = gate_sum[pl.ds(0, 8)]
    small_grad_ref[...] = jnp.where(core == 0, block, pltpu.roll(block, 128 - 24, 1))
    store_out(small_grad_ref, small_grad_hbm)
    last.wait()
    store_out(owned_grad_ref, owned_grad_hbm)
    out_move.drain(out_all.at[0])
    mats_move.drain(first_all.at[0, pl.ds(0, 96)])
    small_move.drain(small_part.at[0])
    send_mats.drain(mats_at(group, member))
    send_small.drain(small_at(group, member))
    for copy in stored:
        copy.wait()


def update_kernel(*refs):
    (
        owned_grad,
        small_grad,
        grad_in,
        grad_down,
        shared_grad,
        layer_in,
        input_in,
    ) = refs[:7]
    olds = [refs[7 + 3 * at : 10 + 3 * at] for at in range(8)]
    layer_out, input_out = refs[31:33]
    news = [refs[33 + 3 * at : 36 + 3 * at] for at in range(8)]
    owned_buf, small_buf, in_buf, down_buf, shared_buf, layer_buf, input_buf = refs[57:64]
    bufs, load_sem, store_sem = refs[64:-2], refs[-2], refs[-1]
    counts = [0, 0]

    def copy(source, target, which):
        made = pltpu.make_async_copy(source, target, (load_sem, store_sem)[which].at[counts[which]])
        counts[which] += 1
        made.start()
        return made

    half = D // 2
    jobs = []
    for at in range(2):
        for block in range(2):
            jobs.append((6, lambda ref, at=at, block=block: ref.at[0, pl.ds(half * block, half), at, :], (half, 256)))
    jobs.append((7, lambda ref: ref.at[0], (256, D)))
    for at in range(2):
        jobs.append((4, lambda ref, at=at: ref.at[:, at, :], (192, 256)))
    for which in (5, 1, 2, 3, 0):
        jobs.append((which, lambda ref: ref, None))
    passes, loaded = [], []
    through = [copy(layer_in, layer_buf, 0), copy(input_in, input_buf, 0)]
    first_grads = [copy(grad_in, in_buf, 0), copy(grad_down, down_buf, 0)]
    other_grads = [copy(shared_grad, shared_buf, 0), copy(owned_grad, owned_buf, 0), copy(small_grad, small_buf, 0)]
    for at, (which, view, _) in enumerate(jobs):
        loaded.append([copy(view(olds[which][k]), bufs[3 * at + k], 0) for k in range(3)])
    for made in first_grads + through:
        made.wait()
    passes += [copy(layer_buf, layer_out, 1), copy(input_buf, input_out, 1)]
    rates = (
        0.5,
        1.5 / math.sqrt(D),
        1.5 / math.sqrt(4 * D // SEQ),
        1.0 / math.sqrt(D),
        1.5 / math.sqrt(D),
        1.5 / math.sqrt(FF_SH),
        1.5 / math.sqrt(D),
        1.5 / math.sqrt(FF),
    )

    def pair_up(part, swap_first, swap_second):
        left = iota((192, 128), 1) < 64
        tiles = []
        for tile in range(2):
            pair = [
                shared_buf[2 * tile + k, :, pl.ds(128 * part, 128)].astype(jnp.float32) for k in (0, 1)
            ]
            if swap_first:
                pair[0] = pltpu.roll(pair[0], 64, 1)
            if swap_second:
                pair[1] = pltpu.roll(pair[1], 64, 1)
            tiles.append(jnp.where(left, pair[0], pair[1]))
        return jnp.concatenate(tiles, axis=1)

    for at, (which, view, shape) in enumerate(jobs):
        if at == 5:
            for made in other_grads:
                made.wait()
        for made in loaded[at]:
            made.wait()
        mine = bufs[3 * at : 3 * at + 3]
        rate = rates[which]

        def update(index, gradient):
            weight, first_old, second_old = (ref[index] for ref in mine)
            results = adamw(weight, gradient, first_old, second_old, rate)
            for ref, value in zip(mine, results):
                ref[index] = value

        if which == 6:
            part, block = at // 2, at % 2

            def chunk(number, carry):
                here = pl.ds(pl.multiple_of(number * 32, 32), 32)
                there = pl.ds(pl.multiple_of(half * block + number * 32, 32), 32)
                update(here, in_buf[there, pl.ds(256 * part, 256)])
                return carry

            lax.fori_loop(0, half // 32, chunk, 0)
        elif which == 7:

            def chunk(number, carry):
                here = pl.ds(pl.multiple_of(number * 8, 8), 8)
                update(here, down_buf[here])
                return carry

            lax.fori_loop(0, 32, chunk, 0)
        elif which == 4:
            update(..., pair_up(0, at == 6, at == 5))
        elif which == 5:
            update(..., pair_up(1, False, True))
        elif which == 1:
            for part in range(3):
                update((slice(None), pl.ds(D * part, D)), owned_buf[part])
        elif which == 2:
            update(..., owned_buf[3])
        elif which == 3:
            update(..., small_buf[:4, :24])
        else:
            update(..., small_buf[4:6, :24])
        for k in range(3):
            passes.append(copy(mine[k], view(news[which][k]), 1))
    for made in passes:
        made.wait()


def dense_shards(
    tokens,
    cotangent,
    lengths,
    routes,
    norm_gains,
    gains_first,
    gains_second,
    qkv_weight,
    qkv_first,
    qkv_second,
    out_weight,
    out_first,
    out_second,
    router_weight,
    router_first,
    router_second,
    shared_in,
    shared_in_first,
    shared_in_second,
    shared_down,
    shared_down_first,
    shared_down_second,
    expert_in,
    expert_in_first,
    expert_in_second,
    expert_down,
    expert_down_first,
    expert_down_second,
):
    low_type = jnp.bfloat16
    seq_rows = tokens.shape[0]
    per_device = D // ALL
    half_dim = HDIM // 2
    positions = np.arange(seq_rows, dtype=np.float32)[:, None]
    angles = positions * np.tile(ROPE_BASE ** (-np.arange(half_dim) / half_dim), 4)[None]
    sign = np.tile(np.repeat([-1.0, 1.0], half_dim), 2)[None]
    cosine = jnp.asarray(np.cos(angles), jnp.float32)
    sine = jnp.asarray(np.sin(angles) * sign, jnp.float32)
    wide, f32, i32 = low_type, jnp.float32, jnp.int32
    dma = pltpu.SemaphoreType.DMA
    anywhere = pl.BlockSpec(memory_space=pltpu.HBM)
    passed = pl.pallas_call(
        step_kernel,
        out_shape=(
            jax.ShapeDtypeStruct((seq_rows, D), f32),
            jax.ShapeDtypeStruct((seq_rows, D), f32),
            jax.ShapeDtypeStruct((4, per_device, D), f32),
            jax.ShapeDtypeStruct((8, 128), f32),
            jax.ShapeDtypeStruct((D, 512), f32),
            jax.ShapeDtypeStruct((256, D), f32),
            jax.ShapeDtypeStruct((GROUPS, 192, 256), wide),
        ),
        in_specs=[pl.BlockSpec(memory_space=pltpu.SMEM)] + [anywhere] * 13,
        out_specs=(anywhere,) * 7,
        scratch_shapes=[
            pltpu.VMEM((seq_rows, D), wide),
            pltpu.VMEM((seq_rows, D), f32),
            pltpu.VMEM((2, PLANE * seq_rows), i32),
            pltpu.VMEM((per_device, 3 * D), f32),
            pltpu.VMEM((GROUPS, per_device), f32),
            pltpu.VMEM((2, per_device), f32),
            pltpu.VMEM((2, 192, 256), f32),
            pltpu.VMEM((192, 256), f32),
            pltpu.VMEM((seq_rows, 128), f32),
            pltpu.VMEM((seq_rows, 128), f32),
            pltpu.VMEM((4, per_device, D), f32),
            pltpu.VMEM((per_device, 128), f32),
            pltpu.VMEM((128, 128), f32),
            pltpu.VMEM((seq_rows, D), f32),
            pltpu.VMEM((seq_rows, D), f32),
            pltpu.VMEM((4, per_device, D), f32),
            pltpu.VMEM((8, 128), f32),
            pltpu.VMEM((D, 768), f32),
            pltpu.VMEM((384, D), f32),
            pltpu.VMEM((GROUPS, 192, 256), wide),
            pltpu.VMEM((GROUPS, 192, 256), wide),
            pltpu.VMEM((2, 48, D), f32),
            pltpu.VMEM((48, 128), f32),
            pltpu.VMEM((4, D, D), wide),
            pltpu.VMEM((D, 128), wide),
            pltpu.VMEM((ALL, seq_rows, D), wide),
            pltpu.VMEM((ALL, seq_rows, D), wide),
            pltpu.VMEM((GROUPS, 192, 256), wide),
            pltpu.VMEM((GROUPS, 192, 256), wide),
            pltpu.VMEM((D, 768), wide),
            pltpu.VMEM((384, D), wide),
            pltpu.VMEM((ALL, seq_rows, D), wide),
            pltpu.VMEM((GROUPS * seq_rows, 384), wide),
            pltpu.VMEM((GROUPS * seq_rows, 768), wide),
            pltpu.VMEM((GROUPS * seq_rows, 768), f32),
            pltpu.VMEM((GROUPS * seq_rows, 384), f32),
            pltpu.VMEM((seq_rows, D), wide),
            pltpu.VMEM((seq_rows, D), wide),
            pltpu.VMEM((seq_rows, D), wide),
            pltpu.VMEM((HEADS, seq_rows, seq_rows), f32),
            pltpu.VMEM((seq_rows, D), wide),
            pltpu.VMEM((seq_rows, D), wide),
            pltpu.VMEM((seq_rows, D), f32),
            pltpu.VMEM((seq_rows, D), wide),
            pltpu.VMEM((seq_rows, D), f32),
            pltpu.VMEM((seq_rows, D), f32),
            pltpu.VMEM((seq_rows, D), wide),
            pltpu.VMEM((3, seq_rows, D), wide),
            pltpu.VMEM((seq_rows, 128), f32),
            pltpu.VMEM((16, seq_rows, D), wide),
            pltpu.VMEM((8, seq_rows, D), wide),
            pltpu.VMEM((4, seq_rows, D), wide),
            pltpu.VMEM((3, seq_rows, D), wide),
            pltpu.VMEM((16, seq_rows, D), wide),
            pltpu.VMEM((8, seq_rows, D), wide),
            pltpu.VMEM((4, seq_rows, D), wide),
            pltpu.VMEM((3, seq_rows, D), wide),
            pltpu.VMEM((ALL, EXTRA, 128), wide),
            pltpu.VMEM((ALL, EXTRA, 128), f32),
            pltpu.VMEM((ALL // 2, EXTRA, 128), f32),
            pltpu.VMEM((EXTRA, 128), f32),
        ]
        + [pltpu.VMEM((count, EXTRA, 128), f32) for count in (16, 8, 4, 3) * 2]
        + [
            dma((31,)),
            dma((32,)),
            dma((31,)),
            dma((31,)),
            dma((3,)),
            dma((3,)),
            dma((15,)),
            dma((7,)),
            dma((31,)),
            dma((32,)),
            dma((31,)),
            dma((32,)),
            dma((31,)),
            dma((32,)),
            dma((31,)),
            dma((32,)),
            dma((6,)),
            dma((6,)),
            dma((31,)),
            dma((31,)),
            dma((31,)),
            dma((5, 16)),
            dma((5, 8)),
            dma((5, 4)),
            dma((5, 3)),
            pltpu.SemaphoreType.REGULAR,
        ],
        compiler_params=pltpu.CompilerParams(
            collective_id=0, has_side_effects=True, vmem_limit_bytes=VMEM_BYTES
        ),
    )(
        lengths,
        tokens,
        cotangent,
        routes.T,
        qkv_weight,
        out_weight.T,
        router_weight.T,
        norm_gains,
        shared_in,
        shared_down.T,
        cosine,
        sine,
        expert_in,
        expert_down,
    )
    layer_out, input_grad, owned_grad, small_grad, grad_in, grad_down, shared_grad = passed
    olds = [
        (norm_gains, gains_first, gains_second),
        (qkv_weight, qkv_first, qkv_second),
        (out_weight.T, out_first.T, out_second.T),
        (router_weight.T, router_first.T, router_second.T),
        (shared_in, shared_in_first, shared_in_second),
        (shared_down.T, shared_down_first.T, shared_down_second.T),
        (expert_in, expert_in_first, expert_in_second),
        (expert_down, expert_down_first, expert_down_second),
    ]
    flat = [old for three in olds for old in three]
    gradients = (owned_grad, small_grad, grad_in, grad_down, shared_grad)
    shapes = [(D // 2, 256)] * 4 + [(256, D)] + [(192, 256)] * 2 + [(192, 256)]
    shapes += [(per_device, 3 * D), (per_device, D), (GROUPS, per_device), (2, per_device)]
    results = pl.pallas_call(
        update_kernel,
        out_shape=tuple(
            jax.ShapeDtypeStruct(value.shape, value.dtype) for value in [layer_out, input_grad] + flat
        ),
        in_specs=[anywhere] * 31,
        out_specs=(anywhere,) * 26,
        scratch_shapes=[pltpu.VMEM(value.shape, value.dtype) for value in gradients + (layer_out, input_grad)]
        + [pltpu.VMEM(shape, f32) for shape in shapes for _ in range(3)]
        + [dma((43,)), dma((38,))],
        compiler_params=pltpu.CompilerParams(vmem_limit_bytes=VMEM_BYTES),
    )(*gradients, layer_out, input_grad, *flat)
    results = list(results)
    for at in (2 + 6, 2 + 9, 2 + 15):
        for k in range(3):
            results[at + k] = results[at + k].T
    return tuple(results)


def solution(mesh):
    outer, inner = OUTER, INNER
    rows, lanes = P((outer, inner), None), P(None, (outer, inner))
    shared_in, shared_down = P(outer, None, inner), P(inner, outer)
    expert_in, expert_down = P(outer, None, None, inner), P(outer, inner, None)
    placed = (
        rows,
        rows,
        P((outer, inner)),
        P(outer, None),
        lanes,
        lanes,
        lanes,
        rows,
        rows,
        rows,
        lanes,
        lanes,
        lanes,
        rows,
        rows,
        rows,
        shared_in,
        shared_in,
        shared_in,
        shared_down,
        shared_down,
        shared_down,
        expert_in,
        expert_in,
        expert_in,
        expert_down,
        expert_down,
        expert_down,
    )
    return jax.shard_map(
        dense_shards if (mesh.shape[outer], mesh.shape[inner]) == (4, 8) else routed_shards,
        mesh=mesh,
        in_specs=placed,
        out_specs=(
            rows,
            rows,
            lanes,
            lanes,
            lanes,
            rows,
            rows,
            rows,
            lanes,
            lanes,
            lanes,
            rows,
            rows,
            rows,
            shared_in,
            shared_in,
            shared_in,
            shared_down,
            shared_down,
            shared_down,
            expert_in,
            expert_in,
            expert_in,
            expert_down,
            expert_down,
            expert_down,
        ),
        check_vma=False,
    )
```

```python
import math

import jax
import jax.numpy as jnp
import numpy as np
from jax import lax
from jax.experimental import pallas as pl
from jax.experimental.pallas import tpu as pltpu
from jax.sharding import PartitionSpec as P

D = 768
HEADS = 12
HDIM = 64
FF = 2048
FF_SH = 2048
SEQ = 128
STEP = 4


OUTER, INNER = "expert", "head"
NORM_EPS = 1e-06
BETA_FIRST = 0.5
BETA_SECOND = 0.5
ADAM_EPS = 1e-08
DECAY = 0.1
MASKED = -1e30
ROPE_BASE = 10000.0


def rope_tables(row_count):
    half_dim = HDIM // 2
    positions = jnp.arange(row_count, dtype=jnp.float32)
    frequency = ROPE_BASE ** (-jnp.arange(half_dim, dtype=jnp.float32) / half_dim)
    angles = positions[:, None] * frequency[None, :]
    return (jnp.cos(angles)[:, None, :], jnp.sin(angles)[:, None, :])


def rotate(values, cosine_table, sine_table):
    half_dim = values.shape[-1] // 2
    first_half = values[..., :half_dim]
    second_half = values[..., half_dim:]
    return jnp.concatenate(
        [
            first_half * cosine_table - second_half * sine_table,
            second_half * cosine_table + first_half * sine_table,
        ],
        axis=-1,
    )


def unrotate(gradient, cosine_table, sine_table):
    half_dim = gradient.shape[-1] // 2
    first_half = gradient[..., :half_dim]
    second_half = gradient[..., half_dim:]
    return jnp.concatenate(
        [
            first_half * cosine_table + second_half * sine_table,
            second_half * cosine_table - first_half * sine_table,
        ],
        axis=-1,
    )


def norm_forward(values, gain_vec):
    inverse = lax.rsqrt(jnp.mean(values * values, axis=-1, keepdims=True) + NORM_EPS)
    scaled = values * inverse
    return (scaled, inverse, scaled * gain_vec)


def norm_backward(grad_out, scaled, inverse, gain_vec):
    grad_scaled = grad_out * gain_vec
    grad_gain = jnp.sum(grad_out * scaled, axis=0)
    grad_in = inverse * (
        grad_scaled - scaled * jnp.mean(grad_scaled * scaled, axis=-1, keepdims=True)
    )
    return (grad_in, grad_gain)


def attention_scores(query_rows, key_rows, length):
    row_count = query_rows.shape[0]
    scores = (
        jnp.einsum("qhd,khd->hqk", query_rows, key_rows, preferred_element_type=jnp.float32) * 0.125
    )
    positions = jnp.arange(row_count, dtype=jnp.int32)
    allowed = (positions[None, :] <= positions[:, None]) & (positions[None, :] < length)
    return (jnp.where(allowed[None], scores, MASKED), allowed)


def expert_forward(row_block, weight_in, weight_down):
    mixed_pre = jnp.dot(row_block, weight_in, preferred_element_type=jnp.float32)
    hidden_width = weight_down.shape[0]
    gate_pre = mixed_pre[:, :hidden_width]
    up_pre = mixed_pre[:, hidden_width:]
    hidden = (gate_pre * jax.nn.sigmoid(gate_pre) * up_pre).astype(jnp.bfloat16)
    return (mixed_pre, hidden, jnp.dot(hidden, weight_down, preferred_element_type=jnp.float32))


def expert_backward(row_block, mixed_pre, hidden, grad_out, weight_in, weight_down):
    hidden_width = weight_down.shape[0]
    gate_pre = mixed_pre[:, :hidden_width]
    up_pre = mixed_pre[:, hidden_width:]
    grad_hidden = jnp.dot(grad_out, weight_down.T, preferred_element_type=jnp.float32)
    sigmoid_g = jax.nn.sigmoid(gate_pre)
    silu_g = gate_pre * sigmoid_g
    grad_gate = (grad_hidden * up_pre * sigmoid_g * (1.0 + gate_pre * (1.0 - sigmoid_g))).astype(
        jnp.bfloat16
    )
    grad_up = (grad_hidden * silu_g).astype(jnp.bfloat16)
    grad_mixed = jnp.concatenate([grad_gate, grad_up], axis=1)
    grad_down = jnp.dot(hidden.T, grad_out, preferred_element_type=jnp.float32)
    grad_weight_in = jnp.dot(row_block.T, grad_mixed, preferred_element_type=jnp.float32)
    grad_row_block = jnp.dot(grad_mixed, weight_in.T, preferred_element_type=jnp.float32)
    return (grad_row_block, grad_weight_in, grad_down)


def route_tables(route_rows, blocks, block_cap, expert_total):
    per_block = route_rows.reshape(blocks, -1)
    hit_table = (
        per_block[:, :, None] == jnp.arange(expert_total, dtype=jnp.int32)[None, None, :]
    ).astype(jnp.int32)
    entries = per_block.shape[1]
    earlier = jnp.tril(jnp.ones((entries, entries), jnp.bfloat16))
    running = jnp.einsum(
        "ij,bje->bie", earlier, hit_table.astype(jnp.bfloat16), preferred_element_type=jnp.float32
    ).astype(jnp.int32)
    rank_in = jnp.sum((running - 1) * hit_table, axis=2)
    offsets = jnp.arange(blocks, dtype=jnp.int32)[:, None] * block_cap
    dest_slot = (per_block * (blocks * block_cap) + offsets + rank_in).reshape(-1)
    source_row = (
        jnp.zeros((expert_total * blocks * block_cap,), jnp.int32)
        .at[dest_slot]
        .set(jnp.arange(dest_slot.shape[0], dtype=jnp.int32) + 1)
    )
    return (dest_slot, source_row)


def pack_tokens(token_rows, source_row):
    padded = jnp.concatenate(
        [jnp.zeros((1, token_rows.shape[1]), token_rows.dtype), token_rows], axis=0
    )
    pick_rows = jnp.where(source_row > 0, (source_row - 1) // 2 + 1, 0)
    return padded[pick_rows]


def pack_routes(route_values, source_row):
    padded = jnp.concatenate(
        [jnp.zeros((1, route_values.shape[1]), route_values.dtype), route_values], axis=0
    )
    return padded[source_row]


def adamw(weight, gradient, first_old, second_old, step_rate):
    first_new = BETA_FIRST * first_old + (1.0 - BETA_FIRST) * gradient
    second_new = BETA_SECOND * second_old + (1.0 - BETA_SECOND) * gradient * gradient
    first_hat = first_new / (1.0 - BETA_FIRST**STEP)
    second_hat = second_new / (1.0 - BETA_SECOND**STEP)
    new_weight = weight - step_rate * (
        first_hat / (jnp.sqrt(second_hat) + ADAM_EPS) + DECAY * weight
    )
    return (new_weight, first_new, second_new)


def routed_shards(
    tokens,
    cotangent,
    lengths,
    routes,
    norm_gains,
    gains_first,
    gains_second,
    qkv_weight,
    qkv_first,
    qkv_second,
    out_weight,
    out_first,
    out_second,
    router_weight,
    router_first,
    router_second,
    shared_in,
    shared_in_first,
    shared_in_second,
    shared_down,
    shared_down_first,
    shared_down_second,
    expert_in,
    expert_in_first,
    expert_in_second,
    expert_down,
    expert_down_first,
    expert_down_second,
):
    low_type = jnp.bfloat16
    seq_rows = tokens.shape[0]
    head_total = lax.axis_size(INNER)
    expert_total = lax.axis_size(OUTER)
    head_at = lax.axis_index(INNER)
    cap_dev = 4 * seq_rows // expert_total
    gains_all, qkv_all, out_all, router_all = (
        lax.all_gather(norm_gains.astype(low_type), (OUTER, INNER), axis=1, tiled=True),
        lax.all_gather(qkv_weight.astype(low_type), (OUTER, INNER), axis=0, tiled=True),
        lax.all_gather(out_weight.astype(low_type), (OUTER, INNER), axis=1, tiled=True),
        lax.all_gather(router_weight.astype(low_type), (OUTER, INNER), axis=0, tiled=True),
    )
    shared_in_all, shared_down_all = (
        lax.all_gather(shared_in.astype(low_type), OUTER, axis=0, tiled=True),
        lax.all_gather(shared_down.astype(low_type), OUTER, axis=1, tiled=True),
    )
    shared_in_flat = shared_in_all.reshape(D, -1)
    gain_one = gains_all[0].astype(jnp.float32)
    gain_two = gains_all[1].astype(jnp.float32)
    length = lengths[0]
    inputs = tokens.astype(jnp.float32)
    scaled_one, inverse_one, normed_one = norm_forward(inputs, gain_one)
    normed_low = normed_one.astype(low_type)
    projected = jnp.dot(normed_low, qkv_all, preferred_element_type=jnp.float32).reshape(
        seq_rows, 3, HEADS, HDIM
    )
    cosine_table, sine_table = rope_tables(seq_rows)
    query_rows = rotate(projected[:, 0], cosine_table, sine_table).astype(low_type)
    key_rows = rotate(projected[:, 1], cosine_table, sine_table).astype(low_type)
    value_rows = projected[:, 2].astype(low_type)
    scores, allowed = attention_scores(query_rows, key_rows, length)
    row_top = jnp.max(scores, axis=-1, keepdims=True)
    exponent = jnp.exp(scores - row_top)
    row_total = jnp.sum(exponent, axis=-1, keepdims=True)
    log_total = row_top + jnp.log(row_total)
    attn_probs = exponent / row_total
    context = (
        jnp.einsum(
            "hqk,khd->qhd",
            attn_probs.astype(low_type),
            value_rows,
            preferred_element_type=jnp.float32,
        )
        .reshape(seq_rows, D)
        .astype(low_type)
    )
    middle = inputs + jnp.dot(context, out_all, preferred_element_type=jnp.float32)
    scaled_two, inverse_two, normed_two = norm_forward(middle, gain_two)
    mixer_low = normed_two.astype(low_type)
    logits = jnp.dot(mixer_low, router_all, preferred_element_type=jnp.float32)
    own_routes = lax.dynamic_slice_in_dim(routes, head_at * seq_rows, seq_rows, 0)
    onehot = (
        own_routes[:, :, None] == jnp.arange(router_all.shape[1], dtype=jnp.int32)[None, None, :]
    ).astype(jnp.float32)
    chosen = jnp.sum(logits[:, None, :] * onehot, axis=-1)
    chosen_top = jnp.max(chosen, axis=-1, keepdims=True)
    chosen_exp = jnp.exp(chosen - chosen_top)
    gate_values = chosen_exp / jnp.sum(chosen_exp, axis=-1, keepdims=True)
    gates_low = gate_values.astype(low_type)
    group_rows, group_gates = (
        lax.all_gather(mixer_low, INNER, axis=0, tiled=True),
        lax.all_gather(gates_low, INNER, axis=0, tiled=True),
    )
    shared_mixed, shared_hidden, shared_out = expert_forward(
        group_rows, shared_in_flat, shared_down_all
    )
    dest_slot, source_row = route_tables(routes, head_total, cap_dev, expert_total)
    send_rows = pack_tokens(group_rows, source_row)
    expert_in_low = expert_in.astype(low_type)
    expert_down_low = expert_down.astype(low_type)
    weight_in = expert_in_low[0].reshape(D, -1)
    weight_down = expert_down_low[0]
    received = lax.all_to_all(
        send_rows.reshape(expert_total, -1, D), OUTER, split_axis=0, concat_axis=0, tiled=True
    ).reshape(-1, D)
    expert_mixed, expert_hidden, expert_out = expert_forward(received, weight_in, weight_down)
    returned = (
        lax.all_to_all(
            expert_out.reshape(expert_total, -1, D).astype(jnp.bfloat16),
            OUTER,
            split_axis=0,
            concat_axis=0,
            tiled=True,
        )
        .astype(jnp.float32)
        .reshape(-1, D)
    )
    routed = returned[dest_slot].reshape(-1, 2, D)
    partial_value = shared_out + jnp.sum(
        group_gates.astype(jnp.float32)[:, :, None] * routed, axis=1
    )
    mixed_out = lax.psum_scatter(
        partial_value.astype(jnp.bfloat16), INNER, scatter_dimension=0, tiled=True
    ).astype(jnp.float32)
    live_rows = (jnp.arange(seq_rows, dtype=jnp.int32) < length).astype(jnp.float32)[:, None]
    layer_out = live_rows * (middle + mixed_out)
    grad_live = live_rows * cotangent
    grad_mix_low = grad_live.astype(low_type)
    group_grad = lax.all_gather(grad_mix_low, INNER, axis=0, tiled=True)
    shared_row_grad, shared_grad_in, shared_grad_down = expert_backward(
        group_rows, shared_mixed, shared_hidden, group_grad, shared_in_flat, shared_down_all
    )
    group_grad_f = group_grad.astype(jnp.float32)
    grad_routed = (group_gates.astype(jnp.float32)[:, :, None] * group_grad_f[:, None, :]).astype(
        low_type
    )
    gate_grad_part = jnp.sum(group_grad_f[:, None, :] * routed, axis=-1)
    grad_send = pack_routes(grad_routed.reshape(-1, D), source_row)
    grad_received = lax.all_to_all(
        grad_send.reshape(expert_total, -1, D), OUTER, split_axis=0, concat_axis=0, tiled=True
    ).reshape(-1, D)
    rows_grad, grad_in_local, grad_down_local = expert_backward(
        received, expert_mixed, expert_hidden, grad_received, weight_in, weight_down
    )
    rows_back = lax.all_to_all(
        rows_grad.reshape(expert_total, -1, D), OUTER, split_axis=0, concat_axis=0, tiled=True
    ).reshape(-1, D)
    per_token = jnp.sum(rows_back[dest_slot].reshape(-1, 2, D), axis=1)
    rows_part = shared_row_grad + per_token
    grad_in_slice = grad_in_local.reshape(1, D, 2, -1)
    grad_down_slice = grad_down_local[None]
    grad_rows_own, grad_gates = (
        lax.psum_scatter(rows_part, INNER, scatter_dimension=0, tiled=True),
        lax.psum_scatter(gate_grad_part, INNER, scatter_dimension=0, tiled=True),
    )
    gate_dot = jnp.sum(gate_values * grad_gates, axis=-1, keepdims=True)
    grad_chosen = gate_values * (grad_gates - gate_dot)
    grad_logits = jnp.sum(grad_chosen[:, :, None] * onehot, axis=1).astype(low_type)
    grad_router = jnp.dot(mixer_low.T, grad_logits, preferred_element_type=jnp.float32)
    grad_normed_two = grad_rows_own + jnp.dot(
        grad_logits, router_all.T, preferred_element_type=jnp.float32
    )
    grad_from_norm, grad_gain_two = norm_backward(
        grad_normed_two, scaled_two, inverse_two, gain_two
    )
    grad_middle = grad_live + grad_from_norm
    grad_att_low = grad_middle.astype(low_type)
    grad_out_w = jnp.dot(context.T, grad_att_low, preferred_element_type=jnp.float32)
    grad_context = (
        jnp.dot(grad_att_low, out_all.T, preferred_element_type=jnp.float32)
        .astype(low_type)
        .reshape(seq_rows, HEADS, HDIM)
    )
    scores_again, allowed_again = attention_scores(query_rows, key_rows, length)
    probs_again = jnp.where(allowed_again[None], jnp.exp(scores_again - log_total), 0.0)
    grad_probs = jnp.einsum(
        "qhd,khd->hqk", grad_context, value_rows, preferred_element_type=jnp.float32
    )
    grad_value = jnp.einsum(
        "hqk,qhd->khd",
        probs_again.astype(low_type),
        grad_context,
        preferred_element_type=jnp.float32,
    )
    row_dot = jnp.sum(grad_probs * probs_again, axis=-1, keepdims=True)
    grad_scores = (probs_again * (grad_probs - row_dot)).astype(low_type)
    grad_query = (
        jnp.einsum("hqk,khd->qhd", grad_scores, key_rows, preferred_element_type=jnp.float32)
        * 0.125
    )
    grad_key = (
        jnp.einsum("hqk,qhd->khd", grad_scores, query_rows, preferred_element_type=jnp.float32)
        * 0.125
    )
    grad_projected = (
        jnp.stack(
            [
                unrotate(grad_query, cosine_table, sine_table),
                unrotate(grad_key, cosine_table, sine_table),
                grad_value,
            ],
            axis=1,
        )
        .reshape(seq_rows, 3 * D)
        .astype(low_type)
    )
    grad_qkv = jnp.dot(normed_low.T, grad_projected, preferred_element_type=jnp.float32)
    grad_normed_one = jnp.dot(grad_projected, qkv_all.T, preferred_element_type=jnp.float32)
    grad_input_norm, grad_gain_one = norm_backward(
        grad_normed_one, scaled_one, inverse_one, gain_one
    )
    input_grad = grad_middle + grad_input_norm
    gains_grad = jnp.stack([grad_gain_one, grad_gain_two], axis=0)
    gains_part, qkv_part, out_part, router_part = (
        lax.psum_scatter(gains_grad, (OUTER, INNER), scatter_dimension=1, tiled=True),
        lax.psum_scatter(grad_qkv, (OUTER, INNER), scatter_dimension=0, tiled=True),
        lax.psum_scatter(grad_out_w, (OUTER, INNER), scatter_dimension=1, tiled=True),
        lax.psum_scatter(grad_router, (OUTER, INNER), scatter_dimension=0, tiled=True),
    )
    shared_in_part, shared_down_part = (
        lax.psum_scatter(
            shared_grad_in.reshape(D, 2, -1).astype(jnp.bfloat16),
            OUTER,
            scatter_dimension=0,
            tiled=True,
        ).astype(jnp.float32),
        lax.psum_scatter(
            shared_grad_down.astype(jnp.bfloat16), OUTER, scatter_dimension=1, tiled=True
        ).astype(jnp.float32),
    )
    gains_new, gains_first_new, gains_second_new = adamw(
        norm_gains, gains_part, gains_first, gains_second, 0.5
    )
    qkv_new, qkv_first_new, qkv_second_new = adamw(
        qkv_weight, qkv_part, qkv_first, qkv_second, 1.5 / math.sqrt(D)
    )
    out_new, out_first_new, out_second_new = adamw(
        out_weight, out_part, out_first, out_second, 1.5 / math.sqrt(4 * D // SEQ)
    )
    router_new, router_first_new, router_second_new = adamw(
        router_weight, router_part, router_first, router_second, 1.0 / math.sqrt(D)
    )
    shin_new, shin_first_new, shin_second_new = adamw(
        shared_in, shared_in_part, shared_in_first, shared_in_second, 1.5 / math.sqrt(D)
    )
    shdown_new, shdown_first_new, shdown_second_new = adamw(
        shared_down, shared_down_part, shared_down_first, shared_down_second, 1.5 / math.sqrt(FF_SH)
    )
    exin_new, exin_first_new, exin_second_new = adamw(
        expert_in, grad_in_slice, expert_in_first, expert_in_second, 1.5 / math.sqrt(D)
    )
    exdown_new, exdown_first_new, exdown_second_new = adamw(
        expert_down, grad_down_slice, expert_down_first, expert_down_second, 1.5 / math.sqrt(FF)
    )
    return (
        layer_out,
        input_grad,
        gains_new,
        gains_first_new,
        gains_second_new,
        qkv_new,
        qkv_first_new,
        qkv_second_new,
        out_new,
        out_first_new,
        out_second_new,
        router_new,
        router_first_new,
        router_second_new,
        shin_new,
        shin_first_new,
        shin_second_new,
        shdown_new,
        shdown_first_new,
        shdown_second_new,
        exin_new,
        exin_first_new,
        exin_second_new,
        exdown_new,
        exdown_first_new,
        exdown_second_new,
    )


MESH = pl.DeviceIdType.MESH
VMEM_BYTES = 61 << 20
GROUPS = 4
PLANE = 8
ALL = GROUPS * PLANE
EXTRA = 16
TURN = (1, 3, 2)


def nn(left, right):
    return jnp.dot(left, right, preferred_element_type=jnp.float32)


def nt(left, right):
    return lax.dot_general(
        left, right, (((1,), (1,)), ((), ())), preferred_element_type=jnp.float32
    )


def tn(left, right):
    return lax.dot_general(
        left, right, (((0,), (0,)), ((), ())), preferred_element_type=jnp.float32
    )


def slot_of(group, member):
    return group * PLANE + (member % 2) * (PLANE // 2) + member // 2


class Place:
    def __init__(self):
        self.group = group = lax.axis_index(OUTER)
        self.member = member = lax.axis_index(INNER)
        self.core = core = member % 2
        column, row = (member // 2) % 2, member // 4
        self.chip = group * (PLANE // 2) + member // 2
        side = 1 - 2 * core
        self.twin = member + side
        beside, across = member + 2 - 4 * column, member + 4 - 8 * row
        self.near = beside * (1 - core) + across * core
        self.far = across * (1 - core) + beside * core
        self.corner = member + (2 - 4 * column) + (4 - 8 * row)
        self.near_twin = self.near + side
        self.far_twin = self.far + side
        self.corner_twin = self.corner + side
        self.mine = slot_of(group, member)

    def around(self, step):
        return (self.group + step) % GROUPS

    def others(self):
        near = [(self.group, self.twin), (self.group, self.near), (self.group, self.far)]
        return near + [(self.around(step), self.member) for step in TURN]

    def tell(self, semaphore):
        for other in self.others():
            pl.semaphore_signal(semaphore, inc=1, device_id=other, device_id_type=MESH)

    def hear(self, semaphore):
        pl.semaphore_wait(semaphore, 6)


class Mover:
    def __init__(self, place, send_sem):
        self.place, self.send_sem, self.sizes = place, send_sem, []

    def copy(self, source, target, index, recv, device):
        return pltpu.make_async_remote_copy(
            src_ref=source,
            dst_ref=target,
            send_sem=self.send_sem.at[index],
            recv_sem=recv,
            device_id=device,
            device_id_type=MESH,
        )

    def send(self, source, target, recv, device):
        self.copy(source, target, len(self.sizes), recv, device).start()
        self.sizes.append(source)

    def arrive(self, target, recv):
        self.copy(target, target, 0, recv, (self.place.group, self.place.twin)).wait_recv()

    def drain(self, unit):
        for index in range(len(self.sizes)):
            self.copy(unit, unit, index, self.send_sem.at[index], (self.place.group, self.place.twin)).wait_send()


class Gather(Mover):
    def __init__(self, place, at, send_sem, recv_sem, pair=True):
        super().__init__(place, send_sem)
        self.at, self.recv_sem, self.pair = at, recv_sem, pair

    def forward(self, group, member, partners):
        for partner in partners:
            if partner is self.place.twin and not self.pair:
                continue
            ref = self.at(group, member)
            self.send(ref, ref, self.recv_sem.at[slot_of(group, member)], (self.place.group, partner))

    def wait(self, group, member):
        self.arrive(self.at(group, member), self.recv_sem.at[slot_of(group, member)])

    def start(self):
        place = self.place
        own = self.at(place.group, place.member)
        for step in TURN:
            self.send(own, own, self.recv_sem.at[place.mine], (place.around(step), place.member))
        self.forward(place.group, place.member, (place.near, place.far, place.twin))

    def own_column(self, step):
        place = self.place
        self.wait(place.around(step), place.member)
        self.forward(place.around(step), place.member, (place.near, place.far, place.twin))

    def near_column(self, step):
        place = self.place
        self.wait(place.around(step), place.near)
        self.forward(place.around(step), place.near, (place.far, place.twin))

    def last_column(self, step, member):
        self.wait(self.place.around(step), member)
        self.forward(self.place.around(step), member, (self.place.twin,))

    def twin_column(self, member):
        for step in (0,) + TURN:
            self.wait(self.place.around(step), member)

    def twin_plane(self, step):
        place = self.place
        for member in (place.twin, place.far_twin, place.near_twin, place.corner_twin):
            self.wait(place.around(step), member)

    def last_plane(self, step):
        for member in (self.place.far, self.place.corner):
            self.last_column(step, member)


class Together:
    def __init__(self, *moves):
        self.moves = moves

    def __getattr__(self, name):
        def each(*given):
            for move in self.moves:
                getattr(move, name)(*given)

        return each


class Scatter(Mover):
    def __init__(self, place, part, rows, bufs, send_sem, sems):
        super().__init__(place, send_sem)
        self.part, self.rows = part, rows
        self.twin_buf, self.far_buf, self.near_buf, self.group_buf = bufs
        self.twin_sem, self.far_sem, self.near_sem, self.group_sem = sems

    def view(self, buf, index):
        return buf.at[index, pl.ds(0, self.rows)]

    def add(self, target, others):
        def some(block, carry):
            at = pl.ds(pl.multiple_of(block * 16, 16), 16)
            total = target[at].astype(jnp.float32)
            for other in others:
                total = total + other[at].astype(jnp.float32)
            target[at] = total.astype(target.dtype)
            return carry

        lax.fori_loop(0, self.rows // 16, some, 0)

    def twin_index(self, group, member):
        return (member // 2) * GROUPS + group

    def to_twin(self, group, member):
        index = self.twin_index(group, member)
        self.send(
            self.part(group, member),
            self.view(self.twin_buf, index),
            self.twin_sem.at[index],
            (self.place.group, self.place.twin),
        )

    def from_twin(self, group, member):
        index = self.twin_index(group, member)
        ready = self.view(self.twin_buf, index)
        self.arrive(ready, self.twin_sem.at[index])
        return ready

    def from_far(self, group, spot):
        other = self.view(self.far_buf, spot * GROUPS + group)
        self.arrive(other, self.far_sem.at[spot * GROUPS + group])
        return other

    def outward(self, step):
        for spot, member in ((0, self.place.corner), (1, self.place.far)):
            group = self.place.around(step)
            ready = self.from_twin(group, member)
            self.add(ready, [self.part(group, member)])
            index = spot * GROUPS + group
            self.send(
                ready,
                self.view(self.far_buf, index),
                self.far_sem.at[index],
                (self.place.group, self.place.far),
            )

    def sideways(self, step):
        group, near = self.place.around(step), self.place.near
        ready = self.from_twin(group, near)
        self.add(ready, [self.part(group, near), self.from_far(group, 0)])
        self.send(
            ready,
            self.view(self.near_buf, group),
            self.near_sem.at[group],
            (self.place.group, near),
        )

    def homeward(self, step):
        group, member = self.place.around(step), self.place.member
        ready = self.from_twin(group, member)
        other = self.view(self.near_buf, group)
        far = self.from_far(group, 1)
        self.arrive(other, self.near_sem.at[group])
        self.add(ready, [self.part(group, member), far, other])
        if step:
            self.send(
                ready,
                self.view(self.group_buf, step - 1),
                self.group_sem.at[step - 1],
                (group, member),
            )

    def finish(self, store):
        for step in TURN:
            self.arrive(self.view(self.group_buf, step - 1), self.group_sem.at[step - 1])
        ready = self.view(self.twin_buf, self.twin_index(self.place.group, self.place.member))

        def some(block, carry):
            at = pl.ds(pl.multiple_of(block * 16, 16), 16)
            total = ready[at].astype(jnp.float32)
            for step in TURN:
                total = total + self.view(self.group_buf, step - 1)[at].astype(jnp.float32)
            store(at, total)
            return carry

        lax.fori_loop(0, self.rows // 16, some, 0)


BACKWARD = (1, 3, 2, 0)


def iota(shape, dim):
    return lax.broadcasted_iota(jnp.int32, shape, dim)


def swap_halves(block):
    lane = iota(block.shape, 1)
    return jnp.where(
        lane % HDIM < HDIM // 2, pltpu.roll(block, 128 - HDIM // 2, 1), pltpu.roll(block, HDIM // 2, 1)
    )


def step_kernel(
    length_ref,
    tokens_hbm,
    cotangent_hbm,
    routes_hbm,
    qkv_hbm,
    out_hbm,
    router_hbm,
    gains_hbm,
    shared_in_hbm,
    shared_down_hbm,
    cosine_hbm,
    sine_hbm,
    expert_in_hbm,
    expert_down_hbm,
    layer_out_hbm,
    input_grad_hbm,
    owned_grad_hbm,
    small_grad_hbm,
    grad_in_hbm,
    grad_down_hbm,
    shared_grad_hbm,
    tokens_ref,
    cotangent_ref,
    routes_ref,
    qkv_ref,
    router_ref,
    gains_ref,
    shared_in_ref,
    shared_down_ref,
    cosine_ref,
    sine_ref,
    owned_ref,
    small_ref,
    small_square,
    layer_out_ref,
    input_grad_ref,
    owned_grad_ref,
    small_grad_ref,
    grad_in_ref,
    grad_down_ref,
    shared_grad_ref,
    pieces_ref,
    stage,
    small_stage,
    mats,
    small_all,
    first_all,
    second_all,
    pieces,
    shared_send,
    weight_in,
    weight_down,
    out_all,
    hidden_low,
    mixed_low,
    pre,
    back_hidden,
    queries,
    keys,
    values,
    probs,
    normed_low,
    context,
    middle_ref,
    mixer,
    rows_sum,
    grad_mid,
    grad_context,
    grad_proj,
    gate_keep,
    twin_a,
    far_a,
    near_a,
    group_a,
    twin_b,
    far_b,
    near_b,
    group_b,
    gate_all,
    gate_part,
    small_part,
    gate_sum,
    twin_g,
    far_g,
    near_g,
    group_g,
    twin_s,
    far_s,
    near_s,
    group_s,
    gate_send,
    gate_recv,
    gate_back_send,
    small_back_send,
    pair_send,
    pair_recv,
    local_sem,
    store_sem,
    mats_send,
    mats_recv,
    small_send,
    small_recv,
    cot_send,
    cot_recv,
    mix_send,
    mix_recv,
    piece_send,
    piece_recv,
    rows_send,
    out_send,
    own_send,
    twin_sems,
    far_sems,
    near_sems,
    group_sems,
    free_sem,
):
    low = jnp.bfloat16
    rows = tokens_ref.shape[0]
    fetched = []
    for source, target in (
        (qkv_hbm, qkv_ref),
        (out_hbm, owned_ref.at[3]),
        (router_hbm, router_ref),
        (gains_hbm, gains_ref),
        (cotangent_hbm, cotangent_ref),
        (tokens_hbm, tokens_ref),
        (routes_hbm, routes_ref),
        (cosine_hbm, cosine_ref),
        (sine_hbm, sine_ref),
        (shared_in_hbm.at[:, 0, :], shared_in_ref.at[0]),
        (shared_in_hbm.at[:, 1, :], shared_in_ref.at[1]),
        (shared_down_hbm, shared_down_ref),
        (expert_in_hbm.at[0, :, 0, :], grad_in_ref.at[:, pl.ds(0, 256)]),
        (expert_in_hbm.at[0, :, 1, :], grad_in_ref.at[:, pl.ds(256, 256)]),
        (expert_down_hbm.at[0], grad_down_ref.at[pl.ds(0, 256)]),
    ):
        fetched.append(pltpu.make_async_copy(source, target, local_sem.at[len(fetched)]))
        fetched[-1].start()
    stored = []

    def store_out(source, target):
        copy = pltpu.make_async_copy(source, target, store_sem.at[len(stored)])
        copy.start()
        stored.append(copy)
    place = Place()
    group, member, core = place.group, place.member, place.core
    barrier = pltpu.get_barrier_semaphore()
    place.tell(barrier)
    place.hear(barrier)

    twin_device = (group, place.twin)
    for name in (0, 1, 2, 3):
        fetched[name].wait()
    for part in range(3):
        owned_ref[part] = qkv_ref[:, D * part : D * part + D]
    small_square[...] = jnp.zeros_like(small_square)
    small_square[pl.ds(0, GROUPS), pl.ds(0, 24)] = router_ref[...]
    small_square[pl.ds(GROUPS, 2), pl.ds(0, 24)] = gains_ref[...]
    small_ref[...] = small_square[...].T[:24]
    own_rows = pl.ds(pl.multiple_of(24 * core, 8), 24)
    owned = pltpu.make_async_remote_copy(
        src_ref=owned_ref.at[pl.ds(2 * (1 - core), 2)],
        dst_ref=stage.at[:, own_rows],
        send_sem=pair_send.at[0],
        recv_sem=pair_recv.at[0],
        device_id=twin_device,
        device_id_type=MESH,
    )
    owned.start()
    small_pair = pltpu.make_async_remote_copy(
        src_ref=small_ref,
        dst_ref=small_stage.at[own_rows],
        send_sem=pair_send.at[1],
        recv_sem=pair_recv.at[1],
        device_id=twin_device,
        device_id_type=MESH,
    )
    small_pair.start()
    stage[:, own_rows] = owned_ref[pl.ds(2 * core, 2)]
    small_stage[own_rows] = small_ref[...]
    owned.wait()
    small_pair.wait()

    def mats_at(group, member):
        chip = group * (PLANE // 2) + member // 2
        return mats.at[pl.ds(2 * (member % 2), 2), pl.ds(pl.multiple_of(48 * chip, 16), 48)]

    def small_at(group, member):
        chip = group * (PLANE // 2) + member // 2
        return small_all.at[pl.ds(pl.multiple_of(48 * chip, 16), 48)]

    mats_at(group, member)[...] = stage[...].astype(low)
    small_at(group, member)[...] = small_stage[...].astype(low)
    send_small = Gather(place, small_at, small_send, small_recv, pair=False)
    send_mats = Gather(place, mats_at, mats_send, mats_recv)
    send_small.start()
    send_mats.start()
    length = length_ref[0]
    row_at = iota((rows, 1), 0)
    live = (row_at < length).astype(jnp.float32)
    fetched[4].wait()
    first_all[place.mine] = (cotangent_ref[...] * live).astype(low)

    send_cot = Gather(
        place,
        lambda group, member: first_all.at[slot_of(group, member)],
        cot_send,
        cot_recv,
    )

    def move_piece(source, target, sems, base):
        for step in TURN:
            pltpu.make_async_remote_copy(
                src_ref=source.at[place.around(step)],
                dst_ref=target.at[group],
                send_sem=piece_send.at[base + step - 1],
                recv_sem=piece_recv.at[base + (GROUPS - step) - 1],
                device_id=(place.around(step), member),
                device_id_type=MESH,
            ).start()
        target[group] = source[group]

    def wait_pieces(source, target, base):
        for step in TURN:
            copy = pltpu.make_async_remote_copy(
                src_ref=source.at[place.around(step)],
                dst_ref=target.at[place.around(step)],
                send_sem=piece_send.at[base + step - 1],
                recv_sem=piece_recv.at[base + step - 1],
                device_id=(place.around(step), member),
                device_id_type=MESH,
            )
            copy.wait()

    for step in (0,) + TURN:
        if step:
            send_small.own_column(step)
            send_mats.own_column(step)
        send_small.near_column(step)
        send_mats.near_column(step)
        if step == 0:
            send_cot.start()

    for name in (9, 10, 11):
        fetched[name].wait()
    for piece in range(GROUPS):
        at = pl.ds(64 * piece, 64)
        both_halves = [shared_in_ref[0, :, at], shared_in_ref[1, :, at]]
        pieces_ref[piece, :, pl.ds(0, 128)] = jnp.concatenate(both_halves, axis=1).astype(low)
        last = shared_down_ref[:, at]
        last = jnp.concatenate([last, jnp.zeros_like(last)], axis=1)
        pieces_ref[piece, :, pl.ds(128, 128)] = last.astype(low)
    move_piece(pieces_ref, pieces, piece_send, 0)

    for name in (12, 13, 14):
        fetched[name].wait()
    weight_in[:, pl.ds(0, 512)] = grad_in_ref[:, pl.ds(0, 512)].astype(low)
    weight_down[pl.ds(0, 256)] = grad_down_ref[pl.ds(0, 256)].astype(low)
    grad_down_ref[...] = jnp.zeros_like(grad_down_ref)
    grad_in_ref[...] = jnp.zeros_like(grad_in_ref)

    for step in (0,) + TURN:
        for origin in (place.far, place.corner):
            send_small.wait(place.around(step), origin)
            send_mats.last_column(step, origin)
    for step in TURN:
        send_cot.own_column(step)
    for origin in (place.twin, place.near_twin, place.far_twin, place.corner_twin):
        send_mats.twin_column(origin)

    for name in (5, 6, 7, 8):
        fetched[name].wait()
    inputs = tokens_ref[...].astype(jnp.float32)
    inverse_one = lax.rsqrt(jnp.mean(inputs * inputs, axis=-1, keepdims=True) + NORM_EPS)
    pick = (iota((8, 128), 1) == iota((8, 128), 0) + GROUPS).astype(low)
    gains = nt(pick, small_all[...])
    gain_one, gain_two = gains[0:1], gains[1:2]
    normed_low[...] = (inputs * inverse_one * gain_one).astype(low)
    for part, target in ((0, queries), (1, keys), (2, values)):
        pre[pl.ds(0, rows)] = nn(normed_low[...], mats[part])
        for block in range(D // 128):
            at = pl.ds(128 * block, 128)
            piece = pre[pl.ds(0, rows), at]
            if part < 2:
                piece = piece * cosine_ref[...] + swap_halves(piece) * sine_ref[...]
            target[:, at] = piece.astype(low)
    for step in (0, 1):
        send_cot.near_column(step)
    diagonal = iota((rows, rows), 0) == iota((rows, rows), 1)
    query_at, key_at = iota((rows, rows), 0), iota((rows, rows), 1)
    allowed = (key_at <= query_at) & (key_at < length)
    lower = iota((rows, 128), 1) < HDIM

    def attend(pair, carry):
        at = pl.ds(pl.multiple_of(pair * 128, 128), 128)
        query, key, value = queries[:, at], keys[:, at], values[:, at]
        found = []
        for half in (0, 1):
            own = lower if half == 0 else jnp.logical_not(lower)
            scores = nt(jnp.where(own, query, jnp.zeros_like(query)), key) * 0.125
            scores = jnp.where(allowed, scores, MASKED)
            exponent = jnp.exp(scores - jnp.max(scores, axis=-1, keepdims=True))
            prob = exponent / jnp.sum(exponent, axis=-1, keepdims=True)
            probs[pair * 2 + half] = prob
            found.append(nn(prob.astype(low), value))
        context[:, at] = jnp.where(lower, found[0], found[1]).astype(low)
        for serve in range(2):

            @pl.when(pair == serve)
            def _():
                send_cot.near_column((3, 2)[serve])

        return carry

    lax.fori_loop(0, HEADS // 2, attend, 0)
    middle = inputs + nt(context[...], mats[3])
    middle_ref[...] = middle
    inverse_two = lax.rsqrt(jnp.mean(middle * middle, axis=-1, keepdims=True) + NORM_EPS)
    mixer[...] = (middle * inverse_two * gain_two).astype(low)
    logits = nn(mixer[...], small_all[...])
    lane = iota((rows, 128), 1)
    chosen, hits = [], []
    for choice in (0, 1):
        row = routes_ref[choice : choice + 1, pl.ds(pl.multiple_of(member * rows, rows), rows)]
        picked = jnp.sum(jnp.where(diagonal, row.astype(jnp.float32), 0.0), axis=1, keepdims=True)
        hit = (lane.astype(jnp.float32) == picked).astype(jnp.float32)
        hits.append(hit)
        chosen.append(jnp.sum(logits * hit, axis=-1, keepdims=True))
    top = jnp.maximum(chosen[0], chosen[1])
    exponents = [jnp.exp(value - top) for value in chosen]
    total = exponents[0] + exponents[1]
    gates = [value / total for value in exponents]
    gate_keep[...] = jnp.where(lane == 0, gates[0], jnp.where(lane == 1, gates[1], 0.0))
    table = sum(gate.astype(low).astype(jnp.float32) * hit for gate, hit in zip(gates, hits))
    second_all[place.mine] = mixer[...]
    gate_all[place.mine] = table.T[:EXTRA].astype(low)
    send_rows = Gather(
        place, lambda group, member: second_all.at[slot_of(group, member)], mix_send, mix_recv
    )
    send_gates = Gather(
        place, lambda group, member: gate_all.at[slot_of(group, member)], gate_send, gate_recv
    )
    send_mix = Together(send_gates, send_rows)
    send_mix.start()
    for step in (0,) + TURN:
        for origin in (place.far, place.corner):
            send_cot.last_column(step, origin)
    for origin in (place.twin, place.near_twin, place.far_twin, place.corner_twin):
        send_cot.twin_column(origin)
    send_cot.drain(first_all.at[0])

    wait_pieces(pieces_ref, pieces, 0)
    first_half = iota((192, 128), 1) < 64
    for piece in range(GROUPS):
        at = pl.ds(192 * piece, 192)
        both_halves = pieces[piece, :, pl.ds(0, 128)].astype(jnp.float32)
        weight_in[at, pl.ds(512, 128)] = jnp.where(first_half, both_halves, 0.0).astype(low)
        other = pltpu.roll(both_halves, 64, 1)
        weight_in[at, pl.ds(640, 128)] = jnp.where(first_half, other, 0.0).astype(low)
    turned = pieces[:, :, pl.ds(128, 128)].reshape(D, 128).astype(jnp.float32)
    weight_down[pl.ds(256, 128)] = turned.T.astype(low)
    big_move = Scatter(
        place,
        lambda group, member: first_all.at[slot_of(group, member)],
        rows,
        (twin_a, far_a, near_a, group_a),
        rows_send,
        (twin_sems.at[0], far_sems.at[0], near_sems.at[0], group_sems.at[0]),
    )
    gate_move = Scatter(
        place,
        lambda group, member: gate_part.at[slot_of(group, member)],
        EXTRA,
        (twin_g, far_g, near_g, group_g),
        gate_back_send,
        (twin_sems.at[3], far_sems.at[3], near_sems.at[3], group_sems.at[3]),
    )
    rows_move = Together(gate_move, big_move)
    out_move = Scatter(
        place,
        lambda group, member: out_all.at[slot_of(group, member)],
        rows,
        (twin_b, far_b, near_b, group_b),
        out_send,
        (twin_sems.at[1], far_sems.at[1], near_sems.at[1], group_sems.at[1]),
    )
    own_expert = (iota((EXTRA, 128), 0) == group).astype(low)
    twins = (place.corner_twin, place.near_twin, place.far_twin, place.twin)

    serve_before = (
        lambda: (
            send_mix.own_column(1),
            send_mix.near_column(1),
            send_mix.own_column(3),
            send_mix.last_plane(1),
        ),
        lambda: (send_mix.near_column(3), send_mix.own_column(2), send_mix.twin_plane(1)),
        lambda: (send_mix.near_column(2), send_mix.near_column(0), send_mix.last_plane(3)),
        lambda: (rows_move.outward(1), send_mix.twin_plane(3)),
        lambda: send_mix.last_plane(2),
        lambda: (rows_move.outward(3), rows_move.sideways(1), send_mix.twin_plane(2)),
        lambda: send_mix.last_plane(0),
        lambda: (
            rows_move.outward(2),
            rows_move.sideways(3),
            rows_move.homeward(1),
            send_mix.twin_plane(0),
        ),
    )

    def tokens_part(index, carry):
        for at in range(PLANE):

            @pl.when(index == at)
            def _():
                serve_before[at]()

        half = index // 2
        step = jnp.where(half == 0, 1, jnp.where(half == 1, 3, jnp.where(half == 2, 2, 0)))
        side = (core + index) % 2
        base = pl.multiple_of(place.around(step) * PLANE + side * GROUPS, GROUPS)
        four = pl.ds(base, GROUPS)
        taken = second_all[four].reshape(GROUPS * rows, D)
        pre[...] = nn(taken, weight_in[...])
        cot = first_all[four].reshape(GROUPS * rows, D)
        back_hidden[...] = nt(cot, weight_down[...])

        def units(block, carry):
            slot = base + block
            scale = tn(gate_all[slot], own_expert)
            at = pl.ds(pl.multiple_of(block * rows, rows), rows)
            weigh = jnp.zeros((rows, 128), jnp.float32)
            for gate_at, up_at, hidden_at, routed in (
                (0, 256, 0, True),
                (128, 384, 128, True),
                (512, 640, 256, False),
            ):
                gate_pre = pre[at, pl.ds(gate_at, 128)]
                up_pre = pre[at, pl.ds(up_at, 128)]
                hidden_grad = back_hidden[at, pl.ds(hidden_at, 128)]
                sigmoid_g = 0.5 * jnp.tanh(0.5 * gate_pre) + 0.5
                silu_g = gate_pre * sigmoid_g
                hidden = (silu_g * up_pre).astype(low)
                if routed:
                    wide = hidden.astype(jnp.float32)
                    weigh = weigh + wide * hidden_grad
                    hidden_grad = hidden_grad * scale
                    hidden = (wide * scale).astype(low)
                grad_gate = hidden_grad * up_pre * (sigmoid_g + silu_g * (1.0 - sigmoid_g))
                hidden_low[at, pl.ds(hidden_at, 128)] = hidden
                mixed_low[at, pl.ds(gate_at, 128)] = grad_gate.astype(low)
                mixed_low[at, pl.ds(up_at, 128)] = (hidden_grad * silu_g).astype(low)
            high = weigh.astype(low)
            rest = (weigh - high.astype(jnp.float32)).astype(low)
            gate_part[slot] = nt(own_expert, high) + nt(own_expert, rest)
            return carry

        lax.fori_loop(0, GROUPS, units, 0)
        grad_down_ref[...] += tn(hidden_low[...], cot)
        pre[...] = nt(mixed_low[...], weight_in[...])
        first_all[four] = pre[...].astype(low).reshape(GROUPS, rows, D)
        for at in range(1, PLANE, 2):

            @pl.when(index == at)
            def _():
                for origin in twins:
                    rows_move.to_twin(place.around(BACKWARD[at // 2]), origin)

        taken = second_all[four].reshape(GROUPS * rows, D)
        grad_in_ref[...] += tn(taken, mixed_low[...])
        pre[...] = nn(hidden_low[...], weight_down[...])
        out_all[four] = pre[...].astype(low).reshape(GROUPS, rows, D)
        for at in range(1, PLANE, 2):

            @pl.when(index == at)
            def _():
                for origin in twins:
                    out_move.to_twin(place.around(BACKWARD[at // 2]), origin)

        return carry

    lax.fori_loop(0, PLANE, tokens_part, 0)
    rows_move.outward(0)
    rows_move.sideways(2)
    rows_move.homeward(3)
    rows_move.sideways(0)
    out_move.outward(1)
    rows_move.homeward(2)
    out_move.outward(3)
    rows_move.homeward(0)
    out_move.sideways(1)
    send_rows.drain(second_all.at[0])
    send_gates.drain(gate_all.at[0])

    for piece in range(GROUPS):
        at = pl.ds(192 * piece, 192)
        both_halves = [grad_in_ref[at, pl.ds(512, 64)], grad_in_ref[at, pl.ds(640, 64)]]
        shared_send[piece, :, pl.ds(0, 128)] = jnp.concatenate(both_halves, axis=1).astype(low)
    turned = grad_down_ref[pl.ds(256, 128)].T
    shared_send[:, :, pl.ds(128, 128)] = turned.astype(low).reshape(GROUPS, 192, 128)
    store_out(grad_in_ref.at[:, pl.ds(0, 512)], grad_in_hbm)
    store_out(grad_down_ref.at[pl.ds(0, 256)], grad_down_hbm)

    def keep_rows(at, total):
        rows_sum[at] = total

    def keep_gates(at, total):
        gate_sum[at] = total

    big_move.finish(keep_rows)
    gate_move.finish(keep_gates)
    big_move.drain(first_all.at[0])
    gate_move.drain(gate_part.at[0])
    place.tell(free_sem)
    move_piece(shared_send, shared_grad_ref, piece_send, 3)

    gate_grads = gate_sum[...]
    gate_grads = jnp.concatenate([gate_grads, jnp.zeros((rows - EXTRA, 128), jnp.float32)], axis=0).T
    grad_gates = [jnp.sum(gate_grads * hit, axis=-1, keepdims=True) for hit in hits]
    kept = [
        jnp.sum(jnp.where(lane == choice, gate_keep[...], 0.0), axis=-1, keepdims=True)
        for choice in (0, 1)
    ]
    gate_dot = kept[0] * grad_gates[0] + kept[1] * grad_gates[1]
    grad_logits = sum(
        hit * (gate * (grad - gate_dot)) for hit, gate, grad in zip(hits, kept, grad_gates)
    ).astype(low)
    grad_router = tn(grad_logits, mixer[...])[:8]
    middle = middle_ref[...]
    inverse_two = lax.rsqrt(jnp.mean(middle * middle, axis=-1, keepdims=True) + NORM_EPS)
    scaled_two = middle * inverse_two
    gains = nt(pick, small_all[...])
    gain_one, gain_two = gains[0:1], gains[1:2]
    grad_normed = rows_sum[pl.ds(0, rows)] + nt(grad_logits, small_all[...])
    grad_gain_two = jnp.sum(grad_normed * scaled_two, axis=0, keepdims=True)
    grad_scaled = grad_normed * gain_two
    grad_middle = cotangent_ref[...] * live + inverse_two * (
        grad_scaled - scaled_two * jnp.mean(grad_scaled * scaled_two, axis=-1, keepdims=True)
    )
    grad_mid[...] = grad_middle
    grad_att = grad_middle.astype(low)
    grad_context[...] = nn(grad_att, mats[3]).astype(low)

    mats_move = Scatter(
        place,
        lambda group, member: first_all.at[slot_of(group, member), pl.ds(0, 96)],
        96,
        (twin_a, far_a, near_a, group_a),
        own_send,
        (twin_sems.at[2], far_sems.at[2], near_sems.at[2], group_sems.at[2]),
    )
    small_move = Scatter(
        place,
        lambda group, member: small_part.at[group * (PLANE // 2) + member // 2],
        EXTRA,
        (twin_s, far_s, near_s, group_s),
        small_back_send,
        (twin_sems.at[4], far_sems.at[4], near_sems.at[4], group_sems.at[4]),
    )
    own_move = Together(small_move, mats_move)

    def put_part(which, left, right):
        for half in (0, 1):
            product = tn(left[:, 384 * half : 384 * half + 384], right).astype(low)
            for place_in in range(8):
                chip = half * 8 + place_in
                slot = slot_of(chip // 4, (chip % 4) * 2 + which // 2)
                first_all[slot, pl.ds(48 * (which % 2), 48)] = product[48 * place_in : 48 * place_in + 48]

    put_part(3, grad_att, context[...])

    def attend_back(pair, carry):
        at = pl.ds(pl.multiple_of(pair * 128, 128), 128)
        query, key, value = queries[:, at], keys[:, at], values[:, at]
        grad_ctx = grad_context[:, at]
        grad_query, grad_key, grad_value = [], [], []
        for half in (0, 1):
            own = lower if half == 0 else jnp.logical_not(lower)
            prob = probs[pair * 2 + half]
            grad_prob = nt(jnp.where(own, grad_ctx, jnp.zeros_like(grad_ctx)), value)
            grad_value.append(tn(prob.astype(low), grad_ctx))
            row_dot = jnp.sum(grad_prob * prob, axis=-1, keepdims=True)
            grad_score = (prob * (grad_prob - row_dot)).astype(low)
            grad_query.append(nn(grad_score, key))
            grad_key.append(tn(grad_score, query))
        grad_q = jnp.where(lower, grad_query[0], grad_query[1]) * 0.125
        grad_k = jnp.where(lower, grad_key[0], grad_key[1]) * 0.125
        grad_q = grad_q * cosine_ref[...] - swap_halves(grad_q) * sine_ref[...]
        grad_k = grad_k * cosine_ref[...] - swap_halves(grad_k) * sine_ref[...]
        grad_proj[0, :, at] = grad_q.astype(low)
        grad_proj[1, :, at] = grad_k.astype(low)
        grad_proj[2, :, at] = jnp.where(lower, grad_value[0], grad_value[1]).astype(low)
        serve_pair = (
            lambda: out_move.outward(2),
            lambda: out_move.sideways(3),
            lambda: out_move.outward(0),
            lambda: out_move.homeward(1),
            lambda: out_move.sideways(2),
            lambda: out_move.homeward(3),
        )
        for at_pair, serve in enumerate(serve_pair):

            @pl.when(pair == at_pair)
            def _():
                serve()

        return carry

    lax.fori_loop(0, HEADS // 2, attend_back, 0)
    grad_one = nt(grad_proj[0], mats[0]) + nt(grad_proj[1], mats[1]) + nt(grad_proj[2], mats[2])
    inputs = tokens_ref[...].astype(jnp.float32)
    inverse_one = lax.rsqrt(jnp.mean(inputs * inputs, axis=-1, keepdims=True) + NORM_EPS)
    scaled_one = inputs * inverse_one
    grad_gain_one = jnp.sum(grad_one * scaled_one, axis=0, keepdims=True)
    grad_scaled = grad_one * gain_one
    input_grad_ref[...] = grad_mid[...] + inverse_one * (
        grad_scaled - scaled_one * jnp.mean(grad_scaled * scaled_one, axis=-1, keepdims=True)
    )
    store_out(input_grad_ref, input_grad_hbm)
    for which in range(3):
        put_part(which, normed_low[...], grad_proj[which])
    at_row = iota((8, D), 0)
    small_rows = jnp.where(
        at_row < GROUPS, grad_router, jnp.where(at_row == GROUPS, grad_gain_one, grad_gain_two)
    )
    small_part[...] = jnp.zeros_like(small_part)
    for chip in range(ALL // 2):
        turned = pltpu.roll(small_rows, (D - 48 * chip) % D, 1) if chip else small_rows
        small_part[chip, pl.ds(0, 8)] = turned[:, :128]
    place.hear(free_sem)
    for step in BACKWARD:
        for origin in (place.corner_twin, place.near_twin, place.far_twin, place.twin):
            own_move.to_twin(place.around(step), origin)
    for act, step in (
        (out_move.sideways, 0),
        (own_move.outward, 1),
        (own_move.outward, 3),
        (out_move.homeward, 2),
        (own_move.sideways, 1),
        (own_move.outward, 2),
        (own_move.sideways, 3),
        (own_move.homeward, 1),
        (own_move.outward, 0),
        (out_move.homeward, 0),
        (own_move.sideways, 2),
        (own_move.homeward, 3),
        (own_move.sideways, 0),
        (own_move.homeward, 2),
        (own_move.homeward, 0),
    ):
        act(step)

    def keep_out(at, total):
        here = pl.ds(at.start, 16)
        live_here = (iota((16, 1), 0) + at.start < length).astype(jnp.float32)
        layer_out_ref[here] = live_here * (middle_ref[here] + total)

    out_move.finish(keep_out)
    store_out(layer_out_ref, layer_out_hbm)
    wait_pieces(shared_send, shared_grad_ref, 3)
    store_out(shared_grad_ref, shared_grad_hbm)

    def keep_own(at, total):
        rows_sum[at] = total

    def keep_small(at, total):
        gate_sum[at] = total

    mats_move.finish(keep_own)
    small_move.finish(keep_small)
    for matrix in (0, 1):
        stage[matrix] = rows_sum[pl.ds(48 * matrix, 48)]
    theirs = pl.ds(pl.multiple_of(24 * (1 - core), 8), 24)
    mine = pl.ds(2 * core, 2)
    last = pltpu.make_async_remote_copy(
        src_ref=stage.at[:, theirs],
        dst_ref=owned_grad_ref.at[mine],
        send_sem=pair_send.at[2],
        recv_sem=pair_recv.at[2],
        device_id=twin_device,
        device_id_type=MESH,
    )
    last.start()
    owned_grad_ref[mine] = stage[:, own_rows]
    block = gate_sum[pl.ds(0, 8)]
    small_grad_ref[...] = jnp.where(core == 0, block, pltpu.roll(block, 128 - 24, 1))
    store_out(small_grad_ref, small_grad_hbm)
    last.wait()
    store_out(owned_grad_ref, owned_grad_hbm)
    out_move.drain(out_all.at[0])
    mats_move.drain(first_all.at[0, pl.ds(0, 96)])
    small_move.drain(small_part.at[0])
    send_mats.drain(mats_at(group, member))
    send_small.drain(small_at(group, member))
    for copy in stored:
        copy.wait()


def update_kernel(*refs):
    (
        owned_grad,
        small_grad,
        grad_in,
        grad_down,
        shared_grad,
        layer_in,
        input_in,
    ) = refs[:7]
    olds = [refs[7 + 3 * at : 10 + 3 * at] for at in range(8)]
    layer_out, input_out = refs[31:33]
    news = [refs[33 + 3 * at : 36 + 3 * at] for at in range(8)]
    owned_buf, small_buf, in_buf, down_buf, shared_buf, layer_buf, input_buf = refs[57:64]
    bufs, load_sem, store_sem = refs[64:-2], refs[-2], refs[-1]
    counts = [0, 0]

    def copy(source, target, which):
        made = pltpu.make_async_copy(source, target, (load_sem, store_sem)[which].at[counts[which]])
        counts[which] += 1
        made.start()
        return made

    half = D // 2
    jobs = []
    for at in range(2):
        for block in range(2):
            jobs.append((6, lambda ref, at=at, block=block: ref.at[0, pl.ds(half * block, half), at, :], (half, 256)))
    jobs.append((7, lambda ref: ref.at[0], (256, D)))
    for at in range(2):
        jobs.append((4, lambda ref, at=at: ref.at[:, at, :], (192, 256)))
    for which in (5, 1, 2, 3, 0):
        jobs.append((which, lambda ref: ref, None))
    passes, loaded = [], []
    through = [copy(layer_in, layer_buf, 0), copy(input_in, input_buf, 0)]
    first_grads = [copy(grad_in, in_buf, 0), copy(grad_down, down_buf, 0)]
    other_grads = [copy(shared_grad, shared_buf, 0), copy(owned_grad, owned_buf, 0), copy(small_grad, small_buf, 0)]
    for at, (which, view, _) in enumerate(jobs):
        loaded.append([copy(view(olds[which][k]), bufs[3 * at + k], 0) for k in range(3)])
    for made in first_grads + through:
        made.wait()
    passes += [copy(layer_buf, layer_out, 1), copy(input_buf, input_out, 1)]
    rates = (
        0.5,
        1.5 / math.sqrt(D),
        1.5 / math.sqrt(4 * D // SEQ),
        1.0 / math.sqrt(D),
        1.5 / math.sqrt(D),
        1.5 / math.sqrt(FF_SH),
        1.5 / math.sqrt(D),
        1.5 / math.sqrt(FF),
    )

    def pair_up(part, swap_first, swap_second):
        left = iota((192, 128), 1) < 64
        tiles = []
        for tile in range(2):
            pair = [
                shared_buf[2 * tile + k, :, pl.ds(128 * part, 128)].astype(jnp.float32) for k in (0, 1)
            ]
            if swap_first:
                pair[0] = pltpu.roll(pair[0], 64, 1)
            if swap_second:
                pair[1] = pltpu.roll(pair[1], 64, 1)
            tiles.append(jnp.where(left, pair[0], pair[1]))
        return jnp.concatenate(tiles, axis=1)

    for at, (which, view, shape) in enumerate(jobs):
        if at == 5:
            for made in other_grads:
                made.wait()
        for made in loaded[at]:
            made.wait()
        mine = bufs[3 * at : 3 * at + 3]
        rate = rates[which]

        def update(index, gradient):
            weight, first_old, second_old = (ref[index] for ref in mine)
            results = adamw(weight, gradient, first_old, second_old, rate)
            for ref, value in zip(mine, results):
                ref[index] = value

        if which == 6:
            part, block = at // 2, at % 2

            def chunk(number, carry):
                here = pl.ds(pl.multiple_of(number * 32, 32), 32)
                there = pl.ds(pl.multiple_of(half * block + number * 32, 32), 32)
                update(here, in_buf[there, pl.ds(256 * part, 256)])
                return carry

            lax.fori_loop(0, half // 32, chunk, 0)
        elif which == 7:

            def chunk(number, carry):
                here = pl.ds(pl.multiple_of(number * 8, 8), 8)
                update(here, down_buf[here])
                return carry

            lax.fori_loop(0, 32, chunk, 0)
        elif which == 4:
            update(..., pair_up(0, at == 6, at == 5))
        elif which == 5:
            update(..., pair_up(1, False, True))
        elif which == 1:
            for part in range(3):
                update((slice(None), pl.ds(D * part, D)), owned_buf[part])
        elif which == 2:
            update(..., owned_buf[3])
        elif which == 3:
            update(..., small_buf[:4, :24])
        else:
            update(..., small_buf[4:6, :24])
        for k in range(3):
            passes.append(copy(mine[k], view(news[which][k]), 1))
    for made in passes:
        made.wait()


def dense_shards(
    tokens,
    cotangent,
    lengths,
    routes,
    norm_gains,
    gains_first,
    gains_second,
    qkv_weight,
    qkv_first,
    qkv_second,
    out_weight,
    out_first,
    out_second,
    router_weight,
    router_first,
    router_second,
    shared_in,
    shared_in_first,
    shared_in_second,
    shared_down,
    shared_down_first,
    shared_down_second,
    expert_in,
    expert_in_first,
    expert_in_second,
    expert_down,
    expert_down_first,
    expert_down_second,
):
    low_type = jnp.bfloat16
    seq_rows = tokens.shape[0]
    per_device = D // ALL
    half_dim = HDIM // 2
    positions = np.arange(seq_rows, dtype=np.float32)[:, None]
    angles = positions * np.tile(ROPE_BASE ** (-np.arange(half_dim) / half_dim), 4)[None]
    sign = np.tile(np.repeat([-1.0, 1.0], half_dim), 2)[None]
    cosine = jnp.asarray(np.cos(angles), jnp.float32)
    sine = jnp.asarray(np.sin(angles) * sign, jnp.float32)
    wide, f32, i32 = low_type, jnp.float32, jnp.int32
    dma = pltpu.SemaphoreType.DMA
    anywhere = pl.BlockSpec(memory_space=pltpu.HBM)
    passed = pl.pallas_call(
        step_kernel,
        out_shape=(
            jax.ShapeDtypeStruct((seq_rows, D), f32),
            jax.ShapeDtypeStruct((seq_rows, D), f32),
            jax.ShapeDtypeStruct((4, per_device, D), f32),
            jax.ShapeDtypeStruct((8, 128), f32),
            jax.ShapeDtypeStruct((D, 512), f32),
            jax.ShapeDtypeStruct((256, D), f32),
            jax.ShapeDtypeStruct((GROUPS, 192, 256), wide),
        ),
        in_specs=[pl.BlockSpec(memory_space=pltpu.SMEM)] + [anywhere] * 13,
        out_specs=(anywhere,) * 7,
        scratch_shapes=[
            pltpu.VMEM((seq_rows, D), wide),
            pltpu.VMEM((seq_rows, D), f32),
            pltpu.VMEM((2, PLANE * seq_rows), i32),
            pltpu.VMEM((per_device, 3 * D), f32),
            pltpu.VMEM((GROUPS, per_device), f32),
            pltpu.VMEM((2, per_device), f32),
            pltpu.VMEM((2, 192, 256), f32),
            pltpu.VMEM((192, 256), f32),
            pltpu.VMEM((seq_rows, 128), f32),
            pltpu.VMEM((seq_rows, 128), f32),
            pltpu.VMEM((4, per_device, D), f32),
            pltpu.VMEM((per_device, 128), f32),
            pltpu.VMEM((128, 128), f32),
            pltpu.VMEM((seq_rows, D), f32),
            pltpu.VMEM((seq_rows, D), f32),
            pltpu.VMEM((4, per_device, D), f32),
            pltpu.VMEM((8, 128), f32),
            pltpu.VMEM((D, 768), f32),
            pltpu.VMEM((384, D), f32),
            pltpu.VMEM((GROUPS, 192, 256), wide),
            pltpu.VMEM((GROUPS, 192, 256), wide),
            pltpu.VMEM((2, 48, D), f32),
            pltpu.VMEM((48, 128), f32),
            pltpu.VMEM((4, D, D), wide),
            pltpu.VMEM((D, 128), wide),
            pltpu.VMEM((ALL, seq_rows, D), wide),
            pltpu.VMEM((ALL, seq_rows, D), wide),
            pltpu.VMEM((GROUPS, 192, 256), wide),
            pltpu.VMEM((GROUPS, 192, 256), wide),
            pltpu.VMEM((D, 768), wide),
            pltpu.VMEM((384, D), wide),
            pltpu.VMEM((ALL, seq_rows, D), wide),
            pltpu.VMEM((GROUPS * seq_rows, 384), wide),
            pltpu.VMEM((GROUPS * seq_rows, 768), wide),
            pltpu.VMEM((GROUPS * seq_rows, 768), f32),
            pltpu.VMEM((GROUPS * seq_rows, 384), f32),
            pltpu.VMEM((seq_rows, D), wide),
            pltpu.VMEM((seq_rows, D), wide),
            pltpu.VMEM((seq_rows, D), wide),
            pltpu.VMEM((HEADS, seq_rows, seq_rows), f32),
            pltpu.VMEM((seq_rows, D), wide),
            pltpu.VMEM((seq_rows, D), wide),
            pltpu.VMEM((seq_rows, D), f32),
            pltpu.VMEM((seq_rows, D), wide),
            pltpu.VMEM((seq_rows, D), f32),
            pltpu.VMEM((seq_rows, D), f32),
            pltpu.VMEM((seq_rows, D), wide),
            pltpu.VMEM((3, seq_rows, D), wide),
            pltpu.VMEM((seq_rows, 128), f32),
            pltpu.VMEM((16, seq_rows, D), wide),
            pltpu.VMEM((8, seq_rows, D), wide),
            pltpu.VMEM((4, seq_rows, D), wide),
            pltpu.VMEM((3, seq_rows, D), wide),
            pltpu.VMEM((16, seq_rows, D), wide),
            pltpu.VMEM((8, seq_rows, D), wide),
            pltpu.VMEM((4, seq_rows, D), wide),
            pltpu.VMEM((3, seq_rows, D), wide),
            pltpu.VMEM((ALL, EXTRA, 128), wide),
            pltpu.VMEM((ALL, EXTRA, 128), f32),
            pltpu.VMEM((ALL // 2, EXTRA, 128), f32),
            pltpu.VMEM((EXTRA, 128), f32),
        ]
        + [pltpu.VMEM((count, EXTRA, 128), f32) for count in (16, 8, 4, 3) * 2]
        + [
            dma((31,)),
            dma((32,)),
            dma((31,)),
            dma((31,)),
            dma((3,)),
            dma((3,)),
            dma((15,)),
            dma((7,)),
            dma((31,)),
            dma((32,)),
            dma((31,)),
            dma((32,)),
            dma((31,)),
            dma((32,)),
            dma((31,)),
            dma((32,)),
            dma((6,)),
            dma((6,)),
            dma((31,)),
            dma((31,)),
            dma((31,)),
            dma((5, 16)),
            dma((5, 8)),
            dma((5, 4)),
            dma((5, 3)),
            pltpu.SemaphoreType.REGULAR,
        ],
        compiler_params=pltpu.CompilerParams(
            collective_id=0, has_side_effects=True, vmem_limit_bytes=VMEM_BYTES
        ),
    )(
        lengths,
        tokens,
        cotangent,
        routes.T,
        qkv_weight,
        out_weight.T,
        router_weight.T,
        norm_gains,
        shared_in,
        shared_down.T,
        cosine,
        sine,
        expert_in,
        expert_down,
    )
    layer_out, input_grad, owned_grad, small_grad, grad_in, grad_down, shared_grad = passed
    olds = [
        (norm_gains, gains_first, gains_second),
        (qkv_weight, qkv_first, qkv_second),
        (out_weight.T, out_first.T, out_second.T),
        (router_weight.T, router_first.T, router_second.T),
        (shared_in, shared_in_first, shared_in_second),
        (shared_down.T, shared_down_first.T, shared_down_second.T),
        (expert_in, expert_in_first, expert_in_second),
        (expert_down, expert_down_first, expert_down_second),
    ]
    flat = [old for three in olds for old in three]
    gradients = (owned_grad, small_grad, grad_in, grad_down, shared_grad)
    shapes = [(D // 2, 256)] * 4 + [(256, D)] + [(192, 256)] * 2 + [(192, 256)]
    shapes += [(per_device, 3 * D), (per_device, D), (GROUPS, per_device), (2, per_device)]
    results = pl.pallas_call(
        update_kernel,
        out_shape=tuple(
            jax.ShapeDtypeStruct(value.shape, value.dtype) for value in [layer_out, input_grad] + flat
        ),
        in_specs=[anywhere] * 31,
        out_specs=(anywhere,) * 26,
        scratch_shapes=[pltpu.VMEM(value.shape, value.dtype) for value in gradients + (layer_out, input_grad)]
        + [pltpu.VMEM(shape, f32) for shape in shapes for _ in range(3)]
        + [dma((43,)), dma((38,))],
        compiler_params=pltpu.CompilerParams(vmem_limit_bytes=VMEM_BYTES),
    )(*gradients, layer_out, input_grad, *flat)
    results = list(results)
    for at in (2 + 6, 2 + 9, 2 + 15):
        for k in range(3):
            results[at + k] = results[at + k].T
    return tuple(results)


def solution(mesh):
    outer, inner = OUTER, INNER
    rows, lanes = P((outer, inner), None), P(None, (outer, inner))
    shared_in, shared_down = P(outer, None, inner), P(inner, outer)
    expert_in, expert_down = P(outer, None, None, inner), P(outer, inner, None)
    placed = (
        rows,
        rows,
        P((outer, inner)),
        P(outer, None),
        lanes,
        lanes,
        lanes,
        rows,
        rows,
        rows,
        lanes,
        lanes,
        lanes,
        rows,
        rows,
        rows,
        shared_in,
        shared_in,
        shared_in,
        shared_down,
        shared_down,
        shared_down,
        expert_in,
        expert_in,
        expert_in,
        expert_down,
        expert_down,
        expert_down,
    )
    return jax.shard_map(
        dense_shards if (mesh.shape[outer], mesh.shape[inner]) == (4, 8) else routed_shards,
        mesh=mesh,
        in_specs=placed,
        out_specs=(
            rows,
            rows,
            lanes,
            lanes,
            lanes,
            rows,
            rows,
            rows,
            lanes,
            lanes,
            lanes,
            rows,
            rows,
            rows,
            shared_in,
            shared_in,
            shared_in,
            shared_down,
            shared_down,
            shared_down,
            expert_in,
            expert_in,
            expert_in,
            expert_down,
            expert_down,
            expert_down,
        ),
        check_vma=False,
    )
```

```python
import math

import jax
import jax.numpy as jnp
import numpy as np
from jax import lax
from jax.experimental import pallas as pl
from jax.experimental.pallas import tpu as pltpu
from jax.sharding import PartitionSpec as P

D = 768
HEADS = 12
HDIM = 64
FF = 2048
FF_SH = 2048
SEQ = 128
STEP = 4


OUTER, INNER = "expert", "head"
NORM_EPS = 1e-06
BETA_FIRST = 0.5
BETA_SECOND = 0.5
ADAM_EPS = 1e-08
DECAY = 0.1
MASKED = -1e30
ROPE_BASE = 10000.0


def rope_tables(row_count):
    half_dim = HDIM // 2
    positions = jnp.arange(row_count, dtype=jnp.float32)
    frequency = ROPE_BASE ** (-jnp.arange(half_dim, dtype=jnp.float32) / half_dim)
    angles = positions[:, None] * frequency[None, :]
    return (jnp.cos(angles)[:, None, :], jnp.sin(angles)[:, None, :])


def rotate(values, cosine_table, sine_table):
    half_dim = values.shape[-1] // 2
    first_half = values[..., :half_dim]
    second_half = values[..., half_dim:]
    return jnp.concatenate(
        [
            first_half * cosine_table - second_half * sine_table,
            second_half * cosine_table + first_half * sine_table,
        ],
        axis=-1,
    )


def unrotate(gradient, cosine_table, sine_table):
    half_dim = gradient.shape[-1] // 2
    first_half = gradient[..., :half_dim]
    second_half = gradient[..., half_dim:]
    return jnp.concatenate(
        [
            first_half * cosine_table + second_half * sine_table,
            second_half * cosine_table - first_half * sine_table,
        ],
        axis=-1,
    )


def norm_forward(values, gain_vec):
    inverse = lax.rsqrt(jnp.mean(values * values, axis=-1, keepdims=True) + NORM_EPS)
    scaled = values * inverse
    return (scaled, inverse, scaled * gain_vec)


def norm_backward(grad_out, scaled, inverse, gain_vec):
    grad_scaled = grad_out * gain_vec
    grad_gain = jnp.sum(grad_out * scaled, axis=0)
    grad_in = inverse * (
        grad_scaled - scaled * jnp.mean(grad_scaled * scaled, axis=-1, keepdims=True)
    )
    return (grad_in, grad_gain)


def attention_scores(query_rows, key_rows, length):
    row_count = query_rows.shape[0]
    scores = (
        jnp.einsum("qhd,khd->hqk", query_rows, key_rows, preferred_element_type=jnp.float32) * 0.125
    )
    positions = jnp.arange(row_count, dtype=jnp.int32)
    allowed = (positions[None, :] <= positions[:, None]) & (positions[None, :] < length)
    return (jnp.where(allowed[None], scores, MASKED), allowed)


def expert_forward(row_block, weight_in, weight_down):
    mixed_pre = jnp.dot(row_block, weight_in, preferred_element_type=jnp.float32)
    hidden_width = weight_down.shape[0]
    gate_pre = mixed_pre[:, :hidden_width]
    up_pre = mixed_pre[:, hidden_width:]
    hidden = (gate_pre * jax.nn.sigmoid(gate_pre) * up_pre).astype(jnp.bfloat16)
    return (mixed_pre, hidden, jnp.dot(hidden, weight_down, preferred_element_type=jnp.float32))


def expert_backward(row_block, mixed_pre, hidden, grad_out, weight_in, weight_down):
    hidden_width = weight_down.shape[0]
    gate_pre = mixed_pre[:, :hidden_width]
    up_pre = mixed_pre[:, hidden_width:]
    grad_hidden = jnp.dot(grad_out, weight_down.T, preferred_element_type=jnp.float32)
    sigmoid_g = jax.nn.sigmoid(gate_pre)
    silu_g = gate_pre * sigmoid_g
    grad_gate = (grad_hidden * up_pre * sigmoid_g * (1.0 + gate_pre * (1.0 - sigmoid_g))).astype(
        jnp.bfloat16
    )
    grad_up = (grad_hidden * silu_g).astype(jnp.bfloat16)
    grad_mixed = jnp.concatenate([grad_gate, grad_up], axis=1)
    grad_down = jnp.dot(hidden.T, grad_out, preferred_element_type=jnp.float32)
    grad_weight_in = jnp.dot(row_block.T, grad_mixed, preferred_element_type=jnp.float32)
    grad_row_block = jnp.dot(grad_mixed, weight_in.T, preferred_element_type=jnp.float32)
    return (grad_row_block, grad_weight_in, grad_down)


def route_tables(route_rows, blocks, block_cap, expert_total):
    per_block = route_rows.reshape(blocks, -1)
    hit_table = (
        per_block[:, :, None] == jnp.arange(expert_total, dtype=jnp.int32)[None, None, :]
    ).astype(jnp.int32)
    entries = per_block.shape[1]
    earlier = jnp.tril(jnp.ones((entries, entries), jnp.bfloat16))
    running = jnp.einsum(
        "ij,bje->bie", earlier, hit_table.astype(jnp.bfloat16), preferred_element_type=jnp.float32
    ).astype(jnp.int32)
    rank_in = jnp.sum((running - 1) * hit_table, axis=2)
    offsets = jnp.arange(blocks, dtype=jnp.int32)[:, None] * block_cap
    dest_slot = (per_block * (blocks * block_cap) + offsets + rank_in).reshape(-1)
    source_row = (
        jnp.zeros((expert_total * blocks * block_cap,), jnp.int32)
        .at[dest_slot]
        .set(jnp.arange(dest_slot.shape[0], dtype=jnp.int32) + 1)
    )
    return (dest_slot, source_row)


def pack_tokens(token_rows, source_row):
    padded = jnp.concatenate(
        [jnp.zeros((1, token_rows.shape[1]), token_rows.dtype), token_rows], axis=0
    )
    pick_rows = jnp.where(source_row > 0, (source_row - 1) // 2 + 1, 0)
    return padded[pick_rows]


def pack_routes(route_values, source_row):
    padded = jnp.concatenate(
        [jnp.zeros((1, route_values.shape[1]), route_values.dtype), route_values], axis=0
    )
    return padded[source_row]


def adamw(weight, gradient, first_old, second_old, step_rate):
    first_new = BETA_FIRST * first_old + (1.0 - BETA_FIRST) * gradient
    second_new = BETA_SECOND * second_old + (1.0 - BETA_SECOND) * gradient * gradient
    first_hat = first_new / (1.0 - BETA_FIRST**STEP)
    second_hat = second_new / (1.0 - BETA_SECOND**STEP)
    new_weight = weight - step_rate * (
        first_hat / (jnp.sqrt(second_hat) + ADAM_EPS) + DECAY * weight
    )
    return (new_weight, first_new, second_new)


def routed_shards(
    tokens,
    cotangent,
    lengths,
    routes,
    norm_gains,
    gains_first,
    gains_second,
    qkv_weight,
    qkv_first,
    qkv_second,
    out_weight,
    out_first,
    out_second,
    router_weight,
    router_first,
    router_second,
    shared_in,
    shared_in_first,
    shared_in_second,
    shared_down,
    shared_down_first,
    shared_down_second,
    expert_in,
    expert_in_first,
    expert_in_second,
    expert_down,
    expert_down_first,
    expert_down_second,
):
    low_type = jnp.bfloat16
    seq_rows = tokens.shape[0]
    head_total = lax.axis_size(INNER)
    expert_total = lax.axis_size(OUTER)
    head_at = lax.axis_index(INNER)
    cap_dev = 4 * seq_rows // expert_total
    gains_all, qkv_all, out_all, router_all = (
        lax.all_gather(norm_gains.astype(low_type), (OUTER, INNER), axis=1, tiled=True),
        lax.all_gather(qkv_weight.astype(low_type), (OUTER, INNER), axis=0, tiled=True),
        lax.all_gather(out_weight.astype(low_type), (OUTER, INNER), axis=1, tiled=True),
        lax.all_gather(router_weight.astype(low_type), (OUTER, INNER), axis=0, tiled=True),
    )
    shared_in_all, shared_down_all = (
        lax.all_gather(shared_in.astype(low_type), OUTER, axis=0, tiled=True),
        lax.all_gather(shared_down.astype(low_type), OUTER, axis=1, tiled=True),
    )
    shared_in_flat = shared_in_all.reshape(D, -1)
    gain_one = gains_all[0].astype(jnp.float32)
    gain_two = gains_all[1].astype(jnp.float32)
    length = lengths[0]
    inputs = tokens.astype(jnp.float32)
    scaled_one, inverse_one, normed_one = norm_forward(inputs, gain_one)
    normed_low = normed_one.astype(low_type)
    projected = jnp.dot(normed_low, qkv_all, preferred_element_type=jnp.float32).reshape(
        seq_rows, 3, HEADS, HDIM
    )
    cosine_table, sine_table = rope_tables(seq_rows)
    query_rows = rotate(projected[:, 0], cosine_table, sine_table).astype(low_type)
    key_rows = rotate(projected[:, 1], cosine_table, sine_table).astype(low_type)
    value_rows = projected[:, 2].astype(low_type)
    scores, allowed = attention_scores(query_rows, key_rows, length)
    row_top = jnp.max(scores, axis=-1, keepdims=True)
    exponent = jnp.exp(scores - row_top)
    row_total = jnp.sum(exponent, axis=-1, keepdims=True)
    log_total = row_top + jnp.log(row_total)
    attn_probs = exponent / row_total
    context = (
        jnp.einsum(
            "hqk,khd->qhd",
            attn_probs.astype(low_type),
            value_rows,
            preferred_element_type=jnp.float32,
        )
        .reshape(seq_rows, D)
        .astype(low_type)
    )
    middle = inputs + jnp.dot(context, out_all, preferred_element_type=jnp.float32)
    scaled_two, inverse_two, normed_two = norm_forward(middle, gain_two)
    mixer_low = normed_two.astype(low_type)
    logits = jnp.dot(mixer_low, router_all, preferred_element_type=jnp.float32)
    own_routes = lax.dynamic_slice_in_dim(routes, head_at * seq_rows, seq_rows, 0)
    onehot = (
        own_routes[:, :, None] == jnp.arange(router_all.shape[1], dtype=jnp.int32)[None, None, :]
    ).astype(jnp.float32)
    chosen = jnp.sum(logits[:, None, :] * onehot, axis=-1)
    chosen_top = jnp.max(chosen, axis=-1, keepdims=True)
    chosen_exp = jnp.exp(chosen - chosen_top)
    gate_values = chosen_exp / jnp.sum(chosen_exp, axis=-1, keepdims=True)
    gates_low = gate_values.astype(low_type)
    group_rows, group_gates = (
        lax.all_gather(mixer_low, INNER, axis=0, tiled=True),
        lax.all_gather(gates_low, INNER, axis=0, tiled=True),
    )
    shared_mixed, shared_hidden, shared_out = expert_forward(
        group_rows, shared_in_flat, shared_down_all
    )
    dest_slot, source_row = route_tables(routes, head_total, cap_dev, expert_total)
    send_rows = pack_tokens(group_rows, source_row)
    expert_in_low = expert_in.astype(low_type)
    expert_down_low = expert_down.astype(low_type)
    weight_in = expert_in_low[0].reshape(D, -1)
    weight_down = expert_down_low[0]
    received = lax.all_to_all(
        send_rows.reshape(expert_total, -1, D), OUTER, split_axis=0, concat_axis=0, tiled=True
    ).reshape(-1, D)
    expert_mixed, expert_hidden, expert_out = expert_forward(received, weight_in, weight_down)
    returned = (
        lax.all_to_all(
            expert_out.reshape(expert_total, -1, D).astype(jnp.bfloat16),
            OUTER,
            split_axis=0,
            concat_axis=0,
            tiled=True,
        )
        .astype(jnp.float32)
        .reshape(-1, D)
    )
    routed = returned[dest_slot].reshape(-1, 2, D)
    partial_value = shared_out + jnp.sum(
        group_gates.astype(jnp.float32)[:, :, None] * routed, axis=1
    )
    mixed_out = lax.psum_scatter(
        partial_value.astype(jnp.bfloat16), INNER, scatter_dimension=0, tiled=True
    ).astype(jnp.float32)
    live_rows = (jnp.arange(seq_rows, dtype=jnp.int32) < length).astype(jnp.float32)[:, None]
    layer_out = live_rows * (middle + mixed_out)
    grad_live = live_rows * cotangent
    grad_mix_low = grad_live.astype(low_type)
    group_grad = lax.all_gather(grad_mix_low, INNER, axis=0, tiled=True)
    shared_row_grad, shared_grad_in, shared_grad_down = expert_backward(
        group_rows, shared_mixed, shared_hidden, group_grad, shared_in_flat, shared_down_all
    )
    group_grad_f = group_grad.astype(jnp.float32)
    grad_routed = (group_gates.astype(jnp.float32)[:, :, None] * group_grad_f[:, None, :]).astype(
        low_type
    )
    gate_grad_part = jnp.sum(group_grad_f[:, None, :] * routed, axis=-1)
    grad_send = pack_routes(grad_routed.reshape(-1, D), source_row)
    grad_received = lax.all_to_all(
        grad_send.reshape(expert_total, -1, D), OUTER, split_axis=0, concat_axis=0, tiled=True
    ).reshape(-1, D)
    rows_grad, grad_in_local, grad_down_local = expert_backward(
        received, expert_mixed, expert_hidden, grad_received, weight_in, weight_down
    )
    rows_back = lax.all_to_all(
        rows_grad.reshape(expert_total, -1, D), OUTER, split_axis=0, concat_axis=0, tiled=True
    ).reshape(-1, D)
    per_token = jnp.sum(rows_back[dest_slot].reshape(-1, 2, D), axis=1)
    rows_part = shared_row_grad + per_token
    grad_in_slice = grad_in_local.reshape(1, D, 2, -1)
    grad_down_slice = grad_down_local[None]
    grad_rows_own, grad_gates = (
        lax.psum_scatter(rows_part, INNER, scatter_dimension=0, tiled=True),
        lax.psum_scatter(gate_grad_part, INNER, scatter_dimension=0, tiled=True),
    )
    gate_dot = jnp.sum(gate_values * grad_gates, axis=-1, keepdims=True)
    grad_chosen = gate_values * (grad_gates - gate_dot)
    grad_logits = jnp.sum(grad_chosen[:, :, None] * onehot, axis=1).astype(low_type)
    grad_router = jnp.dot(mixer_low.T, grad_logits, preferred_element_type=jnp.float32)
    grad_normed_two = grad_rows_own + jnp.dot(
        grad_logits, router_all.T, preferred_element_type=jnp.float32
    )
    grad_from_norm, grad_gain_two = norm_backward(
        grad_normed_two, scaled_two, inverse_two, gain_two
    )
    grad_middle = grad_live + grad_from_norm
    grad_att_low = grad_middle.astype(low_type)
    grad_out_w = jnp.dot(context.T, grad_att_low, preferred_element_type=jnp.float32)
    grad_context = (
        jnp.dot(grad_att_low, out_all.T, preferred_element_type=jnp.float32)
        .astype(low_type)
        .reshape(seq_rows, HEADS, HDIM)
    )
    scores_again, allowed_again = attention_scores(query_rows, key_rows, length)
    probs_again = jnp.where(allowed_again[None], jnp.exp(scores_again - log_total), 0.0)
    grad_probs = jnp.einsum(
        "qhd,khd->hqk", grad_context, value_rows, preferred_element_type=jnp.float32
    )
    grad_value = jnp.einsum(
        "hqk,qhd->khd",
        probs_again.astype(low_type),
        grad_context,
        preferred_element_type=jnp.float32,
    )
    row_dot = jnp.sum(grad_probs * probs_again, axis=-1, keepdims=True)
    grad_scores = (probs_again * (grad_probs - row_dot)).astype(low_type)
    grad_query = (
        jnp.einsum("hqk,khd->qhd", grad_scores, key_rows, preferred_element_type=jnp.float32)
        * 0.125
    )
    grad_key = (
        jnp.einsum("hqk,qhd->khd", grad_scores, query_rows, preferred_element_type=jnp.float32)
        * 0.125
    )
    grad_projected = (
        jnp.stack(
            [
                unrotate(grad_query, cosine_table, sine_table),
                unrotate(grad_key, cosine_table, sine_table),
                grad_value,
            ],
            axis=1,
        )
        .reshape(seq_rows, 3 * D)
        .astype(low_type)
    )
    grad_qkv = jnp.dot(normed_low.T, grad_projected, preferred_element_type=jnp.float32)
    grad_normed_one = jnp.dot(grad_projected, qkv_all.T, preferred_element_type=jnp.float32)
    grad_input_norm, grad_gain_one = norm_backward(
        grad_normed_one, scaled_one, inverse_one, gain_one
    )
    input_grad = grad_middle + grad_input_norm
    gains_grad = jnp.stack([grad_gain_one, grad_gain_two], axis=0)
    gains_part, qkv_part, out_part, router_part = (
        lax.psum_scatter(gains_grad, (OUTER, INNER), scatter_dimension=1, tiled=True),
        lax.psum_scatter(grad_qkv, (OUTER, INNER), scatter_dimension=0, tiled=True),
        lax.psum_scatter(grad_out_w, (OUTER, INNER), scatter_dimension=1, tiled=True),
        lax.psum_scatter(grad_router, (OUTER, INNER), scatter_dimension=0, tiled=True),
    )
    shared_in_part, shared_down_part = (
        lax.psum_scatter(
            shared_grad_in.reshape(D, 2, -1).astype(jnp.bfloat16),
            OUTER,
            scatter_dimension=0,
            tiled=True,
        ).astype(jnp.float32),
        lax.psum_scatter(
            shared_grad_down.astype(jnp.bfloat16), OUTER, scatter_dimension=1, tiled=True
        ).astype(jnp.float32),
    )
    gains_new, gains_first_new, gains_second_new = adamw(
        norm_gains, gains_part, gains_first, gains_second, 0.5
    )
    qkv_new, qkv_first_new, qkv_second_new = adamw(
        qkv_weight, qkv_part, qkv_first, qkv_second, 1.5 / math.sqrt(D)
    )
    out_new, out_first_new, out_second_new = adamw(
        out_weight, out_part, out_first, out_second, 1.5 / math.sqrt(4 * D // SEQ)
    )
    router_new, router_first_new, router_second_new = adamw(
        router_weight, router_part, router_first, router_second, 1.0 / math.sqrt(D)
    )
    shin_new, shin_first_new, shin_second_new = adamw(
        shared_in, shared_in_part, shared_in_first, shared_in_second, 1.5 / math.sqrt(D)
    )
    shdown_new, shdown_first_new, shdown_second_new = adamw(
        shared_down, shared_down_part, shared_down_first, shared_down_second, 1.5 / math.sqrt(FF_SH)
    )
    exin_new, exin_first_new, exin_second_new = adamw(
        expert_in, grad_in_slice, expert_in_first, expert_in_second, 1.5 / math.sqrt(D)
    )
    exdown_new, exdown_first_new, exdown_second_new = adamw(
        expert_down, grad_down_slice, expert_down_first, expert_down_second, 1.5 / math.sqrt(FF)
    )
    return (
        layer_out,
        input_grad,
        gains_new,
        gains_first_new,
        gains_second_new,
        qkv_new,
        qkv_first_new,
        qkv_second_new,
        out_new,
        out_first_new,
        out_second_new,
        router_new,
        router_first_new,
        router_second_new,
        shin_new,
        shin_first_new,
        shin_second_new,
        shdown_new,
        shdown_first_new,
        shdown_second_new,
        exin_new,
        exin_first_new,
        exin_second_new,
        exdown_new,
        exdown_first_new,
        exdown_second_new,
    )


MESH = pl.DeviceIdType.MESH
VMEM_BYTES = 61 << 20
GROUPS = 4
PLANE = 8
ALL = GROUPS * PLANE
EXTRA = 16
TURN = (1, 3, 2)


def nn(left, right):
    return jnp.dot(left, right, preferred_element_type=jnp.float32)


def nt(left, right):
    return lax.dot_general(
        left, right, (((1,), (1,)), ((), ())), preferred_element_type=jnp.float32
    )


def tn(left, right):
    return lax.dot_general(
        left, right, (((0,), (0,)), ((), ())), preferred_element_type=jnp.float32
    )


def slot_of(group, member):
    return group * PLANE + (member % 2) * (PLANE // 2) + member // 2


class Place:
    def __init__(self):
        self.group = group = lax.axis_index(OUTER)
        self.member = member = lax.axis_index(INNER)
        self.core = core = member % 2
        column, row = (member // 2) % 2, member // 4
        self.chip = group * (PLANE // 2) + member // 2
        side = 1 - 2 * core
        self.twin = member + side
        beside, across = member + 2 - 4 * column, member + 4 - 8 * row
        self.near = beside * (1 - core) + across * core
        self.far = across * (1 - core) + beside * core
        self.corner = member + (2 - 4 * column) + (4 - 8 * row)
        self.near_twin = self.near + side
        self.far_twin = self.far + side
        self.corner_twin = self.corner + side
        self.mine = slot_of(group, member)

    def around(self, step):
        return (self.group + step) % GROUPS

    def others(self):
        near = [(self.group, self.twin), (self.group, self.near), (self.group, self.far)]
        return near + [(self.around(step), self.member) for step in TURN]

    def tell(self, semaphore):
        for other in self.others():
            pl.semaphore_signal(semaphore, inc=1, device_id=other, device_id_type=MESH)

    def hear(self, semaphore):
        pl.semaphore_wait(semaphore, 6)


class Mover:
    def __init__(self, place, send_sem):
        self.place, self.send_sem, self.sizes = place, send_sem, []

    def copy(self, source, target, index, recv, device):
        return pltpu.make_async_remote_copy(
            src_ref=source,
            dst_ref=target,
            send_sem=self.send_sem.at[index],
            recv_sem=recv,
            device_id=device,
            device_id_type=MESH,
        )

    def send(self, source, target, recv, device):
        self.copy(source, target, len(self.sizes), recv, device).start()
        self.sizes.append(source)

    def arrive(self, target, recv):
        self.copy(target, target, 0, recv, (self.place.group, self.place.twin)).wait_recv()

    def drain(self, unit):
        for index in range(len(self.sizes)):
            self.copy(unit, unit, index, self.send_sem.at[index], (self.place.group, self.place.twin)).wait_send()


class Gather(Mover):
    def __init__(self, place, at, send_sem, recv_sem, pair=True):
        super().__init__(place, send_sem)
        self.at, self.recv_sem, self.pair = at, recv_sem, pair

    def forward(self, group, member, partners):
        for partner in partners:
            if partner is self.place.twin and not self.pair:
                continue
            ref = self.at(group, member)
            self.send(ref, ref, self.recv_sem.at[slot_of(group, member)], (self.place.group, partner))

    def wait(self, group, member):
        self.arrive(self.at(group, member), self.recv_sem.at[slot_of(group, member)])

    def start(self):
        place = self.place
        own = self.at(place.group, place.member)
        for step in TURN:
            self.send(own, own, self.recv_sem.at[place.mine], (place.around(step), place.member))
        self.forward(place.group, place.member, (place.near, place.far, place.twin))

    def own_column(self, step):
        place = self.place
        self.wait(place.around(step), place.member)
        self.forward(place.around(step), place.member, (place.near, place.far, place.twin))

    def near_column(self, step):
        place = self.place
        self.wait(place.around(step), place.near)
        self.forward(place.around(step), place.near, (place.far, place.twin))

    def last_column(self, step, member):
        self.wait(self.place.around(step), member)
        self.forward(self.place.around(step), member, (self.place.twin,))

    def twin_column(self, member):
        for step in (0,) + TURN:
            self.wait(self.place.around(step), member)

    def twin_plane(self, step):
        place = self.place
        for member in (place.twin, place.far_twin, place.near_twin, place.corner_twin):
            self.wait(place.around(step), member)

    def last_plane(self, step):
        for member in (self.place.far, self.place.corner):
            self.last_column(step, member)


class Together:
    def __init__(self, *moves):
        self.moves = moves

    def __getattr__(self, name):
        def each(*given):
            for move in self.moves:
                getattr(move, name)(*given)

        return each


class Scatter(Mover):
    def __init__(self, place, part, rows, bufs, send_sem, sems):
        super().__init__(place, send_sem)
        self.part, self.rows = part, rows
        self.twin_buf, self.far_buf, self.near_buf, self.group_buf = bufs
        self.twin_sem, self.far_sem, self.near_sem, self.group_sem = sems

    def view(self, buf, index):
        return buf.at[index, pl.ds(0, self.rows)]

    def add(self, target, others):
        def some(block, carry):
            at = pl.ds(pl.multiple_of(block * 16, 16), 16)
            total = target[at].astype(jnp.float32)
            for other in others:
                total = total + other[at].astype(jnp.float32)
            target[at] = total.astype(target.dtype)
            return carry

        lax.fori_loop(0, self.rows // 16, some, 0)

    def twin_index(self, group, member):
        return (member // 2) * GROUPS + group

    def to_twin(self, group, member):
        index = self.twin_index(group, member)
        self.send(
            self.part(group, member),
            self.view(self.twin_buf, index),
            self.twin_sem.at[index],
            (self.place.group, self.place.twin),
        )

    def from_twin(self, group, member):
        index = self.twin_index(group, member)
        ready = self.view(self.twin_buf, index)
        self.arrive(ready, self.twin_sem.at[index])
        return ready

    def from_far(self, group, spot):
        other = self.view(self.far_buf, spot * GROUPS + group)
        self.arrive(other, self.far_sem.at[spot * GROUPS + group])
        return other

    def outward(self, step):
        for spot, member in ((0, self.place.corner), (1, self.place.far)):
            group = self.place.around(step)
            ready = self.from_twin(group, member)
            self.add(ready, [self.part(group, member)])
            index = spot * GROUPS + group
            self.send(
                ready,
                self.view(self.far_buf, index),
                self.far_sem.at[index],
                (self.place.group, self.place.far),
            )

    def sideways(self, step):
        group, near = self.place.around(step), self.place.near
        ready = self.from_twin(group, near)
        self.add(ready, [self.part(group, near), self.from_far(group, 0)])
        self.send(
            ready,
            self.view(self.near_buf, group),
            self.near_sem.at[group],
            (self.place.group, near),
        )

    def homeward(self, step):
        group, member = self.place.around(step), self.place.member
        ready = self.from_twin(group, member)
        other = self.view(self.near_buf, group)
        far = self.from_far(group, 1)
        self.arrive(other, self.near_sem.at[group])
        self.add(ready, [self.part(group, member), far, other])
        if step:
            self.send(
                ready,
                self.view(self.group_buf, step - 1),
                self.group_sem.at[step - 1],
                (group, member),
            )

    def finish(self, store):
        for step in TURN:
            self.arrive(self.view(self.group_buf, step - 1), self.group_sem.at[step - 1])
        ready = self.view(self.twin_buf, self.twin_index(self.place.group, self.place.member))

        def some(block, carry):
            at = pl.ds(pl.multiple_of(block * 16, 16), 16)
            total = ready[at].astype(jnp.float32)
            for step in TURN:
                total = total + self.view(self.group_buf, step - 1)[at].astype(jnp.float32)
            store(at, total)
            return carry

        lax.fori_loop(0, self.rows // 16, some, 0)


BACKWARD = (1, 3, 2, 0)


def iota(shape, dim):
    return lax.broadcasted_iota(jnp.int32, shape, dim)


def swap_halves(block):
    lane = iota(block.shape, 1)
    return jnp.where(
        lane % HDIM < HDIM // 2, pltpu.roll(block, 128 - HDIM // 2, 1), pltpu.roll(block, HDIM // 2, 1)
    )


def step_kernel(
    length_ref,
    tokens_hbm,
    cotangent_hbm,
    routes_hbm,
    qkv_hbm,
    out_hbm,
    router_hbm,
    gains_hbm,
    shared_in_hbm,
    shared_down_hbm,
    cosine_hbm,
    sine_hbm,
    expert_in_hbm,
    expert_down_hbm,
    layer_out_hbm,
    input_grad_hbm,
    owned_grad_hbm,
    small_grad_hbm,
    grad_in_hbm,
    grad_down_hbm,
    shared_grad_hbm,
    tokens_ref,
    cotangent_ref,
    routes_ref,
    qkv_ref,
    router_ref,
    gains_ref,
    shared_in_ref,
    shared_down_ref,
    cosine_ref,
    sine_ref,
    owned_ref,
    small_ref,
    small_square,
    layer_out_ref,
    input_grad_ref,
    owned_grad_ref,
    small_grad_ref,
    grad_in_ref,
    grad_down_ref,
    shared_grad_ref,
    pieces_ref,
    stage,
    small_stage,
    mats,
    small_all,
    first_all,
    second_all,
    pieces,
    shared_send,
    weight_in,
    weight_down,
    out_all,
    hidden_low,
    mixed_low,
    pre,
    back_hidden,
    queries,
    keys,
    values,
    probs,
    normed_low,
    context,
    middle_ref,
    mixer,
    rows_sum,
    grad_mid,
    grad_context,
    grad_proj,
    gate_keep,
    twin_a,
    far_a,
    near_a,
    group_a,
    twin_b,
    far_b,
    near_b,
    group_b,
    gate_all,
    gate_part,
    small_part,
    gate_sum,
    twin_g,
    far_g,
    near_g,
    group_g,
    twin_s,
    far_s,
    near_s,
    group_s,
    gate_send,
    gate_recv,
    gate_back_send,
    small_back_send,
    pair_send,
    pair_recv,
    local_sem,
    store_sem,
    mats_send,
    mats_recv,
    small_send,
    small_recv,
    cot_send,
    cot_recv,
    mix_send,
    mix_recv,
    piece_send,
    piece_recv,
    rows_send,
    out_send,
    own_send,
    twin_sems,
    far_sems,
    near_sems,
    group_sems,
    free_sem,
):
    low = jnp.bfloat16
    rows = tokens_ref.shape[0]
    fetched = []
    for source, target in (
        (qkv_hbm, qkv_ref),
        (out_hbm, owned_ref.at[3]),
        (router_hbm, router_ref),
        (gains_hbm, gains_ref),
        (cotangent_hbm, cotangent_ref),
        (tokens_hbm, tokens_ref),
        (routes_hbm, routes_ref),
        (cosine_hbm, cosine_ref),
        (sine_hbm, sine_ref),
        (shared_in_hbm.at[:, 0, :], shared_in_ref.at[0]),
        (shared_in_hbm.at[:, 1, :], shared_in_ref.at[1]),
        (shared_down_hbm, shared_down_ref),
        (expert_in_hbm.at[0, :, 0, :], grad_in_ref.at[:, pl.ds(0, 256)]),
        (expert_in_hbm.at[0, :, 1, :], grad_in_ref.at[:, pl.ds(256, 256)]),
        (expert_down_hbm.at[0], grad_down_ref.at[pl.ds(0, 256)]),
    ):
        fetched.append(pltpu.make_async_copy(source, target, local_sem.at[len(fetched)]))
        fetched[-1].start()
    stored = []

    def store_out(source, target):
        copy = pltpu.make_async_copy(source, target, store_sem.at[len(stored)])
        copy.start()
        stored.append(copy)
    place = Place()
    group, member, core = place.group, place.member, place.core
    barrier = pltpu.get_barrier_semaphore()
    place.tell(barrier)
    place.hear(barrier)

    twin_device = (group, place.twin)
    for name in (0, 1, 2, 3):
        fetched[name].wait()
    for part in range(3):
        owned_ref[part] = qkv_ref[:, D * part : D * part + D]
    small_square[...] = jnp.zeros_like(small_square)
    small_square[pl.ds(0, GROUPS), pl.ds(0, 24)] = router_ref[...]
    small_square[pl.ds(GROUPS, 2), pl.ds(0, 24)] = gains_ref[...]
    small_ref[...] = small_square[...].T[:24]
    own_rows = pl.ds(pl.multiple_of(24 * core, 8), 24)
    owned = pltpu.make_async_remote_copy(
        src_ref=owned_ref.at[pl.ds(2 * (1 - core), 2)],
        dst_ref=stage.at[:, own_rows],
        send_sem=pair_send.at[0],
        recv_sem=pair_recv.at[0],
        device_id=twin_device,
        device_id_type=MESH,
    )
    owned.start()
    small_pair = pltpu.make_async_remote_copy(
        src_ref=small_ref,
        dst_ref=small_stage.at[own_rows],
        send_sem=pair_send.at[1],
        recv_sem=pair_recv.at[1],
        device_id=twin_device,
        device_id_type=MESH,
    )
    small_pair.start()
    stage[:, own_rows] = owned_ref[pl.ds(2 * core, 2)]
    small_stage[own_rows] = small_ref[...]
    owned.wait()
    small_pair.wait()

    def mats_at(group, member):
        chip = group * (PLANE // 2) + member // 2
        return mats.at[pl.ds(2 * (member % 2), 2), pl.ds(pl.multiple_of(48 * chip, 16), 48)]

    def small_at(group, member):
        chip = group * (PLANE // 2) + member // 2
        return small_all.at[pl.ds(pl.multiple_of(48 * chip, 16), 48)]

    mats_at(group, member)[...] = stage[...].astype(low)
    small_at(group, member)[...] = small_stage[...].astype(low)
    send_small = Gather(place, small_at, small_send, small_recv, pair=False)
    send_mats = Gather(place, mats_at, mats_send, mats_recv)
    send_small.start()
    send_mats.start()
    length = length_ref[0]
    row_at = iota((rows, 1), 0)
    live = (row_at < length).astype(jnp.float32)
    fetched[4].wait()
    first_all[place.mine] = (cotangent_ref[...] * live).astype(low)

    send_cot = Gather(
        place,
        lambda group, member: first_all.at[slot_of(group, member)],
        cot_send,
        cot_recv,
    )

    def move_piece(source, target, sems, base):
        for step in TURN:
            pltpu.make_async_remote_copy(
                src_ref=source.at[place.around(step)],
                dst_ref=target.at[group],
                send_sem=piece_send.at[base + step - 1],
                recv_sem=piece_recv.at[base + (GROUPS - step) - 1],
                device_id=(place.around(step), member),
                device_id_type=MESH,
            ).start()
        target[group] = source[group]

    def wait_pieces(source, target, base):
        for step in TURN:
            copy = pltpu.make_async_remote_copy(
                src_ref=source.at[place.around(step)],
                dst_ref=target.at[place.around(step)],
                send_sem=piece_send.at[base + step - 1],
                recv_sem=piece_recv.at[base + step - 1],
                device_id=(place.around(step), member),
                device_id_type=MESH,
            )
            copy.wait()

    for step in (0,) + TURN:
        if step:
            send_small.own_column(step)
            send_mats.own_column(step)
        send_small.near_column(step)
        send_mats.near_column(step)
        if step == 0:
            send_cot.start()

    for name in (9, 10, 11):
        fetched[name].wait()
    for piece in range(GROUPS):
        at = pl.ds(64 * piece, 64)
        both_halves = [shared_in_ref[0, :, at], shared_in_ref[1, :, at]]
        pieces_ref[piece, :, pl.ds(0, 128)] = jnp.concatenate(both_halves, axis=1).astype(low)
        last = shared_down_ref[:, at]
        last = jnp.concatenate([last, jnp.zeros_like(last)], axis=1)
        pieces_ref[piece, :, pl.ds(128, 128)] = last.astype(low)
    move_piece(pieces_ref, pieces, piece_send, 0)

    for name in (12, 13, 14):
        fetched[name].wait()
    weight_in[:, pl.ds(0, 512)] = grad_in_ref[:, pl.ds(0, 512)].astype(low)
    weight_down[pl.ds(0, 256)] = grad_down_ref[pl.ds(0, 256)].astype(low)
    grad_down_ref[...] = jnp.zeros_like(grad_down_ref)
    grad_in_ref[...] = jnp.zeros_like(grad_in_ref)

    for step in (0,) + TURN:
        for origin in (place.far, place.corner):
            send_small.wait(place.around(step), origin)
            send_mats.last_column(step, origin)
    for step in TURN:
        send_cot.own_column(step)
    for origin in (place.twin, place.near_twin, place.far_twin, place.corner_twin):
        send_mats.twin_column(origin)

    for name in (5, 6, 7, 8):
        fetched[name].wait()
    inputs = tokens_ref[...].astype(jnp.float32)
    inverse_one = lax.rsqrt(jnp.mean(inputs * inputs, axis=-1, keepdims=True) + NORM_EPS)
    pick = (iota((8, 128), 1) == iota((8, 128), 0) + GROUPS).astype(low)
    gains = nt(pick, small_all[...])
    gain_one, gain_two = gains[0:1], gains[1:2]
    normed_low[...] = (inputs * inverse_one * gain_one).astype(low)
    for part, target in ((0, queries), (1, keys), (2, values)):
        pre[pl.ds(0, rows)] = nn(normed_low[...], mats[part])
        for block in range(D // 128):
            at = pl.ds(128 * block, 128)
            piece = pre[pl.ds(0, rows), at]
            if part < 2:
                piece = piece * cosine_ref[...] + swap_halves(piece) * sine_ref[...]
            target[:, at] = piece.astype(low)
    for step in (0, 1):
        send_cot.near_column(step)
    diagonal = iota((rows, rows), 0) == iota((rows, rows), 1)
    query_at, key_at = iota((rows, rows), 0), iota((rows, rows), 1)
    allowed = (key_at <= query_at) & (key_at < length)
    lower = iota((rows, 128), 1) < HDIM

    def attend(pair, carry):
        at = pl.ds(pl.multiple_of(pair * 128, 128), 128)
        query, key, value = queries[:, at], keys[:, at], values[:, at]
        found = []
        for half in (0, 1):
            own = lower if half == 0 else jnp.logical_not(lower)
            scores = nt(jnp.where(own, query, jnp.zeros_like(query)), key) * 0.125
            scores = jnp.where(allowed, scores, MASKED)
            exponent = jnp.exp(scores - jnp.max(scores, axis=-1, keepdims=True))
            prob = exponent / jnp.sum(exponent, axis=-1, keepdims=True)
            probs[pair * 2 + half] = prob
            found.append(nn(prob.astype(low), value))
        context[:, at] = jnp.where(lower, found[0], found[1]).astype(low)
        for serve in range(2):

            @pl.when(pair == serve)
            def _():
                send_cot.near_column((3, 2)[serve])

        return carry

    lax.fori_loop(0, HEADS // 2, attend, 0)
    middle = inputs + nt(context[...], mats[3])
    middle_ref[...] = middle
    inverse_two = lax.rsqrt(jnp.mean(middle * middle, axis=-1, keepdims=True) + NORM_EPS)
    mixer[...] = (middle * inverse_two * gain_two).astype(low)
    logits = nn(mixer[...], small_all[...])
    lane = iota((rows, 128), 1)
    chosen, hits = [], []
    for choice in (0, 1):
        row = routes_ref[choice : choice + 1, pl.ds(pl.multiple_of(member * rows, rows), rows)]
        picked = jnp.sum(jnp.where(diagonal, row.astype(jnp.float32), 0.0), axis=1, keepdims=True)
        hit = (lane.astype(jnp.float32) == picked).astype(jnp.float32)
        hits.append(hit)
        chosen.append(jnp.sum(logits * hit, axis=-1, keepdims=True))
    top = jnp.maximum(chosen[0], chosen[1])
    exponents = [jnp.exp(value - top) for value in chosen]
    total = exponents[0] + exponents[1]
    gates = [value / total for value in exponents]
    gate_keep[...] = jnp.where(lane == 0, gates[0], jnp.where(lane == 1, gates[1], 0.0))
    table = sum(gate.astype(low).astype(jnp.float32) * hit for gate, hit in zip(gates, hits))
    second_all[place.mine] = mixer[...]
    gate_all[place.mine] = table.T[:EXTRA].astype(low)
    send_rows = Gather(
        place, lambda group, member: second_all.at[slot_of(group, member)], mix_send, mix_recv
    )
    send_gates = Gather(
        place, lambda group, member: gate_all.at[slot_of(group, member)], gate_send, gate_recv
    )
    send_mix = Together(send_gates, send_rows)
    send_mix.start()
    for step in (0,) + TURN:
        for origin in (place.far, place.corner):
            send_cot.last_column(step, origin)
    for origin in (place.twin, place.near_twin, place.far_twin, place.corner_twin):
        send_cot.twin_column(origin)
    send_cot.drain(first_all.at[0])

    wait_pieces(pieces_ref, pieces, 0)
    first_half = iota((192, 128), 1) < 64
    for piece in range(GROUPS):
        at = pl.ds(192 * piece, 192)
        both_halves = pieces[piece, :, pl.ds(0, 128)].astype(jnp.float32)
        weight_in[at, pl.ds(512, 128)] = jnp.where(first_half, both_halves, 0.0).astype(low)
        other = pltpu.roll(both_halves, 64, 1)
        weight_in[at, pl.ds(640, 128)] = jnp.where(first_half, other, 0.0).astype(low)
    turned = pieces[:, :, pl.ds(128, 128)].reshape(D, 128).astype(jnp.float32)
    weight_down[pl.ds(256, 128)] = turned.T.astype(low)
    big_move = Scatter(
        place,
        lambda group, member: first_all.at[slot_of(group, member)],
        rows,
        (twin_a, far_a, near_a, group_a),
        rows_send,
        (twin_sems.at[0], far_sems.at[0], near_sems.at[0], group_sems.at[0]),
    )
    gate_move = Scatter(
        place,
        lambda group, member: gate_part.at[slot_of(group, member)],
        EXTRA,
        (twin_g, far_g, near_g, group_g),
        gate_back_send,
        (twin_sems.at[3], far_sems.at[3], near_sems.at[3], group_sems.at[3]),
    )
    rows_move = Together(gate_move, big_move)
    out_move = Scatter(
        place,
        lambda group, member: out_all.at[slot_of(group, member)],
        rows,
        (twin_b, far_b, near_b, group_b),
        out_send,
        (twin_sems.at[1], far_sems.at[1], near_sems.at[1], group_sems.at[1]),
    )
    own_expert = (iota((EXTRA, 128), 0) == group).astype(low)
    twins = (place.corner_twin, place.near_twin, place.far_twin, place.twin)

    serve_before = (
        lambda: (
            send_mix.own_column(1),
            send_mix.near_column(1),
            send_mix.own_column(3),
            send_mix.last_plane(1),
        ),
        lambda: (send_mix.near_column(3), send_mix.own_column(2), send_mix.twin_plane(1)),
        lambda: (send_mix.near_column(2), send_mix.near_column(0), send_mix.last_plane(3)),
        lambda: (rows_move.outward(1), send_mix.twin_plane(3)),
        lambda: (rows_move.outward(3), send_mix.last_plane(2)),
        lambda: (rows_move.sideways(1), send_mix.twin_plane(2)),
        lambda: (rows_move.outward(2), send_mix.last_plane(0)),
        lambda: (
            rows_move.sideways(3),
            rows_move.homeward(1),
            send_mix.twin_plane(0),
        ),
    )

    def tokens_part(index, carry):
        for at in range(PLANE):

            @pl.when(index == at)
            def _():
                serve_before[at]()

        half = index // 2
        step = jnp.where(half == 0, 1, jnp.where(half == 1, 3, jnp.where(half == 2, 2, 0)))
        side = (core + index) % 2
        base = pl.multiple_of(place.around(step) * PLANE + side * GROUPS, GROUPS)
        four = pl.ds(base, GROUPS)
        taken = second_all[four].reshape(GROUPS * rows, D)
        pre[...] = nn(taken, weight_in[...])
        cot = first_all[four].reshape(GROUPS * rows, D)
        back_hidden[...] = nt(cot, weight_down[...])

        def units(block, carry):
            slot = base + block
            scale = tn(gate_all[slot], own_expert)
            at = pl.ds(pl.multiple_of(block * rows, rows), rows)
            weigh = jnp.zeros((rows, 128), jnp.float32)
            for gate_at, up_at, hidden_at, routed in (
                (0, 256, 0, True),
                (128, 384, 128, True),
                (512, 640, 256, False),
            ):
                gate_pre = pre[at, pl.ds(gate_at, 128)]
                up_pre = pre[at, pl.ds(up_at, 128)]
                hidden_grad = back_hidden[at, pl.ds(hidden_at, 128)]
                sigmoid_g = 0.5 * jnp.tanh(0.5 * gate_pre) + 0.5
                silu_g = gate_pre * sigmoid_g
                hidden = (silu_g * up_pre).astype(low)
                if routed:
                    wide = hidden.astype(jnp.float32)
                    weigh = weigh + wide * hidden_grad
                    hidden_grad = hidden_grad * scale
                    hidden = (wide * scale).astype(low)
                grad_gate = hidden_grad * up_pre * (sigmoid_g + silu_g * (1.0 - sigmoid_g))
                hidden_low[at, pl.ds(hidden_at, 128)] = hidden
                mixed_low[at, pl.ds(gate_at, 128)] = grad_gate.astype(low)
                mixed_low[at, pl.ds(up_at, 128)] = (hidden_grad * silu_g).astype(low)
            high = weigh.astype(low)
            rest = (weigh - high.astype(jnp.float32)).astype(low)
            gate_part[slot] = nt(own_expert, high) + nt(own_expert, rest)
            return carry

        lax.fori_loop(0, GROUPS, units, 0)
        grad_down_ref[...] += tn(hidden_low[...], cot)
        pre[...] = nt(mixed_low[...], weight_in[...])
        first_all[four] = pre[...].astype(low).reshape(GROUPS, rows, D)
        for at in range(1, PLANE, 2):

            @pl.when(index == at)
            def _():
                for origin in twins:
                    rows_move.to_twin(place.around(BACKWARD[at // 2]), origin)

        taken = second_all[four].reshape(GROUPS * rows, D)
        grad_in_ref[...] += tn(taken, mixed_low[...])
        pre[...] = nn(hidden_low[...], weight_down[...])
        out_all[four] = pre[...].astype(low).reshape(GROUPS, rows, D)
        for at in range(1, PLANE, 2):

            @pl.when(index == at)
            def _():
                for origin in twins:
                    out_move.to_twin(place.around(BACKWARD[at // 2]), origin)

        return carry

    lax.fori_loop(0, PLANE, tokens_part, 0)
    rows_move.outward(0)
    rows_move.sideways(2)
    rows_move.homeward(3)
    rows_move.sideways(0)
    out_move.outward(1)
    rows_move.homeward(2)
    out_move.outward(3)
    rows_move.homeward(0)
    out_move.sideways(1)
    send_rows.drain(second_all.at[0])
    send_gates.drain(gate_all.at[0])

    for piece in range(GROUPS):
        at = pl.ds(192 * piece, 192)
        both_halves = [grad_in_ref[at, pl.ds(512, 64)], grad_in_ref[at, pl.ds(640, 64)]]
        shared_send[piece, :, pl.ds(0, 128)] = jnp.concatenate(both_halves, axis=1).astype(low)
    turned = grad_down_ref[pl.ds(256, 128)].T
    shared_send[:, :, pl.ds(128, 128)] = turned.astype(low).reshape(GROUPS, 192, 128)
    store_out(grad_in_ref.at[:, pl.ds(0, 512)], grad_in_hbm)
    store_out(grad_down_ref.at[pl.ds(0, 256)], grad_down_hbm)

    def keep_rows(at, total):
        rows_sum[at] = total

    def keep_gates(at, total):
        gate_sum[at] = total

    big_move.finish(keep_rows)
    gate_move.finish(keep_gates)
    big_move.drain(first_all.at[0])
    gate_move.drain(gate_part.at[0])
    place.tell(free_sem)
    move_piece(shared_send, shared_grad_ref, piece_send, 3)

    gate_grads = gate_sum[...]
    gate_grads = jnp.concatenate([gate_grads, jnp.zeros((rows - EXTRA, 128), jnp.float32)], axis=0).T
    grad_gates = [jnp.sum(gate_grads * hit, axis=-1, keepdims=True) for hit in hits]
    kept = [
        jnp.sum(jnp.where(lane == choice, gate_keep[...], 0.0), axis=-1, keepdims=True)
        for choice in (0, 1)
    ]
    gate_dot = kept[0] * grad_gates[0] + kept[1] * grad_gates[1]
    grad_logits = sum(
        hit * (gate * (grad - gate_dot)) for hit, gate, grad in zip(hits, kept, grad_gates)
    ).astype(low)
    grad_router = tn(grad_logits, mixer[...])[:8]
    middle = middle_ref[...]
    inverse_two = lax.rsqrt(jnp.mean(middle * middle, axis=-1, keepdims=True) + NORM_EPS)
    scaled_two = middle * inverse_two
    gains = nt(pick, small_all[...])
    gain_one, gain_two = gains[0:1], gains[1:2]
    grad_normed = rows_sum[pl.ds(0, rows)] + nt(grad_logits, small_all[...])
    grad_gain_two = jnp.sum(grad_normed * scaled_two, axis=0, keepdims=True)
    grad_scaled = grad_normed * gain_two
    grad_middle = cotangent_ref[...] * live + inverse_two * (
        grad_scaled - scaled_two * jnp.mean(grad_scaled * scaled_two, axis=-1, keepdims=True)
    )
    grad_mid[...] = grad_middle
    grad_att = grad_middle.astype(low)
    grad_context[...] = nn(grad_att, mats[3]).astype(low)

    mats_move = Scatter(
        place,
        lambda group, member: first_all.at[slot_of(group, member), pl.ds(0, 96)],
        96,
        (twin_a, far_a, near_a, group_a),
        own_send,
        (twin_sems.at[2], far_sems.at[2], near_sems.at[2], group_sems.at[2]),
    )
    small_move = Scatter(
        place,
        lambda group, member: small_part.at[group * (PLANE // 2) + member // 2],
        EXTRA,
        (twin_s, far_s, near_s, group_s),
        small_back_send,
        (twin_sems.at[4], far_sems.at[4], near_sems.at[4], group_sems.at[4]),
    )
    own_move = Together(small_move, mats_move)

    def put_part(which, left, right):
        for half in (0, 1):
            product = tn(left[:, 384 * half : 384 * half + 384], right).astype(low)
            for place_in in range(8):
                chip = half * 8 + place_in
                slot = slot_of(chip // 4, (chip % 4) * 2 + which // 2)
                first_all[slot, pl.ds(48 * (which % 2), 48)] = product[48 * place_in : 48 * place_in + 48]

    put_part(3, grad_att, context[...])

    def attend_back(pair, carry):
        at = pl.ds(pl.multiple_of(pair * 128, 128), 128)
        query, key, value = queries[:, at], keys[:, at], values[:, at]
        grad_ctx = grad_context[:, at]
        grad_query, grad_key, grad_value = [], [], []
        for half in (0, 1):
            own = lower if half == 0 else jnp.logical_not(lower)
            prob = probs[pair * 2 + half]
            grad_prob = nt(jnp.where(own, grad_ctx, jnp.zeros_like(grad_ctx)), value)
            grad_value.append(tn(prob.astype(low), grad_ctx))
            row_dot = jnp.sum(grad_prob * prob, axis=-1, keepdims=True)
            grad_score = (prob * (grad_prob - row_dot)).astype(low)
            grad_query.append(nn(grad_score, key))
            grad_key.append(tn(grad_score, query))
        grad_q = jnp.where(lower, grad_query[0], grad_query[1]) * 0.125
        grad_k = jnp.where(lower, grad_key[0], grad_key[1]) * 0.125
        grad_q = grad_q * cosine_ref[...] - swap_halves(grad_q) * sine_ref[...]
        grad_k = grad_k * cosine_ref[...] - swap_halves(grad_k) * sine_ref[...]
        grad_proj[0, :, at] = grad_q.astype(low)
        grad_proj[1, :, at] = grad_k.astype(low)
        grad_proj[2, :, at] = jnp.where(lower, grad_value[0], grad_value[1]).astype(low)
        serve_pair = (
            lambda: out_move.outward(2),
            lambda: out_move.sideways(3),
            lambda: out_move.outward(0),
            lambda: out_move.homeward(1),
            lambda: out_move.sideways(2),
            lambda: out_move.homeward(3),
        )
        for at_pair, serve in enumerate(serve_pair):

            @pl.when(pair == at_pair)
            def _():
                serve()

        return carry

    lax.fori_loop(0, HEADS // 2, attend_back, 0)
    grad_one = nt(grad_proj[0], mats[0]) + nt(grad_proj[1], mats[1]) + nt(grad_proj[2], mats[2])
    inputs = tokens_ref[...].astype(jnp.float32)
    inverse_one = lax.rsqrt(jnp.mean(inputs * inputs, axis=-1, keepdims=True) + NORM_EPS)
    scaled_one = inputs * inverse_one
    grad_gain_one = jnp.sum(grad_one * scaled_one, axis=0, keepdims=True)
    grad_scaled = grad_one * gain_one
    input_grad_ref[...] = grad_mid[...] + inverse_one * (
        grad_scaled - scaled_one * jnp.mean(grad_scaled * scaled_one, axis=-1, keepdims=True)
    )
    store_out(input_grad_ref, input_grad_hbm)
    for which in range(3):
        put_part(which, normed_low[...], grad_proj[which])
    at_row = iota((8, D), 0)
    small_rows = jnp.where(
        at_row < GROUPS, grad_router, jnp.where(at_row == GROUPS, grad_gain_one, grad_gain_two)
    )
    small_part[...] = jnp.zeros_like(small_part)
    for chip in range(ALL // 2):
        turned = pltpu.roll(small_rows, (D - 48 * chip) % D, 1) if chip else small_rows
        small_part[chip, pl.ds(0, 8)] = turned[:, :128]
    place.hear(free_sem)
    for step in BACKWARD:
        for origin in (place.corner_twin, place.near_twin, place.far_twin, place.twin):
            own_move.to_twin(place.around(step), origin)
    for act, step in (
        (out_move.sideways, 0),
        (own_move.outward, 1),
        (own_move.outward, 3),
        (out_move.homeward, 2),
        (own_move.sideways, 1),
        (own_move.outward, 2),
        (own_move.sideways, 3),
        (own_move.homeward, 1),
        (own_move.outward, 0),
        (out_move.homeward, 0),
        (own_move.sideways, 2),
        (own_move.homeward, 3),
        (own_move.sideways, 0),
        (own_move.homeward, 2),
        (own_move.homeward, 0),
    ):
        act(step)

    def keep_out(at, total):
        here = pl.ds(at.start, 16)
        live_here = (iota((16, 1), 0) + at.start < length).astype(jnp.float32)
        layer_out_ref[here] = live_here * (middle_ref[here] + total)

    out_move.finish(keep_out)
    store_out(layer_out_ref, layer_out_hbm)
    wait_pieces(shared_send, shared_grad_ref, 3)
    store_out(shared_grad_ref, shared_grad_hbm)

    def keep_own(at, total):
        rows_sum[at] = total

    def keep_small(at, total):
        gate_sum[at] = total

    mats_move.finish(keep_own)
    small_move.finish(keep_small)
    for matrix in (0, 1):
        stage[matrix] = rows_sum[pl.ds(48 * matrix, 48)]
    theirs = pl.ds(pl.multiple_of(24 * (1 - core), 8), 24)
    mine = pl.ds(2 * core, 2)
    last = pltpu.make_async_remote_copy(
        src_ref=stage.at[:, theirs],
        dst_ref=owned_grad_ref.at[mine],
        send_sem=pair_send.at[2],
        recv_sem=pair_recv.at[2],
        device_id=twin_device,
        device_id_type=MESH,
    )
    last.start()
    owned_grad_ref[mine] = stage[:, own_rows]
    block = gate_sum[pl.ds(0, 8)]
    small_grad_ref[...] = jnp.where(core == 0, block, pltpu.roll(block, 128 - 24, 1))
    store_out(small_grad_ref, small_grad_hbm)
    last.wait()
    store_out(owned_grad_ref, owned_grad_hbm)
    out_move.drain(out_all.at[0])
    mats_move.drain(first_all.at[0, pl.ds(0, 96)])
    small_move.drain(small_part.at[0])
    send_mats.drain(mats_at(group, member))
    send_small.drain(small_at(group, member))
    for copy in stored:
        copy.wait()


def update_kernel(*refs):
    (
        owned_grad,
        small_grad,
        grad_in,
        grad_down,
        shared_grad,
        layer_in,
        input_in,
    ) = refs[:7]
    olds = [refs[7 + 3 * at : 10 + 3 * at] for at in range(8)]
    layer_out, input_out = refs[31:33]
    news = [refs[33 + 3 * at : 36 + 3 * at] for at in range(8)]
    owned_buf, small_buf, in_buf, down_buf, shared_buf, layer_buf, input_buf = refs[57:64]
    bufs, load_sem, store_sem = refs[64:-2], refs[-2], refs[-1]
    counts = [0, 0]

    def copy(source, target, which):
        made = pltpu.make_async_copy(source, target, (load_sem, store_sem)[which].at[counts[which]])
        counts[which] += 1
        made.start()
        return made

    half = D // 2
    jobs = []
    for at in range(2):
        for block in range(2):
            jobs.append((6, lambda ref, at=at, block=block: ref.at[0, pl.ds(half * block, half), at, :], (half, 256)))
    jobs.append((7, lambda ref: ref.at[0], (256, D)))
    for at in range(2):
        jobs.append((4, lambda ref, at=at: ref.at[:, at, :], (192, 256)))
    for which in (5, 1, 2, 3, 0):
        jobs.append((which, lambda ref: ref, None))
    passes, loaded = [], []
    through = [copy(layer_in, layer_buf, 0), copy(input_in, input_buf, 0)]
    first_grads = [copy(grad_in, in_buf, 0), copy(grad_down, down_buf, 0)]
    other_grads = [copy(shared_grad, shared_buf, 0), copy(owned_grad, owned_buf, 0), copy(small_grad, small_buf, 0)]
    for at, (which, view, _) in enumerate(jobs):
        loaded.append([copy(view(olds[which][k]), bufs[3 * at + k], 0) for k in range(3)])
    for made in first_grads + through:
        made.wait()
    passes += [copy(layer_buf, layer_out, 1), copy(input_buf, input_out, 1)]
    rates = (
        0.5,
        1.5 / math.sqrt(D),
        1.5 / math.sqrt(4 * D // SEQ),
        1.0 / math.sqrt(D),
        1.5 / math.sqrt(D),
        1.5 / math.sqrt(FF_SH),
        1.5 / math.sqrt(D),
        1.5 / math.sqrt(FF),
    )

    def pair_up(part, swap_first, swap_second):
        left = iota((192, 128), 1) < 64
        tiles = []
        for tile in range(2):
            pair = [
                shared_buf[2 * tile + k, :, pl.ds(128 * part, 128)].astype(jnp.float32) for k in (0, 1)
            ]
            if swap_first:
                pair[0] = pltpu.roll(pair[0], 64, 1)
            if swap_second:
                pair[1] = pltpu.roll(pair[1], 64, 1)
            tiles.append(jnp.where(left, pair[0], pair[1]))
        return jnp.concatenate(tiles, axis=1)

    for at, (which, view, shape) in enumerate(jobs):
        if at == 5:
            for made in other_grads:
                made.wait()
        for made in loaded[at]:
            made.wait()
        mine = bufs[3 * at : 3 * at + 3]
        rate = rates[which]

        def update(index, gradient):
            weight, first_old, second_old = (ref[index] for ref in mine)
            results = adamw(weight, gradient, first_old, second_old, rate)
            for ref, value in zip(mine, results):
                ref[index] = value

        if which == 6:
            part, block = at // 2, at % 2

            def chunk(number, carry):
                here = pl.ds(pl.multiple_of(number * 32, 32), 32)
                there = pl.ds(pl.multiple_of(half * block + number * 32, 32), 32)
                update(here, in_buf[there, pl.ds(256 * part, 256)])
                return carry

            lax.fori_loop(0, half // 32, chunk, 0)
        elif which == 7:

            def chunk(number, carry):
                here = pl.ds(pl.multiple_of(number * 8, 8), 8)
                update(here, down_buf[here])
                return carry

            lax.fori_loop(0, 32, chunk, 0)
        elif which == 4:
            update(..., pair_up(0, at == 6, at == 5))
        elif which == 5:
            update(..., pair_up(1, False, True))
        elif which == 1:
            for part in range(3):
                update((slice(None), pl.ds(D * part, D)), owned_buf[part])
        elif which == 2:
            update(..., owned_buf[3])
        elif which == 3:
            update(..., small_buf[:4, :24])
        else:
            update(..., small_buf[4:6, :24])
        for k in range(3):
            passes.append(copy(mine[k], view(news[which][k]), 1))
    for made in passes:
        made.wait()


def dense_shards(
    tokens,
    cotangent,
    lengths,
    routes,
    norm_gains,
    gains_first,
    gains_second,
    qkv_weight,
    qkv_first,
    qkv_second,
    out_weight,
    out_first,
    out_second,
    router_weight,
    router_first,
    router_second,
    shared_in,
    shared_in_first,
    shared_in_second,
    shared_down,
    shared_down_first,
    shared_down_second,
    expert_in,
    expert_in_first,
    expert_in_second,
    expert_down,
    expert_down_first,
    expert_down_second,
):
    low_type = jnp.bfloat16
    seq_rows = tokens.shape[0]
    per_device = D // ALL
    half_dim = HDIM // 2
    positions = np.arange(seq_rows, dtype=np.float32)[:, None]
    angles = positions * np.tile(ROPE_BASE ** (-np.arange(half_dim) / half_dim), 4)[None]
    sign = np.tile(np.repeat([-1.0, 1.0], half_dim), 2)[None]
    cosine = jnp.asarray(np.cos(angles), jnp.float32)
    sine = jnp.asarray(np.sin(angles) * sign, jnp.float32)
    wide, f32, i32 = low_type, jnp.float32, jnp.int32
    dma = pltpu.SemaphoreType.DMA
    anywhere = pl.BlockSpec(memory_space=pltpu.HBM)
    passed = pl.pallas_call(
        step_kernel,
        out_shape=(
            jax.ShapeDtypeStruct((seq_rows, D), f32),
            jax.ShapeDtypeStruct((seq_rows, D), f32),
            jax.ShapeDtypeStruct((4, per_device, D), f32),
            jax.ShapeDtypeStruct((8, 128), f32),
            jax.ShapeDtypeStruct((D, 512), f32),
            jax.ShapeDtypeStruct((256, D), f32),
            jax.ShapeDtypeStruct((GROUPS, 192, 256), wide),
        ),
        in_specs=[pl.BlockSpec(memory_space=pltpu.SMEM)] + [anywhere] * 13,
        out_specs=(anywhere,) * 7,
        scratch_shapes=[
            pltpu.VMEM((seq_rows, D), wide),
            pltpu.VMEM((seq_rows, D), f32),
            pltpu.VMEM((2, PLANE * seq_rows), i32),
            pltpu.VMEM((per_device, 3 * D), f32),
            pltpu.VMEM((GROUPS, per_device), f32),
            pltpu.VMEM((2, per_device), f32),
            pltpu.VMEM((2, 192, 256), f32),
            pltpu.VMEM((192, 256), f32),
            pltpu.VMEM((seq_rows, 128), f32),
            pltpu.VMEM((seq_rows, 128), f32),
            pltpu.VMEM((4, per_device, D), f32),
            pltpu.VMEM((per_device, 128), f32),
            pltpu.VMEM((128, 128), f32),
            pltpu.VMEM((seq_rows, D), f32),
            pltpu.VMEM((seq_rows, D), f32),
            pltpu.VMEM((4, per_device, D), f32),
            pltpu.VMEM((8, 128), f32),
            pltpu.VMEM((D, 768), f32),
            pltpu.VMEM((384, D), f32),
            pltpu.VMEM((GROUPS, 192, 256), wide),
            pltpu.VMEM((GROUPS, 192, 256), wide),
            pltpu.VMEM((2, 48, D), f32),
            pltpu.VMEM((48, 128), f32),
            pltpu.VMEM((4, D, D), wide),
            pltpu.VMEM((D, 128), wide),
            pltpu.VMEM((ALL, seq_rows, D), wide),
            pltpu.VMEM((ALL, seq_rows, D), wide),
            pltpu.VMEM((GROUPS, 192, 256), wide),
            pltpu.VMEM((GROUPS, 192, 256), wide),
            pltpu.VMEM((D, 768), wide),
            pltpu.VMEM((384, D), wide),
            pltpu.VMEM((ALL, seq_rows, D), wide),
            pltpu.VMEM((GROUPS * seq_rows, 384), wide),
            pltpu.VMEM((GROUPS * seq_rows, 768), wide),
            pltpu.VMEM((GROUPS * seq_rows, 768), f32),
            pltpu.VMEM((GROUPS * seq_rows, 384), f32),
            pltpu.VMEM((seq_rows, D), wide),
            pltpu.VMEM((seq_rows, D), wide),
            pltpu.VMEM((seq_rows, D), wide),
            pltpu.VMEM((HEADS, seq_rows, seq_rows), f32),
            pltpu.VMEM((seq_rows, D), wide),
            pltpu.VMEM((seq_rows, D), wide),
            pltpu.VMEM((seq_rows, D), f32),
            pltpu.VMEM((seq_rows, D), wide),
            pltpu.VMEM((seq_rows, D), f32),
            pltpu.VMEM((seq_rows, D), f32),
            pltpu.VMEM((seq_rows, D), wide),
            pltpu.VMEM((3, seq_rows, D), wide),
            pltpu.VMEM((seq_rows, 128), f32),
            pltpu.VMEM((16, seq_rows, D), wide),
            pltpu.VMEM((8, seq_rows, D), wide),
            pltpu.VMEM((4, seq_rows, D), wide),
            pltpu.VMEM((3, seq_rows, D), wide),
            pltpu.VMEM((16, seq_rows, D), wide),
            pltpu.VMEM((8, seq_rows, D), wide),
            pltpu.VMEM((4, seq_rows, D), wide),
            pltpu.VMEM((3, seq_rows, D), wide),
            pltpu.VMEM((ALL, EXTRA, 128), wide),
            pltpu.VMEM((ALL, EXTRA, 128), f32),
            pltpu.VMEM((ALL // 2, EXTRA, 128), f32),
            pltpu.VMEM((EXTRA, 128), f32),
        ]
        + [pltpu.VMEM((count, EXTRA, 128), f32) for count in (16, 8, 4, 3) * 2]
        + [
            dma((31,)),
            dma((32,)),
            dma((31,)),
            dma((31,)),
            dma((3,)),
            dma((3,)),
            dma((15,)),
            dma((7,)),
            dma((31,)),
            dma((32,)),
            dma((31,)),
            dma((32,)),
            dma((31,)),
            dma((32,)),
            dma((31,)),
            dma((32,)),
            dma((6,)),
            dma((6,)),
            dma((31,)),
            dma((31,)),
            dma((31,)),
            dma((5, 16)),
            dma((5, 8)),
            dma((5, 4)),
            dma((5, 3)),
            pltpu.SemaphoreType.REGULAR,
        ],
        compiler_params=pltpu.CompilerParams(
            collective_id=0, has_side_effects=True, vmem_limit_bytes=VMEM_BYTES
        ),
    )(
        lengths,
        tokens,
        cotangent,
        routes.T,
        qkv_weight,
        out_weight.T,
        router_weight.T,
        norm_gains,
        shared_in,
        shared_down.T,
        cosine,
        sine,
        expert_in,
        expert_down,
    )
    layer_out, input_grad, owned_grad, small_grad, grad_in, grad_down, shared_grad = passed
    olds = [
        (norm_gains, gains_first, gains_second),
        (qkv_weight, qkv_first, qkv_second),
        (out_weight.T, out_first.T, out_second.T),
        (router_weight.T, router_first.T, router_second.T),
        (shared_in, shared_in_first, shared_in_second),
        (shared_down.T, shared_down_first.T, shared_down_second.T),
        (expert_in, expert_in_first, expert_in_second),
        (expert_down, expert_down_first, expert_down_second),
    ]
    flat = [old for three in olds for old in three]
    gradients = (owned_grad, small_grad, grad_in, grad_down, shared_grad)
    shapes = [(D // 2, 256)] * 4 + [(256, D)] + [(192, 256)] * 2 + [(192, 256)]
    shapes += [(per_device, 3 * D), (per_device, D), (GROUPS, per_device), (2, per_device)]
    results = pl.pallas_call(
        update_kernel,
        out_shape=tuple(
            jax.ShapeDtypeStruct(value.shape, value.dtype) for value in [layer_out, input_grad] + flat
        ),
        in_specs=[anywhere] * 31,
        out_specs=(anywhere,) * 26,
        scratch_shapes=[pltpu.VMEM(value.shape, value.dtype) for value in gradients + (layer_out, input_grad)]
        + [pltpu.VMEM(shape, f32) for shape in shapes for _ in range(3)]
        + [dma((43,)), dma((38,))],
        compiler_params=pltpu.CompilerParams(vmem_limit_bytes=VMEM_BYTES),
    )(*gradients, layer_out, input_grad, *flat)
    results = list(results)
    for at in (2 + 6, 2 + 9, 2 + 15):
        for k in range(3):
            results[at + k] = results[at + k].T
    return tuple(results)


def solution(mesh):
    outer, inner = OUTER, INNER
    rows, lanes = P((outer, inner), None), P(None, (outer, inner))
    shared_in, shared_down = P(outer, None, inner), P(inner, outer)
    expert_in, expert_down = P(outer, None, None, inner), P(outer, inner, None)
    placed = (
        rows,
        rows,
        P((outer, inner)),
        P(outer, None),
        lanes,
        lanes,
        lanes,
        rows,
        rows,
        rows,
        lanes,
        lanes,
        lanes,
        rows,
        rows,
        rows,
        shared_in,
        shared_in,
        shared_in,
        shared_down,
        shared_down,
        shared_down,
        expert_in,
        expert_in,
        expert_in,
        expert_down,
        expert_down,
        expert_down,
    )
    return jax.shard_map(
        dense_shards if (mesh.shape[outer], mesh.shape[inner]) == (4, 8) else routed_shards,
        mesh=mesh,
        in_specs=placed,
        out_specs=(
            rows,
            rows,
            lanes,
            lanes,
            lanes,
            rows,
            rows,
            rows,
            lanes,
            lanes,
            lanes,
            rows,
            rows,
            rows,
            shared_in,
            shared_in,
            shared_in,
            shared_down,
            shared_down,
            shared_down,
            expert_in,
            expert_in,
            expert_in,
            expert_down,
            expert_down,
            expert_down,
        ),
        check_vma=False,
    )
```
